32 devices in a mesh: dp: 4 (over y, core), ctx: 8 (over z, x).
Axes of the slice: x: 2, y: 2, z: 4, core: 2. Of those that a mesh axis runs over, the one named last changes fastest.
Arguments:
- tokens: bfloat16 [2, 4, 1024, 768], P(None, 'dp', 'ctx'), may hold values from -6 to 6
- lengths: int32 [2, 4], P(None, 'dp'), may hold values from 513 to 1024, as said below
- routes: int32 [2, 4, 1024, 2], P(None, 'dp', 'ctx'), may hold values from 0 to 3, all different within a row
- cotangent: bfloat16 [2, 4, 1024, 768], P(None, 'dp', 'ctx'), may hold values from -6 to 6
- attn_gain: bfloat16 [768], P(('dp', 'ctx')), may hold values from 0.5 to 1.5
- attn_in: bfloat16 [768, 2304], P(('dp', 'ctx')), may hold values from -0.21875 to 0.21875
- attn_out: bfloat16 [768, 768], P(('dp', 'ctx')), may hold values from -3.5 to 3.5
- ffn_gain: bfloat16 [768], P(('dp', 'ctx')), may hold values from 0.5 to 1.5
- router: bfloat16 [768, 4], P(('dp', 'ctx')), may hold values from -0.21875 to 0.21875
- dense_in: bfloat16 [768, 4096], P(('dp', 'ctx')), may hold values from -0.21875 to 0.21875
- dense_out: bfloat16 [2048, 768], P(('dp', 'ctx')), may hold values from -0.125 to 0.125
- expert_in: bfloat16 [768, 4, 4096], P(('dp', 'ctx')), may hold values from -0.21875 to 0.21875
- expert_out: bfloat16 [2048, 4, 768], P(('dp', 'ctx')), may hold values from -0.125 to 0.125
Outputs:
- activations: bfloat16 [2, 4, 1024, 768], P(None, 'dp', 'ctx')
- input_grad: bfloat16 [2, 4, 1024, 768], P(None, 'dp', 'ctx')
- attn_gain_grad: float32 [768], P(('dp', 'ctx'))
- attn_in_grad: float32 [768, 2304], P(('dp', 'ctx'))
- attn_out_grad: float32 [768, 768], P(('dp', 'ctx'))
- ffn_gain_grad: float32 [768], P(('dp', 'ctx'))
- router_grad: float32 [768, 4], P(('dp', 'ctx'))
- dense_in_grad: float32 [768, 4096], P(('dp', 'ctx'))
- dense_out_grad: float32 [2048, 768], P(('dp', 'ctx'))
- expert_in_grad: float32 [768, 4, 4096], P(('dp', 'ctx'))
- expert_out_grad: float32 [2048, 4, 768], P(('dp', 'ctx'))
The draws below stay inside these ranges and needn't reach their ends.
Inputs may be any that keep to these rules, and one draw needn't show every extreme that they name: `lengths`: the first sequence of every micro-batch is valid in all 1024 slots. `routes`: each slot names two different experts.
All inputs are finite; a program needn't handle non-finite values.
Results may differ from the reference program's by a relative error of at most 0.014.
Values may be sent and summed in bfloat16 or wider, within the bound.
A program may use at most 384 MiB of HBM per device.

```python
import jax
import jax.numpy as jnp
from jax import lax

D = 768
HEADS = 12
HEAD_DIM = 64
FF = 2048
EXPERTS = 4
MICRO = 2
LEN = 1024
SEQS = 4


def draw_lengths(key, part):
    counts = jax.random.randint(key, (MICRO, SEQS), LEN // 2 + 1, LEN + 1)
    return counts.at[:, 0].set(LEN).astype(jnp.int32)


def level_of(key, dims, split, low, high):
    def one(axis_at, parts):
        draws = jax.random.uniform(jax.random.fold_in(jax.random.fold_in(key, 6), axis_at), (parts,), jnp.float32, low / len(split), high / len(split))
        return jnp.repeat(jnp.exp(draws), dims[axis_at] // parts).reshape((-1,) + (1,) * (len(dims) - axis_at - 1))

    level = one(*split[0])
    for cut in split[1:]:
        level = level * one(*cut)
    return level


def picks_of(rng, rows, number_of, top, lift):
    sequence = jax.random.permutation(jax.random.fold_in(rng, 1), number_of)
    favour = sequence
    for power in range(3):
        favour = favour * favour // number_of
    favour = favour * lift // number_of
    lots = jax.random.randint(jax.random.fold_in(rng, 2), (rows, number_of), 0, 4096) + favour
    holders = jax.random.permutation(jax.random.fold_in(rng, 3), rows)[jnp.arange(number_of) % rows]
    lots = jnp.where(jnp.arange(rows)[:, None] == holders[None, :], 1 << 14, lots)
    priority = lots * number_of + jnp.arange(number_of)
    return lax.top_k(priority.astype(jnp.int32), top)[1].astype(jnp.int32)


def bell_draw(rng, extent, scale, most, split=(), kind=jnp.bfloat16):
    values = scale * jax.random.normal(rng, extent, jnp.float32)
    if split:
        values = values * level_of(rng, extent, split, -0.22, 0.18)
    return jnp.clip(values, -most, most).astype(kind)


def setup_inputs(seed: int = 0) -> dict:
    keys = jax.random.split(jax.random.key(seed), 14)
    return {
        "tokens": bell_draw(keys[0], (MICRO, SEQS, LEN, D), 1.0, 6.0, ((1, 4), (2, 8))),
        "lengths": draw_lengths(jax.random.fold_in(keys[13], 71), 0),
        "routes": picks_of(keys[2], MICRO * SEQS * LEN, EXPERTS, 2, 4096).reshape((MICRO, SEQS, LEN, 2)),
        "cotangent": bell_draw(keys[3], (MICRO, SEQS, LEN, D), 1.0, 6.0, ((1, 4), (2, 8))),
        "attn_gain": jnp.clip(1.0 + 0.1 * jax.random.normal(keys[4], (D,), jnp.float32), 0.5, 1.5).astype(jnp.bfloat16),
        "attn_in": bell_draw(keys[5], (D, 3 * D), D ** -0.5, 0.21875, ((0, 32),)),
        "attn_out": bell_draw(keys[6], (D, D), (max(D // 256, 1)) ** -0.5, 3.5, ((0, 32),)),
        "ffn_gain": jnp.clip(1.0 + 0.1 * jax.random.normal(keys[7], (D,), jnp.float32), 0.5, 1.5).astype(jnp.bfloat16),
        "router": bell_draw(keys[8], (D, EXPERTS), D ** -0.5, 0.21875, ((0, 32),)),
        "dense_in": bell_draw(keys[9], (D, 2 * FF), D ** -0.5, 0.21875, ((0, 32),)),
        "dense_out": bell_draw(keys[10], (FF, D), FF ** -0.5, 0.125, ((0, 32),)),
        "expert_in": bell_draw(keys[11], (D, EXPERTS, 2 * FF), D ** -0.5, 0.21875, ((0, 32),)),
        "expert_out": bell_draw(keys[12], (FF, EXPERTS, D), FF ** -0.5, 0.125, ((0, 32),)),
    }


precise = lax.Precision.HIGHEST
epsilon = 1e-05

@jax.custom_vjp
def low(v):
    return lax.optimization_barrier(v.astype(jnp.bfloat16)).astype(jnp.float32)

@jax.custom_vjp
def low_back(v):
    return v

def low_keep(v):
    return (low(v), None)

def low_pass(kept, grad):
    return (grad,)

def back_keep(v):
    return (v, None)

def back_low(kept, grad):
    return (low(grad),)
low.defvjp(low_keep, low_pass)
low_back.defvjp(back_keep, back_low)

def product(left, right):
    return jnp.matmul(left, right, precision=precise)

def norm_rows(row_data, gain_row):
    inverse = lax.rsqrt(lax.optimization_barrier(jnp.mean(row_data * row_data, axis=-1, keepdims=True)) + epsilon)
    return row_data * inverse * gain_row

def rotate(values, places, direction_sign):
    half_dim = values.shape[-1] // 2
    frequency = 10000.0 ** (-jnp.arange(half_dim, dtype=jnp.float32) / half_dim)
    angles = places.astype(jnp.float32)[:, None] * frequency[None, :]
    cosine = jnp.cos(angles)[:, None, :]
    sine_part = direction_sign * jnp.sin(angles)[:, None, :]
    leading = values[..., :half_dim]
    trailing = values[..., half_dim:]
    return jnp.concatenate([leading * cosine - trailing * sine_part, trailing * cosine + leading * sine_part], axis=-1)

def swiglu(normed, weight_in, weight_out):
    pre_act = low_back(product(normed, weight_in))
    activated = low(jax.nn.silu(pre_act[..., :FF]) * pre_act[..., FF:])
    return low_back(product(activated, weight_out))

def reference(tokens, lengths, routes, cotangent, attn_gain, attn_in, attn_out, ffn_gain, router, dense_in, dense_out, expert_in, expert_out):
    seq_total = MICRO * SEQS
    slot_index = jnp.arange(LEN, dtype=jnp.int32)
    flat_lengths = lengths.reshape(seq_total).astype(jnp.int32)
    choose = (routes.reshape(seq_total, LEN, 2)[..., None] == jnp.arange(EXPERTS, dtype=jnp.int32)).astype(jnp.float32)
    valid_rows = (slot_index[None, :] < flat_lengths[:, None]).astype(jnp.float32)

    def attend(packed):
        queries, key_rows, value_rows, length_one = packed
        scores = low_back(jnp.einsum('qhd,khd->hqk', queries, key_rows, precision=precise) * 0.125)
        allowed = (slot_index[None, :] <= slot_index[:, None]) & (slot_index[None, :] < length_one)
        scores = jnp.where(allowed[None], scores, -1000000000.0)
        probabilities = low(jax.nn.softmax(scores, axis=-1))
        return jnp.einsum('hqk,khd->qhd', probabilities, value_rows, precision=precise)

    def forward(inputs, gain_one, weight_qkv, weight_mix, gain_two, weight_route, dense_up, dense_down, experts_up_raw, experts_down_raw):
        experts_up = jnp.moveaxis(experts_up_raw, 1, 0)
        experts_down = jnp.moveaxis(experts_down_raw, 1, 0)
        shape_heads = (seq_total, LEN, HEADS, HEAD_DIM)
        normed = low(norm_rows(inputs, gain_one))
        projected = product(normed, weight_qkv)
        queries = low(rotate(low_back(projected[..., :D]).reshape(shape_heads), slot_index, 1.0))
        key_rows = low(rotate(low_back(projected[..., D:2 * D]).reshape(shape_heads), slot_index, 1.0))
        value_rows = low(low_back(projected[..., 2 * D:])).reshape(shape_heads)
        attended = lax.map(jax.checkpoint(attend), (queries, key_rows, value_rows, flat_lengths))
        attended = low(low_back(attended.reshape(seq_total, LEN, D)))
        middle = inputs + low_back(product(attended, weight_mix))
        normed_two = low(norm_rows(middle, gain_two))
        logits = low_back(product(normed_two, weight_route))
        picked = lax.optimization_barrier(jnp.sum(choose * logits[..., None, :], axis=-1))
        gate_probs = jax.nn.softmax(picked, axis=-1)
        mixing = lax.optimization_barrier(jnp.sum(gate_probs[..., None] * choose, axis=-2))
        dense_branch = swiglu(normed_two, dense_up, dense_down)

        def one_expert(pair):
            return swiglu(normed_two, pair[0], pair[1])
        expert_rows = lax.map(jax.checkpoint(one_expert), (experts_up, experts_down))
        expert_sum = jnp.einsum('nle,enld->nld', mixing, expert_rows, precision=precise)
        return middle + dense_branch + expert_sum
    inputs = tokens.reshape(seq_total, LEN, D).astype(jnp.float32)
    result, pullback = jax.vjp(forward, inputs, attn_gain.astype(jnp.float32), attn_in.astype(jnp.float32), attn_out.astype(jnp.float32), ffn_gain.astype(jnp.float32), router.astype(jnp.float32), dense_in.astype(jnp.float32), dense_out.astype(jnp.float32), expert_in.astype(jnp.float32), expert_out.astype(jnp.float32))
    seed_rows = cotangent.reshape(seq_total, LEN, D).astype(jnp.float32) * valid_rows[..., None]
    gradients = pullback(seed_rows)
    activations = result.astype(jnp.bfloat16).reshape(MICRO, SEQS, LEN, D)
    input_grad = gradients[0].astype(jnp.bfloat16).reshape(MICRO, SEQS, LEN, D)
    return (activations, input_grad, gradients[1], gradients[2], gradients[3], gradients[4], gradients[5], gradients[6], gradients[7], gradients[8], gradients[9])
```

```python
import functools

import jax
import jax.numpy as jnp
import numpy as np
from jax import lax
from jax.experimental import pallas as pl
from jax.experimental.pallas import tpu as pltpu
from jax.sharding import PartitionSpec as P

HEADS = 12
HEAD_DIM = 64
FF = 2048
EPSILON = 1e-05
HALVES = 2
QUERY_ROWS = 256
MIX_ROWS = 16
MESH = pl.DeviceIdType.MESH
BF16 = jnp.bfloat16
F32 = jnp.float32


def round_up(value, step):
    return -(-value // step) * step


class Plan:
    def __init__(self, dp, ctx, block, width, experts):
        self.dp, self.ctx, self.block, self.width, self.experts = dp, ctx, block, width, experts
        self.quad = ctx // HALVES
        self.devices = dp * ctx
        self.group = dp * self.quad
        self.slots = ctx * block
        self.rows = width // self.devices
        self.heads = -(-HEADS // self.quad)
        self.head_cols = self.heads * HEAD_DIM
        self.qkv_cols = 3 * self.head_cols
        self.wide = round_up(self.qkv_cols + 2 + experts, 128)
        self.own_hidden = FF // self.devices
        self.branches = 1 + experts
        self.hidden = self.branches * HALVES * self.own_hidden
        self.hidden_pad = round_up(self.hidden, 128)
        self.local = HALVES * block


def place():
    return lax.axis_index("dp"), lax.axis_index("ctx")


def params(collective_id=None, limit=60 * 1024 * 1024):
    if collective_id is None:
        return pltpu.CompilerParams(vmem_limit_bytes=limit)
    return pltpu.CompilerParams(
        vmem_limit_bytes=limit, collective_id=collective_id, has_side_effects=True
    )


def remote(src, dst, send_sem, recv_sem, device):
    return pltpu.make_async_remote_copy(
        src_ref=src,
        dst_ref=dst,
        send_sem=send_sem,
        recv_sem=recv_sem,
        device_id=device,
        device_id_type=MESH,
    )


def meet(devices):
    barrier = pltpu.get_barrier_semaphore()
    for device in devices:
        pl.semaphore_signal(barrier, inc=1, device_id=device, device_id_type=MESH)
    pl.semaphore_wait(barrier, len(devices))


def other_devices(plan, dp, ctx):
    flat = dp * plan.ctx + ctx
    result = []
    for step in range(1, plan.devices):
        target = lax.rem(flat + step, plan.devices)
        result.append((lax.div(target, plan.ctx), lax.rem(target, plan.ctx)))
    return result


def quad_members(plan, half, member):
    return [
        (half * plan.quad + lax.rem(member + step, plan.quad), lax.rem(member + step, plan.quad))
        for step in range(1, plan.quad)
    ]


VMEM = pl.BlockSpec(memory_space=pltpu.VMEM)
HBM = pl.BlockSpec(memory_space=pl.ANY)
DMA = pltpu.SemaphoreType.DMA


def spread_kernel(plan, tok, wq, win, xs, wall, winh, x_send, x_recv, q_send, q_recv, f_send, f_recv):
    dp, ctx = place()
    half, member = lax.div(ctx, plan.quad), lax.rem(ctx, plan.quad)
    far = (1 - half) * plan.quad + member
    flat = dp * plan.ctx + ctx
    mine = dp * plan.quad + member
    others = other_devices(plan, dp, ctx)
    meet(others)
    copies = []

    swap = remote(tok.at[1 - half], xs.at[ctx], x_send.at[0], x_recv.at[0], (dp, far))
    swap.start()
    members = quad_members(plan, half, member)
    count = len(members)
    for i, (peer, _) in enumerate(members):
        copy = remote(tok.at[half], xs.at[ctx], x_send.at[1 + i], x_recv.at[1 + i], (dp, peer))
        copy.start()
        copies.append(copy)
    for i, (tdp, tctx) in enumerate(others):
        copy = remote(
            wq.at[lax.rem(tctx, plan.quad)], wall.at[flat], q_send.at[i], q_recv.at[i], (tdp, tctx)
        )
        copy.start()
        copies.append(copy)
    for i in range(plan.group - 1):
        target = lax.rem(mine + 1 + i, plan.group)
        tdp, tmember = lax.div(target, plan.quad), lax.rem(target, plan.quad)
        copy = remote(
            win.at[target],
            winh.at[mine],
            f_send.at[i],
            f_recv.at[i],
            (tdp, half * plan.quad + tmember),
        )
        copy.start()
        copies.append(copy)
    xs[pl.ds(ctx, 1)] = tok[pl.ds(half, 1)]
    wall[pl.ds(flat, 1)] = wq[pl.ds(member, 1)]
    winh[pl.ds(mine, 1)] = win[pl.ds(mine, 1)]
    swap.wait()
    for i, (peer, _) in enumerate(members):
        copy = remote(
            xs.at[far], xs.at[far], x_send.at[1 + count + i], x_recv.at[1 + count + i], (dp, peer)
        )
        copy.start()
        copies.append(copy)
    for copy in copies:
        copy.wait()


def spread(plan, tok, wq, win):
    count = 2 * plan.quad - 1
    return pl.pallas_call(
        functools.partial(spread_kernel, plan),
        out_shape=(
            jax.ShapeDtypeStruct((plan.ctx, plan.block, plan.width), BF16),
            jax.ShapeDtypeStruct((plan.devices, plan.rows, plan.wide), BF16),
            jax.ShapeDtypeStruct((plan.group, plan.rows, 2 * plan.hidden_pad), BF16),
        ),
        in_specs=[VMEM] * 3,
        out_specs=(VMEM,) * 3,
        scratch_shapes=[
            DMA((count,)),
            DMA((count,)),
            DMA((plan.devices - 1,)),
            DMA((plan.devices - 1,)),
            DMA((plan.group - 1,)),
            DMA((plan.group - 1,)),
        ],
        compiler_params=params(1),
        name="spread",
    )(tok, wq, win)


def to_slots_kernel(plan, src, dst, send, recv):
    dp, ctx = place()
    half, member = lax.div(ctx, plan.quad), lax.rem(ctx, plan.quad)
    far = (1 - half) * plan.quad + member
    members = quad_members(plan, half, member)
    meet([(dp, peer) for peer, _ in members])
    copies = []
    for i, (peer, to) in enumerate(members):
        for j, at in enumerate((ctx, far)):
            copy = remote(
                src.at[to, j], dst.at[at], send.at[2 * i + j], recv.at[2 * i + j], (dp, peer)
            )
            copy.start()
            copies.append(copy)
    dst[pl.ds(ctx, 1)] = src[pl.ds(member, 1), 0]
    dst[pl.ds(far, 1)] = src[pl.ds(member, 1), 1]
    for copy in copies:
        copy.wait()


def to_slots(plan, value, collective_id):
    count = 2 * (plan.quad - 1)
    return pl.pallas_call(
        functools.partial(to_slots_kernel, plan),
        out_shape=jax.ShapeDtypeStruct((plan.ctx, plan.block, value.shape[-1]), value.dtype),
        in_specs=[VMEM],
        out_specs=VMEM,
        scratch_shapes=[DMA((count,)), DMA((count,))],
        compiler_params=params(collective_id),
        name="to_slots",
    )(value)


def send_to_owners(plan, dp, half, member, src, dst, send, recv):
    copies = []
    for i, (peer, to) in enumerate(quad_members(plan, half, member)):
        for j, at in enumerate((half * plan.quad + to, (1 - half) * plan.quad + to)):
            copy = remote(
                src.at[at], dst.at[member, j], send.at[2 * i + j], recv.at[2 * i + j], (dp, peer)
            )
            copy.start()
            copies.append(copy)
    return copies


def to_owners_kernel(plan, src, dst, send, recv):
    dp, ctx = place()
    half, member = lax.div(ctx, plan.quad), lax.rem(ctx, plan.quad)
    far = (1 - half) * plan.quad + member
    meet([(dp, peer) for peer, _ in quad_members(plan, half, member)])
    copies = send_to_owners(plan, dp, half, member, src, dst, send, recv)
    dst[pl.ds(member, 1), 0] = src[pl.ds(ctx, 1)]
    dst[pl.ds(member, 1), 1] = src[pl.ds(far, 1)]
    for copy in copies:
        copy.wait()


def to_owners(plan, value, collective_id):
    count = 2 * (plan.quad - 1)
    return pl.pallas_call(
        functools.partial(to_owners_kernel, plan),
        out_shape=jax.ShapeDtypeStruct((plan.quad, 2, plan.block, value.shape[-1]), value.dtype),
        in_specs=[VMEM],
        out_specs=VMEM,
        scratch_shapes=[DMA((count,)), DMA((count,))],
        compiler_params=params(collective_id),
        name="to_owners",
    )(value)


def collect_kernel(plan, dnp, dwq, dwo, dwin, rdn, rwq, rwo, rwin, n_send, n_recv, q_send, q_recv, o_send, o_recv, f_send, f_recv):
    dp, ctx = place()
    half, member = lax.div(ctx, plan.quad), lax.rem(ctx, plan.quad)
    far = (1 - half) * plan.quad + member
    flat = dp * plan.ctx + ctx
    mine = dp * plan.quad + member
    others = other_devices(plan, dp, ctx)
    meet(others)
    copies = send_to_owners(plan, dp, half, member, dnp, rdn, n_send, n_recv)
    for i, (tdp, tctx) in enumerate(others):
        to = tdp * plan.ctx + tctx
        copy = remote(dwq.at[to], rwq.at[flat], q_send.at[i], q_recv.at[i], (tdp, tctx))
        copy.start()
        copies.append(copy)
        copy = remote(dwo.at[to], rwo.at[flat], o_send.at[i], o_recv.at[i], (tdp, tctx))
        copy.start()
        copies.append(copy)
    for i in range(plan.group - 1):
        target = lax.rem(mine + 1 + i, plan.group)
        tdp, tmember = lax.div(target, plan.quad), lax.rem(target, plan.quad)
        copy = remote(
            dwin.at[target],
            rwin.at[mine],
            f_send.at[i],
            f_recv.at[i],
            (tdp, half * plan.quad + tmember),
        )
        copy.start()
        copies.append(copy)
    rdn[pl.ds(member, 1), 0] = dnp[pl.ds(ctx, 1)]
    rdn[pl.ds(member, 1), 1] = dnp[pl.ds(far, 1)]
    rwq[pl.ds(flat, 1)] = dwq[pl.ds(flat, 1)]
    rwo[pl.ds(flat, 1)] = dwo[pl.ds(flat, 1)]
    rwin[pl.ds(mine, 1)] = dwin[pl.ds(mine, 1)]
    for copy in copies:
        copy.wait()


def collect(plan, dnp, dwq, dwo, dwin):
    count = 2 * (plan.quad - 1)
    return pl.pallas_call(
        functools.partial(collect_kernel, plan),
        out_shape=(
            jax.ShapeDtypeStruct((plan.quad, 2, plan.block, plan.width), BF16),
            jax.ShapeDtypeStruct(dwq.shape, BF16),
            jax.ShapeDtypeStruct(dwo.shape, BF16),
            jax.ShapeDtypeStruct(dwin.shape, BF16),
        ),
        in_specs=[VMEM] * 4,
        out_specs=(VMEM,) * 4,
        scratch_shapes=[
            DMA((count,)),
            DMA((count,)),
            DMA((plan.devices - 1,)),
            DMA((plan.devices - 1,)),
            DMA((plan.devices - 1,)),
            DMA((plan.devices - 1,)),
            DMA((plan.group - 1,)),
            DMA((plan.group - 1,)),
        ],
        compiler_params=params(6),
        name="collect",
    )(dnp, dwq, dwo, dwin)


class Grid:
    def __init__(self, plan):
        self.plan = plan
        self.sizes = {"y": plan.dp // 2, "high": plan.quad // 2, "low": 2}

    def here(self):
        dp, ctx = place()
        member = lax.rem(ctx, self.plan.quad)
        return {
            "core": lax.rem(dp, 2),
            "y": lax.div(dp, 2),
            "high": lax.div(member, 2),
            "low": lax.rem(member, 2),
            "half": lax.div(ctx, self.plan.quad),
        }

    def device(self, at):
        return (
            at["y"] * 2 + at["core"],
            at["half"] * self.plan.quad + at["high"] * 2 + at["low"],
        )

    def block(self, at):
        return (at["y"] * 2 + at["core"]) * self.plan.quad + at["high"] * 2 + at["low"]

    def moved(self, at, axis, step):
        result = dict(at)
        if axis == "core":
            result["core"] = 1 - at["core"]
        else:
            result[axis] = lax.rem(at[axis] + step, self.sizes[axis])
        return result

    def peers(self, at):
        result = [self.moved(at, "core", 1)]
        for axis, size in self.sizes.items():
            result += [self.moved(at, axis, step) for step in range(1, size)]
        return [self.device(peer) for peer in result]

    def slot(self, offsets):
        return (offsets["y"] * self.sizes["high"] + offsets["high"]) * 2 + offsets["low"]


GATHER_ORDERS = (("high", "low", "y"), ("low", "y", "high"))


def gather_kernel(plan, src, dst, send, recv, core_send, core_recv):
    grid = Grid(plan)
    at = grid.here()
    meet(grid.peers(at))
    dst[pl.ds(grid.block(at), 1)] = src[...][None]
    zero = {"y": 0, "high": 0, "low": 0}

    def run(order):
        levels = [[dict(zero)], [], [], []]
        for level, axis in enumerate(order):
            base = [o for group in levels[: level + 1] for o in group]
            for offsets in base:
                for step in range(1, grid.sizes[axis]):
                    levels[level + 1].append({**offsets, axis: step})
        sends = []
        counter = [0]

        def absolute(offsets):
            where = dict(at)
            for axis, step in offsets.items():
                if step:
                    where = grid.moved(where, axis, step)
            return where

        for level, group in enumerate(levels):
            for offsets in group:
                where = absolute(offsets)
                block = grid.block(where)
                if level:
                    remote(dst.at[block], dst.at[block], send.at[0], recv.at[grid.slot(offsets)], grid.device(at)).wait_recv()
                source = src if level == 0 else dst.at[block]
                for axis in order[level:]:
                    for step in range(1, grid.sizes[axis]):
                        seen = {**offsets, axis: grid.sizes[axis] - step}
                        copy = remote(
                            source,
                            dst.at[block],
                            send.at[counter[0]],
                            recv.at[grid.slot(seen)],
                            grid.device(grid.moved(at, axis, step)),
                        )
                        copy.start()
                        counter[0] += 1
                        sends.append(copy)
                copy = remote(
                    source,
                    dst.at[block],
                    core_send.at[grid.slot(offsets)],
                    core_recv.at[grid.slot(offsets)],
                    grid.device(grid.moved(at, "core", 1)),
                )
                copy.start()
                sends.append(copy)
        for copy in sends:
            copy.wait_send()
        for slot in range(plan.group // 2):
            remote(src, dst.at[0], core_send.at[slot], core_recv.at[slot], grid.device(at)).wait_recv()

    for color, order in enumerate(GATHER_ORDERS):
        pl.when(at["core"] == color)(functools.partial(run, order))


def gather_sends(plan, order):
    sizes = Grid(plan).sizes
    held, total = 1, 0
    for axis in order:
        total += held * (sizes[axis] - 1)
        held *= sizes[axis]
    return total


def gather(plan, block, collective_id):
    half = plan.group // 2
    count = max(gather_sends(plan, order) for order in GATHER_ORDERS)
    return pl.pallas_call(
        functools.partial(gather_kernel, plan),
        out_shape=jax.ShapeDtypeStruct((plan.group,) + block.shape, block.dtype),
        in_specs=[VMEM],
        out_specs=VMEM,
        scratch_shapes=[DMA((count,)), DMA((half,)), DMA((half,)), DMA((half,))],
        compiler_params=params(collective_id),
        name="gather",
    )(block)


def reduce_kernel(plan, src, out, work, core_buf, bufs, load_sem, core_send, core_recv, send, recv):
    grid = Grid(plan)
    at = grid.here()
    zero = {"y": 0, "high": 0, "low": 0}
    meet(grid.peers(at))

    def run(order):
        levels = [[], [], [], []]
        held = [dict(zero)]
        levels[3] = [dict(zero)]
        for level in (2, 1, 0):
            axis = order[level]
            base = [o for later in levels[level + 1 :] for o in later]
            levels[level] = [
                {**offsets, axis: step} for offsets in base for step in range(1, grid.sizes[axis])
            ]
        del held

        def absolute(offsets):
            where = dict(at)
            for axis, step in offsets.items():
                if step:
                    where = grid.moved(where, axis, step)
            return where

        sequence = [o for group in levels for o in group]
        partner = grid.device(grid.moved(at, "core", 1))
        core_copies = []
        loads = []
        for offsets in sequence:
            where = absolute(offsets)
            slot = grid.slot(offsets)
            copy = remote(
                src.at[grid.block(grid.moved(where, "core", 1))],
                core_buf.at[slot],
                core_send.at[slot],
                core_recv.at[slot],
                partner,
            )
            copy.start()
            core_copies.append(copy)
            load = pltpu.make_async_copy(
                src.at[grid.block(where)], work.at[slot], load_sem.at[slot]
            )
            load.start()
            loads.append(load)
        arrived = {}
        sends = []
        index = 0
        position = 0
        for level in range(4):
            for offsets in levels[level]:
                slot = grid.slot(offsets)
                core_copies[position].wait_recv()
                loads[position].wait()
                position += 1
                total = work[slot].astype(F32) + core_buf[slot].astype(F32)
                for buffer in arrived.get(slot, ()):
                    remote(work.at[slot], bufs.at[buffer], send.at[0], recv.at[buffer], partner).wait_recv()
                    total = total + bufs[buffer].astype(F32)
                if level == 3:
                    out[...] = total.astype(out.dtype)
                    continue
                work[slot] = total.astype(BF16)
                axis = order[level]
                step = offsets[axis]
                copy = remote(
                    work.at[slot],
                    bufs.at[index],
                    send.at[index],
                    recv.at[index],
                    grid.device(grid.moved(at, axis, step)),
                )
                copy.start()
                sends.append(copy)
                landing = grid.slot({**offsets, axis: 0})
                arrived.setdefault(landing, []).append(index)
                index += 1
        for copy in sends:
            copy.wait_send()
        for copy in core_copies:
            copy.wait_send()

    for color, order in enumerate(GATHER_ORDERS):
        pl.when(at["core"] == color)(functools.partial(run, order[::-1]))


def reduce(plan, blocks, collective_id):
    half = plan.group // 2
    shape = blocks.shape[1:]
    count = max(gather_sends(plan, order) for order in GATHER_ORDERS)
    return pl.pallas_call(
        functools.partial(reduce_kernel, plan),
        out_shape=jax.ShapeDtypeStruct(shape, F32),
        in_specs=[HBM],
        out_specs=VMEM,
        scratch_shapes=[
            pltpu.VMEM((half,) + shape, BF16),
            pltpu.VMEM((half,) + shape, BF16),
            pltpu.VMEM((count,) + shape, BF16),
            DMA((half,)),
            DMA((half,)),
            DMA((half,)),
            DMA((count,)),
            DMA((count,)),
        ],
        compiler_params=params(collective_id),
        name="reduce",
    )(blocks)


def nt(left, right):
    return lax.dot_general(left, right, (((1,), (1,)), ((), ())), preferred_element_type=F32)


def nn(left, right):
    return lax.dot_general(left, right, (((1,), (0,)), ((), ())), preferred_element_type=F32)


def tn(left, right):
    return lax.dot_general(left, right, (((0,), (0,)), ((), ())), preferred_element_type=F32)


def swapped_halves(value):
    lane = lax.broadcasted_iota(jnp.int32, value.shape, 1)
    first = lax.rem(lane, HEAD_DIM) < HEAD_DIM // 2
    half = HEAD_DIM // 2
    return jnp.where(
        first, pltpu.roll(value, 2 * HEAD_DIM - half, 1), pltpu.roll(value, half, 1)
    )


def masked_scores(q, k, first_row, length):
    scores = nt(q, k)
    row = lax.broadcasted_iota(jnp.int32, scores.shape, 0) + first_row
    col = lax.broadcasted_iota(jnp.int32, scores.shape, 1)
    return jnp.where((col <= row) & (col < length), scores, -1000000000.0)


def attend_kernel(plan, length_ref, x, gain, w, cosine, sine, mixed, normed, qk_out, v_out, lse_out, qkv):
    length = length_ref[0]
    rows = QUERY_ROWS
    slots = plan.slots
    for start in range(0, slots, rows):
        at = slice(start, start + rows)
        values = x[at].astype(F32)
        inverse = lax.rsqrt(jnp.mean(values * values, axis=-1, keepdims=True) + EPSILON)
        normed[at] = (values * inverse * gain[...]).astype(BF16)
        qkv[at] = nn(normed[at], w[...])
    heads = plan.heads
    qk_width = 2 * HEAD_DIM
    for head in range(heads):
        cols = slice(head * qk_width, (head + 1) * qk_width)
        qk = qkv[:, cols]
        qk_out[:, cols] = (qk * cosine[...] + swapped_halves(qk) * sine[...]).astype(BF16)
    v_cols = slice(heads * qk_width, heads * 3 * HEAD_DIM)
    v_out[...] = qkv[:, v_cols].astype(BF16)
    for head in range(heads):
        base = head * qk_width
        for start in range(0, slots, rows):
            at = slice(start, start + rows)
            end = start + rows
            q = qk_out[at, base : base + HEAD_DIM] * BF16(0.125)
            k = qk_out[:end, base + HEAD_DIM : base + qk_width]
            v = v_out[:end, head * HEAD_DIM : (head + 1) * HEAD_DIM]
            scores = masked_scores(q, k, start, length)
            top = jnp.max(scores, axis=-1, keepdims=True)
            raised = jnp.exp(scores - top)
            total = jnp.sum(raised, axis=-1, keepdims=True)
            lse_out[head, at] = top + jnp.log(total)
            probs = (raised * (1.0 / total)).astype(BF16)
            mixed[at, head * HEAD_DIM : (head + 1) * HEAD_DIM] = nn(probs, v).astype(BF16)


def attend(plan, length, x, gain, w, cosine, sine):
    slots, heads = plan.slots, plan.heads
    return pl.pallas_call(
        functools.partial(attend_kernel, plan),
        out_shape=(
            jax.ShapeDtypeStruct((slots, plan.head_cols), BF16),
            jax.ShapeDtypeStruct((slots, plan.width), BF16),
            jax.ShapeDtypeStruct((slots, 2 * plan.head_cols), BF16),
            jax.ShapeDtypeStruct((slots, plan.head_cols), BF16),
            jax.ShapeDtypeStruct((heads, slots, 1), F32),
        ),
        in_specs=[pl.BlockSpec(memory_space=pltpu.SMEM)] + [VMEM] * 5,
        out_specs=(VMEM,) * 5,
        scratch_shapes=[pltpu.VMEM((slots, plan.wide), F32)],
        compiler_params=params(),
        name="attend",
    )(length, x, gain, w, cosine, sine)


def attend_back_kernel(plan, length_ref, x, w, cosine, sine, normed, qk_in, v_in, lse, dmixed, dnp, dw, gain_grad, dqkv, dq_acc, dk_acc, dv_acc):
    length = length_ref[0]
    rows, slots, heads = QUERY_ROWS, plan.slots, plan.heads
    qk_width = 2 * HEAD_DIM
    dqkv[...] = jnp.zeros_like(dqkv)
    for head in range(heads):
        base = head * qk_width
        v_cols = slice(head * HEAD_DIM, (head + 1) * HEAD_DIM)
        for start in range(slots - rows, -1, -rows):
            at = slice(start, start + rows)
            end = start + rows
            q = qk_in[at, base : base + HEAD_DIM] * BF16(0.125)
            k = qk_in[:end, base + HEAD_DIM : base + qk_width]
            v = v_in[:end, v_cols]
            upstream = dmixed[at, v_cols]
            probs = jnp.exp(masked_scores(q, k, start, length) - lse[head, at])
            dv = tn(probs.astype(BF16), upstream)
            prob_grad = nt(upstream, v)
            inner = jnp.sum(probs * prob_grad, axis=-1, keepdims=True)
            score_grad = (probs * (prob_grad - inner)).astype(BF16)
            dq_acc[at] = nn(score_grad, k) * 0.125
            dk = tn(score_grad, q)
            if end == slots:
                dk_acc[...] = dk
                dv_acc[...] = dv
            else:
                dk_acc[:end] += dk
                dv_acc[:end] += dv
        dqk = jnp.concatenate([dq_acc[...], dk_acc[...]], axis=-1)
        dqkv[:, base : base + qk_width] = (
            dqk * cosine[...] - swapped_halves(dqk) * sine[...]
        ).astype(BF16)
        v_base = heads * qk_width + head * HEAD_DIM
        dqkv[:, v_base : v_base + HEAD_DIM] = dv_acc[...].astype(BF16)
    dw[...] = tn(normed[...], dqkv[...]).astype(dw.dtype)
    gains = jnp.zeros((1, plan.width), F32)
    for start in range(0, slots, rows):
        at = slice(start, start + rows)
        part = nt(dqkv[at], w[...])
        dnp[at] = part.astype(BF16)
        values = x[at].astype(F32)
        inverse = lax.rsqrt(jnp.mean(values * values, axis=-1, keepdims=True) + EPSILON)
        gains = gains + jnp.sum(part * values * inverse, axis=0, keepdims=True)
    gain_grad[...] = gains


def attend_back(plan, length, x, w, cosine, sine, normed, qk, v, lse, dmixed):
    slots = plan.slots
    return pl.pallas_call(
        functools.partial(attend_back_kernel, plan),
        out_shape=(
            jax.ShapeDtypeStruct((slots, plan.width), BF16),
            jax.ShapeDtypeStruct((plan.width, plan.wide), F32),
            jax.ShapeDtypeStruct((1, plan.width), F32),
        ),
        in_specs=[pl.BlockSpec(memory_space=pltpu.SMEM)] + [VMEM] * 9,
        out_specs=(VMEM,) * 3,
        scratch_shapes=[
            pltpu.VMEM((slots, plan.wide), BF16),
            pltpu.VMEM((slots, HEAD_DIM), F32),
            pltpu.VMEM((slots, HEAD_DIM), F32),
            pltpu.VMEM((slots, HEAD_DIM), F32),
        ],
        compiler_params=params(),
        name="attend_back",
    )(length, x, w, cosine, sine, normed, qk, v, lse, dmixed)


def ffn_kernel(plan, members, n2x, gy, w_in, w_out, pick, out, n2g, dw_in, dw_out):
    hidden, local = plan.hidden_pad, plan.local

    @pl.when(pl.program_id(0) == 0)
    def start():
        dw_in[...] = jnp.zeros_like(dw_in)
        dw_out[...] = jnp.zeros_like(dw_out)

    tokens = members * local
    width = plan.width
    normed = n2x[:, :local].reshape(tokens, width)
    upstream = gy[...].reshape(tokens, width)
    mixing = jnp.concatenate(
        [tn(n2x[i, local:, :local], pick[...]) for i in range(members)], axis=0
    )
    pre = nn(normed, w_in[...])
    gate, up = pre[:, :hidden], pre[:, hidden:]
    sigmoid = jax.nn.sigmoid(gate)
    silu = gate * sigmoid
    act = (silu * up).astype(BF16).astype(F32)
    act_mixed = (act * mixing).astype(BF16)
    out[...] = nn(act_mixed, w_out[...]).astype(BF16).reshape(members, local, width)
    act_grad = nt(upstream, w_out[...])
    choice = nt(pick[...], (act * act_grad).astype(BF16)).astype(BF16)
    act_grad = act_grad * mixing
    gate_grad = act_grad * up * sigmoid * (1.0 + gate * (1.0 - sigmoid))
    pre_grad = jnp.concatenate([gate_grad, act_grad * silu], axis=-1).astype(BF16)
    n2g[:, :local] = nt(pre_grad, w_in[...]).astype(BF16).reshape(members, local, width)
    pad = jnp.zeros((MIX_ROWS, width - local), BF16)
    for i in range(members):
        n2g[i, local:] = jnp.concatenate(
            [choice[:, i * local : (i + 1) * local], pad], axis=-1
        )
    dw_in[...] += tn(normed, pre_grad)
    dw_out[...] += tn(act_mixed, upstream)


def ffn(plan, n2x, gy, w_in, w_out, pick):
    members = 2
    local, width, hidden = plan.local, plan.width, plan.hidden_pad
    whole = lambda i: (0, 0)
    part = lambda i: (i, 0, 0)
    return pl.pallas_call(
        functools.partial(ffn_kernel, plan, members),
        grid=(plan.group // members,),
        out_shape=(
            jax.ShapeDtypeStruct((plan.group, local, width), BF16),
            jax.ShapeDtypeStruct((plan.group, local + MIX_ROWS, width), BF16),
            jax.ShapeDtypeStruct((width, 2 * hidden), F32),
            jax.ShapeDtypeStruct((hidden, width), F32),
        ),
        in_specs=[
            pl.BlockSpec((members, local + MIX_ROWS, width), part),
            pl.BlockSpec((members, local, width), part),
            pl.BlockSpec((width, 2 * hidden), whole),
            pl.BlockSpec((hidden, width), whole),
            pl.BlockSpec((MIX_ROWS, hidden), whole),
        ],
        out_specs=(
            pl.BlockSpec((members, local, width), part),
            pl.BlockSpec((members, local + MIX_ROWS, width), part),
            pl.BlockSpec((width, 2 * hidden), whole),
            pl.BlockSpec((hidden, width), whole),
        ),
        compiler_params=params(),
        name="ffn",
    )(n2x, gy, w_in, w_out, pick)


def by_half(half, mine, far, axis):
    return jnp.where(
        half == 0, jnp.stack([mine, far], axis), jnp.stack([far, mine], axis)
    )


def rope_tables(plan):
    half = HEAD_DIM // 2
    frequency = np.float32(10000.0) ** (-np.arange(half, dtype=np.float32) / np.float32(half))
    angles = np.arange(plan.slots, dtype=np.float32)[:, None] * frequency[None, :]
    cosine = np.cos(angles.astype(np.float64)).astype(np.float32)
    sine = np.sin(angles.astype(np.float64)).astype(np.float32)
    return np.tile(cosine, (1, 4)), np.tile(np.concatenate([-sine, sine], 1), (1, 2))


def pick_table(plan):
    table = np.zeros((MIX_ROWS, plan.hidden_pad), np.float32)
    span = HALVES * plan.own_hidden
    for expert in range(plan.experts):
        cols = slice((1 + expert) * span, (2 + expert) * span)
        table[expert, cols] = 1.0
        table[plan.experts + expert, cols] = 1.0
    table[2 * plan.experts, :span] = 1.0
    return jnp.asarray(table, BF16)


def pack_qkv(plan, attn_in, attn_gain, ffn_gain, router):
    rows, quad, heads = plan.rows, plan.quad, plan.heads
    qkv = attn_in.reshape(rows, 3, HEADS, HEAD_DIM)
    qkv = jnp.pad(qkv, ((0, 0), (0, 0), (0, quad * heads - HEADS), (0, 0)))
    qkv = qkv.reshape(rows, 3, quad, heads, HEAD_DIM)
    qk = jnp.transpose(qkv[:, :2], (2, 0, 3, 1, 4)).reshape(quad, rows, 2 * plan.head_cols)
    v = jnp.transpose(qkv[:, 2], (1, 0, 2, 3)).reshape(quad, rows, plan.head_cols)
    extra = jnp.concatenate([attn_gain[:, None], ffn_gain[:, None], router], axis=1)
    extra = jnp.pad(extra, ((0, 0), (0, plan.wide - plan.qkv_cols - extra.shape[1])))
    extra = jnp.broadcast_to(extra[None], (quad,) + extra.shape)
    return jnp.concatenate([qk, v, extra], axis=-1)


def unpack_qkv(plan, packed):
    rows, quad, heads = plan.rows, plan.quad, plan.heads
    qk = packed[..., : 2 * plan.head_cols].reshape(quad, rows, heads, 2, HEAD_DIM)
    v = packed[..., 2 * plan.head_cols : plan.qkv_cols].reshape(quad, rows, heads, 1, HEAD_DIM)
    qkv = jnp.transpose(jnp.concatenate([qk, v], axis=3), (1, 3, 0, 2, 4))
    qkv = qkv.reshape(rows, 3, quad * heads, HEAD_DIM)[:, :, :HEADS]
    return qkv.reshape(rows, 3 * HEADS * HEAD_DIM)


def pack_in(plan, dense_in, expert_in):
    rows, own = plan.rows, plan.own_hidden
    both = jnp.concatenate([dense_in[:, None], expert_in], axis=1)
    both = both.reshape(rows, plan.branches, 2, plan.dp, HALVES, plan.quad, own)
    both = jnp.transpose(both, (3, 5, 0, 2, 1, 4, 6))
    both = both.reshape(plan.group, rows, 2, plan.hidden)
    both = jnp.pad(both, ((0, 0), (0, 0), (0, 0), (0, plan.hidden_pad - plan.hidden)))
    return both.reshape(plan.group, rows, 2 * plan.hidden_pad)


def unpack_in(plan, packed):
    rows, own = plan.rows, plan.own_hidden
    both = packed.reshape(plan.group, rows, 2, plan.hidden_pad)[..., : plan.hidden]
    both = both.reshape(plan.dp, plan.quad, rows, 2, plan.branches, HALVES, own)
    both = jnp.transpose(both, (2, 4, 3, 0, 5, 1, 6))
    both = both.reshape(rows, plan.branches, 2 * FF).astype(F32)
    return both[:, 0], both[:, 1:]


def shards(
    tokens,
    lengths,
    routes,
    cotangent,
    attn_gain,
    attn_in,
    attn_out,
    ffn_gain,
    router,
    dense_in,
    dense_out,
    expert_in,
    expert_out,
):
    micro, seqs, block, width = tokens.shape
    experts = expert_in.shape[1]
    plan = Plan(lax.axis_size("dp"), lax.axis_size("ctx"), block, width, experts)
    assert micro == HALVES and seqs == 1 and plan.ctx % 4 == 0 and plan.dp % 2 == 0
    quad, local = plan.quad, plan.local
    dp, ctx = place()
    half, member = lax.div(ctx, quad), lax.rem(ctx, quad)
    across = [(i, (i + quad) % plan.ctx) for i in range(plan.ctx)]

    def swap(value):
        return lax.ppermute(value, "ctx", across)

    def pick_mine(value):
        return lax.dynamic_index_in_dim(value, half, 0, keepdims=False)

    def pick_far(value):
        return lax.dynamic_index_in_dim(value, 1 - half, 0, keepdims=False)

    cot, route = cotangent[:, 0], routes[:, 0]
    length = pick_mine(lengths)
    out_own = jnp.concatenate([dense_out[:, None], expert_out], axis=1)
    out_own = jnp.transpose(out_own, (1, 0, 2))
    cot_local = jnp.stack([pick_mine(cot), swap(pick_far(cot))])
    route_local = jnp.stack([pick_mine(route), swap(pick_far(route))]).reshape(local, 2)
    out_far = swap(out_own)
    w_mix = lax.all_gather(attn_out, ("dp", "ctx"), axis=0, tiled=True)

    xs, wall, win_mine = spread(
        plan,
        tokens[:, 0],
        pack_qkv(plan, attn_in, attn_gain, ffn_gain, router),
        pack_in(plan, dense_in, expert_in),
    )
    win_far = swap(win_mine)

    x_seq = xs.reshape(plan.slots, width)
    w_seq = wall.reshape(width, plan.wide)
    extra = w_seq[:, plan.qkv_cols :]
    gain_one = extra[:, 0].astype(F32)[None]
    gain_two = extra[:, 1].astype(F32)[None]
    w_route = extra[:, 2 : 2 + experts]
    cosine, sine = (jnp.asarray(table) for table in rope_tables(plan))
    mixed_seq, normed_seq, qk, v, lse = attend(plan, length, x_seq, gain_one, w_seq, cosine, sine)
    mixed = to_owners(plan, mixed_seq.reshape(plan.ctx, block, plan.head_cols), 2)
    mixed = jnp.transpose(mixed, (1, 2, 0, 3)).reshape(local, quad * plan.head_cols)[:, :width]

    x = jnp.stack(
        [
            lax.dynamic_index_in_dim(xs, ctx, 0, keepdims=False),
            lax.dynamic_index_in_dim(xs, (1 - half) * quad + member, 0, keepdims=False),
        ]
    )
    x = x.reshape(local, width).astype(F32)
    middle = x + nn(mixed, w_mix)
    inverse_two = lax.rsqrt(jnp.mean(middle * middle, axis=-1, keepdims=True) + EPSILON)
    normed_two = (middle * inverse_two * gain_two).astype(BF16)
    logits = nn(normed_two, w_route)
    choose = (route_local[..., None] == jnp.arange(experts, dtype=jnp.int32)).astype(F32)
    picked = jnp.sum(choose * logits[:, None, :], axis=-1)
    gates = jax.nn.softmax(picked, axis=-1)
    mixing = jnp.sum(gates[..., None] * choose, axis=1)
    mixing_t = mixing.T
    mixing_high = mixing_t.astype(BF16)
    mixing_low = (mixing_t - mixing_high.astype(F32)).astype(BF16)
    mix_rows = jnp.concatenate(
        [
            mixing_high,
            mixing_low,
            jnp.ones((1, local), BF16),
            jnp.zeros((MIX_ROWS - 2 * experts - 1, local), BF16),
        ]
    )
    mix_rows = jnp.pad(mix_rows, ((0, 0), (0, width - local)))
    n2x = gather(plan, jnp.concatenate([normed_two, mix_rows]), 3)

    starts = jnp.stack([ctx, (1 - half) * quad + member]) * block
    slot = (starts[:, None] + jnp.arange(block, dtype=jnp.int32)[None]).reshape(local)
    valid = (slot < length[0]).astype(BF16)[:, None]
    grad_y = cot_local.reshape(local, width) * valid
    gy = gather(plan, grad_y, 4)

    rows_in = (plan.dp, quad, plan.rows, 2 * plan.hidden_pad)
    w_in = by_half(half, win_mine.reshape(rows_in), win_far.reshape(rows_in), 1)
    w_in = w_in.reshape(width, 2 * plan.hidden_pad)
    w_out = by_half(half, out_own, out_far, 1).reshape(plan.hidden, width)
    w_out = jnp.pad(w_out, ((0, plan.hidden_pad - plan.hidden), (0, 0)))
    out_part, n2g_part, dw_in, dw_out = ffn(plan, n2x, gy, w_in, w_out, pick_table(plan))
    n2g_sum = reduce(plan, n2g_part, 5)
    out_sum = reduce(plan, out_part, 7)
    activations = (middle + out_sum).astype(BF16).reshape(2, block, width)

    dw_out = dw_out[: plan.hidden].reshape(plan.branches, HALVES, plan.own_hidden, width)
    dw_out = jnp.moveaxis(dw_out, 1, 0)
    dw_out = pick_mine(dw_out) + swap(pick_far(dw_out).astype(BF16)).astype(F32)
    dw_in = dw_in.reshape(plan.dp, HALVES, quad, plan.rows, 2 * plan.hidden_pad)
    dw_in = jnp.moveaxis(dw_in, 1, 0)
    dw_in = pick_mine(dw_in) + swap(pick_far(dw_in).astype(BF16)).astype(F32)
    dw_in = dw_in.astype(BF16).reshape(plan.group, plan.rows, 2 * plan.hidden_pad)

    normed_two_grad = n2g_sum[:local]
    mixing_grad = n2g_sum[local : local + experts, :local].T
    choice_grad = jnp.sum(choose * mixing_grad[:, None, :], axis=-1)
    pick_grad = gates * (choice_grad - jnp.sum(gates * choice_grad, axis=-1, keepdims=True))
    logit_grad = jnp.sum(pick_grad[..., None] * choose, axis=1).astype(BF16)
    router_grad = tn(normed_two, logit_grad)
    normed_two_grad = normed_two_grad + nt(logit_grad, w_route)
    gain_two_grad = jnp.sum(normed_two_grad * middle * inverse_two, axis=0)
    scaled = normed_two_grad * gain_two
    middle_grad = (
        grad_y.astype(F32)
        + inverse_two * scaled
        - middle * inverse_two**3 * jnp.mean(scaled * middle, axis=-1, keepdims=True)
    )
    attn_grad = middle_grad.astype(BF16)
    dw_mix = tn(mixed, attn_grad).astype(BF16).reshape(plan.devices, plan.rows, width)
    mixed_grad = nt(attn_grad, w_mix).astype(BF16)
    mixed_grad = jnp.pad(mixed_grad, ((0, 0), (0, quad * plan.head_cols - width)))
    mixed_grad = mixed_grad.reshape(2, block, quad, plan.head_cols)
    dmixed = to_slots(plan, jnp.transpose(mixed_grad, (2, 0, 1, 3)), 8)
    dnp, dw_qkv, gain_one_grad = attend_back(
        plan,
        length,
        x_seq,
        w_seq,
        cosine,
        sine,
        normed_seq,
        qk,
        v,
        lse,
        dmixed.reshape(plan.slots, plan.head_cols),
    )
    small = jnp.concatenate([gain_one_grad.T, gain_two_grad[:, None], router_grad], axis=1)
    small = jnp.pad(small, ((0, 0), (0, plan.wide - plan.qkv_cols - small.shape[1])))
    dw_qkv = jnp.concatenate([dw_qkv[:, : plan.qkv_cols], small], axis=1).astype(BF16)
    dn, r_qkv, r_mix, r_in = collect(
        plan,
        dnp.reshape(plan.ctx, block, width),
        dw_qkv.reshape(plan.devices, plan.rows, plan.wide),
        dw_mix,
        dw_in,
    )

    normed_grad = jnp.sum(dn.astype(F32), axis=0).reshape(local, width)
    inverse_one = lax.rsqrt(jnp.mean(x * x, axis=-1, keepdims=True) + EPSILON)
    scaled = normed_grad * gain_one
    input_grad = (
        middle_grad
        + inverse_one * scaled
        - x * inverse_one**3 * jnp.mean(scaled * x, axis=-1, keepdims=True)
    )
    input_grad = input_grad.astype(BF16).reshape(2, block, width)
    r_qkv = r_qkv.astype(F32).reshape(plan.dp * HALVES, quad, plan.rows, plan.wide)
    r_qkv = jnp.sum(r_qkv, axis=0)
    attn_in_grad = unpack_qkv(plan, r_qkv)
    small = jnp.sum(r_qkv[:, :, plan.qkv_cols :], axis=0)
    attn_out_grad = jnp.sum(r_mix.astype(F32), axis=0)
    dense_in_grad, expert_in_grad = unpack_in(plan, r_in)
    return (
        by_half(half, activations[0], swap(activations[1]), 0)[:, None],
        by_half(half, input_grad[0], swap(input_grad[1]), 0)[:, None],
        small[:, 0],
        attn_in_grad,
        attn_out_grad,
        small[:, 1],
        small[:, 2 : 2 + experts],
        dense_in_grad,
        dw_out[0],
        expert_in_grad,
        jnp.transpose(dw_out[1:], (1, 0, 2)),
    )


def solution(mesh):
    rows = P(("dp", "ctx"))
    matrix = P(("dp", "ctx"), None)
    cube = P(("dp", "ctx"), None, None)
    slots = P(None, "dp", "ctx", None)
    in_specs = (
        slots,
        P(None, "dp"),
        slots,
        slots,
        rows,
        matrix,
        matrix,
        rows,
        matrix,
        matrix,
        matrix,
        cube,
        cube,
    )
    out_specs = (
        slots,
        slots,
        rows,
        matrix,
        matrix,
        rows,
        matrix,
        matrix,
        matrix,
        cube,
        cube,
    )
    return jax.shard_map(shards, mesh=mesh, in_specs=in_specs, out_specs=out_specs, check_vma=False)
```

```python
import functools

import jax
import jax.numpy as jnp
import numpy as np
from jax import lax
from jax.experimental import pallas as pl
from jax.experimental.pallas import tpu as pltpu
from jax.sharding import PartitionSpec as P

HEADS = 12
HEAD_DIM = 64
FF = 2048
EPSILON = 1e-05
HALVES = 2
QUERY_ROWS = 256
MIX_ROWS = 16
MESH = pl.DeviceIdType.MESH
BF16 = jnp.bfloat16
F32 = jnp.float32


def round_up(value, step):
    return -(-value // step) * step


class Plan:
    def __init__(self, dp, ctx, block, width, experts):
        self.dp, self.ctx, self.block, self.width, self.experts = dp, ctx, block, width, experts
        self.quad = ctx // HALVES
        self.devices = dp * ctx
        self.group = dp * self.quad
        self.slots = ctx * block
        self.rows = width // self.devices
        self.heads = -(-HEADS // self.quad)
        self.head_cols = self.heads * HEAD_DIM
        self.qkv_cols = 3 * self.head_cols
        self.wide = round_up(self.qkv_cols + 2 + experts, 128)
        self.own_hidden = FF // self.devices
        self.branches = 1 + experts
        self.hidden = self.branches * HALVES * self.own_hidden
        self.hidden_pad = round_up(self.hidden, 128)
        self.local = HALVES * block


def place():
    return lax.axis_index("dp"), lax.axis_index("ctx")


def params(collective_id=None, limit=60 * 1024 * 1024):
    if collective_id is None:
        return pltpu.CompilerParams(vmem_limit_bytes=limit)
    return pltpu.CompilerParams(
        vmem_limit_bytes=limit, collective_id=collective_id, has_side_effects=True
    )


def remote(src, dst, send_sem, recv_sem, device):
    return pltpu.make_async_remote_copy(
        src_ref=src,
        dst_ref=dst,
        send_sem=send_sem,
        recv_sem=recv_sem,
        device_id=device,
        device_id_type=MESH,
    )


def meet(devices):
    barrier = pltpu.get_barrier_semaphore()
    for device in devices:
        pl.semaphore_signal(barrier, inc=1, device_id=device, device_id_type=MESH)
    pl.semaphore_wait(barrier, len(devices))


def other_devices(plan, dp, ctx):
    flat = dp * plan.ctx + ctx
    result = []
    for step in range(1, plan.devices):
        target = lax.rem(flat + step, plan.devices)
        result.append((lax.div(target, plan.ctx), lax.rem(target, plan.ctx)))
    return result


def quad_members(plan, half, member):
    return [
        (half * plan.quad + lax.rem(member + step, plan.quad), lax.rem(member + step, plan.quad))
        for step in range(1, plan.quad)
    ]


VMEM = pl.BlockSpec(memory_space=pltpu.VMEM)
HBM = pl.BlockSpec(memory_space=pl.ANY)
DMA = pltpu.SemaphoreType.DMA


def spread_kernel(plan, tok, wq, win, xs, wall, winh, x_send, x_recv, q_send, q_recv, f_send, f_recv):
    dp, ctx = place()
    half, member = lax.div(ctx, plan.quad), lax.rem(ctx, plan.quad)
    far = (1 - half) * plan.quad + member
    flat = dp * plan.ctx + ctx
    mine = dp * plan.quad + member
    others = other_devices(plan, dp, ctx)
    meet(others)
    copies = []

    swap = remote(tok.at[1 - half], xs.at[ctx], x_send.at[0], x_recv.at[0], (dp, far))
    swap.start()
    members = quad_members(plan, half, member)
    count = len(members)
    for i, (peer, _) in enumerate(members):
        copy = remote(tok.at[half], xs.at[ctx], x_send.at[1 + i], x_recv.at[1 + i], (dp, peer))
        copy.start()
        copies.append(copy)
    for i, (tdp, tctx) in enumerate(others):
        copy = remote(
            wq.at[lax.rem(tctx, plan.quad)], wall.at[flat], q_send.at[i], q_recv.at[i], (tdp, tctx)
        )
        copy.start()
        copies.append(copy)
    for i in range(plan.group - 1):
        target = lax.rem(mine + 1 + i, plan.group)
        tdp, tmember = lax.div(target, plan.quad), lax.rem(target, plan.quad)
        copy = remote(
            win.at[target],
            winh.at[mine],
            f_send.at[i],
            f_recv.at[i],
            (tdp, half * plan.quad + tmember),
        )
        copy.start()
        copies.append(copy)
    xs[pl.ds(ctx, 1)] = tok[pl.ds(half, 1)]
    wall[pl.ds(flat, 1)] = wq[pl.ds(member, 1)]
    winh[pl.ds(mine, 1)] = win[pl.ds(mine, 1)]
    swap.wait()
    for i, (peer, _) in enumerate(members):
        copy = remote(
            xs.at[far], xs.at[far], x_send.at[1 + count + i], x_recv.at[1 + count + i], (dp, peer)
        )
        copy.start()
        copies.append(copy)
    for copy in copies:
        copy.wait()


def spread(plan, tok, wq, win):
    count = 2 * plan.quad - 1
    return pl.pallas_call(
        functools.partial(spread_kernel, plan),
        out_shape=(
            jax.ShapeDtypeStruct((plan.ctx, plan.block, plan.width), BF16),
            jax.ShapeDtypeStruct((plan.devices, plan.rows, plan.wide), BF16),
            jax.ShapeDtypeStruct((plan.group, plan.rows, 2 * plan.hidden_pad), BF16),
        ),
        in_specs=[VMEM] * 3,
        out_specs=(VMEM,) * 3,
        scratch_shapes=[
            DMA((count,)),
            DMA((count,)),
            DMA((plan.devices - 1,)),
            DMA((plan.devices - 1,)),
            DMA((plan.group - 1,)),
            DMA((plan.group - 1,)),
        ],
        compiler_params=params(1),
        name="spread",
    )(tok, wq, win)


def to_slots_kernel(plan, src, dst, send, recv):
    dp, ctx = place()
    half, member = lax.div(ctx, plan.quad), lax.rem(ctx, plan.quad)
    far = (1 - half) * plan.quad + member
    members = quad_members(plan, half, member)
    meet([(dp, peer) for peer, _ in members])
    copies = []
    for i, (peer, to) in enumerate(members):
        for j, at in enumerate((ctx, far)):
            copy = remote(
                src.at[to, j], dst.at[at], send.at[2 * i + j], recv.at[2 * i + j], (dp, peer)
            )
            copy.start()
            copies.append(copy)
    dst[pl.ds(ctx, 1)] = src[pl.ds(member, 1), 0]
    dst[pl.ds(far, 1)] = src[pl.ds(member, 1), 1]
    for copy in copies:
        copy.wait()


def to_slots(plan, value, collective_id):
    count = 2 * (plan.quad - 1)
    return pl.pallas_call(
        functools.partial(to_slots_kernel, plan),
        out_shape=jax.ShapeDtypeStruct((plan.ctx, plan.block, value.shape[-1]), value.dtype),
        in_specs=[VMEM],
        out_specs=VMEM,
        scratch_shapes=[DMA((count,)), DMA((count,))],
        compiler_params=params(collective_id),
        name="to_slots",
    )(value)


def send_to_owners(plan, dp, half, member, src, dst, send, recv):
    copies = []
    for i, (peer, to) in enumerate(quad_members(plan, half, member)):
        for j, at in enumerate((half * plan.quad + to, (1 - half) * plan.quad + to)):
            copy = remote(
                src.at[at], dst.at[member, j], send.at[2 * i + j], recv.at[2 * i + j], (dp, peer)
            )
            copy.start()
            copies.append(copy)
    return copies


def to_owners_kernel(plan, src, dst, send, recv):
    dp, ctx = place()
    half, member = lax.div(ctx, plan.quad), lax.rem(ctx, plan.quad)
    far = (1 - half) * plan.quad + member
    meet([(dp, peer) for peer, _ in quad_members(plan, half, member)])
    copies = send_to_owners(plan, dp, half, member, src, dst, send, recv)
    dst[pl.ds(member, 1), 0] = src[pl.ds(ctx, 1)]
    dst[pl.ds(member, 1), 1] = src[pl.ds(far, 1)]
    for copy in copies:
        copy.wait()


def to_owners(plan, value, collective_id):
    count = 2 * (plan.quad - 1)
    return pl.pallas_call(
        functools.partial(to_owners_kernel, plan),
        out_shape=jax.ShapeDtypeStruct((plan.quad, 2, plan.block, value.shape[-1]), value.dtype),
        in_specs=[VMEM],
        out_specs=VMEM,
        scratch_shapes=[DMA((count,)), DMA((count,))],
        compiler_params=params(collective_id),
        name="to_owners",
    )(value)


def collect_kernel(plan, dnp, dwq, dwo, dwin, rdn, rwq, rwo, rwin, n_send, n_recv, q_send, q_recv, o_send, o_recv, f_send, f_recv):
    dp, ctx = place()
    half, member = lax.div(ctx, plan.quad), lax.rem(ctx, plan.quad)
    far = (1 - half) * plan.quad + member
    flat = dp * plan.ctx + ctx
    mine = dp * plan.quad + member
    others = other_devices(plan, dp, ctx)
    meet(others)
    copies = send_to_owners(plan, dp, half, member, dnp, rdn, n_send, n_recv)
    for i, (tdp, tctx) in enumerate(others):
        to = tdp * plan.ctx + tctx
        copy = remote(dwq.at[to], rwq.at[flat], q_send.at[i], q_recv.at[i], (tdp, tctx))
        copy.start()
        copies.append(copy)
        copy = remote(dwo.at[to], rwo.at[flat], o_send.at[i], o_recv.at[i], (tdp, tctx))
        copy.start()
        copies.append(copy)
    for i in range(plan.group - 1):
        target = lax.rem(mine + 1 + i, plan.group)
        tdp, tmember = lax.div(target, plan.quad), lax.rem(target, plan.quad)
        copy = remote(
            dwin.at[target],
            rwin.at[mine],
            f_send.at[i],
            f_recv.at[i],
            (tdp, half * plan.quad + tmember),
        )
        copy.start()
        copies.append(copy)
    rdn[pl.ds(member, 1), 0] = dnp[pl.ds(ctx, 1)]
    rdn[pl.ds(member, 1), 1] = dnp[pl.ds(far, 1)]
    rwq[pl.ds(flat, 1)] = dwq[pl.ds(flat, 1)]
    rwo[pl.ds(flat, 1)] = dwo[pl.ds(flat, 1)]
    rwin[pl.ds(mine, 1)] = dwin[pl.ds(mine, 1)]
    for copy in copies:
        copy.wait()


def collect(plan, dnp, dwq, dwo, dwin):
    count = 2 * (plan.quad - 1)
    return pl.pallas_call(
        functools.partial(collect_kernel, plan),
        out_shape=(
            jax.ShapeDtypeStruct((plan.quad, 2, plan.block, plan.width), BF16),
            jax.ShapeDtypeStruct(dwq.shape, BF16),
            jax.ShapeDtypeStruct(dwo.shape, BF16),
            jax.ShapeDtypeStruct(dwin.shape, BF16),
        ),
        in_specs=[VMEM] * 4,
        out_specs=(VMEM,) * 4,
        scratch_shapes=[
            DMA((count,)),
            DMA((count,)),
            DMA((plan.devices - 1,)),
            DMA((plan.devices - 1,)),
            DMA((plan.devices - 1,)),
            DMA((plan.devices - 1,)),
            DMA((plan.group - 1,)),
            DMA((plan.group - 1,)),
        ],
        compiler_params=params(6),
        name="collect",
    )(dnp, dwq, dwo, dwin)


class Grid:
    def __init__(self, plan):
        self.plan = plan
        self.sizes = {"y": plan.dp // 2, "high": plan.quad // 2, "low": 2}

    def here(self):
        dp, ctx = place()
        member = lax.rem(ctx, self.plan.quad)
        return {
            "core": lax.rem(dp, 2),
            "y": lax.div(dp, 2),
            "high": lax.div(member, 2),
            "low": lax.rem(member, 2),
            "half": lax.div(ctx, self.plan.quad),
        }

    def device(self, at):
        return (
            at["y"] * 2 + at["core"],
            at["half"] * self.plan.quad + at["high"] * 2 + at["low"],
        )

    def block(self, at):
        return (at["y"] * 2 + at["core"]) * self.plan.quad + at["high"] * 2 + at["low"]

    def moved(self, at, axis, step):
        result = dict(at)
        if axis == "core":
            result["core"] = 1 - at["core"]
        else:
            result[axis] = lax.rem(at[axis] + step, self.sizes[axis])
        return result

    def peers(self, at):
        result = [self.moved(at, "core", 1)]
        for axis, size in self.sizes.items():
            result += [self.moved(at, axis, step) for step in range(1, size)]
        return [self.device(peer) for peer in result]

    def slot(self, offsets):
        return (offsets["y"] * self.sizes["high"] + offsets["high"]) * 2 + offsets["low"]


GATHER_ORDERS = (("high", "low", "y"), ("low", "y", "high"))


def gather_kernel(plan, src, dst, send, recv, core_send, core_recv):
    grid = Grid(plan)
    at = grid.here()
    meet(grid.peers(at))
    dst[pl.ds(grid.block(at), 1)] = src[...][None]
    zero = {"y": 0, "high": 0, "low": 0}

    def run(order):
        levels = [[dict(zero)], [], [], []]
        for level, axis in enumerate(order):
            base = [o for group in levels[: level + 1] for o in group]
            for offsets in base:
                for step in range(1, grid.sizes[axis]):
                    levels[level + 1].append({**offsets, axis: step})
        sends = []
        counter = [0]

        def absolute(offsets):
            where = dict(at)
            for axis, step in offsets.items():
                if step:
                    where = grid.moved(where, axis, step)
            return where

        for level, group in enumerate(levels):
            for offsets in group:
                where = absolute(offsets)
                block = grid.block(where)
                if level:
                    remote(dst.at[block], dst.at[block], send.at[0], recv.at[grid.slot(offsets)], grid.device(at)).wait_recv()
                source = src if level == 0 else dst.at[block]
                for axis in order[level:]:
                    for step in range(1, grid.sizes[axis]):
                        seen = {**offsets, axis: grid.sizes[axis] - step}
                        copy = remote(
                            source,
                            dst.at[block],
                            send.at[counter[0]],
                            recv.at[grid.slot(seen)],
                            grid.device(grid.moved(at, axis, step)),
                        )
                        copy.start()
                        counter[0] += 1
                        sends.append(copy)
                copy = remote(
                    source,
                    dst.at[block],
                    core_send.at[grid.slot(offsets)],
                    core_recv.at[grid.slot(offsets)],
                    grid.device(grid.moved(at, "core", 1)),
                )
                copy.start()
                sends.append(copy)
        for copy in sends:
            copy.wait_send()
        for slot in range(plan.group // 2):
            remote(src, dst.at[0], core_send.at[slot], core_recv.at[slot], grid.device(at)).wait_recv()

    for color, order in enumerate(GATHER_ORDERS):
        pl.when(at["core"] == color)(functools.partial(run, order))


def gather_sends(plan, order):
    sizes = Grid(plan).sizes
    held, total = 1, 0
    for axis in order:
        total += held * (sizes[axis] - 1)
        held *= sizes[axis]
    return total


def gather(plan, block, collective_id):
    half = plan.group // 2
    count = max(gather_sends(plan, order) for order in GATHER_ORDERS)
    return pl.pallas_call(
        functools.partial(gather_kernel, plan),
        out_shape=jax.ShapeDtypeStruct((plan.group,) + block.shape, block.dtype),
        in_specs=[VMEM],
        out_specs=VMEM,
        scratch_shapes=[DMA((count,)), DMA((half,)), DMA((half,)), DMA((half,))],
        compiler_params=params(collective_id),
        name="gather",
    )(block)


def reduce_kernel(plan, src, out, work, core_buf, bufs, load_sem, core_send, core_recv, send, recv):
    grid = Grid(plan)
    at = grid.here()
    zero = {"y": 0, "high": 0, "low": 0}
    meet(grid.peers(at))

    def run(order):
        levels = [[], [], [], []]
        held = [dict(zero)]
        levels[3] = [dict(zero)]
        for level in (2, 1, 0):
            axis = order[level]
            base = [o for later in levels[level + 1 :] for o in later]
            levels[level] = [
                {**offsets, axis: step} for offsets in base for step in range(1, grid.sizes[axis])
            ]
        del held

        def absolute(offsets):
            where = dict(at)
            for axis, step in offsets.items():
                if step:
                    where = grid.moved(where, axis, step)
            return where

        sequence = [o for group in levels for o in group]
        partner = grid.device(grid.moved(at, "core", 1))
        core_copies = []
        loads = []
        for offsets in sequence:
            where = absolute(offsets)
            slot = grid.slot(offsets)
            copy = remote(
                src.at[grid.block(grid.moved(where, "core", 1))],
                core_buf.at[slot],
                core_send.at[slot],
                core_recv.at[slot],
                partner,
            )
            copy.start()
            core_copies.append(copy)
            load = pltpu.make_async_copy(
                src.at[grid.block(where)], work.at[slot], load_sem.at[slot]
            )
            load.start()
            loads.append(load)
        arrived = {}
        sends = []
        index = 0
        position = 0
        for level in range(4):
            for offsets in levels[level]:
                slot = grid.slot(offsets)
                core_copies[position].wait_recv()
                loads[position].wait()
                position += 1
                total = work[slot].astype(F32) + core_buf[slot].astype(F32)
                for buffer in arrived.get(slot, ()):
                    remote(work.at[slot], bufs.at[buffer], send.at[0], recv.at[buffer], partner).wait_recv()
                    total = total + bufs[buffer].astype(F32)
                if level == 3:
                    out[...] = total.astype(out.dtype)
                    continue
                work[slot] = total.astype(BF16)
                axis = order[level]
                step = offsets[axis]
                copy = remote(
                    work.at[slot],
                    bufs.at[index],
                    send.at[index],
                    recv.at[index],
                    grid.device(grid.moved(at, axis, step)),
                )
                copy.start()
                sends.append(copy)
                landing = grid.slot({**offsets, axis: 0})
                arrived.setdefault(landing, []).append(index)
                index += 1
        for copy in sends:
            copy.wait_send()
        for copy in core_copies:
            copy.wait_send()

    for color, order in enumerate(GATHER_ORDERS):
        pl.when(at["core"] == color)(functools.partial(run, order[::-1]))


def reduce(plan, blocks, collective_id):
    half = plan.group // 2
    shape = blocks.shape[1:]
    count = max(gather_sends(plan, order) for order in GATHER_ORDERS)
    return pl.pallas_call(
        functools.partial(reduce_kernel, plan),
        out_shape=jax.ShapeDtypeStruct(shape, F32),
        in_specs=[HBM],
        out_specs=VMEM,
        scratch_shapes=[
            pltpu.VMEM((half,) + shape, BF16),
            pltpu.VMEM((half,) + shape, BF16),
            pltpu.VMEM((count,) + shape, BF16),
            DMA((half,)),
            DMA((half,)),
            DMA((half,)),
            DMA((count,)),
            DMA((count,)),
        ],
        compiler_params=params(collective_id),
        name="reduce",
    )(blocks)


def nt(left, right):
    return lax.dot_general(left, right, (((1,), (1,)), ((), ())), preferred_element_type=F32)


def nn(left, right):
    return lax.dot_general(left, right, (((1,), (0,)), ((), ())), preferred_element_type=F32)


def tn(left, right):
    return lax.dot_general(left, right, (((0,), (0,)), ((), ())), preferred_element_type=F32)


def swapped_halves(value):
    lane = lax.broadcasted_iota(jnp.int32, value.shape, 1)
    first = lax.rem(lane, HEAD_DIM) < HEAD_DIM // 2
    half = HEAD_DIM // 2
    return jnp.where(
        first, pltpu.roll(value, 2 * HEAD_DIM - half, 1), pltpu.roll(value, half, 1)
    )


def masked_scores(q, k, first_row, length):
    scores = nt(q, k)
    row = lax.broadcasted_iota(jnp.int32, scores.shape, 0) + first_row
    col = lax.broadcasted_iota(jnp.int32, scores.shape, 1)
    return jnp.where((col <= row) & (col < length), scores, -1000000000.0)


def attend_kernel(plan, length_ref, x, gain, w, cosine, sine, mixed, normed, qk_out, v_out, lse_out, qkv):
    length = length_ref[0]
    rows = QUERY_ROWS
    slots = plan.slots
    for start in range(0, slots, rows):
        at = slice(start, start + rows)
        values = x[at].astype(F32)
        inverse = lax.rsqrt(jnp.mean(values * values, axis=-1, keepdims=True) + EPSILON)
        normed[at] = (values * inverse * gain[...]).astype(BF16)
        qkv[at] = nn(normed[at], w[...])
    heads = plan.heads
    qk_width = 2 * HEAD_DIM
    for head in range(heads):
        cols = slice(head * qk_width, (head + 1) * qk_width)
        qk = qkv[:, cols]
        qk_out[:, cols] = (qk * cosine[...] + swapped_halves(qk) * sine[...]).astype(BF16)
    v_cols = slice(heads * qk_width, heads * 3 * HEAD_DIM)
    v_out[...] = qkv[:, v_cols].astype(BF16)
    for head in range(heads):
        base = head * qk_width
        for start in range(0, slots, rows):
            at = slice(start, start + rows)
            end = start + rows
            q = qk_out[at, base : base + HEAD_DIM] * BF16(0.125)
            k = qk_out[:end, base + HEAD_DIM : base + qk_width]
            v = v_out[:end, head * HEAD_DIM : (head + 1) * HEAD_DIM]
            scores = masked_scores(q, k, start, length)
            top = jnp.max(scores, axis=-1, keepdims=True)
            raised = jnp.exp(scores - top)
            total = jnp.sum(raised, axis=-1, keepdims=True)
            lse_out[head, at] = top + jnp.log(total)
            probs = (raised * (1.0 / total)).astype(BF16)
            mixed[at, head * HEAD_DIM : (head + 1) * HEAD_DIM] = nn(probs, v).astype(BF16)


def attend(plan, length, x, gain, w, cosine, sine):
    slots, heads = plan.slots, plan.heads
    return pl.pallas_call(
        functools.partial(attend_kernel, plan),
        out_shape=(
            jax.ShapeDtypeStruct((slots, plan.head_cols), BF16),
            jax.ShapeDtypeStruct((slots, plan.width), BF16),
            jax.ShapeDtypeStruct((slots, 2 * plan.head_cols), BF16),
            jax.ShapeDtypeStruct((slots, plan.head_cols), BF16),
            jax.ShapeDtypeStruct((heads, slots, 1), F32),
        ),
        in_specs=[pl.BlockSpec(memory_space=pltpu.SMEM)] + [VMEM] * 5,
        out_specs=(VMEM,) * 5,
        scratch_shapes=[pltpu.VMEM((slots, plan.wide), F32)],
        compiler_params=params(),
        name="attend",
    )(length, x, gain, w, cosine, sine)


def attend_back_kernel(plan, length_ref, x, w, cosine, sine, normed, qk_in, v_in, lse, dmixed, dnp, dw, gain_grad, dqkv, dq_acc, dk_acc, dv_acc):
    length = length_ref[0]
    rows, slots, heads = QUERY_ROWS, plan.slots, plan.heads
    qk_width = 2 * HEAD_DIM
    dqkv[...] = jnp.zeros_like(dqkv)
    for head in range(heads):
        base = head * qk_width
        v_cols = slice(head * HEAD_DIM, (head + 1) * HEAD_DIM)
        for start in range(slots - rows, -1, -rows):
            at = slice(start, start + rows)
            end = start + rows
            q = qk_in[at, base : base + HEAD_DIM] * BF16(0.125)
            k = qk_in[:end, base + HEAD_DIM : base + qk_width]
            v = v_in[:end, v_cols]
            upstream = dmixed[at, v_cols]
            probs = jnp.exp(masked_scores(q, k, start, length) - lse[head, at])
            dv = tn(probs.astype(BF16), upstream)
            prob_grad = nt(upstream, v)
            inner = jnp.sum(probs * prob_grad, axis=-1, keepdims=True)
            score_grad = (probs * (prob_grad - inner)).astype(BF16)
            dq_acc[at] = nn(score_grad, k) * 0.125
            dk = tn(score_grad, q)
            if end == slots:
                dk_acc[...] = dk
                dv_acc[...] = dv
            else:
                dk_acc[:end] += dk
                dv_acc[:end] += dv
        dqk = jnp.concatenate([dq_acc[...], dk_acc[...]], axis=-1)
        dqkv[:, base : base + qk_width] = (
            dqk * cosine[...] - swapped_halves(dqk) * sine[...]
        ).astype(BF16)
        v_base = heads * qk_width + head * HEAD_DIM
        dqkv[:, v_base : v_base + HEAD_DIM] = dv_acc[...].astype(BF16)
    dw[...] = tn(normed[...], dqkv[...]).astype(dw.dtype)
    gains = jnp.zeros((1, plan.width), F32)
    for start in range(0, slots, rows):
        at = slice(start, start + rows)
        part = nt(dqkv[at], w[...])
        dnp[at] = part.astype(BF16)
        values = x[at].astype(F32)
        inverse = lax.rsqrt(jnp.mean(values * values, axis=-1, keepdims=True) + EPSILON)
        gains = gains + jnp.sum(part * values * inverse, axis=0, keepdims=True)
    gain_grad[...] = gains


def attend_back(plan, length, x, w, cosine, sine, normed, qk, v, lse, dmixed):
    slots = plan.slots
    return pl.pallas_call(
        functools.partial(attend_back_kernel, plan),
        out_shape=(
            jax.ShapeDtypeStruct((slots, plan.width), BF16),
            jax.ShapeDtypeStruct((plan.width, plan.wide), F32),
            jax.ShapeDtypeStruct((1, plan.width), F32),
        ),
        in_specs=[pl.BlockSpec(memory_space=pltpu.SMEM)] + [VMEM] * 9,
        out_specs=(VMEM,) * 3,
        scratch_shapes=[
            pltpu.VMEM((slots, plan.wide), BF16),
            pltpu.VMEM((slots, HEAD_DIM), F32),
            pltpu.VMEM((slots, HEAD_DIM), F32),
            pltpu.VMEM((slots, HEAD_DIM), F32),
        ],
        compiler_params=params(),
        name="attend_back",
    )(length, x, w, cosine, sine, normed, qk, v, lse, dmixed)


def ffn_kernel(plan, members, n2x, gy, w_in, w_out, pick, out, n2g, dw_in, dw_out):
    hidden, local = plan.hidden_pad, plan.local

    @pl.when(pl.program_id(0) == 0)
    def start():
        dw_in[...] = jnp.zeros_like(dw_in)
        dw_out[...] = jnp.zeros_like(dw_out)

    tokens = members * local
    width = plan.width
    normed = n2x[:, :local].reshape(tokens, width)
    upstream = gy[...].reshape(tokens, width)
    mixing = jnp.concatenate(
        [tn(n2x[i, local:, :local], pick[...]) for i in range(members)], axis=0
    )
    pre = nn(normed, w_in[...])
    gate, up = pre[:, :hidden], pre[:, hidden:]
    sigmoid = jax.nn.sigmoid(gate)
    silu = gate * sigmoid
    act = (silu * up).astype(BF16).astype(F32)
    act_mixed = (act * mixing).astype(BF16)
    out[...] = nn(act_mixed, w_out[...]).astype(BF16).reshape(members, local, width)
    act_grad = nt(upstream, w_out[...])
    choice = nt(pick[...], (act * act_grad).astype(BF16)).astype(BF16)
    act_grad = act_grad * mixing
    gate_grad = act_grad * up * sigmoid * (1.0 + gate * (1.0 - sigmoid))
    pre_grad = jnp.concatenate([gate_grad, act_grad * silu], axis=-1).astype(BF16)
    n2g[:, :local] = nt(pre_grad, w_in[...]).astype(BF16).reshape(members, local, width)
    pad = jnp.zeros((MIX_ROWS, width - local), BF16)
    for i in range(members):
        n2g[i, local:] = jnp.concatenate(
            [choice[:, i * local : (i + 1) * local], pad], axis=-1
        )
    dw_in[...] += tn(normed, pre_grad)
    dw_out[...] += tn(act_mixed, upstream)


def ffn(plan, n2x, gy, w_in, w_out, pick):
    members = 2
    local, width, hidden = plan.local, plan.width, plan.hidden_pad
    whole = lambda i: (0, 0)
    part = lambda i: (i, 0, 0)
    return pl.pallas_call(
        functools.partial(ffn_kernel, plan, members),
        grid=(plan.group // members,),
        out_shape=(
            jax.ShapeDtypeStruct((plan.group, local, width), BF16),
            jax.ShapeDtypeStruct((plan.group, local + MIX_ROWS, width), BF16),
            jax.ShapeDtypeStruct((width, 2 * hidden), F32),
            jax.ShapeDtypeStruct((hidden, width), F32),
        ),
        in_specs=[
            pl.BlockSpec((members, local + MIX_ROWS, width), part),
            pl.BlockSpec((members, local, width), part),
            pl.BlockSpec((width, 2 * hidden), whole),
            pl.BlockSpec((hidden, width), whole),
            pl.BlockSpec((MIX_ROWS, hidden), whole),
        ],
        out_specs=(
            pl.BlockSpec((members, local, width), part),
            pl.BlockSpec((members, local + MIX_ROWS, width), part),
            pl.BlockSpec((width, 2 * hidden), whole),
            pl.BlockSpec((hidden, width), whole),
        ),
        compiler_params=params(),
        name="ffn",
    )(n2x, gy, w_in, w_out, pick)


STEP_ORDER = ((0, 0, 0), (0, 1, 0), (0, 1, 1), (1, 1, 0), (1, 1, 1), (1, 0, 1), (1, 0, 0), (0, 0, 1))
FUSED_GATHER = (("high", "low", "y"), ("y", "low", "high"))
FUSED_REDUCE = (("low", "high", "y"), ("y", "high", "low"))


def named(offset):
    return dict(zip(("high", "low", "y"), offset))


def sum_plan(order):
    taken = {offset: step for step, offset in enumerate(STEP_ORDER)}
    names = ("high", "low", "y")
    rows, ready = [], {}
    for phase in range(4):
        for offset in STEP_ORDER:
            at = named(offset)
            if any(at[axis] for axis in order[:phase]) or (phase < 3 and not at[order[phase]]):
                continue
            if phase == 3 and any(offset):
                continue
            feeds = [
                tuple(1 if name == axis else at[name] for name in names) for axis in order[:phase]
            ]
            when = max([taken[offset] + 1] + [ready[feed] for feed in feeds])
            rows.append((when, phase, offset, order[phase] if phase < 3 else None, feeds))
            ready[offset] = when + 2
    rows.sort(key=lambda row: (row[0], row[1]))
    return rows


def fused_kernel(plan, n2x, gy, w_in, w_out, pick, total, dw_in, dw_out, n2all, gybuf, acc, away, work, core_buf, bufs, gy_sem, g_send, g_recv, gc_send, gc_recv, c_send, c_recv, r_send, r_recv):
    grid = Grid(plan)
    at = grid.here()
    local, width, hidden = plan.local, plan.width, plan.hidden_pad
    steps = len(STEP_ORDER)
    partner = grid.device(grid.moved(at, "core", 1))
    here = grid.device(at)
    colors = range(2)

    def absolute(offset):
        where = dict(at)
        for axis, step in named(offset).items():
            if step:
                where = grid.moved(where, axis, step)
        return where

    def slot_of(offset):
        return grid.slot(named(offset))

    send_index = [{}, {}]
    for color in colors:
        for offset in STEP_ORDER:
            order = FUSED_GATHER[color]
            reached = named(offset)
            level = max([i + 1 for i, axis in enumerate(order) if reached[axis]], default=0)
            for axis in order[level:]:
                send_index[color][(offset, axis)] = len(send_index[color])

    def pass_on(color, offset):
        order = FUSED_GATHER[color]
        reached = named(offset)
        level = max([i + 1 for i, axis in enumerate(order) if reached[axis]], default=0)
        where = absolute(offset)
        block = grid.block(where)
        slot = slot_of(offset)
        if level:
            remote(n2all.at[block], n2all.at[block], g_send.at[0], g_recv.at[slot], here).wait_recv()
        source = n2all.at[block] if level else n2x
        remote(source, n2all.at[block], gc_send.at[slot], gc_recv.at[slot], partner).start()
        for axis in order[level:]:
            seen = grid.slot({**reached, axis: 1})
            remote(
                source,
                n2all.at[block],
                g_send.at[send_index[color][(offset, axis)]],
                g_recv.at[seen],
                grid.device(grid.moved(at, axis, 1)),
            ).start()

    plans = [sum_plan(order) for order in FUSED_REDUCE]
    buf_index = [{row[2]: i for i, row in enumerate(rows) if row[3]} for rows in plans]

    def add_up(color, row):
        _, _, offset, axis, feeds = row
        slot = slot_of(offset)
        remote(away.at[0], core_buf.at[slot], c_send.at[0], c_recv.at[slot], here).wait_recv()
        for feed in feeds:
            index = buf_index[color][feed]
            remote(away.at[0], bufs.at[index], r_send.at[0], r_recv.at[index], here).wait_recv()
        rows = work.shape[1]
        chunk = 48

        @pl.loop(0, rows // chunk)
        def _(i):
            span = pl.ds(pl.multiple_of(i * chunk, 16), chunk)
            value = work[slot, span].astype(F32) + core_buf[slot, span].astype(F32)
            for feed in feeds:
                value = value + bufs[buf_index[color][feed], span].astype(F32)
            if axis is None:
                total[span] = value
            else:
                work[slot, span] = value.astype(BF16)

        if axis is not None:
            index = buf_index[color][offset]
            remote(
                work.at[slot],
                bufs.at[index],
                r_send.at[index],
                r_recv.at[index],
                grid.device(grid.moved(at, axis, 1)),
            ).start()

    def pump(step):
        def run(color):
            for offset in STEP_ORDER:
                if 0 < step == sum(offset):
                    pass_on(color, offset)
            for row in plans[color]:
                if row[0] == step or (step == steps and row[0] > steps):
                    add_up(color, row)

        for color in colors:
            pl.when(at["core"] == color)(functools.partial(run, color))

    def bit(step, index):
        value = 0
        for i, offset in enumerate(STEP_ORDER):
            if offset[index]:
                value = value + jnp.where(step == i, 1, 0)
        return value

    def blocks_of(step):
        where = dict(at)
        offsets = {}
        for index, axis in enumerate(("high", "low", "y")):
            offsets[axis] = bit(step, index)
            where[axis] = lax.rem(at[axis] + offsets[axis], 2)
        mine = grid.block(where)
        other = grid.block(grid.moved(where, "core", 1))
        return mine, other, grid.slot(offsets)

    def gy_loads(step, turn):
        mine, other, _ = blocks_of(step)
        return [
            pltpu.make_async_copy(gy.at[mine], gybuf.at[turn, 0], gy_sem.at[turn, 0]),
            pltpu.make_async_copy(gy.at[other], gybuf.at[turn, 1], gy_sem.at[turn, 1]),
        ]

    for load in gy_loads(0, 0):
        load.start()
    meet(grid.peers(at))
    for color in colors:
        pl.when(at["core"] == color)(functools.partial(pass_on, color, STEP_ORDER[0]))
    n2all[pl.ds(grid.block(at), 1)] = n2x[...][None]
    acc[...] = jnp.zeros_like(acc)
    dw_out[...] = jnp.zeros_like(dw_out)

    @pl.loop(0, steps)
    def _(step):
        for i in range(1, steps):
            pl.when(step == i)(functools.partial(pump, i))
        mine, other, slot = blocks_of(step)
        turn = lax.rem(step, 2)

        @pl.when(step + 1 < steps)
        def _():
            for load in gy_loads(step + 1, 1 - turn):
                load.start()

        remote(n2x, n2all.at[other], gc_send.at[0], gc_recv.at[slot], here).wait_recv()
        for load in gy_loads(step, turn):
            load.wait()
        pair = (mine, other)
        normed = jnp.concatenate([n2all[b, :local] for b in pair], axis=0)
        upstream = gybuf[turn].reshape(2 * local, width)
        mixing = jnp.concatenate([tn(n2all[b, local:, :local], pick[...]) for b in pair], axis=0)
        pre = nn(normed, w_in[...])
        gate, up = pre[:, :hidden], pre[:, hidden:]
        sigmoid = jax.nn.sigmoid(gate)
        silu = gate * sigmoid
        act = (silu * up).astype(BF16).astype(F32)
        act_mixed = (act * mixing).astype(BF16)
        out = nn(act_mixed, w_out[...]).astype(BF16)
        act_grad = nt(upstream, w_out[...])
        choice = nt(pick[...], (act * act_grad).astype(BF16)).astype(BF16)
        act_grad = act_grad * mixing
        gate_grad = act_grad * up * sigmoid * (1.0 + gate * (1.0 - sigmoid))
        pre_grad = jnp.concatenate([gate_grad, act_grad * silu], axis=-1).astype(BF16)
        n2g = nt(pre_grad, w_in[...]).astype(BF16)

        @pl.when(step >= 2)
        def _():
            remote(away.at[turn], core_buf.at[0], c_send.at[turn], c_recv.at[0], partner).wait_send()

        pad = jnp.zeros((MIX_ROWS, width - local), BF16)
        for i, (ref, index) in enumerate(((work, slot), (away, turn))):
            span = slice(i * local, (i + 1) * local)
            ref[index, :local] = n2g[span]
            ref[index, local : local + MIX_ROWS] = jnp.concatenate([choice[:, span], pad], axis=-1)
            ref[index, local + MIX_ROWS :] = out[span]
        remote(away.at[turn], core_buf.at[slot], c_send.at[turn], c_recv.at[slot], partner).start()
        acc[...] += tn(normed, pre_grad)
        dw_out[...] += tn(act_mixed, upstream)

    pump(steps)
    dw_in[...] = acc[...].astype(BF16)
    for turn in range(2):
        remote(away.at[turn], core_buf.at[0], c_send.at[turn], c_recv.at[0], partner).wait_send()
    for slot in range(steps):
        remote(n2x, n2all.at[0], gc_send.at[slot], gc_recv.at[0], partner).wait_send()
    for index in range(steps - 1):
        remote(n2x, n2all.at[0], g_send.at[index], g_recv.at[0], partner).wait_send()
        remote(work.at[0], bufs.at[index], r_send.at[index], r_recv.at[0], partner).wait_send()


def fused(plan, n2x, gy, w_in, w_out, pick, collective_id):
    local, width, hidden = plan.local, plan.width, plan.hidden_pad
    steps = len(STEP_ORDER)
    rows = 2 * local + MIX_ROWS
    return pl.pallas_call(
        functools.partial(fused_kernel, plan),
        out_shape=(
            jax.ShapeDtypeStruct((rows, width), F32),
            jax.ShapeDtypeStruct((width, 2 * hidden), BF16),
            jax.ShapeDtypeStruct((hidden, width), F32),
        ),
        in_specs=[VMEM, HBM, VMEM, VMEM, VMEM],
        out_specs=(VMEM,) * 3,
        scratch_shapes=[
            pltpu.VMEM((plan.group, local + MIX_ROWS, width), BF16),
            pltpu.VMEM((2, 2, local, width), BF16),
            pltpu.VMEM((width, 2 * hidden), F32),
            pltpu.VMEM((2, rows, width), BF16),
            pltpu.VMEM((steps, rows, width), BF16),
            pltpu.VMEM((steps, rows, width), BF16),
            pltpu.VMEM((steps - 1, rows, width), BF16),
            DMA((2, 2)),
            DMA((steps - 1,)),
            DMA((steps,)),
            DMA((steps,)),
            DMA((steps,)),
            DMA((2,)),
            DMA((steps,)),
            DMA((steps - 1,)),
            DMA((steps - 1,)),
        ],
        compiler_params=params(collective_id),
        name="fused",
    )(n2x, gy, w_in, w_out, pick)


def by_half(half, mine, far, axis):
    return jnp.where(
        half == 0, jnp.stack([mine, far], axis), jnp.stack([far, mine], axis)
    )


def rope_tables(plan):
    half = HEAD_DIM // 2
    frequency = np.float32(10000.0) ** (-np.arange(half, dtype=np.float32) / np.float32(half))
    angles = np.arange(plan.slots, dtype=np.float32)[:, None] * frequency[None, :]
    cosine = np.cos(angles.astype(np.float64)).astype(np.float32)
    sine = np.sin(angles.astype(np.float64)).astype(np.float32)
    return np.tile(cosine, (1, 4)), np.tile(np.concatenate([-sine, sine], 1), (1, 2))


def pick_table(plan):
    table = np.zeros((MIX_ROWS, plan.hidden_pad), np.float32)
    span = HALVES * plan.own_hidden
    for expert in range(plan.experts):
        cols = slice((1 + expert) * span, (2 + expert) * span)
        table[expert, cols] = 1.0
        table[plan.experts + expert, cols] = 1.0
    table[2 * plan.experts, :span] = 1.0
    return jnp.asarray(table, BF16)


def pack_qkv(plan, attn_in, attn_gain, ffn_gain, router):
    rows, quad, heads = plan.rows, plan.quad, plan.heads
    qkv = attn_in.reshape(rows, 3, HEADS, HEAD_DIM)
    qkv = jnp.pad(qkv, ((0, 0), (0, 0), (0, quad * heads - HEADS), (0, 0)))
    qkv = qkv.reshape(rows, 3, quad, heads, HEAD_DIM)
    qk = jnp.transpose(qkv[:, :2], (2, 0, 3, 1, 4)).reshape(quad, rows, 2 * plan.head_cols)
    v = jnp.transpose(qkv[:, 2], (1, 0, 2, 3)).reshape(quad, rows, plan.head_cols)
    extra = jnp.concatenate([attn_gain[:, None], ffn_gain[:, None], router], axis=1)
    extra = jnp.pad(extra, ((0, 0), (0, plan.wide - plan.qkv_cols - extra.shape[1])))
    extra = jnp.broadcast_to(extra[None], (quad,) + extra.shape)
    return jnp.concatenate([qk, v, extra], axis=-1)


def unpack_qkv(plan, packed):
    rows, quad, heads = plan.rows, plan.quad, plan.heads
    qk = packed[..., : 2 * plan.head_cols].reshape(quad, rows, heads, 2, HEAD_DIM)
    v = packed[..., 2 * plan.head_cols : plan.qkv_cols].reshape(quad, rows, heads, 1, HEAD_DIM)
    qkv = jnp.transpose(jnp.concatenate([qk, v], axis=3), (1, 3, 0, 2, 4))
    qkv = qkv.reshape(rows, 3, quad * heads, HEAD_DIM)[:, :, :HEADS]
    return qkv.reshape(rows, 3 * HEADS * HEAD_DIM)


def pack_in(plan, dense_in, expert_in):
    rows, own = plan.rows, plan.own_hidden
    both = jnp.concatenate([dense_in[:, None], expert_in], axis=1)
    both = both.reshape(rows, plan.branches, 2, plan.dp, HALVES, plan.quad, own)
    both = jnp.transpose(both, (3, 5, 0, 2, 1, 4, 6))
    both = both.reshape(plan.group, rows, 2, plan.hidden)
    both = jnp.pad(both, ((0, 0), (0, 0), (0, 0), (0, plan.hidden_pad - plan.hidden)))
    return both.reshape(plan.group, rows, 2 * plan.hidden_pad)


def unpack_in(plan, packed):
    rows, own = plan.rows, plan.own_hidden
    both = packed.reshape(plan.group, rows, 2, plan.hidden_pad)[..., : plan.hidden]
    both = both.reshape(plan.dp, plan.quad, rows, 2, plan.branches, HALVES, own)
    both = jnp.transpose(both, (2, 4, 3, 0, 5, 1, 6))
    both = both.reshape(rows, plan.branches, 2 * FF).astype(F32)
    return both[:, 0], both[:, 1:]


def shards(
    tokens,
    lengths,
    routes,
    cotangent,
    attn_gain,
    attn_in,
    attn_out,
    ffn_gain,
    router,
    dense_in,
    dense_out,
    expert_in,
    expert_out,
):
    micro, seqs, block, width = tokens.shape
    experts = expert_in.shape[1]
    plan = Plan(lax.axis_size("dp"), lax.axis_size("ctx"), block, width, experts)
    assert micro == HALVES and seqs == 1 and plan.ctx % 4 == 0 and plan.dp % 2 == 0
    quad, local = plan.quad, plan.local
    dp, ctx = place()
    half, member = lax.div(ctx, quad), lax.rem(ctx, quad)
    across = [(i, (i + quad) % plan.ctx) for i in range(plan.ctx)]

    def swap(value):
        return lax.ppermute(value, "ctx", across)

    def pick_mine(value):
        return lax.dynamic_index_in_dim(value, half, 0, keepdims=False)

    def pick_far(value):
        return lax.dynamic_index_in_dim(value, 1 - half, 0, keepdims=False)

    cot, route = cotangent[:, 0], routes[:, 0]
    length = pick_mine(lengths)
    out_own = jnp.concatenate([dense_out[:, None], expert_out], axis=1)
    out_own = jnp.transpose(out_own, (1, 0, 2))
    cot_local = jnp.stack([pick_mine(cot), swap(pick_far(cot))])
    route_local = jnp.stack([pick_mine(route), swap(pick_far(route))]).reshape(local, 2)
    out_far = swap(out_own)
    w_mix = lax.all_gather(attn_out, ("dp", "ctx"), axis=0, tiled=True)

    xs, wall, win_mine = spread(
        plan,
        tokens[:, 0],
        pack_qkv(plan, attn_in, attn_gain, ffn_gain, router),
        pack_in(plan, dense_in, expert_in),
    )
    win_far = swap(win_mine)

    x_seq = xs.reshape(plan.slots, width)
    w_seq = wall.reshape(width, plan.wide)
    extra = w_seq[:, plan.qkv_cols :]
    gain_one = extra[:, 0].astype(F32)[None]
    gain_two = extra[:, 1].astype(F32)[None]
    w_route = extra[:, 2 : 2 + experts]
    cosine, sine = (jnp.asarray(table) for table in rope_tables(plan))
    mixed_seq, normed_seq, qk, v, lse = attend(plan, length, x_seq, gain_one, w_seq, cosine, sine)
    mixed = to_owners(plan, mixed_seq.reshape(plan.ctx, block, plan.head_cols), 2)
    mixed = jnp.transpose(mixed, (1, 2, 0, 3)).reshape(local, quad * plan.head_cols)[:, :width]

    x = jnp.stack(
        [
            lax.dynamic_index_in_dim(xs, ctx, 0, keepdims=False),
            lax.dynamic_index_in_dim(xs, (1 - half) * quad + member, 0, keepdims=False),
        ]
    )
    x = x.reshape(local, width).astype(F32)
    middle = x + nn(mixed, w_mix)
    inverse_two = lax.rsqrt(jnp.mean(middle * middle, axis=-1, keepdims=True) + EPSILON)
    normed_two = (middle * inverse_two * gain_two).astype(BF16)
    logits = nn(normed_two, w_route)
    choose = (route_local[..., None] == jnp.arange(experts, dtype=jnp.int32)).astype(F32)
    picked = jnp.sum(choose * logits[:, None, :], axis=-1)
    gates = jax.nn.softmax(picked, axis=-1)
    mixing = jnp.sum(gates[..., None] * choose, axis=1)
    mixing_t = mixing.T
    mixing_high = mixing_t.astype(BF16)
    mixing_low = (mixing_t - mixing_high.astype(F32)).astype(BF16)
    mix_rows = jnp.concatenate(
        [
            mixing_high,
            mixing_low,
            jnp.ones((1, local), BF16),
            jnp.zeros((MIX_ROWS - 2 * experts - 1, local), BF16),
        ]
    )
    mix_rows = jnp.pad(mix_rows, ((0, 0), (0, width - local)))
    n2x = jnp.concatenate([normed_two, mix_rows])

    starts = jnp.stack([ctx, (1 - half) * quad + member]) * block
    slot = (starts[:, None] + jnp.arange(block, dtype=jnp.int32)[None]).reshape(local)
    valid = (slot < length[0]).astype(BF16)[:, None]
    grad_y = cot_local.reshape(local, width) * valid
    gy = gather(plan, grad_y, 4)

    rows_in = (plan.dp, quad, plan.rows, 2 * plan.hidden_pad)
    w_in = by_half(half, win_mine.reshape(rows_in), win_far.reshape(rows_in), 1)
    w_in = w_in.reshape(width, 2 * plan.hidden_pad)
    w_out = by_half(half, out_own, out_far, 1).reshape(plan.hidden, width)
    w_out = jnp.pad(w_out, ((0, plan.hidden_pad - plan.hidden), (0, 0)))
    if plan.dp == 4 and quad == 4:
        sums, dw_in, dw_out = fused(plan, n2x, gy, w_in, w_out, pick_table(plan), 3)
        n2g_sum, out_sum = sums[: local + MIX_ROWS], sums[local + MIX_ROWS :]
    else:
        n2x = gather(plan, n2x, 3)
        out_part, n2g_part, dw_in, dw_out = ffn(plan, n2x, gy, w_in, w_out, pick_table(plan))
        n2g_sum = reduce(plan, n2g_part, 5)
        out_sum = reduce(plan, out_part, 7)
    activations = (middle + out_sum).astype(BF16).reshape(2, block, width)

    dw_out = dw_out[: plan.hidden].reshape(plan.branches, HALVES, plan.own_hidden, width)
    dw_out = jnp.moveaxis(dw_out, 1, 0)
    dw_out = pick_mine(dw_out) + swap(pick_far(dw_out).astype(BF16)).astype(F32)
    dw_in = dw_in.reshape(plan.dp, HALVES, quad, plan.rows, 2 * plan.hidden_pad)
    dw_in = jnp.moveaxis(dw_in, 1, 0)
    dw_in = pick_mine(dw_in).astype(F32) + swap(pick_far(dw_in).astype(BF16)).astype(F32)
    dw_in = dw_in.astype(BF16).reshape(plan.group, plan.rows, 2 * plan.hidden_pad)

    normed_two_grad = n2g_sum[:local]
    mixing_grad = n2g_sum[local : local + experts, :local].T
    choice_grad = jnp.sum(choose * mixing_grad[:, None, :], axis=-1)
    pick_grad = gates * (choice_grad - jnp.sum(gates * choice_grad, axis=-1, keepdims=True))
    logit_grad = jnp.sum(pick_grad[..., None] * choose, axis=1).astype(BF16)
    router_grad = tn(normed_two, logit_grad)
    normed_two_grad = normed_two_grad + nt(logit_grad, w_route)
    gain_two_grad = jnp.sum(normed_two_grad * middle * inverse_two, axis=0)
    scaled = normed_two_grad * gain_two
    middle_grad = (
        grad_y.astype(F32)
        + inverse_two * scaled
        - middle * inverse_two**3 * jnp.mean(scaled * middle, axis=-1, keepdims=True)
    )
    attn_grad = middle_grad.astype(BF16)
    dw_mix = tn(mixed, attn_grad).astype(BF16).reshape(plan.devices, plan.rows, width)
    mixed_grad = nt(attn_grad, w_mix).astype(BF16)
    mixed_grad = jnp.pad(mixed_grad, ((0, 0), (0, quad * plan.head_cols - width)))
    mixed_grad = mixed_grad.reshape(2, block, quad, plan.head_cols)
    dmixed = to_slots(plan, jnp.transpose(mixed_grad, (2, 0, 1, 3)), 8)
    dnp, dw_qkv, gain_one_grad = attend_back(
        plan,
        length,
        x_seq,
        w_seq,
        cosine,
        sine,
        normed_seq,
        qk,
        v,
        lse,
        dmixed.reshape(plan.slots, plan.head_cols),
    )
    small = jnp.concatenate([gain_one_grad.T, gain_two_grad[:, None], router_grad], axis=1)
    small = jnp.pad(small, ((0, 0), (0, plan.wide - plan.qkv_cols - small.shape[1])))
    dw_qkv = jnp.concatenate([dw_qkv[:, : plan.qkv_cols], small], axis=1).astype(BF16)
    dn, r_qkv, r_mix, r_in = collect(
        plan,
        dnp.reshape(plan.ctx, block, width),
        dw_qkv.reshape(plan.devices, plan.rows, plan.wide),
        dw_mix,
        dw_in,
    )

    normed_grad = jnp.sum(dn.astype(F32), axis=0).reshape(local, width)
    inverse_one = lax.rsqrt(jnp.mean(x * x, axis=-1, keepdims=True) + EPSILON)
    scaled = normed_grad * gain_one
    input_grad = (
        middle_grad
        + inverse_one * scaled
        - x * inverse_one**3 * jnp.mean(scaled * x, axis=-1, keepdims=True)
    )
    input_grad = input_grad.astype(BF16).reshape(2, block, width)
    r_qkv = r_qkv.astype(F32).reshape(plan.dp * HALVES, quad, plan.rows, plan.wide)
    r_qkv = jnp.sum(r_qkv, axis=0)
    attn_in_grad = unpack_qkv(plan, r_qkv)
    small = jnp.sum(r_qkv[:, :, plan.qkv_cols :], axis=0)
    attn_out_grad = jnp.sum(r_mix.astype(F32), axis=0)
    dense_in_grad, expert_in_grad = unpack_in(plan, r_in)
    return (
        by_half(half, activations[0], swap(activations[1]), 0)[:, None],
        by_half(half, input_grad[0], swap(input_grad[1]), 0)[:, None],
        small[:, 0],
        attn_in_grad,
        attn_out_grad,
        small[:, 1],
        small[:, 2 : 2 + experts],
        dense_in_grad,
        dw_out[0],
        expert_in_grad,
        jnp.transpose(dw_out[1:], (1, 0, 2)),
    )


def solution(mesh):
    rows = P(("dp", "ctx"))
    matrix = P(("dp", "ctx"), None)
    cube = P(("dp", "ctx"), None, None)
    slots = P(None, "dp", "ctx", None)
    in_specs = (
        slots,
        P(None, "dp"),
        slots,
        slots,
        rows,
        matrix,
        matrix,
        rows,
        matrix,
        matrix,
        matrix,
        cube,
        cube,
    )
    out_specs = (
        slots,
        slots,
        rows,
        matrix,
        matrix,
        rows,
        matrix,
        matrix,
        matrix,
        cube,
        cube,
    )
    return jax.shard_map(shards, mesh=mesh, in_specs=in_specs, out_specs=out_specs, check_vma=False)
```

```python
import functools

import jax
import jax.numpy as jnp
import numpy as np
from jax import lax
from jax.experimental import pallas as pl
from jax.experimental.pallas import tpu as pltpu
from jax.sharding import PartitionSpec as P

HEADS = 12
HEAD_DIM = 64
FF = 2048
EPSILON = 1e-05
HALVES = 2
QUERY_ROWS = 256
MIX_ROWS = 16
MESH = pl.DeviceIdType.MESH
BF16 = jnp.bfloat16
F32 = jnp.float32


def round_up(value, step):
    return -(-value // step) * step


class Plan:
    def __init__(self, dp, ctx, block, width, experts):
        self.dp, self.ctx, self.block, self.width, self.experts = dp, ctx, block, width, experts
        self.quad = ctx // HALVES
        self.devices = dp * ctx
        self.group = dp * self.quad
        self.slots = ctx * block
        self.rows = width // self.devices
        self.pad_rows = round_up(self.rows, 8)
        self.heads = -(-HEADS // self.quad)
        self.head_cols = self.heads * HEAD_DIM
        self.qkv_cols = 3 * self.head_cols
        self.wide = round_up(self.qkv_cols + 2 + experts, 128)
        self.own_hidden = FF // self.devices
        self.branches = 1 + experts
        self.hidden = self.branches * HALVES * self.own_hidden
        self.hidden_pad = round_up(self.hidden, 128)
        self.local = HALVES * block


def place():
    return lax.axis_index("dp"), lax.axis_index("ctx")


def params(collective_id=None, limit=60 * 1024 * 1024):
    if collective_id is None:
        return pltpu.CompilerParams(vmem_limit_bytes=limit)
    return pltpu.CompilerParams(
        vmem_limit_bytes=limit, collective_id=collective_id, has_side_effects=True
    )


def remote(src, dst, send_sem, recv_sem, device):
    return pltpu.make_async_remote_copy(
        src_ref=src,
        dst_ref=dst,
        send_sem=send_sem,
        recv_sem=recv_sem,
        device_id=device,
        device_id_type=MESH,
    )


def busy(microseconds):
    return pl.CostEstimate(
        flops=0, bytes_accessed=int(microseconds * 3.4e6), transcendentals=0
    )


def meet(devices):
    barrier = pltpu.get_barrier_semaphore()
    for device in devices:
        pl.semaphore_signal(barrier, inc=1, device_id=device, device_id_type=MESH)
    pl.semaphore_wait(barrier, len(devices))


def other_devices(plan, dp, ctx):
    flat = dp * plan.ctx + ctx
    result = []
    for step in range(1, plan.devices):
        target = lax.rem(flat + step, plan.devices)
        result.append((lax.div(target, plan.ctx), lax.rem(target, plan.ctx)))
    return result


def quad_members(plan, half, member):
    return [
        (half * plan.quad + lax.rem(member + step, plan.quad), lax.rem(member + step, plan.quad))
        for step in range(1, plan.quad)
    ]


VMEM = pl.BlockSpec(memory_space=pltpu.VMEM)
HBM = pl.BlockSpec(memory_space=pl.ANY)
DMA = pltpu.SemaphoreType.DMA


def half_members(plan, mine):
    return [lax.rem(mine + step, plan.group) for step in range(1, plan.group)]


class Grid:
    def __init__(self, plan):
        self.plan = plan
        self.sizes = {"y": plan.dp // 2, "high": plan.quad // 2, "low": 2}

    def here(self):
        dp, ctx = place()
        member = lax.rem(ctx, self.plan.quad)
        return {
            "core": lax.rem(dp, 2),
            "y": lax.div(dp, 2),
            "high": lax.div(member, 2),
            "low": lax.rem(member, 2),
            "half": lax.div(ctx, self.plan.quad),
        }

    def device(self, at):
        return (
            at["y"] * 2 + at["core"],
            at["half"] * self.plan.quad + at["high"] * 2 + at["low"],
        )

    def block(self, at):
        return (at["y"] * 2 + at["core"]) * self.plan.quad + at["high"] * 2 + at["low"]

    def moved(self, at, axis, step):
        result = dict(at)
        if axis == "core":
            result["core"] = 1 - at["core"]
        else:
            result[axis] = lax.rem(at[axis] + step, self.sizes[axis])
        return result

    def peers(self, at):
        result = [self.moved(at, "core", 1)]
        for axis, size in self.sizes.items():
            result += [self.moved(at, axis, step) for step in range(1, size)]
        return [self.device(peer) for peer in result]

    def slot(self, offsets):
        return (offsets["y"] * self.sizes["high"] + offsets["high"]) * 2 + offsets["low"]


GATHER_ORDERS = (("high", "low", "y"), ("high", "y", "low"))


class Gather:
    def __init__(self, grid, at, src, dst, send, recv, core_send, core_recv):
        self.grid, self.at, self.src, self.dst = grid, at, src, dst
        self.send, self.recv, self.core_send, self.core_recv = send, recv, core_send, core_recv

    def groups(self, order):
        sizes = self.grid.sizes
        levels = [[{"y": 0, "high": 0, "low": 0}], [], [], []]
        for level, axis in enumerate(order):
            base = [o for group in levels[: level + 1] for o in group]
            levels[level + 1] = [
                {**offsets, axis: step} for offsets in base for step in range(1, sizes[axis])
            ]
        return levels

    def absolute(self, offsets):
        where = dict(self.at)
        for axis, step in offsets.items():
            if step:
                where = self.grid.moved(where, axis, step)
        return where

    def run_level(self, order, level):
        grid, at = self.grid, self.at
        index = 0
        for current, group in enumerate(self.groups(order)):
            for offsets in group:
                if current == level:
                    block = grid.block(self.absolute(offsets))
                    if level:
                        remote(
                            self.src,
                            self.dst.at[block],
                            self.send.at[0],
                            self.recv.at[grid.slot(offsets)],
                            grid.device(at),
                        ).wait_recv()
                    source = self.dst.at[block] if level else self.src
                    remote(
                        source,
                        self.dst.at[block],
                        self.core_send.at[grid.slot(offsets)],
                        self.core_recv.at[grid.slot(offsets)],
                        grid.device(grid.moved(at, "core", 1)),
                    ).start()
                for axis in order[current:]:
                    for step in range(1, grid.sizes[axis]):
                        if current == level:
                            seen = {**offsets, axis: grid.sizes[axis] - step}
                            remote(
                                source,
                                self.dst.at[block],
                                self.send.at[index],
                                self.recv.at[grid.slot(seen)],
                                grid.device(grid.moved(at, axis, step)),
                            ).start()
                        index += 1

    def level(self, level):
        for color, order in enumerate(GATHER_ORDERS):
            pl.when(self.at["core"] == color)(functools.partial(self.run_level, order, level))

    def finish(self):
        plan, here = self.grid.plan, self.grid.device(self.at)

        def sent(order):
            for index in range(gather_sends(plan, order)):
                remote(self.src, self.dst.at[0], self.send.at[index], self.recv.at[0], here).wait_send()

        for color, order in enumerate(GATHER_ORDERS):
            pl.when(self.at["core"] == color)(functools.partial(sent, order))
        for slot in range(plan.group // 2):
            remote(
                self.src, self.dst.at[0], self.core_send.at[slot], self.core_recv.at[slot], here
            ).wait()


def gather_kernel(plan, src, dst, send, recv, core_send, core_recv):
    grid = Grid(plan)
    at = grid.here()
    meet(grid.peers(at))
    dst[pl.ds(grid.block(at), 1)] = src[...][None]
    blocks = Gather(grid, at, src, dst, send, recv, core_send, core_recv)
    for level in range(4):
        blocks.level(level)
    blocks.finish()


def gather_sems(plan):
    half = plan.group // 2
    count = max(gather_sends(plan, order) for order in GATHER_ORDERS)
    return [DMA((count,)), DMA((half,)), DMA((half,)), DMA((half,))]


def gather_sends(plan, order):
    sizes = Grid(plan).sizes
    held, total = 1, 0
    for axis in order:
        total += held * (sizes[axis] - 1)
        held *= sizes[axis]
    return total


def gather(plan, block, collective_id):
    return pl.pallas_call(
        functools.partial(gather_kernel, plan),
        out_shape=jax.ShapeDtypeStruct((plan.group,) + block.shape, block.dtype),
        in_specs=[VMEM],
        out_specs=VMEM,
        scratch_shapes=gather_sems(plan),
        compiler_params=params(collective_id),
        cost_estimate=busy(35),
        name="gather",
    )(block)


def reduce_kernel(plan, src, out, work, core_buf, bufs, load_sem, core_send, core_recv, send, recv):
    grid = Grid(plan)
    at = grid.here()
    zero = {"y": 0, "high": 0, "low": 0}
    meet(grid.peers(at))

    def run(order):
        levels = [[], [], [], []]
        held = [dict(zero)]
        levels[3] = [dict(zero)]
        for level in (2, 1, 0):
            axis = order[level]
            base = [o for later in levels[level + 1 :] for o in later]
            levels[level] = [
                {**offsets, axis: step} for offsets in base for step in range(1, grid.sizes[axis])
            ]
        del held

        def absolute(offsets):
            where = dict(at)
            for axis, step in offsets.items():
                if step:
                    where = grid.moved(where, axis, step)
            return where

        sequence = [o for group in levels for o in group]
        partner = grid.device(grid.moved(at, "core", 1))
        core_copies = []
        loads = []
        for offsets in sequence:
            where = absolute(offsets)
            slot = grid.slot(offsets)
            copy = remote(
                src.at[grid.block(grid.moved(where, "core", 1))],
                core_buf.at[slot],
                core_send.at[slot],
                core_recv.at[slot],
                partner,
            )
            copy.start()
            core_copies.append(copy)
            load = pltpu.make_async_copy(
                src.at[grid.block(where)], work.at[slot], load_sem.at[slot]
            )
            load.start()
            loads.append(load)
        arrived = {}
        sends = []
        index = 0
        position = 0
        for level in range(4):
            for offsets in levels[level]:
                slot = grid.slot(offsets)
                core_copies[position].wait_recv()
                loads[position].wait()
                position += 1
                total = work[slot].astype(F32) + core_buf[slot].astype(F32)
                for buffer in arrived.get(slot, ()):
                    remote(work.at[slot], bufs.at[buffer], send.at[0], recv.at[buffer], partner).wait_recv()
                    total = total + bufs[buffer].astype(F32)
                if level == 3:
                    out[...] = total.astype(out.dtype)
                    continue
                work[slot] = total.astype(BF16)
                axis = order[level]
                step = offsets[axis]
                copy = remote(
                    work.at[slot],
                    bufs.at[index],
                    send.at[index],
                    recv.at[index],
                    grid.device(grid.moved(at, axis, step)),
                )
                copy.start()
                sends.append(copy)
                landing = grid.slot({**offsets, axis: 0})
                arrived.setdefault(landing, []).append(index)
                index += 1
        for copy in sends:
            copy.wait_send()
        for copy in core_copies:
            copy.wait_send()

    for color, order in enumerate(GATHER_ORDERS):
        pl.when(at["core"] == color)(functools.partial(run, order[::-1]))


def reduce(plan, blocks, collective_id):
    half = plan.group // 2
    shape = blocks.shape[1:]
    count = max(gather_sends(plan, order) for order in GATHER_ORDERS)
    return pl.pallas_call(
        functools.partial(reduce_kernel, plan),
        out_shape=jax.ShapeDtypeStruct(shape, F32),
        in_specs=[HBM],
        out_specs=VMEM,
        scratch_shapes=[
            pltpu.VMEM((half,) + shape, BF16),
            pltpu.VMEM((half,) + shape, BF16),
            pltpu.VMEM((count,) + shape, BF16),
            DMA((half,)),
            DMA((half,)),
            DMA((half,)),
            DMA((count,)),
            DMA((count,)),
        ],
        compiler_params=params(collective_id),
        name="reduce",
    )(blocks)


def nt(left, right):
    return lax.dot_general(left, right, (((1,), (1,)), ((), ())), preferred_element_type=F32)


def nn(left, right):
    return lax.dot_general(left, right, (((1,), (0,)), ((), ())), preferred_element_type=F32)


def tn(left, right):
    return lax.dot_general(left, right, (((0,), (0,)), ((), ())), preferred_element_type=F32)


def swapped_halves(value):
    lane = lax.broadcasted_iota(jnp.int32, value.shape, 1)
    first = lax.rem(lane, HEAD_DIM) < HEAD_DIM // 2
    half = HEAD_DIM // 2
    return jnp.where(
        first, pltpu.roll(value, 2 * HEAD_DIM - half, 1), pltpu.roll(value, half, 1)
    )


def masked_scores(q, k, first_row, length):
    scores = nt(q, k)
    row = lax.broadcasted_iota(jnp.int32, scores.shape, 0) + first_row
    col = lax.broadcasted_iota(jnp.int32, scores.shape, 1)
    return jnp.where((col <= row) & (col < length), scores, -1000000000.0)


def natural_rows(plan, blocks):
    flat = blocks.astype(F32).reshape(plan.devices * plan.pad_rows, blocks.shape[-1])
    if plan.pad_rows == plan.rows:
        return flat.astype(BF16)
    row = lax.broadcasted_iota(jnp.int32, (plan.width, flat.shape[0]), 0)
    col = lax.broadcasted_iota(jnp.int32, (plan.width, flat.shape[0]), 1)
    source = lax.div(row, plan.rows) * plan.pad_rows + lax.rem(row, plan.rows)
    return nn((col == source).astype(BF16), flat.astype(BF16)).astype(BF16)


def front_kernel(plan, length_ref, tok, wq, win, wo, gyw, cosine, sine, xs, w_seq, normed, qk_out, v_out, lse_out, mixed, gyall, w_in, w_out, wall, wqx, win_all, gysrc, qkv, made, x_send, x_recv, s_send, s_recv, q_send, q_recv, f_send, f_recv, z_send, z_recv, o_send, o_recv, own_sem, m_send, m_recv, *gather_sem):
    dp, ctx = place()
    half, member = lax.div(ctx, plan.quad), lax.rem(ctx, plan.quad)
    far = (1 - half) * plan.quad + member
    flat, flat_far = dp * plan.ctx + ctx, dp * plan.ctx + far
    mine = dp * plan.quad + member
    grid = Grid(plan)
    spot = grid.here()
    here = (dp, ctx)
    across = (dp, far)
    targets = half_members(plan, mine)
    devices = [
        (lax.div(target, plan.quad), half * plan.quad + lax.rem(target, plan.quad))
        for target in targets
    ]
    members = quad_members(plan, half, member)
    highs, ys = grid.sizes["high"], grid.sizes["y"]
    meet(devices + [across])
    pending = []

    def send(*args):
        copy = remote(*args)
        copy.start()
        pending.append(copy)

    swap_x = remote(tok.at[1 - half], xs.at[ctx], s_send.at[0], s_recv.at[0], across)
    swap_w = remote(wq, wqx, s_send.at[1], s_recv.at[1], across)
    swap_gy = remote(gyw.at[1 - half], gysrc.at[1], s_send.at[2], s_recv.at[2], across)
    swap_x.start()
    swap_w.start()

    def member_of(high, low):
        return half * plan.quad + lax.rem(spot["high"] + high, highs) * 2 + lax.rem(spot["low"] + low, 2)

    def token_block(side, high):
        at = half if side == 0 else 1 - half
        return at * plan.quad + lax.rem(spot["high"] + high, highs) * 2 + spot["low"]

    def token_sends(side, source):
        block = token_block(side, 0)
        for step in range(1, highs):
            index = side * (highs - 1) + step - 1
            send(source, xs.at[block], x_send.at[0, index], x_recv.at[0, side, highs - step - 1], (dp, member_of(step, 0)))
        send(source, xs.at[block], x_send.at[1, side * highs], x_recv.at[1, side, 0], (dp, member_of(0, 1)))

    def token_forward(side):
        for high in range(1, highs):
            block = token_block(side, high)
            remote(xs.at[block], xs.at[block], x_send.at[0, 0], x_recv.at[0, side, high - 1], here).wait_recv()
            send(xs.at[block], xs.at[block], x_send.at[1, side * highs + high], x_recv.at[1, side, high], (dp, member_of(0, 1)))

    def slice_sends(side, source, block):
        for i, (peer, to) in enumerate(members):
            send(source.at[to], wall.at[block], q_send.at[0, side, i], q_recv.at[block], (dp, peer))

    core_device = grid.device(grid.moved(spot, "core", 1))
    counter = [0, 0]

    def slice_on(block, source, along_y):
        if along_y:
            for step in range(1, ys):
                send(source, wall.at[block], q_send.at[1, 0, counter[0]], q_recv.at[block], grid.device(grid.moved(spot, "y", step)))
                counter[0] += 1
        send(source, wall.at[block], q_send.at[1, 1, counter[1]], q_recv.at[block], core_device)
        counter[1] += 1

    def slice_wait(block):
        remote(wq.at[0], wall.at[block], q_send.at[0, 0, 0], q_recv.at[block], here).wait_recv()

    token_sends(0, tok.at[half])
    slice_sends(0, wq, flat)
    slice_on(flat, wq.at[member], True)
    gysrc[0] = gyw[pl.ds(half, 1)][0]
    xs[pl.ds(ctx, 1)] = tok[pl.ds(half, 1)]
    wall[pl.ds(flat, 1)] = wq[pl.ds(member, 1)]
    w_out[:, pl.ds(half, 1)] = wo[...][:, None]
    swap_x.wait()
    token_sends(1, xs.at[far])
    swap_w.wait()
    slice_sends(1, wqx, flat_far)
    slice_on(flat_far, wqx.at[member], True)
    swap_gy.start()
    token_forward(0)
    for i, (peer, _) in enumerate(members):
        block = dp * plan.ctx + peer
        slice_wait(block)
        slice_on(block, wall.at[block], True)
    token_forward(1)
    for _, to in members:
        block = dp * plan.ctx + (1 - half) * plan.quad + to
        slice_wait(block)
        slice_on(block, wall.at[block], True)
    swap_o = remote(wo, w_out.at[:, half], o_send, o_recv, across)
    swap_o.start()
    wall[pl.ds(flat_far, 1)] = wqx[pl.ds(member, 1)]

    for i, (target, device) in enumerate(zip(targets, devices)):
        send(win.at[target], win_all.at[flat], f_send.at[i], f_recv.at[i], device)
    send(win.at[mine], win_all.at[flat], z_send.at[0], z_recv.at[0], across)
    win_all[pl.ds(flat, 1)] = win[pl.ds(mine, 1)]

    def columns_on(i):
        source = lax.rem(mine + plan.group - 1 - i, plan.group)
        block = lax.div(source, plan.quad) * plan.ctx + half * plan.quad + lax.rem(source, plan.quad)
        remote(win.at[0], win_all.at[block], f_send.at[0], f_recv.at[i], here).wait_recv()
        send(win_all.at[block], win_all.at[block], z_send.at[1 + i], z_recv.at[1 + i], across)

    for step in range(1, ys):
        other = lax.rem(spot["y"] + step, ys) * 2 + spot["core"]
        for place_ctx in range(plan.ctx):
            block = other * plan.ctx + place_ctx
            slice_wait(block)
            slice_on(block, wall.at[block], False)
    swap_gy.wait()
    gather = Gather(grid, spot, gysrc, gyall, *gather_sem)
    own = pltpu.make_async_copy(gysrc, gyall.at[grid.block(spot)], own_sem)
    own.start()
    gather.level(0)
    for y in range(ys):
        for place_ctx in range(plan.ctx):
            slice_wait((y * 2 + 1 - spot["core"]) * plan.ctx + place_ctx)
    for side in range(2):
        for high in range(highs):
            block = half if side == 0 else 1 - half
            block = block * plan.quad + lax.rem(spot["high"] + high, highs) * 2 + 1 - spot["low"]
            remote(xs.at[block], xs.at[block], x_send.at[0, 0], x_recv.at[1, side, high], here).wait_recv()

    length = length_ref[0]
    rows, block = QUERY_ROWS, plan.block
    slots = plan.slots
    w_seq[...] = natural_rows(plan, wall[...])
    tail = w_seq[:, plan.wide - 128 :].astype(F32)
    gain = jnp.transpose(tail, (1, 0))[plan.qkv_cols - plan.wide + 128 :][:1]
    for start in range(0, slots, rows):
        at = slice(start, start + rows)
        values = xs[start // block : (start + rows) // block].reshape(rows, plan.width).astype(F32)
        inverse = lax.rsqrt(jnp.mean(values * values, axis=-1, keepdims=True) + EPSILON)
        normed[at] = (values * inverse * gain).astype(BF16)
        qkv[at] = nn(normed[at], w_seq[...])
    heads = plan.heads
    qk_width = 2 * HEAD_DIM
    third = (plan.group - 1) // 3
    for i in range(third):
        columns_on(i)
    for head in range(heads):
        cols = slice(head * qk_width, (head + 1) * qk_width)
        qk = qkv[:, cols]
        qk_out[:, cols] = (qk * cosine[...] + swapped_halves(qk) * sine[...]).astype(BF16)
    v_cols = slice(heads * qk_width, heads * 3 * HEAD_DIM)
    v_out[...] = qkv[:, v_cols].astype(BF16)
    gather.level(1)
    for i in range(third, 2 * third):
        columns_on(i)

    def mixed_copy(index):
        side, to = divmod(index, plan.quad)
        turn = lax.rem(half + side, 2)
        return remote(
            made.at[index],
            mixed.at[member, turn],
            m_send.at[index],
            m_recv.at[member, turn],
            (dp, half * plan.quad + to),
        )

    spans = list(range(0, slots, rows))
    for number, start in enumerate(spans):
        at = slice(start, start + rows)
        end = start + rows
        for head in range(heads):
            base = head * qk_width
            q = qk_out[at, base : base + HEAD_DIM] * BF16(0.125)
            k = qk_out[:end, base + HEAD_DIM : base + qk_width]
            v = v_out[:end, head * HEAD_DIM : (head + 1) * HEAD_DIM]
            scores = masked_scores(q, k, start, length)
            top = jnp.max(scores, axis=-1, keepdims=True)
            raised = jnp.exp(scores - top)
            total = jnp.sum(raised, axis=-1, keepdims=True)
            lse_out[head, at] = top + jnp.log(total)
            probs = (raised * (1.0 / total)).astype(BF16)
            part = nn(probs, v).astype(BF16)
            for i in range(rows // block):
                made[start // block + i, :, head * HEAD_DIM : (head + 1) * HEAD_DIM] = part[
                    i * block : (i + 1) * block
                ]
        for i in range(rows // block):
            index = start // block + i
            pl.when(member != index % plan.quad)(lambda index=index: mixed_copy(index).start())

            @pl.when(member == index % plan.quad)
            def _(index=index):
                turn = lax.rem(half + index // plan.quad, 2)
                mixed[pl.ds(member, 1), pl.ds(turn, 1)] = made[index][None, None]

        if number == len(spans) // 2:
            for i in range(2 * third, plan.group - 1):
                columns_on(i)
            gather.level(2)
    gather.level(3)
    for index in range(plan.ctx):
        pl.when(member != index % plan.quad)(lambda index=index: mixed_copy(index).wait_send())
    for source in range(plan.quad):

        @pl.when(member != source)
        def _(source=source):
            for turn in range(2):
                remote(
                    made.at[0], mixed.at[source, turn], m_send.at[0], m_recv.at[source, turn], here
                ).wait_recv()

    for copy in pending:
        copy.wait_send()
    for i in range(plan.group):
        remote(win.at[0], win_all.at[0], z_send.at[0], z_recv.at[i], here).wait_recv()
    pad, hidden = plan.pad_rows, plan.hidden_pad
    w_in[:, :hidden] = natural_rows(plan, win_all[:, :pad])
    w_in[:, hidden:] = natural_rows(plan, win_all[:, pad:])
    swap_o.wait()
    gather.finish()
    own.wait()


def front(plan, length, tok, wq, win, wo, gyw, cosine, sine, collective_id):
    slots, heads, block, width = plan.slots, plan.heads, plan.block, plan.width
    highs, ys = plan.quad // 2, plan.dp // 2
    on = max(2 * plan.quad * max(ys - 1, 1), 2 * plan.quad + (ys - 1) * plan.ctx, plan.quad)
    return pl.pallas_call(
        functools.partial(front_kernel, plan),
        out_shape=(
            jax.ShapeDtypeStruct((plan.ctx, block, width), BF16),
            jax.ShapeDtypeStruct((width, plan.wide), BF16),
            jax.ShapeDtypeStruct((slots, width), BF16),
            jax.ShapeDtypeStruct((slots, 2 * plan.head_cols), BF16),
            jax.ShapeDtypeStruct((slots, plan.head_cols), BF16),
            jax.ShapeDtypeStruct((heads, slots, 1), F32),
            jax.ShapeDtypeStruct((plan.quad, 2, block, plan.head_cols), BF16),
            jax.ShapeDtypeStruct((plan.group, 2) + gyw.shape[1:], BF16),
            jax.ShapeDtypeStruct((width, 2 * plan.hidden_pad), BF16),
            jax.ShapeDtypeStruct((plan.branches, HALVES) + wo.shape[1:], BF16),
        ),
        in_specs=[pl.BlockSpec(memory_space=pltpu.SMEM)] + [VMEM] * 7,
        out_specs=(VMEM,) * 7 + (HBM, VMEM, VMEM),
        scratch_shapes=[
            pltpu.VMEM((plan.devices,) + wq.shape[1:], BF16),
            pltpu.VMEM(wq.shape, BF16),
            pltpu.VMEM((plan.devices,) + win.shape[1:], BF16),
            pltpu.VMEM(gyw.shape, BF16),
            pltpu.VMEM((slots, plan.wide), F32),
            pltpu.VMEM((plan.ctx, block, plan.head_cols), BF16),
            DMA((2, 2 * highs)),
            DMA((2, 2, highs)),
            DMA((3,)),
            DMA((3,)),
            DMA((2, 2, on)),
            DMA((plan.devices,)),
            DMA((plan.group - 1,)),
            DMA((plan.group - 1,)),
            DMA((plan.group,)),
            DMA((plan.group,)),
            DMA,
            DMA,
            DMA,
            DMA((plan.ctx,)),
            DMA((plan.quad, 2)),
        ]
        + gather_sems(plan),
        compiler_params=params(collective_id),
        cost_estimate=busy(90),
        name="front",
    )(length, tok, wq, win, wo, gyw, cosine, sine)


class Fold:
    def __init__(self, plan, src, dst, core_buf, y_buf, added, sems):
        self.plan, self.src, self.dst = plan, src, dst
        self.core_buf, self.y_buf, self.added = core_buf, y_buf, added
        self.core_send, self.core_recv, self.y_send, self.y_recv, self.send, self.recv = sems
        self.dp, self.ctx = place()
        self.core, self.y = lax.rem(self.dp, 2), lax.div(self.dp, 2)
        self.ys = plan.dp // 2

    def core_copies(self):
        partner = (self.dp + 1 - 2 * self.core, self.ctx)
        return [
            remote(
                self.src.at[y * 2 + 1 - self.core],
                self.core_buf.at[y],
                self.core_send.at[y],
                self.core_recv.at[y],
                partner,
            )
            for y in range(self.ys)
        ]

    def y_copies(self):
        copies = []
        for step in range(1, self.ys):
            to = lax.rem(self.y + step, self.ys)
            copies.append(
                remote(
                    self.core_buf.at[to],
                    self.y_buf.at[step - 1],
                    self.y_send.at[step - 1],
                    self.y_recv.at[step - 1],
                    (to * 2 + self.core, self.ctx),
                )
            )
        return copies

    def owner_copies(self):
        copies = []
        for step in range(1, self.plan.ctx):
            to = lax.rem(self.ctx + step, self.plan.ctx)
            copies.append(
                remote(
                    self.added.at[to],
                    self.dst.at[self.ctx],
                    self.send.at[step - 1],
                    self.recv.at[step - 1],
                    (self.dp, to),
                )
            )
        return copies

    def start(self):
        for copy in self.core_copies():
            copy.start()

    def along_y(self):
        for copy in self.core_copies():
            copy.wait()
        for y in range(self.ys):
            mine = self.src[y * 2 + self.core].astype(F32)
            self.core_buf[y] = (mine + self.core_buf[y].astype(F32)).astype(BF16)
        for copy in self.y_copies():
            copy.start()

    def to_owners(self):
        for copy in self.y_copies():
            copy.wait()
        total = self.core_buf[self.y].astype(F32)
        for step in range(1, self.ys):
            total = total + self.y_buf[step - 1].astype(F32)
        self.added[...] = total.astype(BF16)
        for copy in self.owner_copies():
            copy.start()
        self.dst[pl.ds(self.ctx, 1)] = self.added[pl.ds(self.ctx, 1)]

    def finish(self):
        for copy in self.owner_copies():
            copy.wait()


def padded_rows(plan, value, count):
    if plan.pad_rows != plan.rows:
        row = lax.broadcasted_iota(jnp.int32, (count * plan.pad_rows, count * plan.rows), 0)
        col = lax.broadcasted_iota(jnp.int32, (count * plan.pad_rows, count * plan.rows), 1)
        inside = lax.rem(row, plan.pad_rows)
        wanted = lax.div(row, plan.pad_rows) * plan.rows + inside
        hit = (col == wanted) & (inside < plan.rows)
        value = nn(hit.astype(BF16), value.astype(BF16))
    return value.reshape(count, plan.pad_rows, value.shape[-1])


def fold_scratch(plan, rows, width):
    shape = (plan.ctx, rows, width)
    ys = plan.dp // 2
    return [
        pltpu.VMEM((ys,) + shape, BF16),
        pltpu.VMEM((max(ys - 1, 1),) + shape, BF16),
        pltpu.VMEM(shape, BF16),
        DMA((ys,)),
        DMA((ys,)),
        DMA((max(ys - 1, 1),)),
        DMA((max(ys - 1, 1),)),
        DMA((plan.ctx - 1,)),
        DMA((plan.ctx - 1,)),
    ]


def back_kernel(plan, length_ref, x, w, cosine, sine, normed, qk_in, v_in, lse, dmixed, dwo, small, dw_in, dw_out, acts, x_own, middle_grad, gain, rwq, rwo, rwin, dw_out_sum, act_out, grad_out, dqkv, dq_acc, dk_acc, dv_acc, upstream_all, dnp, rdn, dwq, far_in, dealt, far_out, out_away, grad_away, d_send, d_recv, n_send, n_recv, w_send, w_recv, e_send, e_recv, s_send, s_recv, *fold_refs):
    dp, ctx = place()
    core, y = lax.rem(dp, 2), lax.div(dp, 2)
    half, member = lax.div(ctx, plan.quad), lax.rem(ctx, plan.quad)
    far = (1 - half) * plan.quad + member
    mine = dp * plan.quad + member
    across = (dp, far)
    members = quad_members(plan, half, member)
    targets = half_members(plan, mine)
    devices = [
        (lax.div(target, plan.quad), half * plan.quad + lax.rem(target, plan.quad))
        for target in targets
    ]
    meet(
        devices
        + [across]
        + [
            (dp, (1 - half) * plan.quad + lax.rem(member + step, plan.quad))
            for step in range(1, plan.quad)
        ]
    )
    swaps = []
    for i in range(plan.dp):
        copy = remote(dw_in.at[2 * i + 1 - half], far_in.at[i], w_send.at[i], w_recv.at[i], across)
        copy.start()
        swaps.append(copy)
    arriving = []
    for i, (peer, to) in enumerate(members):
        for j, at in enumerate((ctx, far)):
            copy = remote(
                dmixed.at[to, j],
                upstream_all.at[at],
                d_send.at[2 * i + j],
                d_recv.at[2 * i + j],
                (dp, peer),
            )
            copy.start()
            arriving.append(copy)
    count = len(fold_refs) // 2
    mix_fold = Fold(plan, dwo, rwo, *fold_refs[:3], fold_refs[3:count])
    qkv_fold = Fold(plan, dwq, rwq, *fold_refs[count : count + 3], fold_refs[count + 3 :])
    mix_fold.start()
    upstream_all[pl.ds(ctx, 1)] = dmixed[pl.ds(member, 1), 0]
    upstream_all[pl.ds(far, 1)] = dmixed[pl.ds(member, 1), 1]
    act_out[pl.ds(half, 1)] = acts[pl.ds(0, 1)]
    out_away[...] = dw_out[:, pl.ds(1 - half, 1)][:, 0].astype(BF16)
    length = length_ref[0]
    rows, slots, heads, block = QUERY_ROWS, plan.slots, plan.heads, plan.block
    qk_width = 2 * HEAD_DIM
    dqkv[...] = jnp.zeros_like(dqkv)
    for copy in arriving:
        copy.wait()
    for head in range(heads):
        base = head * qk_width
        v_cols = slice(head * HEAD_DIM, (head + 1) * HEAD_DIM)
        for start in range(slots - rows, -1, -rows):
            at = slice(start, start + rows)
            end = start + rows
            q = qk_in[at, base : base + HEAD_DIM] * BF16(0.125)
            k = qk_in[:end, base + HEAD_DIM : base + qk_width]
            v = v_in[:end, v_cols]
            upstream = jnp.concatenate(
                [upstream_all[start // block + i, :, v_cols] for i in range(rows // block)], axis=0
            )
            probs = jnp.exp(masked_scores(q, k, start, length) - lse[head, at])
            dv = tn(probs.astype(BF16), upstream)
            prob_grad = nt(upstream, v)
            inner = jnp.sum(probs * prob_grad, axis=-1, keepdims=True)
            score_grad = (probs * (prob_grad - inner)).astype(BF16)
            dq_acc[at] = nn(score_grad, k) * 0.125
            dk = tn(score_grad, q)
            if end == slots:
                dk_acc[...] = dk
                dv_acc[...] = dv
            else:
                dk_acc[:end] += dk
                dv_acc[:end] += dv
        dqk = jnp.concatenate([dq_acc[...], dk_acc[...]], axis=-1)
        dqkv[:, base : base + qk_width] = (
            dqk * cosine[...] - swapped_halves(dqk) * sine[...]
        ).astype(BF16)
        v_base = heads * qk_width + head * HEAD_DIM
        dqkv[:, v_base : v_base + HEAD_DIM] = dv_acc[...].astype(BF16)
        if head == 0:
            mix_fold.along_y()
        if head == 1:
            mix_fold.to_owners()
    gains = jnp.zeros((1, plan.width), F32)
    for start in range(0, slots, rows):
        at = slice(start, start + rows)
        part = nt(dqkv[at], w[...])
        for i in range(rows // block):
            dnp[start // block + i] = part[i * block : (i + 1) * block].astype(BF16)
        values = x[at].astype(F32)
        inverse = lax.rsqrt(jnp.mean(values * values, axis=-1, keepdims=True) + EPSILON)
        gains = gains + jnp.sum(part * values * inverse, axis=0, keepdims=True)
    sends = []
    for i, (peer, to) in enumerate(members):
        for j, at in enumerate((half * plan.quad + to, (1 - half) * plan.quad + to)):
            copy = remote(
                dnp.at[at], rdn.at[member, j], n_send.at[2 * i + j], n_recv.at[2 * i + j], (dp, peer)
            )
            copy.start()
            sends.append(copy)
    rdn[pl.ds(member, 1), 0] = dnp[pl.ds(ctx, 1)]
    rdn[pl.ds(member, 1), 1] = dnp[pl.ds(far, 1)]
    column = jnp.transpose(jnp.broadcast_to(gains, (128, plan.width)), (1, 0))
    lane = lax.broadcasted_iota(jnp.int32, column.shape, 1)
    first = plan.qkv_cols - (plan.wide - 128)
    extra = jnp.where(lane == first, column, small[...])
    for start in range(0, plan.wide, 128):
        cols = slice(start, start + 128)
        value = tn(normed[...], dqkv[:, cols])
        if start + 128 == plan.wide:
            value = value + extra
        value = padded_rows(plan, value, plan.devices).astype(BF16)
        dwq[:, :, :, cols] = value.reshape(plan.dp, plan.ctx, plan.pad_rows, 128)
    qkv_fold.start()
    mix_fold.finish()
    qkv_fold.along_y()
    swap_act = remote(acts.at[1], act_out.at[half], s_send.at[0], s_recv.at[0], across)
    swap_act.start()
    for copy in sends:
        copy.wait()
    local, width = plan.local, plan.width
    total = rdn[0].astype(F32)
    for i in range(1, plan.quad):
        total = total + rdn[i].astype(F32)
    total = total.reshape(local, width)
    values = x_own[...]
    inverse = lax.rsqrt(jnp.mean(values * values, axis=-1, keepdims=True) + EPSILON)
    scaled = total * gain[...]
    result = (
        middle_grad[...]
        + inverse * scaled
        - values * inverse * inverse * inverse * jnp.mean(scaled * values, axis=-1, keepdims=True)
    )
    result = result.astype(BF16).reshape(2, block, width)
    grad_away[...] = result[1]
    grad_out[pl.ds(half, 1)] = result[:1]
    swap_grad = remote(grad_away, grad_out.at[half], s_send.at[1], s_recv.at[1], across)
    swap_grad.start()
    qkv_fold.to_owners()
    hidden, pad = plan.hidden_pad, plan.pad_rows
    for i in range(plan.dp):
        swaps[i].wait()
        value = dw_in[pl.ds(2 * i + half, 1)][0].astype(F32) + far_in[i].astype(F32)
        value = padded_rows(plan, value, plan.quad)
        value = jnp.concatenate([value[:, :, :hidden], value[:, :, hidden:]], axis=1)
        dealt[i * plan.quad : (i + 1) * plan.quad] = value.astype(BF16)
    swap_out = remote(out_away, far_out, s_send.at[2], s_recv.at[2], across)
    swap_out.start()
    deals = []
    for i, (target, device) in enumerate(zip(targets, devices)):
        copy = remote(dealt.at[target], rwin.at[mine], e_send.at[i], e_recv.at[i], device)
        copy.start()
        deals.append(copy)
    rwin[pl.ds(mine, 1)] = dealt[pl.ds(mine, 1)]
    qkv_fold.finish()
    swap_act.wait()
    swap_grad.wait()
    for copy in deals:
        copy.wait()
    swap_out.wait()
    dw_out_sum[...] = dw_out[:, pl.ds(half, 1)][:, 0] + far_out[...].astype(F32)


def back(plan, length, x, w, cosine, sine, normed, qk, v, lse, dmixed, dwo, small, dw_in, dw_out, acts, x_own, middle_grad, gain, collective_id):
    slots, block, width = plan.slots, plan.block, plan.width
    count = 2 * (plan.quad - 1)
    dealt = (plan.group, 2 * plan.pad_rows, plan.hidden_pad)
    own = (plan.branches, plan.own_hidden, width)
    return pl.pallas_call(
        functools.partial(back_kernel, plan),
        out_shape=(
            jax.ShapeDtypeStruct((plan.ctx, plan.pad_rows, plan.wide), BF16),
            jax.ShapeDtypeStruct((plan.ctx, plan.rows, width), BF16),
            jax.ShapeDtypeStruct(dealt, BF16),
            jax.ShapeDtypeStruct(own, F32),
            jax.ShapeDtypeStruct((2, block, width), BF16),
            jax.ShapeDtypeStruct((2, block, width), BF16),
        ),
        in_specs=[pl.BlockSpec(memory_space=pltpu.SMEM)] + [VMEM] * 17,
        out_specs=(VMEM,) * 6,
        scratch_shapes=[
            pltpu.VMEM((slots, plan.wide), BF16),
            pltpu.VMEM((slots, HEAD_DIM), F32),
            pltpu.VMEM((slots, HEAD_DIM), F32),
            pltpu.VMEM((slots, HEAD_DIM), F32),
            pltpu.VMEM((plan.ctx, block, plan.head_cols), BF16),
            pltpu.VMEM((plan.ctx, block, width), BF16),
            pltpu.VMEM((plan.quad, 2, block, width), BF16),
            pltpu.VMEM((plan.dp, plan.ctx, plan.pad_rows, plan.wide), BF16),
            pltpu.VMEM((plan.dp,) + dw_in.shape[1:], BF16),
            pltpu.VMEM(dealt, BF16),
            pltpu.VMEM(own, BF16),
            pltpu.VMEM(own, BF16),
            pltpu.VMEM((block, width), BF16),
            DMA((count,)),
            DMA((count,)),
            DMA((count,)),
            DMA((count,)),
            DMA((plan.dp,)),
            DMA((plan.dp,)),
            DMA((plan.group - 1,)),
            DMA((plan.group - 1,)),
            DMA((3,)),
            DMA((3,)),
        ]
        + fold_scratch(plan, plan.rows, width)
        + fold_scratch(plan, plan.pad_rows, plan.wide),
        compiler_params=params(collective_id),
        cost_estimate=busy(90),
        name="back",
    )(length, x, w, cosine, sine, normed, qk, v, lse, dmixed, dwo, small, dw_in, dw_out, acts, x_own, middle_grad, gain)


def ffn_kernel(plan, members, n2x, gy, w_in, w_out, pick, out, n2g, dw_in, dw_out):
    hidden, local = plan.hidden_pad, plan.local

    @pl.when(pl.program_id(0) == 0)
    def start():
        dw_in[...] = jnp.zeros_like(dw_in)
        dw_out[...] = jnp.zeros_like(dw_out)

    tokens = members * local
    width = plan.width
    normed = n2x[:, :local].reshape(tokens, width)
    upstream = gy[:, :, : plan.block].reshape(tokens, width)
    mixing = jnp.concatenate(
        [tn(n2x[i, local:, :local], pick[...]) for i in range(members)], axis=0
    )
    pre = nn(normed, w_in[...])
    gate, up = pre[:, :hidden], pre[:, hidden:]
    sigmoid = jax.nn.sigmoid(gate)
    silu = gate * sigmoid
    act = (silu * up).astype(BF16).astype(F32)
    act_mixed = (act * mixing).astype(BF16)
    out[...] = nn(act_mixed, w_out[...]).astype(BF16).reshape(members, local, width)
    act_grad = nt(upstream, w_out[...])
    choice = nt(pick[...], (act * act_grad).astype(BF16)).astype(BF16)
    act_grad = act_grad * mixing
    gate_grad = act_grad * up * sigmoid * (1.0 + gate * (1.0 - sigmoid))
    pre_grad = jnp.concatenate([gate_grad, act_grad * silu], axis=-1).astype(BF16)
    n2g[:, :local] = nt(pre_grad, w_in[...]).astype(BF16).reshape(members, local, width)
    pad = jnp.zeros((MIX_ROWS, width - local), BF16)
    for i in range(members):
        n2g[i, local:] = jnp.concatenate(
            [choice[:, i * local : (i + 1) * local], pad], axis=-1
        )
    dw_in[...] += tn(normed, pre_grad)
    dw_out[...] += tn(act_mixed, upstream)


def ffn(plan, n2x, gy, w_in, w_out, pick):
    members = 2
    local, width, hidden = plan.local, plan.width, plan.hidden_pad
    whole = lambda i: (0, 0)
    part = lambda i: (i, 0, 0)
    return pl.pallas_call(
        functools.partial(ffn_kernel, plan, members),
        grid=(plan.group // members,),
        out_shape=(
            jax.ShapeDtypeStruct((plan.group, local, width), BF16),
            jax.ShapeDtypeStruct((plan.group, local + MIX_ROWS, width), BF16),
            jax.ShapeDtypeStruct((width, 2 * hidden), F32),
            jax.ShapeDtypeStruct((hidden, width), F32),
        ),
        in_specs=[
            pl.BlockSpec((members, local + MIX_ROWS, width), part),
            pl.BlockSpec((members,) + gy.shape[1:], lambda i: (i, 0, 0, 0)),
            pl.BlockSpec((width, 2 * hidden), whole),
            pl.BlockSpec((hidden, width), whole),
            pl.BlockSpec((MIX_ROWS, hidden), whole),
        ],
        out_specs=(
            pl.BlockSpec((members, local, width), part),
            pl.BlockSpec((members, local + MIX_ROWS, width), part),
            pl.BlockSpec((width, 2 * hidden), whole),
            pl.BlockSpec((hidden, width), whole),
        ),
        compiler_params=params(),
        name="ffn",
    )(n2x, gy, w_in, w_out, pick)


STEP_ORDER = ((0, 0, 0), (0, 1, 0), (0, 1, 1), (1, 1, 0), (1, 1, 1), (1, 0, 1), (1, 0, 0), (0, 0, 1))
FUSED_GATHER = (("high", "low", "y"), ("y", "low", "high"))
FUSED_REDUCE = (("low", "high", "y"), ("y", "high", "low"))


def named(offset):
    return dict(zip(("high", "low", "y"), offset))


def sum_plan(order):
    taken = {offset: step for step, offset in enumerate(STEP_ORDER)}
    names = ("high", "low", "y")
    rows, ready = [], {}
    for phase in range(4):
        for offset in STEP_ORDER:
            at = named(offset)
            if any(at[axis] for axis in order[:phase]) or (phase < 3 and not at[order[phase]]):
                continue
            if phase == 3 and any(offset):
                continue
            feeds = [
                tuple(1 if name == axis else at[name] for name in names) for axis in order[:phase]
            ]
            when = max([taken[offset] + 1] + [ready[feed] for feed in feeds])
            rows.append((when, phase, offset, order[phase] if phase < 3 else None, feeds))
            ready[offset] = when + 2
    rows.sort(key=lambda row: (row[0], row[1]))
    return rows


def fused_kernel(plan, n2x, gy, w_in, w_out, pick, total, dw_in, dw_out, n2all, gybuf, acc, away, work, core_buf, bufs, gy_sem, g_send, g_recv, gc_send, gc_recv, c_send, c_recv, r_send, r_recv):
    grid = Grid(plan)
    at = grid.here()
    local, width, hidden = plan.local, plan.width, plan.hidden_pad
    steps = len(STEP_ORDER)
    partner = grid.device(grid.moved(at, "core", 1))
    here = grid.device(at)
    colors = range(2)

    def absolute(offset):
        where = dict(at)
        for axis, step in named(offset).items():
            if step:
                where = grid.moved(where, axis, step)
        return where

    def slot_of(offset):
        return grid.slot(named(offset))

    send_index = [{}, {}]
    for color in colors:
        for offset in STEP_ORDER:
            order = FUSED_GATHER[color]
            reached = named(offset)
            level = max([i + 1 for i, axis in enumerate(order) if reached[axis]], default=0)
            for axis in order[level:]:
                send_index[color][(offset, axis)] = len(send_index[color])

    def pass_on(color, offset):
        order = FUSED_GATHER[color]
        reached = named(offset)
        level = max([i + 1 for i, axis in enumerate(order) if reached[axis]], default=0)
        where = absolute(offset)
        block = grid.block(where)
        slot = slot_of(offset)
        if level:
            remote(n2all.at[block], n2all.at[block], g_send.at[0], g_recv.at[slot], here).wait_recv()
        source = n2all.at[block] if level else n2x
        remote(source, n2all.at[block], gc_send.at[slot], gc_recv.at[slot], partner).start()
        for axis in order[level:]:
            seen = grid.slot({**reached, axis: 1})
            remote(
                source,
                n2all.at[block],
                g_send.at[send_index[color][(offset, axis)]],
                g_recv.at[seen],
                grid.device(grid.moved(at, axis, 1)),
            ).start()

    plans = [sum_plan(order) for order in FUSED_REDUCE]
    buf_index = [{row[2]: i for i, row in enumerate(rows) if row[3]} for rows in plans]

    def add_up(color, row):
        _, _, offset, axis, feeds = row
        slot = slot_of(offset)
        remote(away.at[0], core_buf.at[slot], c_send.at[0], c_recv.at[slot], here).wait_recv()
        for feed in feeds:
            index = buf_index[color][feed]
            remote(away.at[0], bufs.at[index], r_send.at[0], r_recv.at[index], here).wait_recv()
        rows = work.shape[1]
        chunk = 48

        @pl.loop(0, rows // chunk)
        def _(i):
            span = pl.ds(pl.multiple_of(i * chunk, 16), chunk)
            value = work[slot, span].astype(F32) + core_buf[slot, span].astype(F32)
            for feed in feeds:
                value = value + bufs[buf_index[color][feed], span].astype(F32)
            if axis is None:
                total[span] = value
            else:
                work[slot, span] = value.astype(BF16)

        if axis is not None:
            index = buf_index[color][offset]
            remote(
                work.at[slot],
                bufs.at[index],
                r_send.at[index],
                r_recv.at[index],
                grid.device(grid.moved(at, axis, 1)),
            ).start()

    def pump(step):
        def run(color):
            for offset in STEP_ORDER:
                if 0 < step == sum(offset):
                    pass_on(color, offset)
            for row in plans[color]:
                if row[0] == step or (step == steps and row[0] > steps):
                    add_up(color, row)

        for color in colors:
            pl.when(at["core"] == color)(functools.partial(run, color))

    def bit(step, index):
        value = 0
        for i, offset in enumerate(STEP_ORDER):
            if offset[index]:
                value = value + jnp.where(step == i, 1, 0)
        return value

    def blocks_of(step):
        where = dict(at)
        offsets = {}
        for index, axis in enumerate(("high", "low", "y")):
            offsets[axis] = bit(step, index)
            where[axis] = lax.rem(at[axis] + offsets[axis], 2)
        mine = grid.block(where)
        other = grid.block(grid.moved(where, "core", 1))
        return mine, other, grid.slot(offsets)

    def gy_loads(step, turn):
        mine, other, _ = blocks_of(step)
        return [
            pltpu.make_async_copy(gy.at[mine, :, : plan.block], gybuf.at[turn, 0], gy_sem.at[turn, 0]),
            pltpu.make_async_copy(gy.at[other, :, : plan.block], gybuf.at[turn, 1], gy_sem.at[turn, 1]),
        ]

    for load in gy_loads(0, 0):
        load.start()
    meet(grid.peers(at))
    for color in colors:
        pl.when(at["core"] == color)(functools.partial(pass_on, color, STEP_ORDER[0]))
    n2all[pl.ds(grid.block(at), 1)] = n2x[...][None]
    acc[...] = jnp.zeros_like(acc)
    dw_out[...] = jnp.zeros_like(dw_out)

    @pl.loop(0, steps)
    def _(step):
        for i in range(1, steps):
            pl.when(step == i)(functools.partial(pump, i))
        mine, other, slot = blocks_of(step)
        turn = lax.rem(step, 2)

        @pl.when(step + 1 < steps)
        def _():
            for load in gy_loads(step + 1, 1 - turn):
                load.start()

        remote(n2x, n2all.at[other], gc_send.at[0], gc_recv.at[slot], here).wait_recv()
        for load in gy_loads(step, turn):
            load.wait()
        pair = (mine, other)
        normed = jnp.concatenate([n2all[b, :local] for b in pair], axis=0)
        upstream = gybuf[turn].reshape(2 * local, width)
        mixing = jnp.concatenate([tn(n2all[b, local:, :local], pick[...]) for b in pair], axis=0)
        pre = nn(normed, w_in[...])
        gate, up = pre[:, :hidden], pre[:, hidden:]
        sigmoid = jax.nn.sigmoid(gate)
        silu = gate * sigmoid
        act = (silu * up).astype(BF16).astype(F32)
        act_mixed = (act * mixing).astype(BF16)
        out = nn(act_mixed, w_out[...]).astype(BF16)
        act_grad = nt(upstream, w_out[...])
        choice = nt(pick[...], (act * act_grad).astype(BF16)).astype(BF16)
        act_grad = act_grad * mixing
        gate_grad = act_grad * up * sigmoid * (1.0 + gate * (1.0 - sigmoid))
        pre_grad = jnp.concatenate([gate_grad, act_grad * silu], axis=-1).astype(BF16)
        n2g = nt(pre_grad, w_in[...]).astype(BF16)

        @pl.when(step >= 2)
        def _():
            remote(away.at[turn], core_buf.at[0], c_send.at[turn], c_recv.at[0], partner).wait_send()

        pad = jnp.zeros((MIX_ROWS, width - local), BF16)
        for i, (ref, index) in enumerate(((work, slot), (away, turn))):
            span = slice(i * local, (i + 1) * local)
            ref[index, :local] = n2g[span]
            ref[index, local : local + MIX_ROWS] = jnp.concatenate([choice[:, span], pad], axis=-1)
            ref[index, local + MIX_ROWS :] = out[span]
        remote(away.at[turn], core_buf.at[slot], c_send.at[turn], c_recv.at[slot], partner).start()
        acc[...] += tn(normed, pre_grad)
        dw_out[...] += tn(act_mixed, upstream)

    pump(steps)
    dw_in[...] = acc[...].astype(BF16)
    for turn in range(2):
        remote(away.at[turn], core_buf.at[0], c_send.at[turn], c_recv.at[0], partner).wait_send()
    for slot in range(steps):
        remote(n2x, n2all.at[0], gc_send.at[slot], gc_recv.at[0], partner).wait_send()
    for index in range(steps - 1):
        remote(n2x, n2all.at[0], g_send.at[index], g_recv.at[0], partner).wait_send()
        remote(work.at[0], bufs.at[index], r_send.at[index], r_recv.at[0], partner).wait_send()


def fused(plan, n2x, gy, w_in, w_out, pick, collective_id):
    local, width, hidden = plan.local, plan.width, plan.hidden_pad
    steps = len(STEP_ORDER)
    rows = 2 * local + MIX_ROWS
    return pl.pallas_call(
        functools.partial(fused_kernel, plan),
        out_shape=(
            jax.ShapeDtypeStruct((rows, width), F32),
            jax.ShapeDtypeStruct((width, 2 * hidden), BF16),
            jax.ShapeDtypeStruct((hidden, width), F32),
        ),
        in_specs=[VMEM, HBM, VMEM, VMEM, VMEM],
        out_specs=(VMEM,) * 3,
        scratch_shapes=[
            pltpu.VMEM((plan.group, local + MIX_ROWS, width), BF16),
            pltpu.VMEM((2, 2, 2, plan.block, width), BF16),
            pltpu.VMEM((width, 2 * hidden), F32),
            pltpu.VMEM((2, rows, width), BF16),
            pltpu.VMEM((steps, rows, width), BF16),
            pltpu.VMEM((steps, rows, width), BF16),
            pltpu.VMEM((steps - 1, rows, width), BF16),
            DMA((2, 2)),
            DMA((steps - 1,)),
            DMA((steps,)),
            DMA((steps,)),
            DMA((steps,)),
            DMA((2,)),
            DMA((steps,)),
            DMA((steps - 1,)),
            DMA((steps - 1,)),
        ],
        compiler_params=params(collective_id),
        cost_estimate=busy(100),
        name="fused",
    )(n2x, gy, w_in, w_out, pick)


def grid_block(plan, dp, ctx):
    return dp * plan.quad + lax.rem(ctx, plan.quad)


def by_half(half, mine, far, axis):
    return jnp.where(
        half == 0, jnp.stack([mine, far], axis), jnp.stack([far, mine], axis)
    )


def rope_tables(plan):
    half = HEAD_DIM // 2
    frequency = np.float32(10000.0) ** (-np.arange(half, dtype=np.float32) / np.float32(half))
    angles = np.arange(plan.slots, dtype=np.float32)[:, None] * frequency[None, :]
    cosine = np.cos(angles.astype(np.float64)).astype(np.float32)
    sine = np.sin(angles.astype(np.float64)).astype(np.float32)
    return np.tile(cosine, (1, 4)), np.tile(np.concatenate([-sine, sine], 1), (1, 2))


def pick_table(plan):
    table = np.zeros((MIX_ROWS, plan.hidden_pad), np.float32)
    span = HALVES * plan.own_hidden
    for expert in range(plan.experts):
        cols = slice((1 + expert) * span, (2 + expert) * span)
        table[expert, cols] = 1.0
        table[plan.experts + expert, cols] = 1.0
    table[2 * plan.experts, :span] = 1.0
    return jnp.asarray(table, BF16)


def pack_qkv(plan, attn_in, attn_gain, ffn_gain, router):
    rows, quad, heads = plan.rows, plan.quad, plan.heads
    qkv = attn_in.reshape(rows, 3, HEADS, HEAD_DIM)
    qkv = jnp.pad(qkv, ((0, 0), (0, 0), (0, quad * heads - HEADS), (0, 0)))
    qkv = qkv.reshape(rows, 3, quad, heads, HEAD_DIM)
    qk = jnp.transpose(qkv[:, :2], (2, 0, 3, 1, 4)).reshape(quad, rows, 2 * plan.head_cols)
    v = jnp.transpose(qkv[:, 2], (1, 0, 2, 3)).reshape(quad, rows, plan.head_cols)
    extra = jnp.concatenate([attn_gain[:, None], ffn_gain[:, None], router], axis=1)
    extra = jnp.pad(extra, ((0, 0), (0, plan.wide - plan.qkv_cols - extra.shape[1])))
    extra = jnp.broadcast_to(extra[None], (quad,) + extra.shape)
    packed = jnp.concatenate([qk, v, extra], axis=-1)
    return jnp.pad(packed, ((0, 0), (0, plan.pad_rows - rows), (0, 0)))


def unpack_qkv(plan, packed):
    rows, quad, heads = plan.rows, plan.quad, plan.heads
    qk = packed[..., : 2 * plan.head_cols].reshape(quad, rows, heads, 2, HEAD_DIM)
    v = packed[..., 2 * plan.head_cols : plan.qkv_cols].reshape(quad, rows, heads, 1, HEAD_DIM)
    qkv = jnp.transpose(jnp.concatenate([qk, v], axis=3), (1, 3, 0, 2, 4))
    qkv = qkv.reshape(rows, 3, quad * heads, HEAD_DIM)[:, :, :HEADS]
    return qkv.reshape(rows, 3 * HEADS * HEAD_DIM)


def pack_in(plan, dense_in, expert_in):
    rows, own = plan.rows, plan.own_hidden
    both = jnp.concatenate([dense_in[:, None], expert_in], axis=1)
    both = both.reshape(rows, plan.branches, 2, plan.dp, HALVES, plan.quad, own)
    both = jnp.transpose(both, (3, 5, 2, 0, 1, 4, 6))
    both = both.reshape(plan.group, 2, rows, plan.hidden)
    pads = ((0, 0), (0, 0), (0, plan.pad_rows - rows), (0, plan.hidden_pad - plan.hidden))
    return jnp.pad(both, pads).reshape(plan.group, 2 * plan.pad_rows, plan.hidden_pad)


def unpack_in(plan, packed):
    rows, own = plan.rows, plan.own_hidden
    both = packed.reshape(plan.group, 2, plan.pad_rows, plan.hidden_pad)
    both = both[:, :, :rows, : plan.hidden]
    both = both.reshape(plan.dp, plan.quad, 2, rows, plan.branches, HALVES, own)
    both = jnp.transpose(both, (3, 4, 2, 0, 5, 1, 6))
    both = both.reshape(rows, plan.branches, 2 * FF).astype(F32)
    return both[:, 0], both[:, 1:]


def shards(
    tokens,
    lengths,
    routes,
    cotangent,
    attn_gain,
    attn_in,
    attn_out,
    ffn_gain,
    router,
    dense_in,
    dense_out,
    expert_in,
    expert_out,
):
    micro, seqs, block, width = tokens.shape
    experts = expert_in.shape[1]
    plan = Plan(lax.axis_size("dp"), lax.axis_size("ctx"), block, width, experts)
    assert micro == HALVES and seqs == 1 and plan.ctx % 4 == 0 and plan.dp % 2 == 0
    quad, local = plan.quad, plan.local
    dp, ctx = place()
    half, member = lax.div(ctx, quad), lax.rem(ctx, quad)
    across = [(i, (i + quad) % plan.ctx) for i in range(plan.ctx)]

    def swap(value):
        return lax.ppermute(value, "ctx", across)

    def pick_mine(value):
        return lax.dynamic_index_in_dim(value, half, 0, keepdims=False)

    def pick_far(value):
        return lax.dynamic_index_in_dim(value, 1 - half, 0, keepdims=False)

    slot = ctx * block + jnp.arange(block, dtype=jnp.int32)
    valid = (slot[None] < lengths).astype(BF16)
    grad_all = cotangent[:, 0] * valid[..., None]
    tail = round_up(plan.rows, 16)
    mix_own = jnp.pad(attn_out, ((0, tail - plan.rows), (0, 0)))
    route = routes[:, 0]
    length = pick_mine(lengths)
    out_own = jnp.concatenate([dense_out[:, None], expert_out], axis=1)
    out_own = jnp.transpose(out_own, (1, 0, 2))
    gyw = jnp.concatenate([grad_all, jnp.broadcast_to(mix_own, (2,) + mix_own.shape)], axis=1)
    route_local = jnp.stack([pick_mine(route), swap(pick_far(route))]).reshape(local, 2)

    cosine, sine = (jnp.asarray(table) for table in rope_tables(plan))
    xs, w_seq, normed_seq, qk, v, lse, mixed, gy, w_in, w_out = front(
        plan,
        length,
        tokens[:, 0],
        pack_qkv(plan, attn_in, attn_gain, ffn_gain, router),
        pack_in(plan, dense_in, expert_in),
        out_own,
        gyw,
        cosine,
        sine,
        1,
    )
    x_seq = xs.reshape(plan.slots, width)
    extra = w_seq[:, plan.qkv_cols :]
    gain_one = extra[:, 0].astype(F32)[None]
    gain_two = extra[:, 1].astype(F32)[None]
    w_route = extra[:, 2 : 2 + experts]
    mixed = jnp.transpose(mixed, (1, 2, 0, 3)).reshape(local, quad * plan.head_cols)[:, :width]
    w_mix = gy[:, :, block : block + plan.rows].reshape(plan.dp, quad, 2, plan.rows, width)
    w_mix = by_half(half, w_mix[:, :, 0], w_mix[:, :, 1], 1).reshape(width, width)

    x = jnp.stack(
        [
            lax.dynamic_index_in_dim(xs, ctx, 0, keepdims=False),
            lax.dynamic_index_in_dim(xs, (1 - half) * quad + member, 0, keepdims=False),
        ]
    )
    x = x.reshape(local, width).astype(F32)
    middle = x + nn(mixed, w_mix)
    inverse_two = lax.rsqrt(jnp.mean(middle * middle, axis=-1, keepdims=True) + EPSILON)
    normed_two = (middle * inverse_two * gain_two).astype(BF16)
    logits = nn(normed_two, w_route)
    choose = (route_local[..., None] == jnp.arange(experts, dtype=jnp.int32)).astype(F32)
    picked = jnp.sum(choose * logits[:, None, :], axis=-1)
    gates = jax.nn.softmax(picked, axis=-1)
    mixing = jnp.sum(gates[..., None] * choose, axis=1)
    mixing_t = mixing.T
    mixing_high = mixing_t.astype(BF16)
    mixing_low = (mixing_t - mixing_high.astype(F32)).astype(BF16)
    mix_rows = jnp.concatenate(
        [
            mixing_high,
            mixing_low,
            jnp.ones((1, local), BF16),
            jnp.zeros((MIX_ROWS - 2 * experts - 1, local), BF16),
        ]
    )
    mix_rows = jnp.pad(mix_rows, ((0, 0), (0, width - local)))
    n2x = jnp.concatenate([normed_two, mix_rows])
    own_block = grid_block(plan, dp, ctx)
    grad_y = lax.dynamic_index_in_dim(gy, own_block, 0, keepdims=False)[:, :block]
    grad_y = grad_y.reshape(local, width)

    w_out = w_out.reshape(plan.hidden, width)
    w_out = jnp.pad(w_out, ((0, plan.hidden_pad - plan.hidden), (0, 0)))
    if plan.dp == 4 and quad == 4:
        sums, dw_in, dw_out = fused(plan, n2x, gy, w_in, w_out, pick_table(plan), 3)
        n2g_sum, out_sum = sums[: local + MIX_ROWS], sums[local + MIX_ROWS :]
    else:
        n2x = gather(plan, n2x, 3)
        out_part, n2g_part, dw_in, dw_out = ffn(plan, n2x, gy, w_in, w_out, pick_table(plan))
        n2g_sum = reduce(plan, n2g_part, 5)
        out_sum = reduce(plan, out_part, 7)

    activations = (middle + out_sum).astype(BF16).reshape(2, block, width)

    normed_two_grad = n2g_sum[:local]
    mixing_grad = n2g_sum[local : local + experts, :local].T
    choice_grad = jnp.sum(choose * mixing_grad[:, None, :], axis=-1)
    pick_grad = gates * (choice_grad - jnp.sum(gates * choice_grad, axis=-1, keepdims=True))
    logit_grad = jnp.sum(pick_grad[..., None] * choose, axis=1).astype(BF16)
    router_grad = tn(normed_two, logit_grad)
    normed_two_grad = normed_two_grad + nt(logit_grad, w_route)
    gain_two_grad = jnp.sum(normed_two_grad * middle * inverse_two, axis=0)
    scaled = normed_two_grad * gain_two
    middle_grad = (
        grad_y.astype(F32)
        + inverse_two * scaled
        - middle * inverse_two**3 * jnp.mean(scaled * middle, axis=-1, keepdims=True)
    )
    attn_grad = middle_grad.astype(BF16)
    dw_mix = tn(mixed, attn_grad).astype(BF16).reshape(plan.dp, plan.ctx, plan.rows, width)
    mixed_grad = nt(attn_grad, w_mix).astype(BF16)
    mixed_grad = jnp.pad(mixed_grad, ((0, 0), (0, quad * plan.head_cols - width)))
    mixed_grad = mixed_grad.reshape(2, block, quad, plan.head_cols)
    first = plan.qkv_cols - (plan.wide - 128)
    small = jnp.concatenate([gain_two_grad[:, None], router_grad], axis=1)
    small = jnp.pad(small, ((0, 0), (first + 1, 127 - first - small.shape[1])))
    r_qkv, r_mix, r_in, dw_out, activations, input_grad = back(
        plan,
        length,
        x_seq,
        w_seq,
        cosine,
        sine,
        normed_seq,
        qk,
        v,
        lse,
        jnp.transpose(mixed_grad, (2, 0, 1, 3)),
        dw_mix,
        small,
        dw_in.astype(BF16).reshape(plan.dp * HALVES, quad * plan.rows, 2 * plan.hidden_pad),
        dw_out[: plan.hidden].reshape(plan.branches, HALVES, plan.own_hidden, width),
        activations,
        x,
        middle_grad,
        gain_one,
        4,
    )

    r_qkv = r_qkv[:, : plan.rows].astype(F32).reshape(HALVES, quad, plan.rows, plan.wide)
    r_qkv = jnp.sum(r_qkv, axis=0)
    attn_in_grad = unpack_qkv(plan, r_qkv)
    small = jnp.sum(r_qkv[:, :, plan.qkv_cols :], axis=0)
    attn_out_grad = jnp.sum(r_mix.astype(F32), axis=0)
    dense_in_grad, expert_in_grad = unpack_in(plan, r_in)
    return (
        activations[:, None],
        input_grad[:, None],
        small[:, 0],
        attn_in_grad,
        attn_out_grad,
        small[:, 1],
        small[:, 2 : 2 + experts],
        dense_in_grad,
        dw_out[0],
        expert_in_grad,
        jnp.transpose(dw_out[1:], (1, 0, 2)),
    )


def solution(mesh):
    rows = P(("dp", "ctx"))
    matrix = P(("dp", "ctx"), None)
    cube = P(("dp", "ctx"), None, None)
    slots = P(None, "dp", "ctx", None)
    in_specs = (
        slots,
        P(None, "dp"),
        slots,
        slots,
        rows,
        matrix,
        matrix,
        rows,
        matrix,
        matrix,
        matrix,
        cube,
        cube,
    )
    out_specs = (
        slots,
        slots,
        rows,
        matrix,
        matrix,
        rows,
        matrix,
        matrix,
        matrix,
        cube,
        cube,
    )
    return jax.shard_map(shards, mesh=mesh, in_specs=in_specs, out_specs=out_specs, check_vma=False)
```

```python
import functools

import jax
import jax.numpy as jnp
import numpy as np
from jax import lax
from jax.experimental import pallas as pl
from jax.experimental.pallas import tpu as pltpu
from jax.sharding import PartitionSpec as P

HEADS = 12
HEAD_DIM = 64
FF = 2048
EPSILON = 1e-05
HALVES = 2
QUERY_ROWS = 256
MIX_ROWS = 16
MESH = pl.DeviceIdType.MESH
BF16 = jnp.bfloat16
F32 = jnp.float32


def round_up(value, step):
    return -(-value // step) * step


class Plan:
    def __init__(self, dp, ctx, block, width, experts):
        self.dp, self.ctx, self.block, self.width, self.experts = dp, ctx, block, width, experts
        self.quad = ctx // HALVES
        self.devices = dp * ctx
        self.group = dp * self.quad
        self.slots = ctx * block
        self.rows = width // self.devices
        self.pad_rows = round_up(self.rows, 8)
        self.heads = -(-HEADS // self.quad)
        self.head_cols = self.heads * HEAD_DIM
        self.qkv_cols = 3 * self.head_cols
        self.wide = round_up(self.qkv_cols + 2 + experts, 128)
        self.own_hidden = FF // self.devices
        self.branches = 1 + experts
        self.hidden = self.branches * HALVES * self.own_hidden
        self.hidden_pad = round_up(self.hidden, 128)
        self.local = HALVES * block


def place():
    return lax.axis_index("dp"), lax.axis_index("ctx")


def params(collective_id=None, limit=60 * 1024 * 1024):
    if collective_id is None:
        return pltpu.CompilerParams(vmem_limit_bytes=limit)
    return pltpu.CompilerParams(
        vmem_limit_bytes=limit, collective_id=collective_id, has_side_effects=True
    )


def remote(src, dst, send_sem, recv_sem, device):
    return pltpu.make_async_remote_copy(
        src_ref=src,
        dst_ref=dst,
        send_sem=send_sem,
        recv_sem=recv_sem,
        device_id=device,
        device_id_type=MESH,
    )


def busy(microseconds):
    return pl.CostEstimate(
        flops=0, bytes_accessed=int(microseconds * 3.4e6), transcendentals=0
    )


def meet(devices):
    barrier = pltpu.get_barrier_semaphore()
    for device in devices:
        pl.semaphore_signal(barrier, inc=1, device_id=device, device_id_type=MESH)
    pl.semaphore_wait(barrier, len(devices))


def other_devices(plan, dp, ctx):
    flat = dp * plan.ctx + ctx
    result = []
    for step in range(1, plan.devices):
        target = lax.rem(flat + step, plan.devices)
        result.append((lax.div(target, plan.ctx), lax.rem(target, plan.ctx)))
    return result


def quad_members(plan, half, member):
    return [
        (half * plan.quad + lax.rem(member + step, plan.quad), lax.rem(member + step, plan.quad))
        for step in range(1, plan.quad)
    ]


VMEM = pl.BlockSpec(memory_space=pltpu.VMEM)
HBM = pl.BlockSpec(memory_space=pl.ANY)
DMA = pltpu.SemaphoreType.DMA


def half_members(plan, mine):
    return [lax.rem(mine + step, plan.group) for step in range(1, plan.group)]


class Grid:
    def __init__(self, plan):
        self.plan = plan
        self.sizes = {"y": plan.dp // 2, "high": plan.quad // 2, "low": 2}

    def here(self):
        dp, ctx = place()
        member = lax.rem(ctx, self.plan.quad)
        return {
            "core": lax.rem(dp, 2),
            "y": lax.div(dp, 2),
            "high": lax.div(member, 2),
            "low": lax.rem(member, 2),
            "half": lax.div(ctx, self.plan.quad),
        }

    def device(self, at):
        return (
            at["y"] * 2 + at["core"],
            at["half"] * self.plan.quad + at["high"] * 2 + at["low"],
        )

    def block(self, at):
        return (at["y"] * 2 + at["core"]) * self.plan.quad + at["high"] * 2 + at["low"]

    def moved(self, at, axis, step):
        result = dict(at)
        if axis == "core":
            result["core"] = 1 - at["core"]
        else:
            result[axis] = lax.rem(at[axis] + step, self.sizes[axis])
        return result

    def peers(self, at):
        result = [self.moved(at, "core", 1)]
        for axis, size in self.sizes.items():
            result += [self.moved(at, axis, step) for step in range(1, size)]
        return [self.device(peer) for peer in result]

    def slot(self, offsets):
        return (offsets["y"] * self.sizes["high"] + offsets["high"]) * 2 + offsets["low"]


GATHER_ORDERS = (("high", "low", "y"), ("high", "y", "low"))


class Gather:
    def __init__(self, grid, at, src, dst, send, recv, core_send, core_recv):
        self.grid, self.at, self.src, self.dst = grid, at, src, dst
        self.send, self.recv, self.core_send, self.core_recv = send, recv, core_send, core_recv

    def groups(self, order):
        sizes = self.grid.sizes
        levels = [[{"y": 0, "high": 0, "low": 0}], [], [], []]
        for level, axis in enumerate(order):
            base = [o for group in levels[: level + 1] for o in group]
            levels[level + 1] = [
                {**offsets, axis: step} for offsets in base for step in range(1, sizes[axis])
            ]
        return levels

    def absolute(self, offsets):
        where = dict(self.at)
        for axis, step in offsets.items():
            if step:
                where = self.grid.moved(where, axis, step)
        return where

    def run_level(self, order, level):
        grid, at = self.grid, self.at
        index = 0
        for current, group in enumerate(self.groups(order)):
            for offsets in group:
                if current == level:
                    block = grid.block(self.absolute(offsets))
                    if level:
                        remote(
                            self.src,
                            self.dst.at[block],
                            self.send.at[0],
                            self.recv.at[grid.slot(offsets)],
                            grid.device(at),
                        ).wait_recv()
                    source = self.dst.at[block] if level else self.src
                    remote(
                        source,
                        self.dst.at[block],
                        self.core_send.at[grid.slot(offsets)],
                        self.core_recv.at[grid.slot(offsets)],
                        grid.device(grid.moved(at, "core", 1)),
                    ).start()
                for axis in order[current:]:
                    for step in range(1, grid.sizes[axis]):
                        if current == level:
                            seen = {**offsets, axis: grid.sizes[axis] - step}
                            remote(
                                source,
                                self.dst.at[block],
                                self.send.at[index],
                                self.recv.at[grid.slot(seen)],
                                grid.device(grid.moved(at, axis, step)),
                            ).start()
                        index += 1

    def level(self, level):
        for color, order in enumerate(GATHER_ORDERS):
            pl.when(self.at["core"] == color)(functools.partial(self.run_level, order, level))

    def finish(self):
        plan, here = self.grid.plan, self.grid.device(self.at)

        def sent(order):
            for index in range(gather_sends(plan, order)):
                remote(self.src, self.dst.at[0], self.send.at[index], self.recv.at[0], here).wait_send()

        for color, order in enumerate(GATHER_ORDERS):
            pl.when(self.at["core"] == color)(functools.partial(sent, order))
        for slot in range(plan.group // 2):
            remote(
                self.src, self.dst.at[0], self.core_send.at[slot], self.core_recv.at[slot], here
            ).wait()


def gather_kernel(plan, src, dst, send, recv, core_send, core_recv):
    grid = Grid(plan)
    at = grid.here()
    meet(grid.peers(at))
    dst[pl.ds(grid.block(at), 1)] = src[...][None]
    blocks = Gather(grid, at, src, dst, send, recv, core_send, core_recv)
    for level in range(4):
        blocks.level(level)
    blocks.finish()


def gather_sems(plan):
    half = plan.group // 2
    count = max(gather_sends(plan, order) for order in GATHER_ORDERS)
    return [DMA((count,)), DMA((half,)), DMA((half,)), DMA((half,))]


def gather_sends(plan, order):
    sizes = Grid(plan).sizes
    held, total = 1, 0
    for axis in order:
        total += held * (sizes[axis] - 1)
        held *= sizes[axis]
    return total


def gather(plan, block, collective_id):
    return pl.pallas_call(
        functools.partial(gather_kernel, plan),
        out_shape=jax.ShapeDtypeStruct((plan.group,) + block.shape, block.dtype),
        in_specs=[VMEM],
        out_specs=VMEM,
        scratch_shapes=gather_sems(plan),
        compiler_params=params(collective_id),
        cost_estimate=busy(35),
        name="gather",
    )(block)


def reduce_kernel(plan, src, out, work, core_buf, bufs, load_sem, core_send, core_recv, send, recv):
    grid = Grid(plan)
    at = grid.here()
    zero = {"y": 0, "high": 0, "low": 0}
    meet(grid.peers(at))

    def run(order):
        levels = [[], [], [], []]
        held = [dict(zero)]
        levels[3] = [dict(zero)]
        for level in (2, 1, 0):
            axis = order[level]
            base = [o for later in levels[level + 1 :] for o in later]
            levels[level] = [
                {**offsets, axis: step} for offsets in base for step in range(1, grid.sizes[axis])
            ]
        del held

        def absolute(offsets):
            where = dict(at)
            for axis, step in offsets.items():
                if step:
                    where = grid.moved(where, axis, step)
            return where

        sequence = [o for group in levels for o in group]
        partner = grid.device(grid.moved(at, "core", 1))
        core_copies = []
        loads = []
        for offsets in sequence:
            where = absolute(offsets)
            slot = grid.slot(offsets)
            copy = remote(
                src.at[grid.block(grid.moved(where, "core", 1))],
                core_buf.at[slot],
                core_send.at[slot],
                core_recv.at[slot],
                partner,
            )
            copy.start()
            core_copies.append(copy)
            load = pltpu.make_async_copy(
                src.at[grid.block(where)], work.at[slot], load_sem.at[slot]
            )
            load.start()
            loads.append(load)
        arrived = {}
        sends = []
        index = 0
        position = 0
        for level in range(4):
            for offsets in levels[level]:
                slot = grid.slot(offsets)
                core_copies[position].wait_recv()
                loads[position].wait()
                position += 1
                total = work[slot].astype(F32) + core_buf[slot].astype(F32)
                for buffer in arrived.get(slot, ()):
                    remote(work.at[slot], bufs.at[buffer], send.at[0], recv.at[buffer], partner).wait_recv()
                    total = total + bufs[buffer].astype(F32)
                if level == 3:
                    out[...] = total.astype(out.dtype)
                    continue
                work[slot] = total.astype(BF16)
                axis = order[level]
                step = offsets[axis]
                copy = remote(
                    work.at[slot],
                    bufs.at[index],
                    send.at[index],
                    recv.at[index],
                    grid.device(grid.moved(at, axis, step)),
                )
                copy.start()
                sends.append(copy)
                landing = grid.slot({**offsets, axis: 0})
                arrived.setdefault(landing, []).append(index)
                index += 1
        for copy in sends:
            copy.wait_send()
        for copy in core_copies:
            copy.wait_send()

    for color, order in enumerate(GATHER_ORDERS):
        pl.when(at["core"] == color)(functools.partial(run, order[::-1]))


def reduce(plan, blocks, collective_id):
    half = plan.group // 2
    shape = blocks.shape[1:]
    count = max(gather_sends(plan, order) for order in GATHER_ORDERS)
    return pl.pallas_call(
        functools.partial(reduce_kernel, plan),
        out_shape=jax.ShapeDtypeStruct(shape, F32),
        in_specs=[HBM],
        out_specs=VMEM,
        scratch_shapes=[
            pltpu.VMEM((half,) + shape, BF16),
            pltpu.VMEM((half,) + shape, BF16),
            pltpu.VMEM((count,) + shape, BF16),
            DMA((half,)),
            DMA((half,)),
            DMA((half,)),
            DMA((count,)),
            DMA((count,)),
        ],
        compiler_params=params(collective_id),
        name="reduce",
    )(blocks)


def nt(left, right):
    return lax.dot_general(left, right, (((1,), (1,)), ((), ())), preferred_element_type=F32)


def nn(left, right):
    return lax.dot_general(left, right, (((1,), (0,)), ((), ())), preferred_element_type=F32)


def tn(left, right):
    return lax.dot_general(left, right, (((0,), (0,)), ((), ())), preferred_element_type=F32)


def swapped_halves(value):
    lane = lax.broadcasted_iota(jnp.int32, value.shape, 1)
    first = lax.rem(lane, HEAD_DIM) < HEAD_DIM // 2
    half = HEAD_DIM // 2
    return jnp.where(
        first, pltpu.roll(value, 2 * HEAD_DIM - half, 1), pltpu.roll(value, half, 1)
    )


def masked_scores(q, k, first_row, length):
    scores = nt(q, k)
    row = lax.broadcasted_iota(jnp.int32, scores.shape, 0) + first_row
    col = lax.broadcasted_iota(jnp.int32, scores.shape, 1)
    return jnp.where((col <= row) & (col < length), scores, -1000000000.0)


def natural_rows(plan, blocks):
    flat = blocks.astype(F32).reshape(plan.devices * plan.pad_rows, blocks.shape[-1])
    if plan.pad_rows == plan.rows:
        return flat.astype(BF16)
    row = lax.broadcasted_iota(jnp.int32, (plan.width, flat.shape[0]), 0)
    col = lax.broadcasted_iota(jnp.int32, (plan.width, flat.shape[0]), 1)
    source = lax.div(row, plan.rows) * plan.pad_rows + lax.rem(row, plan.rows)
    return nn((col == source).astype(BF16), flat.astype(BF16)).astype(BF16)


def front_kernel(plan, length_ref, tok, wq, win, gyw, cosine, sine, xs, w_seq, normed, qk_out, v_out, lse_out, mixed, gyall, w_in, wall, wqx, win_all, gysrc, qkv, made, x_send, x_recv, s_send, s_recv, q_send, q_recv, f_send, f_recv, z_send, z_recv, own_sem, m_send, m_recv, *gather_sem):
    dp, ctx = place()
    half, member = lax.div(ctx, plan.quad), lax.rem(ctx, plan.quad)
    far = (1 - half) * plan.quad + member
    flat, flat_far = dp * plan.ctx + ctx, dp * plan.ctx + far
    mine = dp * plan.quad + member
    grid = Grid(plan)
    spot = grid.here()
    here = (dp, ctx)
    across = (dp, far)
    targets = half_members(plan, mine)
    devices = [
        (lax.div(target, plan.quad), half * plan.quad + lax.rem(target, plan.quad))
        for target in targets
    ]
    members = quad_members(plan, half, member)
    highs, ys = grid.sizes["high"], grid.sizes["y"]
    meet(devices + [across])
    pending = []

    def send(*args):
        copy = remote(*args)
        copy.start()
        pending.append(copy)

    swap_x = remote(tok.at[1 - half], xs.at[ctx], s_send.at[0], s_recv.at[0], across)
    swap_w = remote(wq, wqx, s_send.at[1], s_recv.at[1], across)
    swap_gy = remote(gyw.at[1 - half], gysrc.at[1], s_send.at[2], s_recv.at[2], across)
    swap_x.start()
    swap_w.start()

    def member_of(high, low):
        return half * plan.quad + lax.rem(spot["high"] + high, highs) * 2 + lax.rem(spot["low"] + low, 2)

    def token_block(side, high):
        at = half if side == 0 else 1 - half
        return at * plan.quad + lax.rem(spot["high"] + high, highs) * 2 + spot["low"]

    def token_sends(side, source):
        block = token_block(side, 0)
        for step in range(1, highs):
            index = side * (highs - 1) + step - 1
            send(source, xs.at[block], x_send.at[0, index], x_recv.at[0, side, highs - step - 1], (dp, member_of(step, 0)))
        send(source, xs.at[block], x_send.at[1, side * highs], x_recv.at[1, side, 0], (dp, member_of(0, 1)))

    def token_forward(side):
        for high in range(1, highs):
            block = token_block(side, high)
            remote(xs.at[block], xs.at[block], x_send.at[0, 0], x_recv.at[0, side, high - 1], here).wait_recv()
            send(xs.at[block], xs.at[block], x_send.at[1, side * highs + high], x_recv.at[1, side, high], (dp, member_of(0, 1)))

    def slice_sends(side, source, block):
        for i, (peer, to) in enumerate(members):
            send(source.at[to], wall.at[block], q_send.at[0, side, i], q_recv.at[block], (dp, peer))

    core_device = grid.device(grid.moved(spot, "core", 1))
    counter = [0, 0]

    def slice_on(block, source, along_y):
        if along_y:
            for step in range(1, ys):
                send(source, wall.at[block], q_send.at[1, 0, counter[0]], q_recv.at[block], grid.device(grid.moved(spot, "y", step)))
                counter[0] += 1
        send(source, wall.at[block], q_send.at[1, 1, counter[1]], q_recv.at[block], core_device)
        counter[1] += 1

    def slice_wait(block):
        remote(wq.at[0], wall.at[block], q_send.at[0, 0, 0], q_recv.at[block], here).wait_recv()

    token_sends(0, tok.at[half])
    slice_sends(0, wq, flat)
    slice_on(flat, wq.at[member], True)
    gysrc[0] = gyw[pl.ds(half, 1)][0]
    xs[pl.ds(ctx, 1)] = tok[pl.ds(half, 1)]
    wall[pl.ds(flat, 1)] = wq[pl.ds(member, 1)]
    swap_x.wait()
    token_sends(1, xs.at[far])
    swap_w.wait()
    slice_sends(1, wqx, flat_far)
    slice_on(flat_far, wqx.at[member], True)
    swap_gy.start()
    token_forward(0)
    for i, (peer, _) in enumerate(members):
        block = dp * plan.ctx + peer
        slice_wait(block)
        slice_on(block, wall.at[block], True)
    token_forward(1)
    for _, to in members:
        block = dp * plan.ctx + (1 - half) * plan.quad + to
        slice_wait(block)
        slice_on(block, wall.at[block], True)
    wall[pl.ds(flat_far, 1)] = wqx[pl.ds(member, 1)]

    for i, (target, device) in enumerate(zip(targets, devices)):
        send(win.at[target], win_all.at[flat], f_send.at[i], f_recv.at[i], device)
    send(win.at[mine], win_all.at[flat], z_send.at[0], z_recv.at[0], across)
    win_all[pl.ds(flat, 1)] = win[pl.ds(mine, 1)]

    def columns_on(i):
        source = lax.rem(mine + plan.group - 1 - i, plan.group)
        block = lax.div(source, plan.quad) * plan.ctx + half * plan.quad + lax.rem(source, plan.quad)
        remote(win.at[0], win_all.at[block], f_send.at[0], f_recv.at[i], here).wait_recv()
        send(win_all.at[block], win_all.at[block], z_send.at[1 + i], z_recv.at[1 + i], across)

    for step in range(1, ys):
        other = lax.rem(spot["y"] + step, ys) * 2 + spot["core"]
        for place_ctx in range(plan.ctx):
            block = other * plan.ctx + place_ctx
            slice_wait(block)
            slice_on(block, wall.at[block], False)
    swap_gy.wait()
    gather = Gather(grid, spot, gysrc, gyall, *gather_sem)
    own = pltpu.make_async_copy(gysrc, gyall.at[grid.block(spot)], own_sem)
    own.start()
    gather.level(0)
    for y in range(ys):
        for place_ctx in range(plan.ctx):
            slice_wait((y * 2 + 1 - spot["core"]) * plan.ctx + place_ctx)
    for side in range(2):
        for high in range(highs):
            block = half if side == 0 else 1 - half
            block = block * plan.quad + lax.rem(spot["high"] + high, highs) * 2 + 1 - spot["low"]
            remote(xs.at[block], xs.at[block], x_send.at[0, 0], x_recv.at[1, side, high], here).wait_recv()

    length = length_ref[0]
    rows, block = QUERY_ROWS, plan.block
    slots = plan.slots
    w_seq[...] = natural_rows(plan, wall[...])
    tail = w_seq[:, plan.wide - 128 :].astype(F32)
    gain = jnp.transpose(tail, (1, 0))[plan.qkv_cols - plan.wide + 128 :][:1]
    for start in range(0, slots, rows):
        at = slice(start, start + rows)
        values = xs[start // block : (start + rows) // block].reshape(rows, plan.width).astype(F32)
        inverse = lax.rsqrt(jnp.mean(values * values, axis=-1, keepdims=True) + EPSILON)
        normed[at] = (values * inverse * gain).astype(BF16)
        qkv[at] = nn(normed[at], w_seq[...])
    heads = plan.heads
    qk_width = 2 * HEAD_DIM
    third = (plan.group - 1) // 3
    for i in range(third):
        columns_on(i)
    for head in range(heads):
        cols = slice(head * qk_width, (head + 1) * qk_width)
        qk = qkv[:, cols]
        qk_out[:, cols] = (qk * cosine[...] + swapped_halves(qk) * sine[...]).astype(BF16)
    v_cols = slice(heads * qk_width, heads * 3 * HEAD_DIM)
    v_out[...] = qkv[:, v_cols].astype(BF16)
    gather.level(1)
    for i in range(third, 2 * third):
        columns_on(i)

    def mixed_copy(index):
        side, to = divmod(index, plan.quad)
        turn = lax.rem(half + side, 2)
        return remote(
            made.at[index],
            mixed.at[member, turn],
            m_send.at[index],
            m_recv.at[member, turn],
            (dp, half * plan.quad + to),
        )

    spans = list(range(0, slots, rows))
    for number, start in enumerate(spans):
        at = slice(start, start + rows)
        end = start + rows
        for head in range(heads):
            base = head * qk_width
            q = qk_out[at, base : base + HEAD_DIM] * BF16(0.125)
            k = qk_out[:end, base + HEAD_DIM : base + qk_width]
            v = v_out[:end, head * HEAD_DIM : (head + 1) * HEAD_DIM]
            scores = masked_scores(q, k, start, length)
            top = jnp.max(scores, axis=-1, keepdims=True)
            raised = jnp.exp(scores - top)
            total = jnp.sum(raised, axis=-1, keepdims=True)
            lse_out[head, at] = top + jnp.log(total)
            probs = (raised * (1.0 / total)).astype(BF16)
            part = nn(probs, v).astype(BF16)
            for i in range(rows // block):
                made[start // block + i, :, head * HEAD_DIM : (head + 1) * HEAD_DIM] = part[
                    i * block : (i + 1) * block
                ]
        for i in range(rows // block):
            index = start // block + i
            pl.when(member != index % plan.quad)(lambda index=index: mixed_copy(index).start())

            @pl.when(member == index % plan.quad)
            def _(index=index):
                turn = lax.rem(half + index // plan.quad, 2)
                mixed[pl.ds(member, 1), pl.ds(turn, 1)] = made[index][None, None]

        if number == len(spans) // 2:
            for i in range(2 * third, plan.group - 1):
                columns_on(i)
            gather.level(2)
    gather.level(3)
    for index in range(plan.ctx):
        pl.when(member != index % plan.quad)(lambda index=index: mixed_copy(index).wait_send())
    for source in range(plan.quad):

        @pl.when(member != source)
        def _(source=source):
            for turn in range(2):
                remote(
                    made.at[0], mixed.at[source, turn], m_send.at[0], m_recv.at[source, turn], here
                ).wait_recv()

    for copy in pending:
        copy.wait_send()
    for i in range(plan.group):
        remote(win.at[0], win_all.at[0], z_send.at[0], z_recv.at[i], here).wait_recv()
    pad, hidden = plan.pad_rows, plan.hidden_pad
    w_in[:, :hidden] = natural_rows(plan, win_all[:, :pad])
    w_in[:, hidden:] = natural_rows(plan, win_all[:, pad:])
    gather.finish()
    own.wait()


def front(plan, length, tok, wq, win, gyw, cosine, sine, collective_id):
    slots, heads, block, width = plan.slots, plan.heads, plan.block, plan.width
    highs, ys = plan.quad // 2, plan.dp // 2
    on = max(2 * plan.quad * max(ys - 1, 1), 2 * plan.quad + (ys - 1) * plan.ctx, plan.quad)
    return pl.pallas_call(
        functools.partial(front_kernel, plan),
        out_shape=(
            jax.ShapeDtypeStruct((plan.ctx, block, width), BF16),
            jax.ShapeDtypeStruct((width, plan.wide), BF16),
            jax.ShapeDtypeStruct((slots, width), BF16),
            jax.ShapeDtypeStruct((slots, 2 * plan.head_cols), BF16),
            jax.ShapeDtypeStruct((slots, plan.head_cols), BF16),
            jax.ShapeDtypeStruct((heads, slots, 1), F32),
            jax.ShapeDtypeStruct((plan.quad, 2, block, plan.head_cols), BF16),
            jax.ShapeDtypeStruct((plan.group, 2) + gyw.shape[1:], BF16),
            jax.ShapeDtypeStruct((width, 2 * plan.hidden_pad), BF16),
        ),
        in_specs=[pl.BlockSpec(memory_space=pltpu.SMEM)] + [VMEM] * 6,
        out_specs=(VMEM,) * 7 + (HBM, VMEM),
        scratch_shapes=[
            pltpu.VMEM((plan.devices,) + wq.shape[1:], BF16),
            pltpu.VMEM(wq.shape, BF16),
            pltpu.VMEM((plan.devices,) + win.shape[1:], BF16),
            pltpu.VMEM(gyw.shape, BF16),
            pltpu.VMEM((slots, plan.wide), F32),
            pltpu.VMEM((plan.ctx, block, plan.head_cols), BF16),
            DMA((2, 2 * highs)),
            DMA((2, 2, highs)),
            DMA((3,)),
            DMA((3,)),
            DMA((2, 2, on)),
            DMA((plan.devices,)),
            DMA((plan.group - 1,)),
            DMA((plan.group - 1,)),
            DMA((plan.group,)),
            DMA((plan.group,)),
            DMA,
            DMA((plan.ctx,)),
            DMA((plan.quad, 2)),
        ]
        + gather_sems(plan),
        compiler_params=params(collective_id),
        cost_estimate=busy(90),
        name="front",
    )(length, tok, wq, win, gyw, cosine, sine)


OUT_ORDERS = (("low", "y", "high"), ("y", "low", "high"))


class OutSum:
    def __init__(self, grid, at, src, work, core_buf, bufs, load_sem, core_send, core_recv, send, recv):
        self.grid, self.at, self.src = grid, at, src
        self.work, self.core_buf, self.bufs = work, core_buf, bufs
        self.load_sem, self.core_send, self.core_recv = load_sem, core_send, core_recv
        self.send, self.recv = send, recv
        self.loaded = set()
        rows = work.shape[1] // 2
        self.rows = [slice(0, rows), slice(rows, 2 * rows)]
        self.index = [
            {o: i for i, o in enumerate(o for o in STEP_ORDER if any(o))} for _ in OUT_ORDERS
        ]

    def pair(self, offset):
        where = dict(self.at)
        for axis, step in named(offset).items():
            if step:
                where = self.grid.moved(where, axis, step)
        slot = self.grid.slot(named(offset))
        partner = self.grid.device(self.grid.moved(self.at, "core", 1))
        away = remote(
            self.src.at[self.grid.block(self.grid.moved(where, "core", 1))],
            self.core_buf.at[slot],
            self.core_send.at[slot],
            self.core_recv.at[slot],
            partner,
        )
        load = pltpu.make_async_copy(
            self.src.at[self.grid.block(where)], self.work.at[slot], self.load_sem.at[slot]
        )
        return away, load

    def start(self):
        for offset in STEP_ORDER[::-1]:
            for copy in self.pair(offset):
                copy.start()

    def onward(self, part, offset, axis):
        index, rows = self.index[part][offset], self.rows[part]
        return remote(
            self.work.at[self.grid.slot(named(offset)), rows],
            self.bufs.at[index, rows],
            self.send.at[part, index],
            self.recv.at[part, index],
            self.grid.device(self.grid.moved(self.at, axis, 1)),
        )

    def phase(self, number):
        for offset in STEP_ORDER:
            for part, order in enumerate(OUT_ORDERS):
                phase, feeds = feeds_of(order, offset)
                if phase != number:
                    continue
                if offset not in self.loaded:
                    self.loaded.add(offset)
                    for copy in self.pair(offset):
                        copy.wait()
                for feed, axis in zip(feeds, order):
                    self.onward(part, feed, axis).wait_recv()
                slot, rows = self.grid.slot(named(offset)), self.rows[part]

                @pl.loop(0, (rows.stop - rows.start) // 16)
                def _(i, slot=slot, part=part, feeds=feeds, start=rows.start):
                    span = pl.ds(pl.multiple_of(start + i * 16, 16), 16)
                    value = self.work[slot, span].astype(F32)
                    value = value + self.core_buf[slot, span].astype(F32)
                    for feed in feeds:
                        value = value + self.bufs[self.index[part][feed], span].astype(F32)
                    self.work[slot, span] = value.astype(BF16)

                if number < 3:
                    self.onward(part, offset, order[number]).start()

    def finish(self):
        for offset in STEP_ORDER:
            for part, order in enumerate(OUT_ORDERS):
                phase, _ = feeds_of(order, offset)
                if phase < 3:
                    self.onward(part, offset, order[phase]).wait_send()


class Fold:
    def __init__(self, plan, src, dst, core_buf, y_buf, added, sems):
        self.plan, self.src, self.dst = plan, src, dst
        self.core_buf, self.y_buf, self.added = core_buf, y_buf, added
        self.core_send, self.core_recv, self.y_send, self.y_recv, self.send, self.recv = sems
        self.dp, self.ctx = place()
        self.core, self.y = lax.rem(self.dp, 2), lax.div(self.dp, 2)
        self.ys = plan.dp // 2

    def core_copies(self):
        partner = (self.dp + 1 - 2 * self.core, self.ctx)
        return [
            remote(
                self.src.at[y * 2 + 1 - self.core],
                self.core_buf.at[y],
                self.core_send.at[y],
                self.core_recv.at[y],
                partner,
            )
            for y in range(self.ys)
        ]

    def y_copies(self):
        copies = []
        for step in range(1, self.ys):
            to = lax.rem(self.y + step, self.ys)
            copies.append(
                remote(
                    self.core_buf.at[to],
                    self.y_buf.at[step - 1],
                    self.y_send.at[step - 1],
                    self.y_recv.at[step - 1],
                    (to * 2 + self.core, self.ctx),
                )
            )
        return copies

    def owner_copies(self):
        copies = []
        for step in range(1, self.plan.ctx):
            to = lax.rem(self.ctx + step, self.plan.ctx)
            copies.append(
                remote(
                    self.added.at[to],
                    self.dst.at[self.ctx],
                    self.send.at[step - 1],
                    self.recv.at[step - 1],
                    (self.dp, to),
                )
            )
        return copies

    def start(self):
        for copy in self.core_copies():
            copy.start()

    def along_y(self):
        for copy in self.core_copies():
            copy.wait()
        for y in range(self.ys):
            mine = self.src[y * 2 + self.core].astype(F32)
            self.core_buf[y] = (mine + self.core_buf[y].astype(F32)).astype(BF16)
        for copy in self.y_copies():
            copy.start()

    def to_owners(self):
        for copy in self.y_copies():
            copy.wait()
        total = self.core_buf[self.y].astype(F32)
        for step in range(1, self.ys):
            total = total + self.y_buf[step - 1].astype(F32)
        self.added[...] = total.astype(BF16)
        for copy in self.owner_copies():
            copy.start()
        self.dst[pl.ds(self.ctx, 1)] = self.added[pl.ds(self.ctx, 1)]

    def finish(self):
        for copy in self.owner_copies():
            copy.wait()


def padded_rows(plan, value, count):
    if plan.pad_rows != plan.rows:
        row = lax.broadcasted_iota(jnp.int32, (count * plan.pad_rows, count * plan.rows), 0)
        col = lax.broadcasted_iota(jnp.int32, (count * plan.pad_rows, count * plan.rows), 1)
        inside = lax.rem(row, plan.pad_rows)
        wanted = lax.div(row, plan.pad_rows) * plan.rows + inside
        hit = (col == wanted) & (inside < plan.rows)
        value = nn(hit.astype(BF16), value.astype(BF16))
    return value.reshape(count, plan.pad_rows, value.shape[-1])


def fold_scratch(plan, rows, width):
    shape = (plan.ctx, rows, width)
    ys = plan.dp // 2
    return [
        pltpu.VMEM((ys,) + shape, BF16),
        pltpu.VMEM((max(ys - 1, 1),) + shape, BF16),
        pltpu.VMEM(shape, BF16),
        DMA((ys,)),
        DMA((ys,)),
        DMA((max(ys - 1, 1),)),
        DMA((max(ys - 1, 1),)),
        DMA((plan.ctx - 1,)),
        DMA((plan.ctx - 1,)),
    ]


def back_kernel(plan, summed, length_ref, x, w, cosine, sine, normed, qk_in, v_in, lse, dmixed, dwo, small, dw_in, out_part, middle, x_own, middle_grad, gain, rwq, rwo, rwin, act_out, grad_out, dqkv, dk_acc, dv_acc, upstream_all, dnp, rdn, dwq, far_in, dealt, grad_away, act_away, d_send, d_recv, n_send, n_recv, w_send, w_recv, e_send, e_recv, s_send, s_recv, *refs):
    dp, ctx = place()
    core, y = lax.rem(dp, 2), lax.div(dp, 2)
    half, member = lax.div(ctx, plan.quad), lax.rem(ctx, plan.quad)
    far = (1 - half) * plan.quad + member
    mine = dp * plan.quad + member
    across = (dp, far)
    members = quad_members(plan, half, member)
    targets = half_members(plan, mine)
    devices = [
        (lax.div(target, plan.quad), half * plan.quad + lax.rem(target, plan.quad))
        for target in targets
    ]
    meet(
        devices
        + [across]
        + [
            (dp, (1 - half) * plan.quad + lax.rem(member + step, plan.quad))
            for step in range(1, plan.quad)
        ]
    )
    arriving = []
    for i, (peer, to) in enumerate(members):
        for j, at in enumerate((ctx, far)):
            copy = remote(
                dmixed.at[to, j],
                upstream_all.at[at],
                d_send.at[2 * i + j],
                d_recv.at[2 * i + j],
                (dp, peer),
            )
            copy.start()
            arriving.append(copy)
    fold_refs, out_refs = refs[:18], refs[18:]
    count = len(fold_refs) // 2
    mix_fold = Fold(plan, dwo, rwo, *fold_refs[:3], fold_refs[3:count])
    qkv_fold = Fold(plan, dwq, rwq, *fold_refs[count : count + 3], fold_refs[count + 3 :])
    mix_fold.start()
    out_sum = None
    if not summed:
        grid = Grid(plan)
        out_sum = OutSum(grid, grid.here(), out_part, *out_refs)
        out_sum.start()
    swaps = [
        remote(dw_in.at[2 * i + 1 - half], far_in.at[i], w_send.at[i], w_recv.at[i], across)
        for i in range(plan.dp)
    ]
    hidden, pad = plan.hidden_pad, plan.pad_rows

    def deal_copy(target):
        tdp, tmember = divmod(target, plan.quad)
        return remote(
            dealt.at[target],
            rwin.at[mine],
            e_send.at[target],
            e_recv.at[mine],
            (tdp, half * plan.quad + tmember),
        )

    def deal(i):
        swaps[i].wait()
        value = dw_in[pl.ds(2 * i + half, 1)][0].astype(F32) + far_in[i].astype(F32)
        value = padded_rows(plan, value, plan.quad)
        value = jnp.concatenate([value[:, :, :hidden], value[:, :, hidden:]], axis=1)
        dealt[i * plan.quad : (i + 1) * plan.quad] = value.astype(BF16)
        for target in range(i * plan.quad, (i + 1) * plan.quad):
            pl.when(mine != target)(lambda target=target: deal_copy(target).start())

            @pl.when(mine == target)
            def _(target=target):
                rwin[target] = dealt[target]

    swaps[0].start()
    upstream_all[pl.ds(ctx, 1)] = dmixed[pl.ds(member, 1), 0]
    upstream_all[pl.ds(far, 1)] = dmixed[pl.ds(member, 1), 1]
    length = length_ref[0]
    rows, slots, heads, block = QUERY_ROWS, plan.slots, plan.heads, plan.block
    qk_width = 2 * HEAD_DIM
    dqkv[...] = jnp.zeros_like(dqkv)
    for copy in arriving:
        copy.wait()

    def token_copy(index):
        side, to = divmod(index, plan.quad)
        turn = lax.rem(half + side, 2)
        return remote(
            dnp.at[index],
            rdn.at[member, turn],
            n_send.at[index],
            n_recv.at[member, turn],
            (dp, half * plan.quad + to),
        )

    gains = jnp.zeros((1, plan.width), F32)
    spans = list(range(slots - rows, -1, -rows))
    for number, start in enumerate(spans):
        at = slice(start, start + rows)
        end = start + rows
        for head in range(heads):
            base = head * qk_width
            v_cols = slice(head * HEAD_DIM, (head + 1) * HEAD_DIM)
            q = qk_in[at, base : base + HEAD_DIM] * BF16(0.125)
            k = qk_in[:end, base + HEAD_DIM : base + qk_width]
            v = v_in[:end, v_cols]
            upstream = jnp.concatenate(
                [upstream_all[start // block + i, :, v_cols] for i in range(rows // block)], axis=0
            )
            probs = jnp.exp(masked_scores(q, k, start, length) - lse[head, at])
            dv = tn(probs.astype(BF16), upstream)
            prob_grad = nt(upstream, v)
            inner = jnp.sum(probs * prob_grad, axis=-1, keepdims=True)
            score_grad = (probs * (prob_grad - inner)).astype(BF16)
            dq = nn(score_grad, k) * 0.125
            dk = tn(score_grad, q)
            if end == slots:
                dk_acc[head] = dk
                dv_acc[head] = dv
            else:
                dk_acc[head, :end] += dk
                dv_acc[head, :end] += dv
            dqk = jnp.concatenate([dq, dk_acc[head, at]], axis=-1)
            dqkv[at, base : base + qk_width] = (
                dqk * cosine[at] - swapped_halves(dqk) * sine[at]
            ).astype(BF16)
            v_base = heads * qk_width + head * HEAD_DIM
            dqkv[at, v_base : v_base + HEAD_DIM] = dv_acc[head, at].astype(BF16)
        part = nt(dqkv[at], w[...])
        for i in range(rows // block):
            index = start // block + i
            dnp[index] = part[i * block : (i + 1) * block].astype(BF16)
            pl.when(member != index % plan.quad)(lambda index=index: token_copy(index).start())

            @pl.when(member == index % plan.quad)
            def _(index=index):
                turn = lax.rem(half + index // plan.quad, 2)
                rdn[pl.ds(member, 1), pl.ds(turn, 1)] = dnp[index][None, None]

        values = x[at].astype(F32)
        inverse = lax.rsqrt(jnp.mean(values * values, axis=-1, keepdims=True) + EPSILON)
        gains = gains + jnp.sum(part * values * inverse, axis=0, keepdims=True)
        if number == 0:
            mix_fold.along_y()
            if out_sum:
                out_sum.phase(0)
        if number == len(spans) - 2:
            mix_fold.to_owners()
            if out_sum:
                out_sum.phase(1)
        if number < plan.dp - 1:
            swaps[number + 1].start()
    for i in range(len(spans) + 1, plan.dp):
        swaps[i].start()
    deal(0)
    column = jnp.transpose(jnp.broadcast_to(gains, (128, plan.width)), (1, 0))
    lane = lax.broadcasted_iota(jnp.int32, column.shape, 1)
    first = plan.qkv_cols - (plan.wide - 128)
    extra = jnp.where(lane == first, column, small[...])
    for start in range(0, plan.wide, 128):
        cols = slice(start, start + 128)
        value = tn(normed[...], dqkv[:, cols])
        if start + 128 == plan.wide:
            value = value + extra
        value = padded_rows(plan, value, plan.devices).astype(BF16)
        dwq[:, :, :, cols] = value.reshape(plan.dp, plan.ctx, plan.pad_rows, 128)
    qkv_fold.start()
    local, width = plan.local, plan.width
    if out_sum:
        out_sum.phase(2)
    for source in range(plan.quad):

        @pl.when(member != source)
        def _(source=source):
            for turn in range(2):
                remote(
                    dnp.at[0], rdn.at[source, turn], n_send.at[0], n_recv.at[source, turn], (dp, ctx)
                ).wait_recv()

    total = rdn[0].astype(F32)
    for i in range(1, plan.quad):
        total = total + rdn[i].astype(F32)
    total = total.reshape(local, width)
    values = x_own[...]
    inverse = lax.rsqrt(jnp.mean(values * values, axis=-1, keepdims=True) + EPSILON)
    scaled = total * gain[...]
    result = (
        middle_grad[...]
        + inverse * scaled
        - values * inverse * inverse * inverse * jnp.mean(scaled * values, axis=-1, keepdims=True)
    )
    result = result.astype(BF16).reshape(2, block, width)
    grad_away[...] = result[1]
    grad_out[pl.ds(half, 1)] = result[:1]
    swap_grad = remote(grad_away, grad_out.at[half], s_send.at[1], s_recv.at[1], across)
    swap_grad.start()
    qkv_fold.along_y()
    if out_sum:
        out_sum.phase(3)
        acts = middle[...] + out_sum.work[0].astype(F32)
    else:
        acts = middle[...] + out_part[...].astype(F32)
    acts = acts.astype(BF16).reshape(2, block, width)
    act_away[...] = acts[1]
    act_out[pl.ds(half, 1)] = acts[:1]
    swap_act = remote(act_away, act_out.at[half], s_send.at[0], s_recv.at[0], across)
    swap_act.start()
    for i in range(1, plan.dp):
        deal(i)
        if i == 1:
            qkv_fold.to_owners()
    mix_fold.finish()
    qkv_fold.finish()
    swap_act.wait()
    swap_grad.wait()
    for target in range(plan.group):

        @pl.when(mine != target)
        def _(target=target):
            deal_copy(target).wait_send()
            remote(
                dealt.at[0], rwin.at[target], e_send.at[0], e_recv.at[target], (dp, ctx)
            ).wait_recv()

    for index in range(plan.ctx):
        pl.when(member != index % plan.quad)(lambda index=index: token_copy(index).wait_send())
    if out_sum:
        out_sum.finish()


def back(plan, length, x, w, cosine, sine, normed, qk, v, lse, dmixed, dwo, small, dw_in, out_part, middle, x_own, middle_grad, gain, collective_id):
    slots, block, width = plan.slots, plan.block, plan.width
    count = 2 * (plan.quad - 1)
    dealt = (plan.group, 2 * plan.pad_rows, plan.hidden_pad)
    summed = out_part.ndim == 2
    rows = (plan.local, width)
    out_scratch = [
        pltpu.VMEM((8,) + rows, BF16),
        pltpu.VMEM((8,) + rows, BF16),
        pltpu.VMEM((7,) + rows, BF16),
        DMA((8,)),
        DMA((8,)),
        DMA((8,)),
        DMA((2, 7)),
        DMA((2, 7)),
    ]
    return pl.pallas_call(
        functools.partial(back_kernel, plan, summed),
        out_shape=(
            jax.ShapeDtypeStruct((plan.ctx, plan.pad_rows, plan.wide), BF16),
            jax.ShapeDtypeStruct((plan.ctx, plan.rows, width), BF16),
            jax.ShapeDtypeStruct(dealt, BF16),
            jax.ShapeDtypeStruct((2, block, width), BF16),
            jax.ShapeDtypeStruct((2, block, width), BF16),
        ),
        in_specs=[pl.BlockSpec(memory_space=pltpu.SMEM)]
        + [VMEM] * 12
        + [VMEM if summed else HBM]
        + [VMEM] * 4,
        out_specs=(VMEM,) * 5,
        scratch_shapes=[
            pltpu.VMEM((slots, plan.wide), BF16),
            pltpu.VMEM((plan.heads, slots, HEAD_DIM), F32),
            pltpu.VMEM((plan.heads, slots, HEAD_DIM), F32),
            pltpu.VMEM((plan.ctx, block, plan.head_cols), BF16),
            pltpu.VMEM((plan.ctx, block, width), BF16),
            pltpu.VMEM((plan.quad, 2, block, width), BF16),
            pltpu.VMEM((plan.dp, plan.ctx, plan.pad_rows, plan.wide), BF16),
            pltpu.VMEM((plan.dp,) + dw_in.shape[1:], BF16),
            pltpu.VMEM(dealt, BF16),
            pltpu.VMEM((block, width), BF16),
            pltpu.VMEM((block, width), BF16),
            DMA((count,)),
            DMA((count,)),
            DMA((plan.ctx,)),
            DMA((plan.quad, 2)),
            DMA((plan.dp,)),
            DMA((plan.dp,)),
            DMA((plan.group,)),
            DMA((plan.group,)),
            DMA((3,)),
            DMA((3,)),
        ]
        + fold_scratch(plan, plan.rows, width)
        + fold_scratch(plan, plan.pad_rows, plan.wide)
        + ([] if summed else out_scratch),
        compiler_params=params(collective_id),
        cost_estimate=busy(90),
        name="back",
    )(length, x, w, cosine, sine, normed, qk, v, lse, dmixed, dwo, small, dw_in, out_part, middle, x_own, middle_grad, gain)


def ffn_kernel(plan, members, n2x, gy, w_in, w_out, pick, out, n2g, dw_in, dw_out):
    hidden, local = plan.hidden_pad, plan.local

    @pl.when(pl.program_id(0) == 0)
    def start():
        dw_in[...] = jnp.zeros_like(dw_in)
        dw_out[...] = jnp.zeros_like(dw_out)

    tokens = members * local
    width = plan.width
    normed = n2x[:, :local].reshape(tokens, width)
    upstream = gy[:, :, : plan.block].reshape(tokens, width)
    mixing = jnp.concatenate(
        [tn(n2x[i, local:, :local], pick[...]) for i in range(members)], axis=0
    )
    pre = nn(normed, w_in[...])
    gate, up = pre[:, :hidden], pre[:, hidden:]
    sigmoid = jax.nn.sigmoid(gate)
    silu = gate * sigmoid
    act = (silu * up).astype(BF16).astype(F32)
    act_mixed = (act * mixing).astype(BF16)
    out[...] = nn(act_mixed, w_out[...]).astype(BF16).reshape(members, local, width)
    act_grad = nt(upstream, w_out[...])
    choice = nt(pick[...], (act * act_grad).astype(BF16)).astype(BF16)
    act_grad = act_grad * mixing
    gate_grad = act_grad * up * sigmoid * (1.0 + gate * (1.0 - sigmoid))
    pre_grad = jnp.concatenate([gate_grad, act_grad * silu], axis=-1).astype(BF16)
    n2g[:, :local] = nt(pre_grad, w_in[...]).astype(BF16).reshape(members, local, width)
    pad = jnp.zeros((MIX_ROWS, width - local), BF16)
    for i in range(members):
        n2g[i, local:] = jnp.concatenate(
            [choice[:, i * local : (i + 1) * local], pad], axis=-1
        )
    dw_in[...] += tn(normed, pre_grad)
    dw_out[...] += tn(act_mixed, upstream)


def ffn(plan, n2x, gy, w_in, w_out, pick):
    members = 2
    local, width, hidden = plan.local, plan.width, plan.hidden_pad
    whole = lambda i: (0, 0)
    part = lambda i: (i, 0, 0)
    return pl.pallas_call(
        functools.partial(ffn_kernel, plan, members),
        grid=(plan.group // members,),
        out_shape=(
            jax.ShapeDtypeStruct((plan.group, local, width), BF16),
            jax.ShapeDtypeStruct((plan.group, local + MIX_ROWS, width), BF16),
            jax.ShapeDtypeStruct((width, 2 * hidden), F32),
            jax.ShapeDtypeStruct((hidden, width), F32),
        ),
        in_specs=[
            pl.BlockSpec((members, local + MIX_ROWS, width), part),
            pl.BlockSpec((members,) + gy.shape[1:], lambda i: (i, 0, 0, 0)),
            pl.BlockSpec((width, 2 * hidden), whole),
            pl.BlockSpec((hidden, width), whole),
            pl.BlockSpec((MIX_ROWS, hidden), whole),
        ],
        out_specs=(
            pl.BlockSpec((members, local, width), part),
            pl.BlockSpec((members, local + MIX_ROWS, width), part),
            pl.BlockSpec((width, 2 * hidden), whole),
            pl.BlockSpec((hidden, width), whole),
        ),
        compiler_params=params(),
        name="ffn",
    )(n2x, gy, w_in, w_out, pick)


STEP_ORDER = ((0, 0, 0), (0, 0, 1), (0, 1, 0), (1, 0, 1), (1, 1, 0), (1, 1, 1), (0, 1, 1), (1, 0, 0))
PART_ORDERS = (("high", "low", "y"), ("low", "y", "high"), ("y", "high", "low"))
PAUSES = {
    3: (('g0', 7), ('g0', 2), ('g0', 1), ('g1', 1), ('g2', 1)),
    4: (('g1', 2), ('g2', 7), ('g2', 2), ('g1', 7)),
    5: (('g0', 4), ('g0', 3), ('g1', 3)),
    7: (('g2', 3), ('g0', 6), ('g2', 6), ('s2', 1)),
    8: (('g1', 4), ('g2', 4)),
    9: (('g1', 6),),
    10: (('s1', 2),),
    11: (('g0', 5), ('g2', 5)),
    13: (('g1', 5), ('s0', 3), ('s2', 3)),
    16: (('s0', 4), ('s1', 4)),
    19: (('s0', 5), ('s1', 5), ('s2', 5)),
    20: (('s0', 2),),
    22: (('s1', 6), ('s2', 6)),
    23: (('s1', 3), ('s2', 4), ('s0', 6)),
    24: (('s0', 7), ('s2', 7), ('s1', 1), ('s2', 2), ('s1', 7), ('s0', 1), ('s2', 0), ('s0', 0), ('s1', 0)),
}


def part_rows(rows):
    cuts = [round_up(rows * i // 3, 16) for i in range(3)] + [rows]
    return [slice(a, b) for a, b in zip(cuts, cuts[1:])]


def named(offset):
    return dict(zip(("high", "low", "y"), offset))


def feeds_of(order, offset):
    at = named(offset)
    phase = min([i for i, axis in enumerate(order) if at[axis]], default=3)
    names = ("high", "low", "y")
    return phase, [tuple(1 if n == axis else at[n] for n in names) for axis in order[:phase]]


def fused_kernel(plan, n2x, gy, w_in, w_out, pick, total, dw_in, dw_out, out_all, n2all, gybuf, acc, away, work, core_buf, bufs, outbuf, gy_sem, out_sem, g_send, g_recv, gc_send, gc_recv, c_send, c_recv, r_send, r_recv):
    grid = Grid(plan)
    at = grid.here()
    local, width, hidden = plan.local, plan.width, plan.hidden_pad
    steps = len(STEP_ORDER)
    partner = grid.device(grid.moved(at, "core", 1))
    here = grid.device(at)
    parts = range(len(PART_ORDERS))
    in_rows, sum_rows = part_rows(local + MIX_ROWS), part_rows(local + MIX_ROWS)

    def absolute(offset):
        where = dict(at)
        for axis, step in named(offset).items():
            if step:
                where = grid.moved(where, axis, step)
        return where

    def slot_of(offset):
        return grid.slot(named(offset))

    def level_of(part, offset):
        reached = named(offset)
        return max([i + 1 for i, axis in enumerate(PART_ORDERS[part]) if reached[axis]], default=0)

    send_index = {}
    for part in parts:
        count = 0
        for offset in STEP_ORDER:
            for axis in PART_ORDERS[part][level_of(part, offset) :]:
                send_index[part, offset, axis] = count
                count += 1

    def pass_on(part, offset):
        level = level_of(part, offset)
        block = grid.block(absolute(offset))
        slot = slot_of(offset)
        span = in_rows[part]
        landing = n2all.at[block, span]
        if level:
            remote(landing, landing, g_send.at[part, 0], g_recv.at[part, slot], here).wait_recv()
        source = landing if level else n2x.at[span]
        for axis in PART_ORDERS[part][level:]:
            seen = grid.slot({**named(offset), axis: 1})
            remote(
                source,
                landing,
                g_send.at[part, send_index[part, offset, axis]],
                g_recv.at[part, seen],
                grid.device(grid.moved(at, axis, 1)),
            ).start()
        remote(source, landing, gc_send.at[part, slot], gc_recv.at[part, slot], partner).start()

    listed = [(kind[0], int(kind[1]), STEP_ORDER[place]) for row in PAUSES.values() for kind, place in row]
    buf_index, seen_slots, first_sums = {}, set(), set()
    for kind, part, offset in listed:
        if kind == "s":
            if offset not in seen_slots:
                seen_slots.add(offset)
                first_sums.add((part, offset))
            if any(offset):
                buf_index[part, offset] = sum(1 for other, _ in buf_index if other == part)

    def add_up(part, offset):
        phase, feeds = feeds_of(PART_ORDERS[part], offset)
        axis = PART_ORDERS[part][phase] if phase < 3 else None
        slot = slot_of(offset)
        span = sum_rows[part]
        if (part, offset) in first_sums:
            remote(away.at[0], core_buf.at[slot], c_send.at[0], c_recv.at[slot], here).wait_recv()
        for feed in feeds:
            index = buf_index[part, feed]
            ref = bufs.at[index, span]
            remote(ref, ref, r_send.at[part, 0], r_recv.at[part, index], here).wait_recv()

        @pl.loop(0, (span.stop - span.start) // 16)
        def _(i):
            rows = pl.ds(pl.multiple_of(span.start + i * 16, 16), 16)
            value = work[slot, rows].astype(F32) + core_buf[slot, rows].astype(F32)
            for feed in feeds:
                value = value + bufs[buf_index[part, feed], rows].astype(F32)
            if axis is None:
                total[rows] = value
            else:
                work[slot, rows] = value.astype(BF16)

        if axis is not None:
            index = buf_index[part, offset]
            remote(
                work.at[slot, span],
                bufs.at[index, span],
                r_send.at[part, index],
                r_recv.at[part, index],
                grid.device(grid.moved(at, axis, 1)),
            ).start()

    def pause(number):
        for kind, place in PAUSES.get(number, ()):
            act = pass_on if kind[0] == "g" else add_up
            act(int(kind[1]), STEP_ORDER[place])

    def pauses(step, turn):
        for i in range(steps):
            if 3 * i + turn in PAUSES:
                pl.when(step == i)(functools.partial(pause, 3 * i + turn))

    def bit(step, index):
        value = 0
        for i, offset in enumerate(STEP_ORDER):
            if offset[index]:
                value = value + jnp.where(step == i, 1, 0)
        return value

    def blocks_of(step):
        where = dict(at)
        offsets = {}
        for index, axis in enumerate(("high", "low", "y")):
            offsets[axis] = bit(step, index)
            where[axis] = lax.rem(at[axis] + offsets[axis], 2)
        mine = grid.block(where)
        other = grid.block(grid.moved(where, "core", 1))
        return mine, other, grid.slot(offsets)

    def gy_loads(step, turn):
        mine, other, _ = blocks_of(step)
        return [
            pltpu.make_async_copy(gy.at[mine, :, : plan.block], gybuf.at[turn, 0], gy_sem.at[turn, 0]),
            pltpu.make_async_copy(gy.at[other, :, : plan.block], gybuf.at[turn, 1], gy_sem.at[turn, 1]),
        ]

    def out_copy(turn, i, block):
        return pltpu.make_async_copy(outbuf.at[turn, i], out_all.at[block], out_sem.at[turn, i])

    for load in gy_loads(0, 0):
        load.start()
    meet(grid.peers(at))
    for part in parts:
        pass_on(part, STEP_ORDER[0])
    n2all[pl.ds(grid.block(at), 1)] = n2x[...][None]
    acc[...] = jnp.zeros_like(acc)
    dw_out[...] = jnp.zeros_like(dw_out)

    @pl.loop(0, steps)
    def _(step):
        pauses(step, 0)
        mine, other, slot = blocks_of(step)
        turn = lax.rem(step, 2)

        @pl.when(step + 1 < steps)
        def _():
            for load in gy_loads(step + 1, 1 - turn):
                load.start()

        for part in parts:
            ref = n2all.at[other, in_rows[part]]
            remote(ref, ref, gc_send.at[part, 0], gc_recv.at[part, slot], here).wait_recv()
        for load in gy_loads(step, turn):
            load.wait()
        pair = (mine, other)
        normed = jnp.concatenate([n2all[b, :local] for b in pair], axis=0)
        upstream = gybuf[turn].reshape(2 * local, width)
        mixing = jnp.concatenate([tn(n2all[b, local:, :local], pick[...]) for b in pair], axis=0)
        pre = nn(normed, w_in[...])
        gate, up = pre[:, :hidden], pre[:, hidden:]
        sigmoid = jax.nn.sigmoid(gate)
        silu = gate * sigmoid
        act = (silu * up).astype(BF16).astype(F32)
        act_mixed = (act * mixing).astype(BF16)
        pauses(step, 1)

        @pl.when(step >= 2)
        def _():
            for i, block in enumerate(pair):
                out_copy(turn, i, block).wait()

        out = nn(act_mixed, w_out[...]).astype(BF16)
        for i, block in enumerate(pair):
            outbuf[turn, i] = out[i * local : (i + 1) * local]
            out_copy(turn, i, block).start()
        act_grad = nt(upstream, w_out[...])
        choice = nt(pick[...], (act * act_grad).astype(BF16)).astype(BF16)
        act_grad = act_grad * mixing
        gate_grad = act_grad * up * sigmoid * (1.0 + gate * (1.0 - sigmoid))
        pre_grad = jnp.concatenate([gate_grad, act_grad * silu], axis=-1).astype(BF16)
        n2g = nt(pre_grad, w_in[...]).astype(BF16)

        @pl.when(step >= 2)
        def _():
            remote(away.at[turn], core_buf.at[0], c_send.at[turn], c_recv.at[0], partner).wait_send()

        pad = jnp.zeros((MIX_ROWS, width - local), BF16)
        for i, (ref, index) in enumerate(((work, slot), (away, turn))):
            span = slice(i * local, (i + 1) * local)
            ref[index, :local] = n2g[span]
            ref[index, local:] = jnp.concatenate([choice[:, span], pad], axis=-1)
        remote(away.at[turn], core_buf.at[slot], c_send.at[turn], c_recv.at[slot], partner).start()
        pauses(step, 2)
        acc[...] += tn(normed, pre_grad)
        dw_out[...] += tn(act_mixed, upstream)

    pause(3 * steps)
    for turn in range(2):
        for i in range(2):
            out_copy(turn, i, 0).wait()
    dw_in[...] = acc[...].astype(BF16)
    for turn in range(2):
        remote(away.at[turn], core_buf.at[0], c_send.at[turn], c_recv.at[0], partner).wait_send()
    for part in parts:
        ref, block = n2all.at[0, in_rows[part]], bufs.at[0, sum_rows[part]]
        for slot in range(steps):
            remote(ref, ref, gc_send.at[part, slot], g_recv.at[part, 0], partner).wait_send()
        for index in range(steps - 1):
            remote(ref, ref, g_send.at[part, index], g_recv.at[part, 0], partner).wait_send()
            remote(block, block, r_send.at[part, index], r_recv.at[part, 0], partner).wait_send()


def fused(plan, n2x, gy, w_in, w_out, pick, collective_id):
    local, width, hidden = plan.local, plan.width, plan.hidden_pad
    steps = len(STEP_ORDER)
    rows = local + MIX_ROWS
    return pl.pallas_call(
        functools.partial(fused_kernel, plan),
        out_shape=(
            jax.ShapeDtypeStruct((rows, width), F32),
            jax.ShapeDtypeStruct((width, 2 * hidden), BF16),
            jax.ShapeDtypeStruct((hidden, width), F32),
            jax.ShapeDtypeStruct((plan.group, local, width), BF16),
        ),
        in_specs=[VMEM, HBM, VMEM, VMEM, VMEM],
        out_specs=(VMEM,) * 3 + (HBM,),
        scratch_shapes=[
            pltpu.VMEM((plan.group, local + MIX_ROWS, width), BF16),
            pltpu.VMEM((2, 2, 2, plan.block, width), BF16),
            pltpu.VMEM((width, 2 * hidden), F32),
            pltpu.VMEM((2, rows, width), BF16),
            pltpu.VMEM((steps, rows, width), BF16),
            pltpu.VMEM((steps, rows, width), BF16),
            pltpu.VMEM((steps - 1, rows, width), BF16),
            pltpu.VMEM((2, 2, local, width), BF16),
            DMA((2, 2)),
            DMA((2, 2)),
            DMA((3, steps - 1)),
            DMA((3, steps)),
            DMA((3, steps)),
            DMA((3, steps)),
            DMA((2,)),
            DMA((steps,)),
            DMA((3, steps - 1)),
            DMA((3, steps - 1)),
        ],
        compiler_params=params(collective_id),
        cost_estimate=busy(100),
        name="fused",
    )(n2x, gy, w_in, w_out, pick)


def grid_block(plan, dp, ctx):
    return dp * plan.quad + lax.rem(ctx, plan.quad)


def by_half(half, mine, far, axis):
    return jnp.where(
        half == 0, jnp.stack([mine, far], axis), jnp.stack([far, mine], axis)
    )


def rope_tables(plan):
    half = HEAD_DIM // 2
    frequency = np.float32(10000.0) ** (-np.arange(half, dtype=np.float32) / np.float32(half))
    angles = np.arange(plan.slots, dtype=np.float32)[:, None] * frequency[None, :]
    cosine = np.cos(angles.astype(np.float64)).astype(np.float32)
    sine = np.sin(angles.astype(np.float64)).astype(np.float32)
    return np.tile(cosine, (1, 4)), np.tile(np.concatenate([-sine, sine], 1), (1, 2))


def pick_table(plan):
    table = np.zeros((MIX_ROWS, plan.hidden_pad), np.float32)
    span = HALVES * plan.own_hidden
    for expert in range(plan.experts):
        cols = slice((1 + expert) * span, (2 + expert) * span)
        table[expert, cols] = 1.0
        table[plan.experts + expert, cols] = 1.0
    table[2 * plan.experts, :span] = 1.0
    return jnp.asarray(table, BF16)


def pack_qkv(plan, attn_in, attn_gain, ffn_gain, router):
    rows, quad, heads = plan.rows, plan.quad, plan.heads
    qkv = attn_in.reshape(rows, 3, HEADS, HEAD_DIM)
    qkv = jnp.pad(qkv, ((0, 0), (0, 0), (0, quad * heads - HEADS), (0, 0)))
    qkv = qkv.reshape(rows, 3, quad, heads, HEAD_DIM)
    qk = jnp.transpose(qkv[:, :2], (2, 0, 3, 1, 4)).reshape(quad, rows, 2 * plan.head_cols)
    v = jnp.transpose(qkv[:, 2], (1, 0, 2, 3)).reshape(quad, rows, plan.head_cols)
    extra = jnp.concatenate([attn_gain[:, None], ffn_gain[:, None], router], axis=1)
    extra = jnp.pad(extra, ((0, 0), (0, plan.wide - plan.qkv_cols - extra.shape[1])))
    extra = jnp.broadcast_to(extra[None], (quad,) + extra.shape)
    packed = jnp.concatenate([qk, v, extra], axis=-1)
    return jnp.pad(packed, ((0, 0), (0, plan.pad_rows - rows), (0, 0)))


def unpack_qkv(plan, packed):
    rows, quad, heads = plan.rows, plan.quad, plan.heads
    qk = packed[..., : 2 * plan.head_cols].reshape(quad, rows, heads, 2, HEAD_DIM)
    v = packed[..., 2 * plan.head_cols : plan.qkv_cols].reshape(quad, rows, heads, 1, HEAD_DIM)
    qkv = jnp.transpose(jnp.concatenate([qk, v], axis=3), (1, 3, 0, 2, 4))
    qkv = qkv.reshape(rows, 3, quad * heads, HEAD_DIM)[:, :, :HEADS]
    return qkv.reshape(rows, 3 * HEADS * HEAD_DIM)


def pack_in(plan, dense_in, expert_in):
    rows, own = plan.rows, plan.own_hidden
    both = jnp.concatenate([dense_in[:, None], expert_in], axis=1)
    both = both.reshape(rows, plan.branches, 2, plan.dp, HALVES, plan.quad, own)
    both = jnp.transpose(both, (3, 5, 2, 0, 1, 4, 6))
    both = both.reshape(plan.group, 2, rows, plan.hidden)
    pads = ((0, 0), (0, 0), (0, plan.pad_rows - rows), (0, plan.hidden_pad - plan.hidden))
    return jnp.pad(both, pads).reshape(plan.group, 2 * plan.pad_rows, plan.hidden_pad)


def unpack_in(plan, packed):
    rows, own = plan.rows, plan.own_hidden
    both = packed.reshape(plan.group, 2, plan.pad_rows, plan.hidden_pad)
    both = both[:, :, :rows, : plan.hidden]
    both = both.reshape(plan.dp, plan.quad, 2, rows, plan.branches, HALVES, own)
    both = jnp.transpose(both, (3, 4, 2, 0, 5, 1, 6))
    both = both.reshape(rows, plan.branches, 2 * FF).astype(F32)
    return both[:, 0], both[:, 1:]


def shards(
    tokens,
    lengths,
    routes,
    cotangent,
    attn_gain,
    attn_in,
    attn_out,
    ffn_gain,
    router,
    dense_in,
    dense_out,
    expert_in,
    expert_out,
):
    micro, seqs, block, width = tokens.shape
    experts = expert_in.shape[1]
    plan = Plan(lax.axis_size("dp"), lax.axis_size("ctx"), block, width, experts)
    assert micro == HALVES and seqs == 1 and plan.ctx % 4 == 0 and plan.dp % 2 == 0
    quad, local = plan.quad, plan.local
    dp, ctx = place()
    half, member = lax.div(ctx, quad), lax.rem(ctx, quad)
    across = [(i, (i + quad) % plan.ctx) for i in range(plan.ctx)]

    def swap(value):
        return lax.ppermute(value, "ctx", across)

    def pick_mine(value):
        return lax.dynamic_index_in_dim(value, half, 0, keepdims=False)

    def pick_far(value):
        return lax.dynamic_index_in_dim(value, 1 - half, 0, keepdims=False)

    slot = ctx * block + jnp.arange(block, dtype=jnp.int32)
    valid = (slot[None] < lengths).astype(BF16)
    grad_all = cotangent[:, 0] * valid[..., None]
    tail = round_up(plan.rows + 2, 16)
    route_rows = jnp.transpose(routes[:, 0], (0, 2, 1)).astype(BF16)
    route_rows = jnp.pad(route_rows, ((0, 0), (0, tail - plan.rows - 2), (0, width - block)))
    length = pick_mine(lengths)
    out_own = jnp.concatenate([dense_out[:, None], expert_out], axis=1)
    out_own = jnp.transpose(out_own, (1, 0, 2))
    out_far = swap(out_own)
    gyw = jnp.concatenate(
        [grad_all, jnp.broadcast_to(attn_out, (2,) + attn_out.shape), route_rows], axis=1
    )

    cosine, sine = (jnp.asarray(table) for table in rope_tables(plan))
    xs, w_seq, normed_seq, qk, v, lse, mixed, gy, w_in = front(
        plan,
        length,
        tokens[:, 0],
        pack_qkv(plan, attn_in, attn_gain, ffn_gain, router),
        pack_in(plan, dense_in, expert_in),
        gyw,
        cosine,
        sine,
        1,
    )
    x_seq = xs.reshape(plan.slots, width)
    extra = w_seq[:, plan.qkv_cols :]
    gain_one = extra[:, 0].astype(F32)[None]
    gain_two = extra[:, 1].astype(F32)[None]
    w_route = extra[:, 2 : 2 + experts]
    mixed = jnp.transpose(mixed, (1, 2, 0, 3)).reshape(local, quad * plan.head_cols)[:, :width]
    w_mix = gy[:, :, block : block + plan.rows].reshape(plan.dp, quad, 2, plan.rows, width)
    w_mix = by_half(half, w_mix[:, :, 0], w_mix[:, :, 1], 1).reshape(width, width)

    x = jnp.stack(
        [
            lax.dynamic_index_in_dim(xs, ctx, 0, keepdims=False),
            lax.dynamic_index_in_dim(xs, (1 - half) * quad + member, 0, keepdims=False),
        ]
    )
    x = x.reshape(local, width).astype(F32)
    middle = x + nn(mixed, w_mix)
    inverse_two = lax.rsqrt(jnp.mean(middle * middle, axis=-1, keepdims=True) + EPSILON)
    normed_two = (middle * inverse_two * gain_two).astype(BF16)
    own = lax.dynamic_index_in_dim(gy, grid_block(plan, dp, ctx), 0, keepdims=False)
    grad_y = own[:, :block].reshape(local, width)
    route_local = own[:, block + plan.rows : block + plan.rows + 2, :block]
    route_local = jnp.transpose(route_local, (0, 2, 1)).reshape(local, 2)
    logits = nn(normed_two, w_route)
    choose = (route_local[..., None] == jnp.arange(experts, dtype=BF16)).astype(F32)
    picked = jnp.sum(choose * logits[:, None, :], axis=-1)
    gates = jax.nn.softmax(picked, axis=-1)
    mixing = jnp.sum(gates[..., None] * choose, axis=1)
    mixing_t = mixing.T
    mixing_high = mixing_t.astype(BF16)
    mixing_low = (mixing_t - mixing_high.astype(F32)).astype(BF16)
    mix_rows = jnp.concatenate(
        [
            mixing_high,
            mixing_low,
            jnp.ones((1, local), BF16),
            jnp.zeros((MIX_ROWS - 2 * experts - 1, local), BF16),
        ]
    )
    mix_rows = jnp.pad(mix_rows, ((0, 0), (0, width - local)))
    n2x = jnp.concatenate([normed_two, mix_rows])
    w_out = by_half(half, out_own, out_far, 1).reshape(plan.hidden, width)
    w_out = jnp.pad(w_out, ((0, plan.hidden_pad - plan.hidden), (0, 0)))
    if plan.dp == 4 and quad == 4:
        n2g_sum, dw_in, dw_out, out_part = fused(plan, n2x, gy, w_in, w_out, pick_table(plan), 3)
    else:
        n2x = gather(plan, n2x, 3)
        out_part, n2g_part, dw_in, dw_out = ffn(plan, n2x, gy, w_in, w_out, pick_table(plan))
        n2g_sum = reduce(plan, n2g_part, 5)
        out_part = reduce(plan, out_part, 7)

    normed_two_grad = n2g_sum[:local]
    mixing_grad = n2g_sum[local : local + experts, :local].T
    choice_grad = jnp.sum(choose * mixing_grad[:, None, :], axis=-1)
    pick_grad = gates * (choice_grad - jnp.sum(gates * choice_grad, axis=-1, keepdims=True))
    logit_grad = jnp.sum(pick_grad[..., None] * choose, axis=1).astype(BF16)
    router_grad = tn(normed_two, logit_grad)
    normed_two_grad = normed_two_grad + nt(logit_grad, w_route)
    gain_two_grad = jnp.sum(normed_two_grad * middle * inverse_two, axis=0)
    scaled = normed_two_grad * gain_two
    middle_grad = (
        grad_y.astype(F32)
        + inverse_two * scaled
        - middle * inverse_two**3 * jnp.mean(scaled * middle, axis=-1, keepdims=True)
    )
    attn_grad = middle_grad.astype(BF16)
    dw_mix = tn(mixed, attn_grad).astype(BF16).reshape(plan.dp, plan.ctx, plan.rows, width)
    mixed_grad = nt(attn_grad, w_mix).astype(BF16)
    mixed_grad = jnp.pad(mixed_grad, ((0, 0), (0, quad * plan.head_cols - width)))
    mixed_grad = mixed_grad.reshape(2, block, quad, plan.head_cols)
    first = plan.qkv_cols - (plan.wide - 128)
    small = jnp.concatenate([gain_two_grad[:, None], router_grad], axis=1)
    small = jnp.pad(small, ((0, 0), (first + 1, 127 - first - small.shape[1])))
    r_qkv, r_mix, r_in, activations, input_grad = back(
        plan,
        length,
        x_seq,
        w_seq,
        cosine,
        sine,
        normed_seq,
        qk,
        v,
        lse,
        jnp.transpose(mixed_grad, (2, 0, 1, 3)),
        dw_mix,
        small,
        dw_in.astype(BF16).reshape(plan.dp * HALVES, quad * plan.rows, 2 * plan.hidden_pad),
        out_part,
        middle,
        x,
        middle_grad,
        gain_one,
        4,
    )

    dw_out = dw_out[: plan.hidden].reshape(plan.branches, HALVES, plan.own_hidden, width)
    dw_out = jnp.moveaxis(dw_out, 1, 0)
    dw_out_away, _ = lax.optimization_barrier((pick_far(dw_out).astype(BF16), r_in))
    dw_out = pick_mine(dw_out) + swap(dw_out_away).astype(F32)
    r_qkv = r_qkv[:, : plan.rows].astype(F32).reshape(HALVES, quad, plan.rows, plan.wide)
    r_qkv = jnp.sum(r_qkv, axis=0)
    attn_in_grad = unpack_qkv(plan, r_qkv)
    small = jnp.sum(r_qkv[:, :, plan.qkv_cols :], axis=0)
    attn_out_grad = jnp.sum(r_mix.astype(F32), axis=0)
    dense_in_grad, expert_in_grad = unpack_in(plan, r_in)
    return (
        activations[:, None],
        input_grad[:, None],
        small[:, 0],
        attn_in_grad,
        attn_out_grad,
        small[:, 1],
        small[:, 2 : 2 + experts],
        dense_in_grad,
        dw_out[0],
        expert_in_grad,
        jnp.transpose(dw_out[1:], (1, 0, 2)),
    )


def solution(mesh):
    rows = P(("dp", "ctx"))
    matrix = P(("dp", "ctx"), None)
    cube = P(("dp", "ctx"), None, None)
    slots = P(None, "dp", "ctx", None)
    in_specs = (
        slots,
        P(None, "dp"),
        slots,
        slots,
        rows,
        matrix,
        matrix,
        rows,
        matrix,
        matrix,
        matrix,
        cube,
        cube,
    )
    out_specs = (
        slots,
        slots,
        rows,
        matrix,
        matrix,
        rows,
        matrix,
        matrix,
        matrix,
        cube,
        cube,
    )
    return jax.shard_map(shards, mesh=mesh, in_specs=in_specs, out_specs=out_specs, check_vma=False)
```

```python
import functools

import jax
import jax.numpy as jnp
import numpy as np
from jax import lax
from jax.experimental import pallas as pl
from jax.experimental.pallas import tpu as pltpu
from jax.sharding import PartitionSpec as P

HEADS = 12
HEAD_DIM = 64
FF = 2048
EPSILON = 1e-05
HALVES = 2
QUERY_ROWS = 256
MIX_ROWS = 16
MESH = pl.DeviceIdType.MESH
BF16 = jnp.bfloat16
F32 = jnp.float32


def round_up(value, step):
    return -(-value // step) * step


class Plan:
    def __init__(self, dp, ctx, block, width, experts):
        self.dp, self.ctx, self.block, self.width, self.experts = dp, ctx, block, width, experts
        self.quad = ctx // HALVES
        self.devices = dp * ctx
        self.group = dp * self.quad
        self.slots = ctx * block
        self.rows = width // self.devices
        self.pad_rows = round_up(self.rows, 8)
        self.heads = -(-HEADS // self.quad)
        self.head_cols = self.heads * HEAD_DIM
        self.qkv_cols = 3 * self.head_cols
        self.wide = round_up(self.qkv_cols + 2 + experts, 128)
        self.own_hidden = FF // self.devices
        self.branches = 1 + experts
        self.hidden = self.branches * HALVES * self.own_hidden
        self.hidden_pad = round_up(self.hidden, 128)
        self.local = HALVES * block
        self.tiled = (
            self.own_hidden == 64
            and self.rows % 8 == 0
            and self.quad == 4
            and self.heads == 3
            and self.wide == self.qkv_cols + 64
        )


def place():
    return lax.axis_index("dp"), lax.axis_index("ctx")


def params(collective_id=None, limit=60 * 1024 * 1024):
    if collective_id is None:
        return pltpu.CompilerParams(vmem_limit_bytes=limit)
    return pltpu.CompilerParams(
        vmem_limit_bytes=limit, collective_id=collective_id, has_side_effects=True
    )


def remote(src, dst, send_sem, recv_sem, device):
    return pltpu.make_async_remote_copy(
        src_ref=src,
        dst_ref=dst,
        send_sem=send_sem,
        recv_sem=recv_sem,
        device_id=device,
        device_id_type=MESH,
    )


def busy(microseconds):
    return pl.CostEstimate(
        flops=0, bytes_accessed=int(microseconds * 3.4e6), transcendentals=0
    )


def meet(devices):
    barrier = pltpu.get_barrier_semaphore()
    for device in devices:
        pl.semaphore_signal(barrier, inc=1, device_id=device, device_id_type=MESH)
    pl.semaphore_wait(barrier, len(devices))


def other_devices(plan, dp, ctx):
    flat = dp * plan.ctx + ctx
    result = []
    for step in range(1, plan.devices):
        target = lax.rem(flat + step, plan.devices)
        result.append((lax.div(target, plan.ctx), lax.rem(target, plan.ctx)))
    return result


def quad_members(plan, half, member):
    return [
        (half * plan.quad + lax.rem(member + step, plan.quad), lax.rem(member + step, plan.quad))
        for step in range(1, plan.quad)
    ]


VMEM = pl.BlockSpec(memory_space=pltpu.VMEM)
HBM = pl.BlockSpec(memory_space=pl.ANY)
DMA = pltpu.SemaphoreType.DMA


def half_members(plan, mine):
    return [lax.rem(mine + step, plan.group) for step in range(1, plan.group)]


class Grid:
    def __init__(self, plan):
        self.plan = plan
        self.sizes = {"y": plan.dp // 2, "high": plan.quad // 2, "low": 2}

    def here(self):
        dp, ctx = place()
        member = lax.rem(ctx, self.plan.quad)
        return {
            "core": lax.rem(dp, 2),
            "y": lax.div(dp, 2),
            "high": lax.div(member, 2),
            "low": lax.rem(member, 2),
            "half": lax.div(ctx, self.plan.quad),
        }

    def device(self, at):
        return (
            at["y"] * 2 + at["core"],
            at["half"] * self.plan.quad + at["high"] * 2 + at["low"],
        )

    def block(self, at):
        return (at["y"] * 2 + at["core"]) * self.plan.quad + at["high"] * 2 + at["low"]

    def moved(self, at, axis, step):
        result = dict(at)
        if axis == "core":
            result["core"] = 1 - at["core"]
        else:
            result[axis] = lax.rem(at[axis] + step, self.sizes[axis])
        return result

    def peers(self, at):
        result = [self.moved(at, "core", 1)]
        for axis, size in self.sizes.items():
            result += [self.moved(at, axis, step) for step in range(1, size)]
        return [self.device(peer) for peer in result]

    def slot(self, offsets):
        return (offsets["y"] * self.sizes["high"] + offsets["high"]) * 2 + offsets["low"]


GATHER_ORDERS = (("high", "low", "y"), ("high", "y", "low"))


class Gather:
    def __init__(self, grid, at, src, dst, send, recv, core_send, core_recv):
        self.grid, self.at, self.src, self.dst = grid, at, src, dst
        self.send, self.recv, self.core_send, self.core_recv = send, recv, core_send, core_recv

    def groups(self, order):
        sizes = self.grid.sizes
        levels = [[{"y": 0, "high": 0, "low": 0}], [], [], []]
        for level, axis in enumerate(order):
            base = [o for group in levels[: level + 1] for o in group]
            levels[level + 1] = [
                {**offsets, axis: step} for offsets in base for step in range(1, sizes[axis])
            ]
        return levels

    def absolute(self, offsets):
        where = dict(self.at)
        for axis, step in offsets.items():
            if step:
                where = self.grid.moved(where, axis, step)
        return where

    def run_level(self, order, level):
        grid, at = self.grid, self.at
        index = 0
        for current, group in enumerate(self.groups(order)):
            for offsets in group:
                if current == level:
                    block = grid.block(self.absolute(offsets))
                    if level:
                        remote(
                            self.src,
                            self.dst.at[block],
                            self.send.at[0],
                            self.recv.at[grid.slot(offsets)],
                            grid.device(at),
                        ).wait_recv()
                    source = self.dst.at[block] if level else self.src
                    remote(
                        source,
                        self.dst.at[block],
                        self.core_send.at[grid.slot(offsets)],
                        self.core_recv.at[grid.slot(offsets)],
                        grid.device(grid.moved(at, "core", 1)),
                    ).start()
                for axis in order[current:]:
                    for step in range(1, grid.sizes[axis]):
                        if current == level:
                            seen = {**offsets, axis: grid.sizes[axis] - step}
                            remote(
                                source,
                                self.dst.at[block],
                                self.send.at[index],
                                self.recv.at[grid.slot(seen)],
                                grid.device(grid.moved(at, axis, step)),
                            ).start()
                        index += 1

    def level(self, level):
        for color, order in enumerate(GATHER_ORDERS):
            pl.when(self.at["core"] == color)(functools.partial(self.run_level, order, level))

    def finish(self):
        plan, here = self.grid.plan, self.grid.device(self.at)

        def sent(order):
            for index in range(gather_sends(plan, order)):
                remote(self.src, self.dst.at[0], self.send.at[index], self.recv.at[0], here).wait_send()

        for color, order in enumerate(GATHER_ORDERS):
            pl.when(self.at["core"] == color)(functools.partial(sent, order))
        for slot in range(plan.group // 2):
            remote(
                self.src, self.dst.at[0], self.core_send.at[slot], self.core_recv.at[slot], here
            ).wait()


def gather_kernel(plan, src, dst, send, recv, core_send, core_recv):
    grid = Grid(plan)
    at = grid.here()
    meet(grid.peers(at))
    dst[pl.ds(grid.block(at), 1)] = src[...][None]
    blocks = Gather(grid, at, src, dst, send, recv, core_send, core_recv)
    for level in range(4):
        blocks.level(level)
    blocks.finish()


def gather_sems(plan):
    half = plan.group // 2
    count = max(gather_sends(plan, order) for order in GATHER_ORDERS)
    return [DMA((count,)), DMA((half,)), DMA((half,)), DMA((half,))]


def gather_sends(plan, order):
    sizes = Grid(plan).sizes
    held, total = 1, 0
    for axis in order:
        total += held * (sizes[axis] - 1)
        held *= sizes[axis]
    return total


def gather(plan, block, collective_id):
    return pl.pallas_call(
        functools.partial(gather_kernel, plan),
        out_shape=jax.ShapeDtypeStruct((plan.group,) + block.shape, block.dtype),
        in_specs=[VMEM],
        out_specs=VMEM,
        scratch_shapes=gather_sems(plan),
        compiler_params=params(collective_id),
        cost_estimate=busy(35),
        name="gather",
    )(block)


def reduce_kernel(plan, src, out, work, core_buf, bufs, load_sem, core_send, core_recv, send, recv):
    grid = Grid(plan)
    at = grid.here()
    zero = {"y": 0, "high": 0, "low": 0}
    meet(grid.peers(at))

    def run(order):
        levels = [[], [], [], []]
        held = [dict(zero)]
        levels[3] = [dict(zero)]
        for level in (2, 1, 0):
            axis = order[level]
            base = [o for later in levels[level + 1 :] for o in later]
            levels[level] = [
                {**offsets, axis: step} for offsets in base for step in range(1, grid.sizes[axis])
            ]
        del held

        def absolute(offsets):
            where = dict(at)
            for axis, step in offsets.items():
                if step:
                    where = grid.moved(where, axis, step)
            return where

        sequence = [o for group in levels for o in group]
        partner = grid.device(grid.moved(at, "core", 1))
        core_copies = []
        loads = []
        for offsets in sequence:
            where = absolute(offsets)
            slot = grid.slot(offsets)
            copy = remote(
                src.at[grid.block(grid.moved(where, "core", 1))],
                core_buf.at[slot],
                core_send.at[slot],
                core_recv.at[slot],
                partner,
            )
            copy.start()
            core_copies.append(copy)
            load = pltpu.make_async_copy(
                src.at[grid.block(where)], work.at[slot], load_sem.at[slot]
            )
            load.start()
            loads.append(load)
        arrived = {}
        sends = []
        index = 0
        position = 0
        for level in range(4):
            for offsets in levels[level]:
                slot = grid.slot(offsets)
                core_copies[position].wait_recv()
                loads[position].wait()
                position += 1
                total = work[slot].astype(F32) + core_buf[slot].astype(F32)
                for buffer in arrived.get(slot, ()):
                    remote(work.at[slot], bufs.at[buffer], send.at[0], recv.at[buffer], partner).wait_recv()
                    total = total + bufs[buffer].astype(F32)
                if level == 3:
                    out[...] = total.astype(out.dtype)
                    continue
                work[slot] = total.astype(BF16)
                axis = order[level]
                step = offsets[axis]
                copy = remote(
                    work.at[slot],
                    bufs.at[index],
                    send.at[index],
                    recv.at[index],
                    grid.device(grid.moved(at, axis, step)),
                )
                copy.start()
                sends.append(copy)
                landing = grid.slot({**offsets, axis: 0})
                arrived.setdefault(landing, []).append(index)
                index += 1
        for copy in sends:
            copy.wait_send()
        for copy in core_copies:
            copy.wait_send()

    for color, order in enumerate(GATHER_ORDERS):
        pl.when(at["core"] == color)(functools.partial(run, order[::-1]))


def reduce(plan, blocks, collective_id):
    half = plan.group // 2
    shape = blocks.shape[1:]
    count = max(gather_sends(plan, order) for order in GATHER_ORDERS)
    return pl.pallas_call(
        functools.partial(reduce_kernel, plan),
        out_shape=jax.ShapeDtypeStruct(shape, F32),
        in_specs=[HBM],
        out_specs=VMEM,
        scratch_shapes=[
            pltpu.VMEM((half,) + shape, BF16),
            pltpu.VMEM((half,) + shape, BF16),
            pltpu.VMEM((count,) + shape, BF16),
            DMA((half,)),
            DMA((half,)),
            DMA((half,)),
            DMA((count,)),
            DMA((count,)),
        ],
        compiler_params=params(collective_id),
        name="reduce",
    )(blocks)


def nt(left, right):
    return lax.dot_general(left, right, (((1,), (1,)), ((), ())), preferred_element_type=F32)


def nn(left, right):
    return lax.dot_general(left, right, (((1,), (0,)), ((), ())), preferred_element_type=F32)


def tn(left, right):
    return lax.dot_general(left, right, (((0,), (0,)), ((), ())), preferred_element_type=F32)


def swapped_halves(value):
    lane = lax.broadcasted_iota(jnp.int32, value.shape, 1)
    first = lax.rem(lane, HEAD_DIM) < HEAD_DIM // 2
    half = HEAD_DIM // 2
    return jnp.where(
        first, pltpu.roll(value, 2 * HEAD_DIM - half, 1), pltpu.roll(value, half, 1)
    )


def masked_scores(q, k, first_row, length):
    scores = nt(q, k)
    row = lax.broadcasted_iota(jnp.int32, scores.shape, 0) + first_row
    col = lax.broadcasted_iota(jnp.int32, scores.shape, 1)
    return jnp.where((col <= row) & (col < length), scores, -1000000000.0)


def natural_rows(plan, blocks):
    flat = blocks.astype(F32).reshape(plan.devices * plan.pad_rows, blocks.shape[-1])
    if plan.pad_rows == plan.rows:
        return flat.astype(BF16)
    row = lax.broadcasted_iota(jnp.int32, (plan.width, flat.shape[0]), 0)
    col = lax.broadcasted_iota(jnp.int32, (plan.width, flat.shape[0]), 1)
    source = lax.div(row, plan.rows) * plan.pad_rows + lax.rem(row, plan.rows)
    return nn((col == source).astype(BF16), flat.astype(BF16)).astype(BF16)


def around_gains(plan, w_seq):
    first = plan.qkv_cols - (plan.wide - 128)
    return jnp.transpose(w_seq[:, plan.wide - 128 :].astype(F32), (1, 0))[first : first + 8]


def chosen(local, routes):
    row = lax.broadcasted_iota(jnp.int32, (8, local), 0).astype(F32)
    return row - 2.0 == routes


def owner_forward(plan, ctx, far, half, xs, w_seq, mixed, gysrc, w_tail, n2x, middle, gates, w_mix):
    block, local, width, cols = plan.block, plan.local, plan.width, plan.head_cols
    rows = plan.quad * plan.rows

    @pl.loop(0, HALVES * plan.dp)
    def _(i):
        turn = lax.rem(lax.rem(i, HALVES) + half, 2)
        value = w_tail[pl.ds(lax.div(i, HALVES) * plan.quad, plan.quad), pl.ds(turn, 1)]
        value = value[:, 0].astype(F32)[:, : plan.rows].reshape(rows, width)
        w_mix[pl.ds(pl.multiple_of(i * rows, 16), rows)] = value.astype(BF16)

    total = jnp.concatenate([xs[pl.ds(ctx, 1)][0], xs[pl.ds(far, 1)][0]], axis=0).astype(F32)
    for member in range(plan.quad):
        total = total + nn(
            mixed[member].reshape(local, cols), w_mix[member * cols : (member + 1) * cols]
        )
    middle[...] = total
    inverse = lax.rsqrt(jnp.mean(total * total, axis=-1, keepdims=True) + EPSILON)
    normed = (total * inverse * around_gains(plan, w_seq)[1:2]).astype(BF16)
    n2x[:local] = normed
    first = plan.qkv_cols - (plan.wide - 128)
    logits = jnp.transpose(nn(normed, w_seq[:, plan.wide - 128 :]), (1, 0))[first : first + 8]
    tail = gysrc[:, block + 16 :, :block].astype(F32)
    routes = [
        jnp.concatenate([tail[i, plan.rows - 16 + k : plan.rows - 15 + k] for i in range(2)], axis=1)
        for k in range(2)
    ]
    picks = [chosen(local, route) for route in routes]
    scores = [jnp.sum(jnp.where(pick, logits, 0.0), axis=0, keepdims=True) for pick in picks]
    top = jnp.maximum(scores[0], scores[1])
    raised = [jnp.exp(score - top) for score in scores]
    gate = [value / (raised[0] + raised[1]) for value in raised]
    mixing = jnp.where(picks[0], gate[0], 0.0) + jnp.where(picks[1], gate[1], 0.0)
    high = mixing.astype(BF16).astype(F32)
    row = lax.broadcasted_iota(jnp.int32, (8, local), 0)
    mix_rows = jnp.concatenate([jnp.where(row == 0, 1.0, high), mixing - high], axis=0)
    n2x[local:] = jnp.concatenate(
        [mix_rows.astype(BF16), jnp.zeros((MIX_ROWS, width - local), BF16)], axis=1
    )
    gates[...] = jnp.concatenate(gate + routes + [jnp.zeros((4, local), F32)], axis=0)


def owner_back(plan, n2g_sum, gates, n2x, gysrc, w_mix, mixed, middle, w_seq, dmixed, dwo, rows8, middle_grad):
    block, local, width, cols = plan.block, plan.local, plan.width, plan.head_cols
    around = around_gains(plan, w_seq)
    choice = n2g_sum[local : local + 8, :local]
    picks = [chosen(local, gates[2 + k : 3 + k]) for k in range(2)]
    gate = [gates[k : k + 1] for k in range(2)]
    taken = [jnp.sum(jnp.where(pick, choice, 0.0), axis=0, keepdims=True) for pick in picks]
    inner = gate[0] * taken[0] + gate[1] * taken[1]
    logit_grad = sum(
        jnp.where(picks[k], gate[k] * (taken[k] - inner), 0.0) for k in range(2)
    ).astype(BF16)
    router_grad = nn(logit_grad, n2x[:local])
    grad = n2g_sum[:local] + tn(logit_grad, around.astype(BF16))
    values = middle[...]
    inverse = lax.rsqrt(jnp.mean(values * values, axis=-1, keepdims=True) + EPSILON)
    gain_grad = jnp.sum(grad * values * inverse, axis=0, keepdims=True)
    row = lax.broadcasted_iota(jnp.int32, (8, width), 0)
    rows8[...] = jnp.where(row == 1, gain_grad, router_grad)
    scaled = grad * around[1:2]
    result = (
        gysrc[:, :block].reshape(local, width).astype(F32)
        + inverse * scaled
        - values * inverse * inverse * inverse * jnp.mean(scaled * values, axis=-1, keepdims=True)
    )
    middle_grad[...] = result
    upstream = result.astype(BF16)
    for member in range(plan.quad):
        part = nt(upstream, w_mix[member * cols : (member + 1) * cols])
        dmixed[member] = part.astype(BF16).reshape(2, block, cols)
    return upstream


def front_kernel(plan, length_ref, tok, wq, win, gyw, cosine, sine, xs, w_seq, normed, qk_out, v_out, lse_out, mixed, gyall, w_in, gysrc, *rest):
    owned, rest = (rest[:4], rest[4:]) if plan.tiled else ((), rest)
    front_body(plan, length_ref, tok, wq, win, gyw, cosine, sine, xs, w_seq, normed, qk_out, v_out, lse_out, mixed, gyall, w_in, gysrc, owned, *rest)


def front_body(plan, length_ref, tok, wq, win, gyw, cosine, sine, xs, w_seq, normed, qk_out, v_out, lse_out, mixed, gyall, w_in, gysrc, owned, wall, wqx, win_all, qkv, made, w_tail, x_send, x_recv, s_send, s_recv, q_send, q_recv, f_send, f_recv, z_send, z_recv, own_sem, tail_sem, m_send, m_recv, *gather_sem):
    dp, ctx = place()
    half, member = lax.div(ctx, plan.quad), lax.rem(ctx, plan.quad)
    far = (1 - half) * plan.quad + member
    flat, flat_far = dp * plan.ctx + ctx, dp * plan.ctx + far
    mine = dp * plan.quad + member
    grid = Grid(plan)
    spot = grid.here()
    here = (dp, ctx)
    across = (dp, far)
    targets = half_members(plan, mine)
    devices = [
        (lax.div(target, plan.quad), half * plan.quad + lax.rem(target, plan.quad))
        for target in targets
    ]
    members = quad_members(plan, half, member)
    highs, ys = grid.sizes["high"], grid.sizes["y"]
    meet(devices + [across])
    pending = []

    def send(*args):
        copy = remote(*args)
        copy.start()
        pending.append(copy)

    swap_x = remote(tok.at[1 - half], xs.at[ctx], s_send.at[0], s_recv.at[0], across)
    swap_w = remote(wq, wqx, s_send.at[1], s_recv.at[1], across)
    swap_gy = remote(gyw.at[1 - half], gysrc.at[1], s_send.at[2], s_recv.at[2], across)
    swap_x.start()
    swap_w.start()

    def member_of(high, low):
        return half * plan.quad + lax.rem(spot["high"] + high, highs) * 2 + lax.rem(spot["low"] + low, 2)

    def token_block(side, high):
        at = half if side == 0 else 1 - half
        return at * plan.quad + lax.rem(spot["high"] + high, highs) * 2 + spot["low"]

    def token_sends(side, source):
        block = token_block(side, 0)
        for step in range(1, highs):
            index = side * (highs - 1) + step - 1
            send(source, xs.at[block], x_send.at[0, index], x_recv.at[0, side, highs - step - 1], (dp, member_of(step, 0)))
        send(source, xs.at[block], x_send.at[1, side * highs], x_recv.at[1, side, 0], (dp, member_of(0, 1)))

    def token_forward(side):
        for high in range(1, highs):
            block = token_block(side, high)
            remote(xs.at[block], xs.at[block], x_send.at[0, 0], x_recv.at[0, side, high - 1], here).wait_recv()
            send(xs.at[block], xs.at[block], x_send.at[1, side * highs + high], x_recv.at[1, side, high], (dp, member_of(0, 1)))

    def slice_sends(side, source, block):
        for i, (peer, to) in enumerate(members):
            send(source.at[to], wall.at[block], q_send.at[0, side, i], q_recv.at[block], (dp, peer))

    core_device = grid.device(grid.moved(spot, "core", 1))
    counter = [0, 0]

    def slice_on(block, source, along_y):
        if along_y:
            for step in range(1, ys):
                send(source, wall.at[block], q_send.at[1, 0, counter[0]], q_recv.at[block], grid.device(grid.moved(spot, "y", step)))
                counter[0] += 1
        send(source, wall.at[block], q_send.at[1, 1, counter[1]], q_recv.at[block], core_device)
        counter[1] += 1

    def slice_wait(block):
        remote(wq.at[0], wall.at[block], q_send.at[0, 0, 0], q_recv.at[block], here).wait_recv()

    token_sends(0, tok.at[half])
    slice_sends(0, wq, flat)
    slice_on(flat, wq.at[member], True)
    gysrc[0] = gyw[pl.ds(half, 1)][0]
    xs[pl.ds(ctx, 1)] = tok[pl.ds(half, 1)]
    wall[pl.ds(flat, 1)] = wq[pl.ds(member, 1)]
    swap_x.wait()
    token_sends(1, xs.at[far])
    swap_w.wait()
    slice_sends(1, wqx, flat_far)
    slice_on(flat_far, wqx.at[member], True)
    swap_gy.start()
    token_forward(0)
    for i, (peer, _) in enumerate(members):
        block = dp * plan.ctx + peer
        slice_wait(block)
        slice_on(block, wall.at[block], True)
    token_forward(1)
    for _, to in members:
        block = dp * plan.ctx + (1 - half) * plan.quad + to
        slice_wait(block)
        slice_on(block, wall.at[block], True)
    wall[pl.ds(flat_far, 1)] = wqx[pl.ds(member, 1)]

    for i, (target, device) in enumerate(zip(targets, devices)):
        send(win.at[target], win_all.at[flat], f_send.at[i], f_recv.at[i], device)
    send(win.at[mine], win_all.at[flat], z_send.at[0], z_recv.at[0], across)
    win_all[pl.ds(flat, 1)] = win[pl.ds(mine, 1)]

    def columns_on(i):
        source = lax.rem(mine + plan.group - 1 - i, plan.group)
        block = lax.div(source, plan.quad) * plan.ctx + half * plan.quad + lax.rem(source, plan.quad)
        remote(win.at[0], win_all.at[block], f_send.at[0], f_recv.at[i], here).wait_recv()
        send(win_all.at[block], win_all.at[block], z_send.at[1 + i], z_recv.at[1 + i], across)

    for step in range(1, ys):
        other = lax.rem(spot["y"] + step, ys) * 2 + spot["core"]
        for place_ctx in range(plan.ctx):
            block = other * plan.ctx + place_ctx
            slice_wait(block)
            slice_on(block, wall.at[block], False)
    swap_gy.wait()
    gather = Gather(grid, spot, gysrc, gyall, *gather_sem)
    own = pltpu.make_async_copy(gysrc, gyall.at[grid.block(spot)], own_sem)
    own.start()
    gather.level(0)
    for y in range(ys):
        for place_ctx in range(plan.ctx):
            slice_wait((y * 2 + 1 - spot["core"]) * plan.ctx + place_ctx)
    for side in range(2):
        for high in range(highs):
            block = half if side == 0 else 1 - half
            block = block * plan.quad + lax.rem(spot["high"] + high, highs) * 2 + 1 - spot["low"]
            remote(xs.at[block], xs.at[block], x_send.at[0, 0], x_recv.at[1, side, high], here).wait_recv()

    length = length_ref[0]
    rows, block = QUERY_ROWS, plan.block
    slots = plan.slots
    w_seq[...] = natural_rows(plan, wall[...])
    tail = w_seq[:, plan.wide - 128 :].astype(F32)
    gain = jnp.transpose(tail, (1, 0))[plan.qkv_cols - plan.wide + 128 :][:1]
    for start in range(0, slots, rows):
        at = slice(start, start + rows)
        values = xs[start // block : (start + rows) // block].reshape(rows, plan.width).astype(F32)
        inverse = lax.rsqrt(jnp.mean(values * values, axis=-1, keepdims=True) + EPSILON)
        normed[at] = (values * inverse * gain).astype(BF16)
        qkv[at] = nn(normed[at], w_seq[...])
    heads = plan.heads
    qk_width = 2 * HEAD_DIM
    third = (plan.group - 1) // 3
    for i in range(third):
        columns_on(i)
    for head in range(heads):
        cols = slice(head * qk_width, (head + 1) * qk_width)
        qk = qkv[:, cols]
        qk_out[:, cols] = (qk * cosine[...] + swapped_halves(qk) * sine[...]).astype(BF16)
    v_cols = slice(heads * qk_width, heads * 3 * HEAD_DIM)
    v_out[...] = qkv[:, v_cols].astype(BF16)
    gather.level(1)
    for i in range(third, 2 * third):
        columns_on(i)

    def mixed_copy(index):
        side, to = divmod(index, plan.quad)
        turn = lax.rem(half + side, 2)
        return remote(
            made.at[index],
            mixed.at[member, turn],
            m_send.at[index],
            m_recv.at[member, turn],
            (dp, half * plan.quad + to),
        )

    spans = list(range(0, slots, rows))
    for number, start in enumerate(spans):
        at = slice(start, start + rows)
        end = start + rows
        for head in range(heads):
            base = head * qk_width
            q = qk_out[at, base : base + HEAD_DIM] * BF16(0.125)
            k = qk_out[:end, base + HEAD_DIM : base + qk_width]
            v = v_out[:end, head * HEAD_DIM : (head + 1) * HEAD_DIM]
            scores = masked_scores(q, k, start, length)
            top = jnp.max(scores, axis=-1, keepdims=True)
            raised = jnp.exp(scores - top)
            total = jnp.sum(raised, axis=-1, keepdims=True)
            lse_out[head, at] = top + jnp.log(total)
            probs = (raised * (1.0 / total)).astype(BF16)
            part = nn(probs, v).astype(BF16)
            for i in range(rows // block):
                made[start // block + i, :, head * HEAD_DIM : (head + 1) * HEAD_DIM] = part[
                    i * block : (i + 1) * block
                ]
        for i in range(rows // block):
            index = start // block + i
            pl.when(member != index % plan.quad)(lambda index=index: mixed_copy(index).start())

            @pl.when(member == index % plan.quad)
            def _(index=index):
                turn = lax.rem(half + index // plan.quad, 2)
                mixed[pl.ds(member, 1), pl.ds(turn, 1)] = made[index][None, None]

        if number == len(spans) // 2:
            for i in range(2 * third, plan.group - 1):
                columns_on(i)
            gather.level(2)
    gather.level(3)
    for index in range(plan.ctx):
        pl.when(member != index % plan.quad)(lambda index=index: mixed_copy(index).wait_send())
    for source in range(plan.quad):

        @pl.when(member != source)
        def _(source=source):
            for turn in range(2):
                remote(
                    made.at[0], mixed.at[source, turn], m_send.at[0], m_recv.at[source, turn], here
                ).wait_recv()

    gather.finish()
    own.wait()
    if owned:
        load = pltpu.make_async_copy(gyall.at[:, :, plan.block :], w_tail, tail_sem)
        load.start()
        load.wait()
        owner_forward(plan, ctx, far, half, xs, w_seq, mixed, gysrc, w_tail, *owned)
    for copy in pending:
        copy.wait_send()
    for i in range(plan.group):
        remote(win.at[0], win_all.at[0], z_send.at[0], z_recv.at[i], here).wait_recv()
    pad, hidden = plan.pad_rows, plan.hidden_pad
    w_in[:, :hidden] = natural_rows(plan, win_all[:, :pad])
    w_in[:, hidden:] = natural_rows(plan, win_all[:, pad:])


def front(plan, length, tok, wq, win, gyw, cosine, sine, collective_id):
    slots, heads, block, width = plan.slots, plan.heads, plan.block, plan.width
    highs, ys = plan.quad // 2, plan.dp // 2
    owned = (
        jax.ShapeDtypeStruct((plan.local + MIX_ROWS, width), BF16),
        jax.ShapeDtypeStruct((plan.local, width), F32),
        jax.ShapeDtypeStruct((8, plan.local), F32),
        jax.ShapeDtypeStruct((width, width), BF16),
    )
    on = max(2 * plan.quad * max(ys - 1, 1), 2 * plan.quad + (ys - 1) * plan.ctx, plan.quad)
    return pl.pallas_call(
        functools.partial(front_kernel, plan),
        out_shape=(
            jax.ShapeDtypeStruct((plan.ctx, block, width), BF16),
            jax.ShapeDtypeStruct((width, plan.wide), BF16),
            jax.ShapeDtypeStruct((slots, width), BF16),
            jax.ShapeDtypeStruct((slots, 2 * plan.head_cols), BF16),
            jax.ShapeDtypeStruct((slots, plan.head_cols), BF16),
            jax.ShapeDtypeStruct((heads, slots, 1), F32),
            jax.ShapeDtypeStruct((plan.quad, 2, block, plan.head_cols), BF16),
            jax.ShapeDtypeStruct((plan.group, 2) + gyw.shape[1:], BF16),
            jax.ShapeDtypeStruct((width, 2 * plan.hidden_pad), BF16),
            jax.ShapeDtypeStruct(gyw.shape, BF16),
        )
        + (owned if plan.tiled else ()),
        in_specs=[pl.BlockSpec(memory_space=pltpu.SMEM)] + [VMEM] * 6,
        out_specs=(VMEM,) * 7 + (HBM,) + (VMEM,) * (6 if plan.tiled else 2),
        scratch_shapes=[
            pltpu.VMEM((plan.devices,) + wq.shape[1:], BF16),
            pltpu.VMEM(wq.shape, BF16),
            pltpu.VMEM((plan.devices,) + win.shape[1:], BF16),
            pltpu.VMEM((slots, plan.wide), F32),
            pltpu.VMEM((plan.ctx, block, plan.head_cols), BF16),
            pltpu.VMEM((plan.group, 2, gyw.shape[1] - block, width), BF16),
            DMA((2, 2 * highs)),
            DMA((2, 2, highs)),
            DMA((3,)),
            DMA((3,)),
            DMA((2, 2, on)),
            DMA((plan.devices,)),
            DMA((plan.group - 1,)),
            DMA((plan.group - 1,)),
            DMA((plan.group,)),
            DMA((plan.group,)),
            DMA,
            DMA,
            DMA((plan.ctx,)),
            DMA((plan.quad, 2)),
        ]
        + gather_sems(plan),
        compiler_params=params(collective_id),
        cost_estimate=busy(90),
        name="front",
    )(length, tok, wq, win, gyw, cosine, sine)


OUT_ORDERS = (("low", "y", "high"), ("y", "low", "high"))


class OutSum:
    def __init__(self, grid, at, src, work, core_buf, bufs, load_sem, core_send, core_recv, send, recv):
        self.grid, self.at, self.src = grid, at, src
        self.work, self.core_buf, self.bufs = work, core_buf, bufs
        self.load_sem, self.core_send, self.core_recv = load_sem, core_send, core_recv
        self.send, self.recv = send, recv
        self.loaded = set()
        rows = work.shape[1] // 2
        self.rows = [slice(0, rows), slice(rows, 2 * rows)]
        self.index = [
            {o: i for i, o in enumerate(o for o in STEP_ORDER if any(o))} for _ in OUT_ORDERS
        ]

    def pair(self, offset):
        where = dict(self.at)
        for axis, step in named(offset).items():
            if step:
                where = self.grid.moved(where, axis, step)
        slot = self.grid.slot(named(offset))
        partner = self.grid.device(self.grid.moved(self.at, "core", 1))
        away = remote(
            self.src.at[self.grid.block(self.grid.moved(where, "core", 1))],
            self.core_buf.at[slot],
            self.core_send.at[slot],
            self.core_recv.at[slot],
            partner,
        )
        load = pltpu.make_async_copy(
            self.src.at[self.grid.block(where)], self.work.at[slot], self.load_sem.at[slot]
        )
        return away, load

    def start(self):
        for offset in STEP_ORDER[::-1]:
            for copy in self.pair(offset):
                copy.start()

    def onward(self, part, offset, axis):
        index, rows = self.index[part][offset], self.rows[part]
        return remote(
            self.work.at[self.grid.slot(named(offset)), rows],
            self.bufs.at[index, rows],
            self.send.at[part, index],
            self.recv.at[part, index],
            self.grid.device(self.grid.moved(self.at, axis, 1)),
        )

    def phase(self, number):
        for offset in STEP_ORDER:
            for part, order in enumerate(OUT_ORDERS):
                phase, feeds = feeds_of(order, offset)
                if phase != number:
                    continue
                if offset not in self.loaded:
                    self.loaded.add(offset)
                    for copy in self.pair(offset):
                        copy.wait()
                for feed, axis in zip(feeds, order):
                    self.onward(part, feed, axis).wait_recv()
                slot, rows = self.grid.slot(named(offset)), self.rows[part]

                @pl.loop(0, (rows.stop - rows.start) // 16)
                def _(i, slot=slot, part=part, feeds=feeds, start=rows.start):
                    span = pl.ds(pl.multiple_of(start + i * 16, 16), 16)
                    value = self.work[slot, span].astype(F32)
                    value = value + self.core_buf[slot, span].astype(F32)
                    for feed in feeds:
                        value = value + self.bufs[self.index[part][feed], span].astype(F32)
                    self.work[slot, span] = value.astype(BF16)

                if number < 3:
                    self.onward(part, offset, order[number]).start()

    def finish(self):
        for offset in STEP_ORDER:
            for part, order in enumerate(OUT_ORDERS):
                phase, _ = feeds_of(order, offset)
                if phase < 3:
                    self.onward(part, offset, order[phase]).wait_send()


class Fold:
    def __init__(self, plan, src, dst, core_buf, y_buf, added, sems):
        self.plan, self.src, self.dst = plan, src, dst
        self.core_buf, self.y_buf, self.added = core_buf, y_buf, added
        self.core_send, self.core_recv, self.y_send, self.y_recv, self.send, self.recv = sems
        self.dp, self.ctx = place()
        self.core, self.y = lax.rem(self.dp, 2), lax.div(self.dp, 2)
        self.ys = plan.dp // 2

    def core_copies(self):
        partner = (self.dp + 1 - 2 * self.core, self.ctx)
        return [
            remote(
                self.src.at[y * 2 + 1 - self.core],
                self.core_buf.at[y],
                self.core_send.at[y],
                self.core_recv.at[y],
                partner,
            )
            for y in range(self.ys)
        ]

    def y_copies(self):
        copies = []
        for step in range(1, self.ys):
            to = lax.rem(self.y + step, self.ys)
            copies.append(
                remote(
                    self.core_buf.at[to],
                    self.y_buf.at[step - 1],
                    self.y_send.at[step - 1],
                    self.y_recv.at[step - 1],
                    (to * 2 + self.core, self.ctx),
                )
            )
        return copies

    def owner_copies(self):
        copies = []
        for step in range(1, self.plan.ctx):
            to = lax.rem(self.ctx + step, self.plan.ctx)
            copies.append(
                remote(
                    self.added.at[to],
                    self.dst.at[self.ctx],
                    self.send.at[step - 1],
                    self.recv.at[step - 1],
                    (self.dp, to),
                )
            )
        return copies

    def start(self):
        for copy in self.core_copies():
            copy.start()

    def along_y(self):
        for copy in self.core_copies():
            copy.wait()
        for y in range(self.ys):
            mine = self.src[y * 2 + self.core].astype(F32)
            self.core_buf[y] = (mine + self.core_buf[y].astype(F32)).astype(BF16)
        for copy in self.y_copies():
            copy.start()

    def to_owners(self):
        for copy in self.y_copies():
            copy.wait()
        total = self.core_buf[self.y].astype(F32)
        for step in range(1, self.ys):
            total = total + self.y_buf[step - 1].astype(F32)
        self.added[...] = total.astype(BF16)
        for copy in self.owner_copies():
            copy.start()
        self.dst[pl.ds(self.ctx, 1)] = self.added[pl.ds(self.ctx, 1)]

    def finish(self):
        for copy in self.owner_copies():
            copy.wait()


def padded_rows(plan, value, count):
    if plan.pad_rows != plan.rows:
        row = lax.broadcasted_iota(jnp.int32, (count * plan.pad_rows, count * plan.rows), 0)
        col = lax.broadcasted_iota(jnp.int32, (count * plan.pad_rows, count * plan.rows), 1)
        inside = lax.rem(row, plan.pad_rows)
        wanted = lax.div(row, plan.pad_rows) * plan.rows + inside
        hit = (col == wanted) & (inside < plan.rows)
        value = nn(hit.astype(BF16), value.astype(BF16))
    return value.reshape(count, plan.pad_rows, value.shape[-1])


def fold_scratch(plan, rows, width):
    shape = (plan.ctx, rows, width)
    ys = plan.dp // 2
    return [
        pltpu.VMEM((ys,) + shape, BF16),
        pltpu.VMEM((max(ys - 1, 1),) + shape, BF16),
        pltpu.VMEM(shape, BF16),
        DMA((ys,)),
        DMA((ys,)),
        DMA((max(ys - 1, 1),)),
        DMA((max(ys - 1, 1),)),
        DMA((plan.ctx - 1,)),
        DMA((plan.ctx - 1,)),
    ]


def back_kernel(plan, summed, length_ref, x, w, cosine, sine, normed, qk_in, v_in, lse, dw_in, dw_out, out_part, middle, *rest):
    given = 6 if plan.tiled else 4
    back_body(plan, summed, length_ref, x, w, cosine, sine, normed, qk_in, v_in, lse, dw_in, dw_out, out_part, middle, rest[:given], *rest[given:])


def back_body(plan, summed, length_ref, x, w, cosine, sine, normed, qk_in, v_in, lse, dw_in, dw_out, out_part, middle, given, rwq, rwo, rwin, far_out, act_out, grad_out, dqkv, dk_acc, dv_acc, upstream_all, dnp, rdn, dwq, far_in, dealt, out_away, grad_away, act_away, d_send, d_recv, n_send, n_recv, w_send, w_recv, e_send, e_recv, s_send, s_recv, *refs):
    dp, ctx = place()
    core, y = lax.rem(dp, 2), lax.div(dp, 2)
    half, member = lax.div(ctx, plan.quad), lax.rem(ctx, plan.quad)
    far = (1 - half) * plan.quad + member
    mine = dp * plan.quad + member
    across = (dp, far)
    members = quad_members(plan, half, member)
    targets = half_members(plan, mine)
    devices = [
        (lax.div(target, plan.quad), half * plan.quad + lax.rem(target, plan.quad))
        for target in targets
    ]
    meet(
        devices
        + [across]
        + [
            (dp, (1 - half) * plan.quad + lax.rem(member + step, plan.quad))
            for step in range(1, plan.quad)
        ]
    )
    fold_refs, out_refs = refs[:18], refs[18:]
    out_sum = None
    if not summed:
        grid = Grid(plan)
        out_sum = OutSum(grid, grid.here(), out_part, *out_refs[:8])
        out_sum.start()
    if plan.tiled:
        n2g_sum, gates, n2x, gysrc, w_mix, mixed = given
        dmixed, dwo, rows8, middle_grad = out_refs[8:]
        attn_grad = owner_back(plan, n2g_sum, gates, n2x, gysrc, w_mix, mixed, middle, w, *out_refs[8:])
    else:
        dmixed, dwo, small, middle_grad = given
    arriving = []
    for i, (peer, to) in enumerate(members):
        for j, at in enumerate((ctx, far)):
            copy = remote(
                dmixed.at[to, j],
                upstream_all.at[at],
                d_send.at[2 * i + j],
                d_recv.at[2 * i + j],
                (dp, peer),
            )
            copy.start()
            arriving.append(copy)
    count = len(fold_refs) // 2
    mix_fold = Fold(plan, dwo, rwo, *fold_refs[:3], fold_refs[3:count])
    qkv_fold = Fold(plan, dwq, rwq, *fold_refs[count : count + 3], fold_refs[count + 3 :])
    if plan.tiled:
        for i in range(plan.quad):
            part = tn(mixed[i].reshape(plan.local, plan.head_cols), attn_grad)
            dwo[i] = padded_rows(plan, part, plan.ctx).astype(BF16)
    mix_fold.start()
    swaps = [
        remote(dw_in.at[2 * i + 1 - half], far_in.at[i], w_send.at[i], w_recv.at[i], across)
        for i in range(plan.dp)
    ]
    hidden, pad = plan.hidden_pad, plan.pad_rows

    def deal_copy(target):
        tdp, tmember = divmod(target, plan.quad)
        return remote(
            dealt.at[target],
            rwin.at[mine],
            e_send.at[target],
            e_recv.at[mine],
            (tdp, half * plan.quad + tmember),
        )

    def deal(i):
        swaps[i].wait()
        value = dw_in[pl.ds(2 * i + half, 1)][0].astype(F32) + far_in[i].astype(F32)
        value = padded_rows(plan, value, plan.quad)
        value = jnp.concatenate([value[:, :, :hidden], value[:, :, hidden:]], axis=1)
        dealt[i * plan.quad : (i + 1) * plan.quad] = value.astype(BF16)
        for target in range(i * plan.quad, (i + 1) * plan.quad):
            pl.when(mine != target)(lambda target=target: deal_copy(target).start())

            @pl.when(mine == target)
            def _(target=target):
                rwin[target] = dealt[target]

    swaps[0].start()
    out_away[...] = dw_out[:, pl.ds(1 - half, 1)][:, 0].astype(BF16)
    swap_out = remote(out_away, far_out, s_send.at[2], s_recv.at[2], across)
    upstream_all[pl.ds(ctx, 1)] = dmixed[pl.ds(member, 1), 0]
    upstream_all[pl.ds(far, 1)] = dmixed[pl.ds(member, 1), 1]
    length = length_ref[0]
    rows, slots, heads, block = QUERY_ROWS, plan.slots, plan.heads, plan.block
    qk_width = 2 * HEAD_DIM
    dqkv[...] = jnp.zeros_like(dqkv)
    for copy in arriving:
        copy.wait()

    def token_copy(index):
        side, to = divmod(index, plan.quad)
        turn = lax.rem(half + side, 2)
        return remote(
            dnp.at[index],
            rdn.at[member, turn],
            n_send.at[index],
            n_recv.at[member, turn],
            (dp, half * plan.quad + to),
        )

    gains = jnp.zeros((1, plan.width), F32)
    spans = list(range(slots - rows, -1, -rows))
    for number, start in enumerate(spans):
        at = slice(start, start + rows)
        end = start + rows
        for head in range(heads):
            base = head * qk_width
            v_cols = slice(head * HEAD_DIM, (head + 1) * HEAD_DIM)
            q = qk_in[at, base : base + HEAD_DIM] * BF16(0.125)
            k = qk_in[:end, base + HEAD_DIM : base + qk_width]
            v = v_in[:end, v_cols]
            upstream = jnp.concatenate(
                [upstream_all[start // block + i, :, v_cols] for i in range(rows // block)], axis=0
            )
            probs = jnp.exp(masked_scores(q, k, start, length) - lse[head, at])
            dv = tn(probs.astype(BF16), upstream)
            prob_grad = nt(upstream, v)
            inner = jnp.sum(probs * prob_grad, axis=-1, keepdims=True)
            score_grad = (probs * (prob_grad - inner)).astype(BF16)
            dq = nn(score_grad, k) * 0.125
            dk = tn(score_grad, q)
            if end == slots:
                dk_acc[head] = dk
                dv_acc[head] = dv
            else:
                dk_acc[head, :end] += dk
                dv_acc[head, :end] += dv
            dqk = jnp.concatenate([dq, dk_acc[head, at]], axis=-1)
            dqkv[at, base : base + qk_width] = (
                dqk * cosine[at] - swapped_halves(dqk) * sine[at]
            ).astype(BF16)
            v_base = heads * qk_width + head * HEAD_DIM
            dqkv[at, v_base : v_base + HEAD_DIM] = dv_acc[head, at].astype(BF16)
        part = nt(dqkv[at], w[...])
        for i in range(rows // block):
            index = start // block + i
            dnp[index] = part[i * block : (i + 1) * block].astype(BF16)
            pl.when(member != index % plan.quad)(lambda index=index: token_copy(index).start())

            @pl.when(member == index % plan.quad)
            def _(index=index):
                turn = lax.rem(half + index // plan.quad, 2)
                rdn[pl.ds(member, 1), pl.ds(turn, 1)] = dnp[index][None, None]

        values = x[at].astype(F32)
        inverse = lax.rsqrt(jnp.mean(values * values, axis=-1, keepdims=True) + EPSILON)
        gains = gains + jnp.sum(part * values * inverse, axis=0, keepdims=True)
        if number == 0:
            mix_fold.along_y()
            if out_sum:
                out_sum.phase(0)
        if number == len(spans) - 2:
            mix_fold.to_owners()
            if out_sum:
                out_sum.phase(1)
        if number < plan.dp - 1:
            swaps[number + 1].start()
    for i in range(len(spans) + 1, plan.dp):
        swaps[i].start()
    swap_out.start()
    deal(0)
    first = plan.qkv_cols - (plan.wide - 128)
    if plan.tiled:
        row = lax.broadcasted_iota(jnp.int32, (8, plan.width), 0)
        ends = [jnp.zeros((n, plan.width), F32) for n in (first, 120 - first)]
        extra = jnp.concatenate([ends[0], jnp.where(row == 0, gains, rows8[...]), ends[1]], axis=0)
        extra = jnp.transpose(extra, (1, 0))
    else:
        column = jnp.transpose(jnp.broadcast_to(gains, (128, plan.width)), (1, 0))
        lane = lax.broadcasted_iota(jnp.int32, column.shape, 1)
        extra = jnp.where(lane == first, column, small[...])
    for start in range(0, plan.wide, 128):
        cols = slice(start, start + 128)
        value = tn(normed[...], dqkv[:, cols])
        if start + 128 == plan.wide:
            value = value + extra
        value = padded_rows(plan, value, plan.devices).astype(BF16)
        dwq[:, :, :, cols] = value.reshape(plan.dp, plan.ctx, plan.pad_rows, 128)
    qkv_fold.start()
    local, width = plan.local, plan.width
    if out_sum:
        out_sum.phase(2)
    for source in range(plan.quad):

        @pl.when(member != source)
        def _(source=source):
            for turn in range(2):
                remote(
                    dnp.at[0], rdn.at[source, turn], n_send.at[0], n_recv.at[source, turn], (dp, ctx)
                ).wait_recv()

    total = rdn[0].astype(F32)
    for i in range(1, plan.quad):
        total = total + rdn[i].astype(F32)
    total = total.reshape(local, width)
    values = jnp.concatenate(
        [x[pl.ds(pl.multiple_of(at * block, 16), block)] for at in (ctx, far)], axis=0
    ).astype(F32)
    inverse = lax.rsqrt(jnp.mean(values * values, axis=-1, keepdims=True) + EPSILON)
    scaled = total * around_gains(plan, w)[:1]
    result = (
        middle_grad[...]
        + inverse * scaled
        - values * inverse * inverse * inverse * jnp.mean(scaled * values, axis=-1, keepdims=True)
    )
    result = result.astype(BF16).reshape(2, block, width)
    grad_away[...] = result[1]
    grad_out[pl.ds(half, 1)] = result[:1]
    swap_grad = remote(grad_away, grad_out.at[half], s_send.at[1], s_recv.at[1], across)
    swap_grad.start()
    qkv_fold.along_y()
    if out_sum:
        out_sum.phase(3)
        acts = middle[...] + out_sum.work[0].astype(F32)
    else:
        acts = middle[...] + out_part[...].astype(F32)
    acts = acts.astype(BF16).reshape(2, block, width)
    act_away[...] = acts[1]
    act_out[pl.ds(half, 1)] = acts[:1]
    swap_act = remote(act_away, act_out.at[half], s_send.at[0], s_recv.at[0], across)
    swap_act.start()
    for i in range(1, plan.dp):
        deal(i)
        if i == 1:
            qkv_fold.to_owners()
    mix_fold.finish()
    qkv_fold.finish()
    swap_act.wait()
    swap_grad.wait()
    swap_out.wait()
    for target in range(plan.group):

        @pl.when(mine != target)
        def _(target=target):
            deal_copy(target).wait_send()
            remote(
                dealt.at[0], rwin.at[target], e_send.at[0], e_recv.at[target], (dp, ctx)
            ).wait_recv()

    for index in range(plan.ctx):
        pl.when(member != index % plan.quad)(lambda index=index: token_copy(index).wait_send())
    if out_sum:
        out_sum.finish()


def back(plan, length, x, w, cosine, sine, normed, qk, v, lse, dw_in, dw_out, out_part, middle, given, collective_id):
    slots, block, width = plan.slots, plan.block, plan.width
    count = 2 * (plan.quad - 1)
    dealt = (plan.group, 2 * plan.pad_rows, plan.hidden_pad)
    summed = out_part.ndim == 2
    rows = (plan.local, width)
    out_scratch = [
        pltpu.VMEM((8,) + rows, BF16),
        pltpu.VMEM((8,) + rows, BF16),
        pltpu.VMEM((7,) + rows, BF16),
        DMA((8,)),
        DMA((8,)),
        DMA((8,)),
        DMA((2, 7)),
        DMA((2, 7)),
        pltpu.VMEM((plan.quad, 2, block, plan.head_cols), BF16),
        pltpu.VMEM((plan.dp, plan.ctx, plan.rows, width), BF16),
        pltpu.VMEM((8, width), F32),
        pltpu.VMEM((plan.local, width), F32),
    ]
    return pl.pallas_call(
        functools.partial(back_kernel, plan, summed),
        out_shape=(
            jax.ShapeDtypeStruct((plan.ctx, plan.pad_rows, plan.wide), BF16),
            jax.ShapeDtypeStruct((plan.ctx, plan.rows, width), BF16),
            jax.ShapeDtypeStruct(dealt, BF16),
            jax.ShapeDtypeStruct((plan.branches, plan.own_hidden, width), BF16),
            jax.ShapeDtypeStruct((2, block, width), BF16),
            jax.ShapeDtypeStruct((2, block, width), BF16),
        ),
        in_specs=[pl.BlockSpec(memory_space=pltpu.SMEM)]
        + [VMEM] * 10
        + [VMEM if summed else HBM]
        + [VMEM] * (1 + len(given)),
        out_specs=(VMEM,) * 6,
        scratch_shapes=[
            pltpu.VMEM((slots, plan.wide), BF16),
            pltpu.VMEM((plan.heads, slots, HEAD_DIM), F32),
            pltpu.VMEM((plan.heads, slots, HEAD_DIM), F32),
            pltpu.VMEM((plan.ctx, block, plan.head_cols), BF16),
            pltpu.VMEM((plan.ctx, block, width), BF16),
            pltpu.VMEM((plan.quad, 2, block, width), BF16),
            pltpu.VMEM((plan.dp, plan.ctx, plan.pad_rows, plan.wide), BF16),
            pltpu.VMEM((plan.dp,) + dw_in.shape[1:], BF16),
            pltpu.VMEM(dealt, BF16),
            pltpu.VMEM((plan.branches, plan.own_hidden, width), BF16),
            pltpu.VMEM((block, width), BF16),
            pltpu.VMEM((block, width), BF16),
            DMA((count,)),
            DMA((count,)),
            DMA((plan.ctx,)),
            DMA((plan.quad, 2)),
            DMA((plan.dp,)),
            DMA((plan.dp,)),
            DMA((plan.group,)),
            DMA((plan.group,)),
            DMA((3,)),
            DMA((3,)),
        ]
        + fold_scratch(plan, plan.rows, width)
        + fold_scratch(plan, plan.pad_rows, plan.wide)
        + ([] if summed else out_scratch),
        compiler_params=params(collective_id),
        cost_estimate=busy(90),
        name="back",
    )(length, x, w, cosine, sine, normed, qk, v, lse, dw_in, dw_out, out_part, middle, *given)


def ffn_kernel(plan, members, n2x, gy, w_in, w_out, pick, out, n2g, dw_in, dw_out):
    hidden, local = plan.hidden_pad, plan.local

    @pl.when(pl.program_id(0) == 0)
    def start():
        dw_in[...] = jnp.zeros_like(dw_in)
        dw_out[...] = jnp.zeros_like(dw_out)

    tokens = members * local
    width = plan.width
    normed = n2x[:, :local].reshape(tokens, width)
    upstream = gy[:, :, : plan.block].reshape(tokens, width)
    mixing = jnp.concatenate(
        [tn(n2x[i, local:, :local], pick[...]) for i in range(members)], axis=0
    )
    pre = nn(normed, w_in[...])
    gate, up = pre[:, :hidden], pre[:, hidden:]
    sigmoid = jax.nn.sigmoid(gate)
    silu = gate * sigmoid
    act = (silu * up).astype(BF16).astype(F32)
    act_mixed = (act * mixing).astype(BF16)
    out[...] = nn(act_mixed, w_out[...]).astype(BF16).reshape(members, local, width)
    act_grad = nt(upstream, w_out[...])
    choice = nt(pick[...], (act * act_grad).astype(BF16)).astype(BF16)
    act_grad = act_grad * mixing
    gate_grad = act_grad * up * sigmoid * (1.0 + gate * (1.0 - sigmoid))
    pre_grad = jnp.concatenate([gate_grad, act_grad * silu], axis=-1).astype(BF16)
    n2g[:, :local] = nt(pre_grad, w_in[...]).astype(BF16).reshape(members, local, width)
    pad = jnp.zeros((MIX_ROWS, width - local), BF16)
    for i in range(members):
        n2g[i, local:] = jnp.concatenate(
            [choice[:, i * local : (i + 1) * local], pad], axis=-1
        )
    dw_in[...] += tn(normed, pre_grad)
    dw_out[...] += tn(act_mixed, upstream)


def ffn(plan, n2x, gy, w_in, w_out, pick):
    members = 2
    local, width, hidden = plan.local, plan.width, plan.hidden_pad
    whole = lambda i: (0, 0)
    part = lambda i: (i, 0, 0)
    return pl.pallas_call(
        functools.partial(ffn_kernel, plan, members),
        grid=(plan.group // members,),
        out_shape=(
            jax.ShapeDtypeStruct((plan.group, local, width), BF16),
            jax.ShapeDtypeStruct((plan.group, local + MIX_ROWS, width), BF16),
            jax.ShapeDtypeStruct((width, 2 * hidden), F32),
            jax.ShapeDtypeStruct((hidden, width), F32),
        ),
        in_specs=[
            pl.BlockSpec((members, local + MIX_ROWS, width), part),
            pl.BlockSpec((members,) + gy.shape[1:], lambda i: (i, 0, 0, 0)),
            pl.BlockSpec((width, 2 * hidden), whole),
            pl.BlockSpec((hidden, width), whole),
            pl.BlockSpec((MIX_ROWS, hidden), whole),
        ],
        out_specs=(
            pl.BlockSpec((members, local, width), part),
            pl.BlockSpec((members, local + MIX_ROWS, width), part),
            pl.BlockSpec((width, 2 * hidden), whole),
            pl.BlockSpec((hidden, width), whole),
        ),
        compiler_params=params(),
        name="ffn",
    )(n2x, gy, w_in, w_out, pick)


STEP_ORDER = ((0, 0, 0), (0, 0, 1), (0, 1, 0), (1, 0, 1), (1, 1, 0), (1, 1, 1), (0, 1, 1), (1, 0, 0))
PART_ORDERS = (("high", "low", "y"), ("low", "y", "high"), ("y", "high", "low"))
PAUSES = {
    3: (('g0', 7), ('g0', 2), ('g0', 1), ('g1', 1), ('g2', 1)),
    4: (('g1', 2), ('g2', 7), ('g2', 2), ('g1', 7)),
    5: (('g0', 4), ('g0', 3), ('g1', 3)),
    7: (('g2', 3), ('g0', 6), ('g2', 6), ('s2', 1)),
    8: (('g1', 4), ('g2', 4)),
    9: (('g1', 6),),
    10: (('s1', 2),),
    11: (('g0', 5), ('g2', 5)),
    13: (('g1', 5), ('s0', 3), ('s2', 3)),
    16: (('s0', 4), ('s1', 4)),
    19: (('s0', 5), ('s1', 5), ('s2', 5)),
    20: (('s0', 2),),
    22: (('s1', 6), ('s2', 6)),
    23: (('s1', 3), ('s2', 4), ('s0', 6)),
    24: (('s0', 7), ('s2', 7), ('s1', 1), ('s2', 2), ('s1', 7), ('s0', 1), ('s2', 0), ('s0', 0), ('s1', 0)),
}


def part_rows(rows):
    cuts = [round_up(rows * i // 3, 16) for i in range(3)] + [rows]
    return [slice(a, b) for a, b in zip(cuts, cuts[1:])]


def named(offset):
    return dict(zip(("high", "low", "y"), offset))


def feeds_of(order, offset):
    at = named(offset)
    phase = min([i for i, axis in enumerate(order) if at[axis]], default=3)
    names = ("high", "low", "y")
    return phase, [tuple(1 if n == axis else at[n] for n in names) for axis in order[:phase]]


def fused_kernel(plan, n2x, gy, w_in, w_out, pick, total, dw_in, dw_out, out_all, n2all, gybuf, acc, away, work, core_buf, bufs, outbuf, gy_sem, out_sem, g_send, g_recv, gc_send, gc_recv, c_send, c_recv, r_send, r_recv):
    grid = Grid(plan)
    at = grid.here()
    local, width, hidden = plan.local, plan.width, plan.hidden_pad
    steps = len(STEP_ORDER)
    partner = grid.device(grid.moved(at, "core", 1))
    here = grid.device(at)
    parts = range(len(PART_ORDERS))
    in_rows, sum_rows = part_rows(local + MIX_ROWS), part_rows(local + MIX_ROWS)

    def absolute(offset):
        where = dict(at)
        for axis, step in named(offset).items():
            if step:
                where = grid.moved(where, axis, step)
        return where

    def slot_of(offset):
        return grid.slot(named(offset))

    def level_of(part, offset):
        reached = named(offset)
        return max([i + 1 for i, axis in enumerate(PART_ORDERS[part]) if reached[axis]], default=0)

    send_index = {}
    for part in parts:
        count = 0
        for offset in STEP_ORDER:
            for axis in PART_ORDERS[part][level_of(part, offset) :]:
                send_index[part, offset, axis] = count
                count += 1

    def pass_on(part, offset):
        level = level_of(part, offset)
        block = grid.block(absolute(offset))
        slot = slot_of(offset)
        span = in_rows[part]
        landing = n2all.at[block, span]
        if level:
            remote(landing, landing, g_send.at[part, 0], g_recv.at[part, slot], here).wait_recv()
        source = landing if level else n2x.at[span]
        for axis in PART_ORDERS[part][level:]:
            seen = grid.slot({**named(offset), axis: 1})
            remote(
                source,
                landing,
                g_send.at[part, send_index[part, offset, axis]],
                g_recv.at[part, seen],
                grid.device(grid.moved(at, axis, 1)),
            ).start()
        remote(source, landing, gc_send.at[part, slot], gc_recv.at[part, slot], partner).start()

    listed = [(kind[0], int(kind[1]), STEP_ORDER[place]) for row in PAUSES.values() for kind, place in row]
    buf_index, seen_slots, first_sums = {}, set(), set()
    for kind, part, offset in listed:
        if kind == "s":
            if offset not in seen_slots:
                seen_slots.add(offset)
                first_sums.add((part, offset))
            if any(offset):
                buf_index[part, offset] = sum(1 for other, _ in buf_index if other == part)

    def add_up(part, offset):
        phase, feeds = feeds_of(PART_ORDERS[part], offset)
        axis = PART_ORDERS[part][phase] if phase < 3 else None
        slot = slot_of(offset)
        span = sum_rows[part]
        if (part, offset) in first_sums:
            remote(away.at[0], core_buf.at[slot], c_send.at[0], c_recv.at[slot], here).wait_recv()
        for feed in feeds:
            index = buf_index[part, feed]
            ref = bufs.at[index, span]
            remote(ref, ref, r_send.at[part, 0], r_recv.at[part, index], here).wait_recv()

        @pl.loop(0, (span.stop - span.start) // 16)
        def _(i):
            rows = pl.ds(pl.multiple_of(span.start + i * 16, 16), 16)
            value = work[slot, rows].astype(F32) + core_buf[slot, rows].astype(F32)
            for feed in feeds:
                value = value + bufs[buf_index[part, feed], rows].astype(F32)
            if axis is None:
                total[rows] = value
            else:
                work[slot, rows] = value.astype(BF16)

        if axis is not None:
            index = buf_index[part, offset]
            remote(
                work.at[slot, span],
                bufs.at[index, span],
                r_send.at[part, index],
                r_recv.at[part, index],
                grid.device(grid.moved(at, axis, 1)),
            ).start()

    def pause(number):
        for kind, place in PAUSES.get(number, ()):
            act = pass_on if kind[0] == "g" else add_up
            act(int(kind[1]), STEP_ORDER[place])

    def pauses(step, turn):
        for i in range(steps):
            if 3 * i + turn in PAUSES:
                pl.when(step == i)(functools.partial(pause, 3 * i + turn))

    def bit(step, index):
        value = 0
        for i, offset in enumerate(STEP_ORDER):
            if offset[index]:
                value = value + jnp.where(step == i, 1, 0)
        return value

    def blocks_of(step):
        where = dict(at)
        offsets = {}
        for index, axis in enumerate(("high", "low", "y")):
            offsets[axis] = bit(step, index)
            where[axis] = lax.rem(at[axis] + offsets[axis], 2)
        mine = grid.block(where)
        other = grid.block(grid.moved(where, "core", 1))
        return mine, other, grid.slot(offsets)

    def gy_loads(step, turn):
        mine, other, _ = blocks_of(step)
        return [
            pltpu.make_async_copy(gy.at[mine, :, : plan.block], gybuf.at[turn, 0], gy_sem.at[turn, 0]),
            pltpu.make_async_copy(gy.at[other, :, : plan.block], gybuf.at[turn, 1], gy_sem.at[turn, 1]),
        ]

    def out_copy(turn, i, block):
        return pltpu.make_async_copy(outbuf.at[turn, i], out_all.at[block], out_sem.at[turn, i])

    for load in gy_loads(0, 0):
        load.start()
    meet(grid.peers(at))
    for part in parts:
        pass_on(part, STEP_ORDER[0])
    n2all[pl.ds(grid.block(at), 1)] = n2x[...][None]
    acc[...] = jnp.zeros_like(acc)
    dw_out[...] = jnp.zeros_like(dw_out)

    @pl.loop(0, steps)
    def _(step):
        pauses(step, 0)
        mine, other, slot = blocks_of(step)
        turn = lax.rem(step, 2)

        @pl.when(step + 1 < steps)
        def _():
            for load in gy_loads(step + 1, 1 - turn):
                load.start()

        for part in parts:
            ref = n2all.at[other, in_rows[part]]
            remote(ref, ref, gc_send.at[part, 0], gc_recv.at[part, slot], here).wait_recv()
        for load in gy_loads(step, turn):
            load.wait()
        pair = (mine, other)
        normed = jnp.concatenate([n2all[b, :local] for b in pair], axis=0)
        upstream = gybuf[turn].reshape(2 * local, width)
        mixing = jnp.concatenate([tn(n2all[b, local:, :local], pick[...]) for b in pair], axis=0)
        pre = nn(normed, w_in[...])
        gate, up = pre[:, :hidden], pre[:, hidden:]
        sigmoid = jax.nn.sigmoid(gate)
        silu = gate * sigmoid
        act = (silu * up).astype(BF16).astype(F32)
        act_mixed = (act * mixing).astype(BF16)
        pauses(step, 1)

        @pl.when(step >= 2)
        def _():
            for i, block in enumerate(pair):
                out_copy(turn, i, block).wait()

        out = nn(act_mixed, w_out[...]).astype(BF16)
        for i, block in enumerate(pair):
            outbuf[turn, i] = out[i * local : (i + 1) * local]
            out_copy(turn, i, block).start()
        act_grad = nt(upstream, w_out[...])
        choice = nt(pick[...], (act * act_grad).astype(BF16)).astype(BF16)
        act_grad = act_grad * mixing
        gate_grad = act_grad * up * sigmoid * (1.0 + gate * (1.0 - sigmoid))
        pre_grad = jnp.concatenate([gate_grad, act_grad * silu], axis=-1).astype(BF16)
        n2g = nt(pre_grad, w_in[...]).astype(BF16)

        @pl.when(step >= 2)
        def _():
            remote(away.at[turn], core_buf.at[0], c_send.at[turn], c_recv.at[0], partner).wait_send()

        pad = jnp.zeros((MIX_ROWS, width - local), BF16)
        for i, (ref, index) in enumerate(((work, slot), (away, turn))):
            span = slice(i * local, (i + 1) * local)
            ref[index, :local] = n2g[span]
            ref[index, local:] = jnp.concatenate([choice[:, span], pad], axis=-1)
        remote(away.at[turn], core_buf.at[slot], c_send.at[turn], c_recv.at[slot], partner).start()
        pauses(step, 2)
        acc[...] += tn(normed, pre_grad)
        dw_out[...] += tn(act_mixed, upstream)

    pause(3 * steps)
    for turn in range(2):
        for i in range(2):
            out_copy(turn, i, 0).wait()
    dw_in[...] = acc[...].astype(BF16)
    for turn in range(2):
        remote(away.at[turn], core_buf.at[0], c_send.at[turn], c_recv.at[0], partner).wait_send()
    for part in parts:
        ref, block = n2all.at[0, in_rows[part]], bufs.at[0, sum_rows[part]]
        for slot in range(steps):
            remote(ref, ref, gc_send.at[part, slot], g_recv.at[part, 0], partner).wait_send()
        for index in range(steps - 1):
            remote(ref, ref, g_send.at[part, index], g_recv.at[part, 0], partner).wait_send()
            remote(block, block, r_send.at[part, index], r_recv.at[part, 0], partner).wait_send()


def fused(plan, n2x, gy, w_in, w_out, pick, collective_id):
    local, width, hidden = plan.local, plan.width, plan.hidden_pad
    steps = len(STEP_ORDER)
    rows = local + MIX_ROWS
    return pl.pallas_call(
        functools.partial(fused_kernel, plan),
        out_shape=(
            jax.ShapeDtypeStruct((rows, width), F32),
            jax.ShapeDtypeStruct((width, 2 * hidden), BF16),
            jax.ShapeDtypeStruct((hidden, width), F32),
            jax.ShapeDtypeStruct((plan.group, local, width), BF16),
        ),
        in_specs=[VMEM, HBM, VMEM, VMEM, VMEM],
        out_specs=(VMEM,) * 3 + (HBM,),
        scratch_shapes=[
            pltpu.VMEM((plan.group, local + MIX_ROWS, width), BF16),
            pltpu.VMEM((2, 2, 2, plan.block, width), BF16),
            pltpu.VMEM((width, 2 * hidden), F32),
            pltpu.VMEM((2, rows, width), BF16),
            pltpu.VMEM((steps, rows, width), BF16),
            pltpu.VMEM((steps, rows, width), BF16),
            pltpu.VMEM((steps - 1, rows, width), BF16),
            pltpu.VMEM((2, 2, local, width), BF16),
            DMA((2, 2)),
            DMA((2, 2)),
            DMA((3, steps - 1)),
            DMA((3, steps)),
            DMA((3, steps)),
            DMA((3, steps)),
            DMA((2,)),
            DMA((steps,)),
            DMA((3, steps - 1)),
            DMA((3, steps - 1)),
        ],
        compiler_params=params(collective_id),
        cost_estimate=busy(100),
        name="fused",
    )(n2x, gy, w_in, w_out, pick)


def turned(value):
    return pltpu.roll(value, 64, 1)


def half_tiles(plan):
    return lax.broadcasted_iota(jnp.int32, (plan.rows, 128), 1) < 64


def column_tiles(plan, pair, gate):
    per = plan.quad // 2
    start = gate * FF + lax.div(pair, per) * (plan.ctx * 64) + lax.rem(pair, per) * 128
    first = lax.div(pair, per) * plan.quad + lax.rem(pair, per) * 2
    return [pl.ds(pl.multiple_of(start + half * plan.quad * 64, 128), 128) for half in range(2)], first


def pack_kernel(plan, both, attn, extra, wq, win):
    low = half_tiles(plan)

    @pl.loop(0, plan.group // 2)
    def _(pair):
        for branch in range(plan.branches):
            made = [[], []]
            for gate in range(2):
                cols, first = column_tiles(plan, pair, gate)
                mine, far = (both[branch, :, col].astype(F32) for col in cols)
                made[0].append(jnp.where(low, mine, turned(far)))
                made[1].append(jnp.where(low, turned(mine), far))
            for i in range(2):
                value = jnp.concatenate(made[i], axis=0).astype(BF16)
                win[pl.ds(first + i, 1), :, branch * 128 : (branch + 1) * 128] = value[None]

    def tile(part, head):
        start = part * HEADS * HEAD_DIM + head // 2 * 128
        return attn[:, start : start + 128].astype(F32)

    def placed(part, head, side):
        value = tile(part, head)
        return value if head % 2 == side else turned(value)

    for member in range(plan.quad):
        heads = [member * 3 + i for i in range(3)]
        for i, head in enumerate(heads):
            value = jnp.where(low, placed(0, head, 0), placed(1, head, 1))
            wq[member, :, i * 128 : (i + 1) * 128] = value.astype(BF16)
        value = jnp.where(low, placed(2, heads[0], 0), placed(2, heads[1], 1))
        wq[member, :, 384:512] = value.astype(BF16)
        value = jnp.where(low, placed(2, heads[2], 0), extra[...].astype(F32))
        wq[member, :, 512:640] = value.astype(BF16)


def pack(plan, both, attn, extra):
    return pl.pallas_call(
        functools.partial(pack_kernel, plan),
        out_shape=(
            jax.ShapeDtypeStruct((plan.quad, plan.rows, plan.wide), BF16),
            jax.ShapeDtypeStruct((plan.group, 2 * plan.rows, plan.hidden_pad), BF16),
        ),
        in_specs=[VMEM] * 3,
        out_specs=(VMEM,) * 2,
        compiler_params=params(),
        cost_estimate=busy(3),
        name="pack",
    )(both, attn, extra)


def unpack_kernel(plan, r_in, r_qkv, r_mix, dw_out, far_out, dense_in, expert_in, attn_in, attn_out, small, dense_out, expert_out):
    low = half_tiles(plan)
    rows = plan.rows

    @pl.loop(0, plan.group // 2)
    def _(pair):
        first = column_tiles(plan, pair, 0)[1]
        for branch in range(plan.branches):
            cols = slice(branch * 128, (branch + 1) * 128)
            sources = [r_in[first + i, :, cols].astype(F32) for i in range(2)]
            for gate in range(2):
                one, two = (value[gate * rows : (gate + 1) * rows] for value in sources)
                places = column_tiles(plan, pair, gate)[0]
                values = jnp.where(low, one, turned(two)), jnp.where(low, turned(one), two)
                for place_at, value in zip(places, values):
                    if branch == 0:
                        dense_in[:, place_at] = value
                    else:
                        expert_in[:, branch - 1, place_at] = value

    def tile(member, number):
        cols = slice(number * 128, (number + 1) * 128)
        return r_qkv[member, :, cols].astype(F32) + r_qkv[plan.quad + member, :, cols].astype(F32)

    def put(part, head, value):
        start = part * HEADS * HEAD_DIM + head // 2 * 128
        attn_in[:, start : start + 128] = value

    for head in range(0, HEADS, 2):
        one, two = (tile((head + i) // 3, (head + i) % 3) for i in range(2))
        put(0, head, jnp.where(low, one, turned(two)))
        put(1, head, jnp.where(low, turned(one), two))
        halves = []
        for i in range(2):
            member, at = divmod(head + i, 3)
            value = tile(member, 3 + at // 2)
            halves.append(value if at % 2 == i else turned(value))
        put(2, head, jnp.where(low, halves[0], halves[1]))
    total = tile(0, 4)
    for member in range(1, plan.quad):
        total = total + tile(member, 4)
    small[...] = total
    mixed = r_mix[0].astype(F32)
    for i in range(1, plan.ctx):
        mixed = mixed + r_mix[i].astype(F32)
    attn_out[...] = mixed
    half = lax.div(lax.axis_index("ctx"), plan.quad)
    for branch in range(plan.branches):
        value = dw_out[branch, pl.ds(half, 1)][0] + far_out[branch].astype(F32)
        if branch == 0:
            dense_out[...] = value
        else:
            expert_out[:, branch - 1, :] = value


def unpack(plan, r_in, r_qkv, r_mix, dw_out, far_out):
    rows, width, own = plan.rows, plan.width, plan.own_hidden
    return pl.pallas_call(
        functools.partial(unpack_kernel, plan),
        out_shape=(
            jax.ShapeDtypeStruct((rows, 2 * FF), F32),
            jax.ShapeDtypeStruct((rows, plan.experts, 2 * FF), F32),
            jax.ShapeDtypeStruct((rows, 3 * HEADS * HEAD_DIM), F32),
            jax.ShapeDtypeStruct((rows, width), F32),
            jax.ShapeDtypeStruct((rows, 128), F32),
            jax.ShapeDtypeStruct((own, width), F32),
            jax.ShapeDtypeStruct((own, plan.experts, width), F32),
        ),
        in_specs=[VMEM] * 5,
        out_specs=(VMEM,) * 7,
        compiler_params=params(),
        cost_estimate=busy(5),
        name="unpack",
    )(r_in, r_qkv, r_mix, dw_out, far_out)


def grid_block(plan, dp, ctx):
    return dp * plan.quad + lax.rem(ctx, plan.quad)


def by_half(half, mine, far, axis):
    return jnp.where(
        half == 0, jnp.stack([mine, far], axis), jnp.stack([far, mine], axis)
    )


def rope_tables(plan):
    half, step = HEAD_DIM // 2, 64
    frequency = np.float32(10000.0) ** (-np.arange(half, dtype=np.float32) / np.float32(half))
    frequency = np.tile(frequency.astype(np.float64), 4)[None]
    coarse = np.arange(0, plan.slots, step)[:, None] * frequency
    fine = np.arange(step)[:, None] * frequency
    sign = np.tile(np.repeat([-1.0, 1.0], half), 2)[None]
    (ca, sa), (cb, sb) = (
        (jnp.asarray(np.cos(a), F32), jnp.asarray(np.sin(a), F32)) for a in (coarse, fine)
    )
    ca, sa, cb, sb = ca[:, None], sa[:, None], cb[None], sb[None]
    cosine = (ca * cb - sa * sb).reshape(plan.slots, 128)
    sine = ((sa * cb + ca * sb) * jnp.asarray(sign, F32)).reshape(plan.slots, 128)
    return cosine, sine


def pick_table(plan):
    table = np.zeros((MIX_ROWS, plan.hidden_pad), np.float32)
    span = HALVES * plan.own_hidden
    for expert in range(plan.experts):
        cols = slice((1 + expert) * span, (2 + expert) * span)
        table[2 + expert, cols] = 1.0
        table[10 + expert, cols] = 1.0
    table[0, :span] = 1.0
    return jnp.asarray(table, BF16)


def pack_qkv(plan, attn_in, attn_gain, ffn_gain, router):
    rows, quad, heads = plan.rows, plan.quad, plan.heads
    qkv = attn_in.reshape(rows, 3, HEADS, HEAD_DIM)
    qkv = jnp.pad(qkv, ((0, 0), (0, 0), (0, quad * heads - HEADS), (0, 0)))
    qkv = qkv.reshape(rows, 3, quad, heads, HEAD_DIM)
    qk = jnp.transpose(qkv[:, :2], (2, 0, 3, 1, 4)).reshape(quad, rows, 2 * plan.head_cols)
    v = jnp.transpose(qkv[:, 2], (1, 0, 2, 3)).reshape(quad, rows, plan.head_cols)
    extra = jnp.concatenate([attn_gain[:, None], ffn_gain[:, None], router], axis=1)
    extra = jnp.pad(extra, ((0, 0), (0, plan.wide - plan.qkv_cols - extra.shape[1])))
    extra = jnp.broadcast_to(extra[None], (quad,) + extra.shape)
    packed = jnp.concatenate([qk, v, extra], axis=-1)
    return jnp.pad(packed, ((0, 0), (0, plan.pad_rows - rows), (0, 0)))


def unpack_qkv(plan, packed):
    rows, quad, heads = plan.rows, plan.quad, plan.heads
    qk = packed[..., : 2 * plan.head_cols].reshape(quad, rows, heads, 2, HEAD_DIM)
    v = packed[..., 2 * plan.head_cols : plan.qkv_cols].reshape(quad, rows, heads, 1, HEAD_DIM)
    qkv = jnp.transpose(jnp.concatenate([qk, v], axis=3), (1, 3, 0, 2, 4))
    qkv = qkv.reshape(rows, 3, quad * heads, HEAD_DIM)[:, :, :HEADS]
    return qkv.reshape(rows, 3 * HEADS * HEAD_DIM)


def pack_in(plan, dense_in, expert_in):
    rows, own = plan.rows, plan.own_hidden
    both = jnp.concatenate([dense_in[:, None], expert_in], axis=1)
    both = both.reshape(rows, plan.branches, 2, plan.dp, HALVES, plan.quad, own)
    both = jnp.transpose(both, (3, 5, 2, 0, 1, 4, 6))
    both = both.reshape(plan.group, 2, rows, plan.hidden)
    pads = ((0, 0), (0, 0), (0, plan.pad_rows - rows), (0, plan.hidden_pad - plan.hidden))
    return jnp.pad(both, pads).reshape(plan.group, 2 * plan.pad_rows, plan.hidden_pad)


def unpack_in(plan, packed):
    rows, own = plan.rows, plan.own_hidden
    both = packed.reshape(plan.group, 2, plan.pad_rows, plan.hidden_pad)
    both = both[:, :, :rows, : plan.hidden]
    both = both.reshape(plan.dp, plan.quad, 2, rows, plan.branches, HALVES, own)
    both = jnp.transpose(both, (3, 4, 2, 0, 5, 1, 6))
    both = both.reshape(rows, plan.branches, 2 * FF).astype(F32)
    return both[:, 0], both[:, 1:]


def shards(
    tokens,
    lengths,
    routes,
    cotangent,
    attn_gain,
    attn_in,
    attn_out,
    ffn_gain,
    router,
    dense_in,
    dense_out,
    expert_in,
    expert_out,
):
    micro, seqs, block, width = tokens.shape
    experts = expert_in.shape[1]
    plan = Plan(lax.axis_size("dp"), lax.axis_size("ctx"), block, width, experts)
    assert micro == HALVES and seqs == 1 and plan.ctx % 4 == 0 and plan.dp % 2 == 0
    quad, local = plan.quad, plan.local
    dp, ctx = place()
    half, member = lax.div(ctx, quad), lax.rem(ctx, quad)
    across = [(i, (i + quad) % plan.ctx) for i in range(plan.ctx)]

    def swap(value):
        return lax.ppermute(value, "ctx", across)

    def pick_mine(value):
        return lax.dynamic_index_in_dim(value, half, 0, keepdims=False)

    def pick_far(value):
        return lax.dynamic_index_in_dim(value, 1 - half, 0, keepdims=False)

    slot = ctx * block + jnp.arange(block, dtype=jnp.int32)
    valid = (slot[None] < lengths).astype(BF16)
    grad_all = cotangent[:, 0] * valid[..., None]
    tail = round_up(plan.rows + 2, 16)
    route_rows = jnp.transpose(routes[:, 0], (0, 2, 1)).astype(BF16)
    route_rows = jnp.pad(route_rows, ((0, 0), (0, tail - plan.rows - 2), (0, width - block)))
    length = pick_mine(lengths)
    out_own = jnp.concatenate([dense_out[:, None], expert_out], axis=1)
    out_own = jnp.transpose(out_own, (1, 0, 2))
    out_far = swap(out_own)
    gyw = jnp.concatenate(
        [grad_all, jnp.broadcast_to(attn_out, (2,) + attn_out.shape), route_rows], axis=1
    )

    if plan.tiled:
        both = jnp.concatenate([dense_in[None], jnp.transpose(expert_in, (1, 0, 2))])
        extra = jnp.concatenate([attn_gain[:, None], ffn_gain[:, None], router], axis=1)
        extra = jnp.pad(extra, ((0, 0), (64, 64 - extra.shape[1])))
        wq, win = pack(plan, both, attn_in, extra)
    else:
        wq = pack_qkv(plan, attn_in, attn_gain, ffn_gain, router)
        win = pack_in(plan, dense_in, expert_in)

    cosine, sine = rope_tables(plan)
    xs, w_seq, normed_seq, qk, v, lse, mixed, gy, w_in, gysrc, *owned = front(
        plan,
        length,
        tokens[:, 0],
        wq,
        win,
        gyw,
        cosine,
        sine,
        1,
    )
    x_seq = xs.reshape(plan.slots, width)
    if plan.tiled:
        n2x, middle, gates, w_mix = owned
    else:
        extra = w_seq[:, plan.qkv_cols :]
        gain_one = extra[:, 0].astype(F32)[None]
        gain_two = extra[:, 1].astype(F32)[None]
        w_route = extra[:, 2 : 2 + experts]
        mixed = jnp.transpose(mixed, (1, 2, 0, 3)).reshape(local, quad * plan.head_cols)[:, :width]
        w_mix = gy[:, :, block : block + plan.rows].reshape(plan.dp, quad, 2, plan.rows, width)
        w_mix = by_half(half, w_mix[:, :, 0], w_mix[:, :, 1], 1).reshape(width, width)

        x = jnp.stack(
            [
                lax.dynamic_index_in_dim(xs, ctx, 0, keepdims=False),
                lax.dynamic_index_in_dim(xs, (1 - half) * quad + member, 0, keepdims=False),
            ]
        )
        x = x.reshape(local, width).astype(F32)
        middle = x + nn(mixed, w_mix)
        inverse_two = lax.rsqrt(jnp.mean(middle * middle, axis=-1, keepdims=True) + EPSILON)
        normed_two = (middle * inverse_two * gain_two).astype(BF16)
        own = lax.dynamic_index_in_dim(gy, grid_block(plan, dp, ctx), 0, keepdims=False)
        grad_y = own[:, :block].reshape(local, width)
        route_local = own[:, block + plan.rows : block + plan.rows + 2, :block]
        route_local = jnp.transpose(route_local, (0, 2, 1)).reshape(local, 2)
        logits = nn(normed_two, w_route)
        choose = (route_local[..., None] == jnp.arange(experts, dtype=BF16)).astype(F32)
        picked = jnp.sum(choose * logits[:, None, :], axis=-1)
        gates = jax.nn.softmax(picked, axis=-1)
        mixing = jnp.sum(gates[..., None] * choose, axis=1)
        mixing_t = mixing.T
        mixing_high = mixing_t.astype(BF16)
        mixing_low = (mixing_t - mixing_high.astype(F32)).astype(BF16)
        pads = ((2, 6 - experts), (0, 0))
        mix_rows = jnp.concatenate([jnp.pad(mixing_high, pads), jnp.pad(mixing_low, pads)])
        mix_rows = mix_rows.at[0].set(1.0)
        mix_rows = jnp.pad(mix_rows, ((0, 0), (0, width - local)))
        n2x = jnp.concatenate([normed_two, mix_rows])

    w_out = by_half(half, out_own, out_far, 1).reshape(plan.hidden, width)
    w_out = jnp.pad(w_out, ((0, plan.hidden_pad - plan.hidden), (0, 0)))
    if plan.dp == 4 and quad == 4:
        n2g_sum, dw_in, dw_out, out_part = fused(plan, n2x, gy, w_in, w_out, pick_table(plan), 3)
    else:
        n2x = gather(plan, n2x, 3)
        out_part, n2g_part, dw_in, dw_out = ffn(plan, n2x, gy, w_in, w_out, pick_table(plan))
        n2g_sum = reduce(plan, n2g_part, 5)
        out_part = reduce(plan, out_part, 7)

    if plan.tiled:
        given = (n2g_sum, gates, n2x, gysrc, w_mix, mixed)
    else:
        normed_two_grad = n2g_sum[:local]
        mixing_grad = n2g_sum[local + 2 : local + 2 + experts, :local].T
        choice_grad = jnp.sum(choose * mixing_grad[:, None, :], axis=-1)
        pick_grad = gates * (choice_grad - jnp.sum(gates * choice_grad, axis=-1, keepdims=True))
        logit_grad = jnp.sum(pick_grad[..., None] * choose, axis=1).astype(BF16)
        router_grad = tn(normed_two, logit_grad)
        normed_two_grad = normed_two_grad + nt(logit_grad, w_route)
        gain_two_grad = jnp.sum(normed_two_grad * middle * inverse_two, axis=0)
        scaled = normed_two_grad * gain_two
        middle_grad = (
            grad_y.astype(F32)
            + inverse_two * scaled
            - middle * inverse_two**3 * jnp.mean(scaled * middle, axis=-1, keepdims=True)
        )
        attn_grad = middle_grad.astype(BF16)
        dw_mix = tn(mixed, attn_grad).astype(BF16).reshape(plan.dp, plan.ctx, plan.rows, width)
        mixed_grad = nt(attn_grad, w_mix).astype(BF16)
        mixed_grad = jnp.pad(mixed_grad, ((0, 0), (0, quad * plan.head_cols - width)))
        mixed_grad = mixed_grad.reshape(2, block, quad, plan.head_cols)
        first = plan.qkv_cols - (plan.wide - 128)
        small = jnp.concatenate([gain_two_grad[:, None], router_grad], axis=1)
        small = jnp.pad(small, ((0, 0), (first + 1, 127 - first - small.shape[1])))
        given = (jnp.transpose(mixed_grad, (2, 0, 1, 3)), dw_mix, small, middle_grad)
    dw_out = dw_out[: plan.hidden].reshape(plan.branches, HALVES, plan.own_hidden, width)
    r_qkv, r_mix, r_in, far_out, activations, input_grad = back(
        plan,
        length,
        x_seq,
        w_seq,
        cosine,
        sine,
        normed_seq,
        qk,
        v,
        lse,
        dw_in.astype(BF16).reshape(plan.dp * HALVES, quad * plan.rows, 2 * plan.hidden_pad),
        dw_out,
        out_part,
        middle,
        given,
        4,
    )

    if plan.tiled:
        dense_in_grad, expert_in_grad, attn_in_grad, attn_out_grad, small, dense_out_grad, expert_out_grad = unpack(
            plan, r_in, r_qkv, r_mix, dw_out, far_out
        )
        small = small[:, 64 : 66 + experts]
    else:
        r_qkv = r_qkv[:, : plan.rows].astype(F32).reshape(HALVES, quad, plan.rows, plan.wide)
        r_qkv = jnp.sum(r_qkv, axis=0)
        attn_in_grad = unpack_qkv(plan, r_qkv)
        small = jnp.sum(r_qkv[:, :, plan.qkv_cols :], axis=0)
        attn_out_grad = jnp.sum(r_mix.astype(F32), axis=0)
        dense_in_grad, expert_in_grad = unpack_in(plan, r_in)
        dw_out = pick_mine(jnp.moveaxis(dw_out, 1, 0)) + far_out.astype(F32)
        dense_out_grad, expert_out_grad = dw_out[0], jnp.transpose(dw_out[1:], (1, 0, 2))
    return (
        activations[:, None],
        input_grad[:, None],
        small[:, 0],
        attn_in_grad,
        attn_out_grad,
        small[:, 1],
        small[:, 2 : 2 + experts],
        dense_in_grad,
        dense_out_grad,
        expert_in_grad,
        expert_out_grad,
    )


def solution(mesh):
    rows = P(("dp", "ctx"))
    matrix = P(("dp", "ctx"), None)
    cube = P(("dp", "ctx"), None, None)
    slots = P(None, "dp", "ctx", None)
    in_specs = (
        slots,
        P(None, "dp"),
        slots,
        slots,
        rows,
        matrix,
        matrix,
        rows,
        matrix,
        matrix,
        matrix,
        cube,
        cube,
    )
    out_specs = (
        slots,
        slots,
        rows,
        matrix,
        matrix,
        rows,
        matrix,
        matrix,
        matrix,
        cube,
        cube,
    )
    return jax.shard_map(shards, mesh=mesh, in_specs=in_specs, out_specs=out_specs, check_vma=False)
```

```python
import functools

import jax
import jax.numpy as jnp
import numpy as np
from jax import lax
from jax.experimental import pallas as pl
from jax.experimental.pallas import tpu as pltpu
from jax.sharding import PartitionSpec as P

HEADS = 12
HEAD_DIM = 64
FF = 2048
EPSILON = 1e-05
HALVES = 2
QUERY_ROWS = 256
MIX_ROWS = 16
MESH = pl.DeviceIdType.MESH
BF16 = jnp.bfloat16
F32 = jnp.float32


def round_up(value, step):
    return -(-value // step) * step


class Plan:
    def __init__(self, dp, ctx, block, width, experts):
        self.dp, self.ctx, self.block, self.width, self.experts = dp, ctx, block, width, experts
        self.quad = ctx // HALVES
        self.devices = dp * ctx
        self.group = dp * self.quad
        self.slots = ctx * block
        self.rows = width // self.devices
        self.pad_rows = round_up(self.rows, 8)
        self.heads = -(-HEADS // self.quad)
        self.head_cols = self.heads * HEAD_DIM
        self.qkv_cols = 3 * self.head_cols
        self.wide = round_up(self.qkv_cols + 2 + experts, 128)
        self.own_hidden = FF // self.devices
        self.branches = 1 + experts
        self.hidden = self.branches * HALVES * self.own_hidden
        self.hidden_pad = round_up(self.hidden, 128)
        self.local = HALVES * block
        self.tiled = (
            self.own_hidden == 64
            and self.rows % 8 == 0
            and self.quad == 4
            and self.heads == 3
            and self.wide == self.qkv_cols + 64
        )


def place():
    return lax.axis_index("dp"), lax.axis_index("ctx")


def params(collective_id=None, limit=60 * 1024 * 1024):
    if collective_id is None:
        return pltpu.CompilerParams(vmem_limit_bytes=limit)
    return pltpu.CompilerParams(
        vmem_limit_bytes=limit, collective_id=collective_id, has_side_effects=True
    )


def remote(src, dst, send_sem, recv_sem, device):
    return pltpu.make_async_remote_copy(
        src_ref=src,
        dst_ref=dst,
        send_sem=send_sem,
        recv_sem=recv_sem,
        device_id=device,
        device_id_type=MESH,
    )


def busy(microseconds):
    return pl.CostEstimate(
        flops=0, bytes_accessed=int(microseconds * 3.4e6), transcendentals=0
    )


def meet(devices):
    barrier = pltpu.get_barrier_semaphore()
    for device in devices:
        pl.semaphore_signal(barrier, inc=1, device_id=device, device_id_type=MESH)
    pl.semaphore_wait(barrier, len(devices))


def other_devices(plan, dp, ctx):
    flat = dp * plan.ctx + ctx
    result = []
    for step in range(1, plan.devices):
        target = lax.rem(flat + step, plan.devices)
        result.append((lax.div(target, plan.ctx), lax.rem(target, plan.ctx)))
    return result


def quad_members(plan, half, member):
    return [
        (half * plan.quad + lax.rem(member + step, plan.quad), lax.rem(member + step, plan.quad))
        for step in range(1, plan.quad)
    ]


VMEM = pl.BlockSpec(memory_space=pltpu.VMEM)
HBM = pl.BlockSpec(memory_space=pl.ANY)
DMA = pltpu.SemaphoreType.DMA


def half_members(plan, mine):
    return [lax.rem(mine + step, plan.group) for step in range(1, plan.group)]


class Grid:
    def __init__(self, plan):
        self.plan = plan
        self.sizes = {"y": plan.dp // 2, "high": plan.quad // 2, "low": 2}

    def here(self):
        dp, ctx = place()
        member = lax.rem(ctx, self.plan.quad)
        return {
            "core": lax.rem(dp, 2),
            "y": lax.div(dp, 2),
            "high": lax.div(member, 2),
            "low": lax.rem(member, 2),
            "half": lax.div(ctx, self.plan.quad),
        }

    def device(self, at):
        return (
            at["y"] * 2 + at["core"],
            at["half"] * self.plan.quad + at["high"] * 2 + at["low"],
        )

    def block(self, at):
        return (at["y"] * 2 + at["core"]) * self.plan.quad + at["high"] * 2 + at["low"]

    def moved(self, at, axis, step):
        result = dict(at)
        if axis == "core":
            result["core"] = 1 - at["core"]
        else:
            result[axis] = lax.rem(at[axis] + step, self.sizes[axis])
        return result

    def peers(self, at):
        result = [self.moved(at, "core", 1)]
        for axis, size in self.sizes.items():
            result += [self.moved(at, axis, step) for step in range(1, size)]
        return [self.device(peer) for peer in result]

    def slot(self, offsets):
        return (offsets["y"] * self.sizes["high"] + offsets["high"]) * 2 + offsets["low"]


GATHER_ORDERS = (("high", "low", "y"), ("high", "y", "low"))


class Gather:
    def __init__(self, grid, at, src, dst, send, recv, core_send, core_recv):
        self.grid, self.at, self.src, self.dst = grid, at, src, dst
        self.send, self.recv, self.core_send, self.core_recv = send, recv, core_send, core_recv

    def groups(self, order):
        sizes = self.grid.sizes
        levels = [[{"y": 0, "high": 0, "low": 0}], [], [], []]
        for level, axis in enumerate(order):
            base = [o for group in levels[: level + 1] for o in group]
            levels[level + 1] = [
                {**offsets, axis: step} for offsets in base for step in range(1, sizes[axis])
            ]
        return levels

    def absolute(self, offsets):
        where = dict(self.at)
        for axis, step in offsets.items():
            if step:
                where = self.grid.moved(where, axis, step)
        return where

    def run_level(self, order, level):
        grid, at = self.grid, self.at
        index = 0
        for current, group in enumerate(self.groups(order)):
            for offsets in group:
                if current == level:
                    block = grid.block(self.absolute(offsets))
                    if level:
                        remote(
                            self.src,
                            self.dst.at[block],
                            self.send.at[0],
                            self.recv.at[grid.slot(offsets)],
                            grid.device(at),
                        ).wait_recv()
                    source = self.dst.at[block] if level else self.src
                    remote(
                        source,
                        self.dst.at[block],
                        self.core_send.at[grid.slot(offsets)],
                        self.core_recv.at[grid.slot(offsets)],
                        grid.device(grid.moved(at, "core", 1)),
                    ).start()
                for axis in order[current:]:
                    for step in range(1, grid.sizes[axis]):
                        if current == level:
                            seen = {**offsets, axis: grid.sizes[axis] - step}
                            remote(
                                source,
                                self.dst.at[block],
                                self.send.at[index],
                                self.recv.at[grid.slot(seen)],
                                grid.device(grid.moved(at, axis, step)),
                            ).start()
                        index += 1

    def level(self, level):
        for color, order in enumerate(GATHER_ORDERS):
            pl.when(self.at["core"] == color)(functools.partial(self.run_level, order, level))

    def finish(self):
        plan, here = self.grid.plan, self.grid.device(self.at)

        def sent(order):
            for index in range(gather_sends(plan, order)):
                remote(self.src, self.dst.at[0], self.send.at[index], self.recv.at[0], here).wait_send()

        for color, order in enumerate(GATHER_ORDERS):
            pl.when(self.at["core"] == color)(functools.partial(sent, order))
        for slot in range(plan.group // 2):
            remote(
                self.src, self.dst.at[0], self.core_send.at[slot], self.core_recv.at[slot], here
            ).wait()


def gather_kernel(plan, src, dst, send, recv, core_send, core_recv):
    grid = Grid(plan)
    at = grid.here()
    meet(grid.peers(at))
    dst[pl.ds(grid.block(at), 1)] = src[...][None]
    blocks = Gather(grid, at, src, dst, send, recv, core_send, core_recv)
    for level in range(4):
        blocks.level(level)
    blocks.finish()


def gather_sems(plan):
    half = plan.group // 2
    count = max(gather_sends(plan, order) for order in GATHER_ORDERS)
    return [DMA((count,)), DMA((half,)), DMA((half,)), DMA((half,))]


def gather_sends(plan, order):
    sizes = Grid(plan).sizes
    held, total = 1, 0
    for axis in order:
        total += held * (sizes[axis] - 1)
        held *= sizes[axis]
    return total


def gather(plan, block, collective_id):
    return pl.pallas_call(
        functools.partial(gather_kernel, plan),
        out_shape=jax.ShapeDtypeStruct((plan.group,) + block.shape, block.dtype),
        in_specs=[VMEM],
        out_specs=VMEM,
        scratch_shapes=gather_sems(plan),
        compiler_params=params(collective_id),
        cost_estimate=busy(35),
        name="gather",
    )(block)


def reduce_kernel(plan, src, out, work, core_buf, bufs, load_sem, core_send, core_recv, send, recv):
    grid = Grid(plan)
    at = grid.here()
    zero = {"y": 0, "high": 0, "low": 0}
    meet(grid.peers(at))

    def run(order):
        levels = [[], [], [], []]
        held = [dict(zero)]
        levels[3] = [dict(zero)]
        for level in (2, 1, 0):
            axis = order[level]
            base = [o for later in levels[level + 1 :] for o in later]
            levels[level] = [
                {**offsets, axis: step} for offsets in base for step in range(1, grid.sizes[axis])
            ]
        del held

        def absolute(offsets):
            where = dict(at)
            for axis, step in offsets.items():
                if step:
                    where = grid.moved(where, axis, step)
            return where

        sequence = [o for group in levels for o in group]
        partner = grid.device(grid.moved(at, "core", 1))
        core_copies = []
        loads = []
        for offsets in sequence:
            where = absolute(offsets)
            slot = grid.slot(offsets)
            copy = remote(
                src.at[grid.block(grid.moved(where, "core", 1))],
                core_buf.at[slot],
                core_send.at[slot],
                core_recv.at[slot],
                partner,
            )
            copy.start()
            core_copies.append(copy)
            load = pltpu.make_async_copy(
                src.at[grid.block(where)], work.at[slot], load_sem.at[slot]
            )
            load.start()
            loads.append(load)
        arrived = {}
        sends = []
        index = 0
        position = 0
        for level in range(4):
            for offsets in levels[level]:
                slot = grid.slot(offsets)
                core_copies[position].wait_recv()
                loads[position].wait()
                position += 1
                total = work[slot].astype(F32) + core_buf[slot].astype(F32)
                for buffer in arrived.get(slot, ()):
                    remote(work.at[slot], bufs.at[buffer], send.at[0], recv.at[buffer], partner).wait_recv()
                    total = total + bufs[buffer].astype(F32)
                if level == 3:
                    out[...] = total.astype(out.dtype)
                    continue
                work[slot] = total.astype(BF16)
                axis = order[level]
                step = offsets[axis]
                copy = remote(
                    work.at[slot],
                    bufs.at[index],
                    send.at[index],
                    recv.at[index],
                    grid.device(grid.moved(at, axis, step)),
                )
                copy.start()
                sends.append(copy)
                landing = grid.slot({**offsets, axis: 0})
                arrived.setdefault(landing, []).append(index)
                index += 1
        for copy in sends:
            copy.wait_send()
        for copy in core_copies:
            copy.wait_send()

    for color, order in enumerate(GATHER_ORDERS):
        pl.when(at["core"] == color)(functools.partial(run, order[::-1]))


def reduce(plan, blocks, collective_id):
    half = plan.group // 2
    shape = blocks.shape[1:]
    count = max(gather_sends(plan, order) for order in GATHER_ORDERS)
    return pl.pallas_call(
        functools.partial(reduce_kernel, plan),
        out_shape=jax.ShapeDtypeStruct(shape, F32),
        in_specs=[HBM],
        out_specs=VMEM,
        scratch_shapes=[
            pltpu.VMEM((half,) + shape, BF16),
            pltpu.VMEM((half,) + shape, BF16),
            pltpu.VMEM((count,) + shape, BF16),
            DMA((half,)),
            DMA((half,)),
            DMA((half,)),
            DMA((count,)),
            DMA((count,)),
        ],
        compiler_params=params(collective_id),
        name="reduce",
    )(blocks)


def nt(left, right):
    return lax.dot_general(left, right, (((1,), (1,)), ((), ())), preferred_element_type=F32)


def nn(left, right):
    return lax.dot_general(left, right, (((1,), (0,)), ((), ())), preferred_element_type=F32)


def tn(left, right):
    return lax.dot_general(left, right, (((0,), (0,)), ((), ())), preferred_element_type=F32)


def swapped_halves(value):
    lane = lax.broadcasted_iota(jnp.int32, value.shape, 1)
    first = lax.rem(lane, HEAD_DIM) < HEAD_DIM // 2
    half = HEAD_DIM // 2
    return jnp.where(
        first, pltpu.roll(value, 2 * HEAD_DIM - half, 1), pltpu.roll(value, half, 1)
    )


def masked_scores(q, k, first_row, length):
    scores = nt(q, k)
    row = lax.broadcasted_iota(jnp.int32, scores.shape, 0) + first_row
    col = lax.broadcasted_iota(jnp.int32, scores.shape, 1)
    return jnp.where((col <= row) & (col < length), scores, -1000000000.0)


def natural_rows(plan, blocks):
    flat = blocks.astype(F32).reshape(plan.devices * plan.pad_rows, blocks.shape[-1])
    if plan.pad_rows == plan.rows:
        return flat.astype(BF16)
    row = lax.broadcasted_iota(jnp.int32, (plan.width, flat.shape[0]), 0)
    col = lax.broadcasted_iota(jnp.int32, (plan.width, flat.shape[0]), 1)
    source = lax.div(row, plan.rows) * plan.pad_rows + lax.rem(row, plan.rows)
    return nn((col == source).astype(BF16), flat.astype(BF16)).astype(BF16)


def around_gains(plan, w_seq):
    first = plan.qkv_cols - (plan.wide - 128)
    return jnp.transpose(w_seq[:, plan.wide - 128 :].astype(F32), (1, 0))[first : first + 8]


def chosen(local, routes):
    row = lax.broadcasted_iota(jnp.int32, (8, local), 0).astype(F32)
    return row - 2.0 == routes


def owner_forward(plan, ctx, far, half, xs, w_seq, mixed, gysrc, w_tail, n2x, middle, gates, w_mix):
    block, local, width, cols = plan.block, plan.local, plan.width, plan.head_cols
    rows = plan.quad * plan.rows

    @pl.loop(0, HALVES * plan.dp)
    def _(i):
        turn = lax.rem(lax.rem(i, HALVES) + half, 2)
        value = w_tail[pl.ds(lax.div(i, HALVES) * plan.quad, plan.quad), pl.ds(turn, 1)]
        value = value[:, 0].astype(F32)[:, : plan.rows].reshape(rows, width)
        w_mix[pl.ds(pl.multiple_of(i * rows, 16), rows)] = value.astype(BF16)

    total = jnp.concatenate([xs[pl.ds(ctx, 1)][0], xs[pl.ds(far, 1)][0]], axis=0).astype(F32)
    for member in range(plan.quad):
        total = total + nn(
            mixed[member].reshape(local, cols), w_mix[member * cols : (member + 1) * cols]
        )
    middle[...] = total
    inverse = lax.rsqrt(jnp.mean(total * total, axis=-1, keepdims=True) + EPSILON)
    normed = (total * inverse * around_gains(plan, w_seq)[1:2]).astype(BF16)
    n2x[:local] = normed
    first = plan.qkv_cols - (plan.wide - 128)
    logits = jnp.transpose(nn(normed, w_seq[:, plan.wide - 128 :]), (1, 0))[first : first + 8]
    tail = gysrc[:, block + 16 :, :block].astype(F32)
    routes = [
        jnp.concatenate([tail[i, plan.rows - 16 + k : plan.rows - 15 + k] for i in range(2)], axis=1)
        for k in range(2)
    ]
    picks = [chosen(local, route) for route in routes]
    scores = [jnp.sum(jnp.where(pick, logits, 0.0), axis=0, keepdims=True) for pick in picks]
    top = jnp.maximum(scores[0], scores[1])
    raised = [jnp.exp(score - top) for score in scores]
    gate = [value / (raised[0] + raised[1]) for value in raised]
    mixing = jnp.where(picks[0], gate[0], 0.0) + jnp.where(picks[1], gate[1], 0.0)
    high = mixing.astype(BF16).astype(F32)
    row = lax.broadcasted_iota(jnp.int32, (8, local), 0)
    mix_rows = jnp.concatenate([jnp.where(row == 0, 1.0, high), mixing - high], axis=0)
    n2x[local:] = jnp.concatenate(
        [mix_rows.astype(BF16), jnp.zeros((MIX_ROWS, width - local), BF16)], axis=1
    )
    gates[...] = jnp.concatenate(gate + routes + [jnp.zeros((4, local), F32)], axis=0)


def owner_back(plan, n2g_sum, gates, n2x, gysrc, w_mix, mixed, middle, w_seq, dmixed, dwo, rows8, middle_grad):
    block, local, width, cols = plan.block, plan.local, plan.width, plan.head_cols
    around = around_gains(plan, w_seq)
    choice = n2g_sum[local : local + 8, :local]
    picks = [chosen(local, gates[2 + k : 3 + k]) for k in range(2)]
    gate = [gates[k : k + 1] for k in range(2)]
    taken = [jnp.sum(jnp.where(pick, choice, 0.0), axis=0, keepdims=True) for pick in picks]
    inner = gate[0] * taken[0] + gate[1] * taken[1]
    logit_grad = sum(
        jnp.where(picks[k], gate[k] * (taken[k] - inner), 0.0) for k in range(2)
    ).astype(BF16)
    router_grad = nn(logit_grad, n2x[:local])
    grad = n2g_sum[:local] + tn(logit_grad, around.astype(BF16))
    values = middle[...]
    inverse = lax.rsqrt(jnp.mean(values * values, axis=-1, keepdims=True) + EPSILON)
    gain_grad = jnp.sum(grad * values * inverse, axis=0, keepdims=True)
    row = lax.broadcasted_iota(jnp.int32, (8, width), 0)
    rows8[...] = jnp.where(row == 1, gain_grad, router_grad)
    scaled = grad * around[1:2]
    result = (
        gysrc[:, :block].reshape(local, width).astype(F32)
        + inverse * scaled
        - values * inverse * inverse * inverse * jnp.mean(scaled * values, axis=-1, keepdims=True)
    )
    middle_grad[...] = result
    upstream = result.astype(BF16)
    for member in range(plan.quad):
        part = nt(upstream, w_mix[member * cols : (member + 1) * cols])
        dmixed[member] = part.astype(BF16).reshape(2, block, cols)
    return upstream


def front_kernel(plan, length_ref, tok, wq, win, gyw, cosine, sine, xs, w_seq, normed, qk_out, v_out, lse_out, mixed, gyall, w_in, gysrc, *rest):
    owned, rest = (rest[:4], rest[4:]) if plan.tiled else ((), rest)
    front_body(plan, length_ref, tok, wq, win, gyw, cosine, sine, xs, w_seq, normed, qk_out, v_out, lse_out, mixed, gyall, w_in, gysrc, owned, *rest)


def front_body(plan, length_ref, tok, wq, win, gyw, cosine, sine, xs, w_seq, normed, qk_out, v_out, lse_out, mixed, gyall, w_in, gysrc, owned, wall, wqx, win_all, qkv, made, w_tail, x_send, x_recv, s_send, s_recv, q_send, q_recv, f_send, f_recv, z_send, z_recv, own_sem, tail_sem, m_send, m_recv, *gather_sem):
    dp, ctx = place()
    half, member = lax.div(ctx, plan.quad), lax.rem(ctx, plan.quad)
    far = (1 - half) * plan.quad + member
    flat, flat_far = dp * plan.ctx + ctx, dp * plan.ctx + far
    mine = dp * plan.quad + member
    grid = Grid(plan)
    spot = grid.here()
    here = (dp, ctx)
    across = (dp, far)
    targets = half_members(plan, mine)
    devices = [
        (lax.div(target, plan.quad), half * plan.quad + lax.rem(target, plan.quad))
        for target in targets
    ]
    members = quad_members(plan, half, member)
    highs, ys = grid.sizes["high"], grid.sizes["y"]
    meet(devices + [across])
    pending = []

    def send(*args):
        copy = remote(*args)
        copy.start()
        pending.append(copy)

    swap_x = remote(tok.at[1 - half], xs.at[ctx], s_send.at[0], s_recv.at[0], across)
    swap_w = remote(wq, wqx, s_send.at[1], s_recv.at[1], across)
    swap_gy = remote(gyw.at[1 - half], gysrc.at[1], s_send.at[2], s_recv.at[2], across)
    swap_x.start()
    swap_w.start()

    def member_of(high, low):
        return half * plan.quad + lax.rem(spot["high"] + high, highs) * 2 + lax.rem(spot["low"] + low, 2)

    def token_block(side, high):
        at = half if side == 0 else 1 - half
        return at * plan.quad + lax.rem(spot["high"] + high, highs) * 2 + spot["low"]

    def token_sends(side, source):
        block = token_block(side, 0)
        for step in range(1, highs):
            index = side * (highs - 1) + step - 1
            send(source, xs.at[block], x_send.at[0, index], x_recv.at[0, side, highs - step - 1], (dp, member_of(step, 0)))
        send(source, xs.at[block], x_send.at[1, side * highs], x_recv.at[1, side, 0], (dp, member_of(0, 1)))

    def token_forward(side):
        for high in range(1, highs):
            block = token_block(side, high)
            remote(xs.at[block], xs.at[block], x_send.at[0, 0], x_recv.at[0, side, high - 1], here).wait_recv()
            send(xs.at[block], xs.at[block], x_send.at[1, side * highs + high], x_recv.at[1, side, high], (dp, member_of(0, 1)))

    def slice_sends(side, source, block):
        for i, (peer, to) in enumerate(members):
            send(source.at[to], wall.at[block], q_send.at[0, side, i], q_recv.at[block], (dp, peer))

    core_device = grid.device(grid.moved(spot, "core", 1))
    counter = [0, 0]

    def slice_on(block, source, along_y):
        if along_y:
            for step in range(1, ys):
                send(source, wall.at[block], q_send.at[1, 0, counter[0]], q_recv.at[block], grid.device(grid.moved(spot, "y", step)))
                counter[0] += 1
        send(source, wall.at[block], q_send.at[1, 1, counter[1]], q_recv.at[block], core_device)
        counter[1] += 1

    def slice_wait(block):
        remote(wq.at[0], wall.at[block], q_send.at[0, 0, 0], q_recv.at[block], here).wait_recv()

    token_sends(0, tok.at[half])
    slice_sends(0, wq, flat)
    slice_on(flat, wq.at[member], True)
    gysrc[0] = gyw[pl.ds(half, 1)][0]
    xs[pl.ds(ctx, 1)] = tok[pl.ds(half, 1)]
    wall[pl.ds(flat, 1)] = wq[pl.ds(member, 1)]
    swap_x.wait()
    token_sends(1, xs.at[far])
    swap_w.wait()
    slice_sends(1, wqx, flat_far)
    slice_on(flat_far, wqx.at[member], True)
    swap_gy.start()
    token_forward(0)
    for i, (peer, _) in enumerate(members):
        block = dp * plan.ctx + peer
        slice_wait(block)
        slice_on(block, wall.at[block], True)
    token_forward(1)
    for _, to in members:
        block = dp * plan.ctx + (1 - half) * plan.quad + to
        slice_wait(block)
        slice_on(block, wall.at[block], True)
    wall[pl.ds(flat_far, 1)] = wqx[pl.ds(member, 1)]

    for i, (target, device) in enumerate(zip(targets, devices)):
        send(win.at[target], win_all.at[flat], f_send.at[i], f_recv.at[i], device)
    send(win.at[mine], win_all.at[flat], z_send.at[0], z_recv.at[0], across)
    win_all[pl.ds(flat, 1)] = win[pl.ds(mine, 1)]

    def columns_on(i):
        source = lax.rem(mine + plan.group - 1 - i, plan.group)
        block = lax.div(source, plan.quad) * plan.ctx + half * plan.quad + lax.rem(source, plan.quad)
        remote(win.at[0], win_all.at[block], f_send.at[0], f_recv.at[i], here).wait_recv()
        send(win_all.at[block], win_all.at[block], z_send.at[1 + i], z_recv.at[1 + i], across)

    for step in range(1, ys):
        other = lax.rem(spot["y"] + step, ys) * 2 + spot["core"]
        for place_ctx in range(plan.ctx):
            block = other * plan.ctx + place_ctx
            slice_wait(block)
            slice_on(block, wall.at[block], False)
    swap_gy.wait()
    gather = Gather(grid, spot, gysrc, gyall, *gather_sem)
    own = pltpu.make_async_copy(gysrc, gyall.at[grid.block(spot)], own_sem)
    own.start()
    gather.level(0)
    for y in range(ys):
        for place_ctx in range(plan.ctx):
            slice_wait((y * 2 + 1 - spot["core"]) * plan.ctx + place_ctx)
    for side in range(2):
        for high in range(highs):
            block = half if side == 0 else 1 - half
            block = block * plan.quad + lax.rem(spot["high"] + high, highs) * 2 + 1 - spot["low"]
            remote(xs.at[block], xs.at[block], x_send.at[0, 0], x_recv.at[1, side, high], here).wait_recv()

    length = length_ref[0]
    rows, block = QUERY_ROWS, plan.block
    slots = plan.slots
    w_seq[...] = natural_rows(plan, wall[...])
    tail = w_seq[:, plan.wide - 128 :].astype(F32)
    gain = jnp.transpose(tail, (1, 0))[plan.qkv_cols - plan.wide + 128 :][:1]

    @pl.loop(0, slots // rows)
    def _(i):
        at = pl.ds(pl.multiple_of(i * rows, rows), rows)
        values = xs[pl.ds(i * (rows // block), rows // block)].reshape(rows, plan.width)
        values = values.astype(F32)
        inverse = lax.rsqrt(jnp.mean(values * values, axis=-1, keepdims=True) + EPSILON)
        normed[at] = (values * inverse * gain).astype(BF16)
        qkv[at] = nn(normed[at], w_seq[...])
    heads = plan.heads
    qk_width = 2 * HEAD_DIM
    third = (plan.group - 1) // 3
    for i in range(third):
        columns_on(i)
    for head in range(heads):
        cols = slice(head * qk_width, (head + 1) * qk_width)
        qk = qkv[:, cols]
        qk_out[:, cols] = (qk * cosine[...] + swapped_halves(qk) * sine[...]).astype(BF16)
    v_cols = slice(heads * qk_width, heads * 3 * HEAD_DIM)
    v_out[...] = qkv[:, v_cols].astype(BF16)
    gather.level(1)
    for i in range(third, 2 * third):
        columns_on(i)

    def mixed_copy(index):
        side, to = divmod(index, plan.quad)
        turn = lax.rem(half + side, 2)
        return remote(
            made.at[index],
            mixed.at[member, turn],
            m_send.at[index],
            m_recv.at[member, turn],
            (dp, half * plan.quad + to),
        )

    spans = list(range(0, slots, rows))
    for number, start in enumerate(spans):
        at = slice(start, start + rows)
        end = start + rows
        for head in range(heads):
            base = head * qk_width
            q = qk_out[at, base : base + HEAD_DIM] * BF16(0.125)
            k = qk_out[:end, base + HEAD_DIM : base + qk_width]
            v = v_out[:end, head * HEAD_DIM : (head + 1) * HEAD_DIM]
            scores = masked_scores(q, k, start, length)
            top = jnp.max(scores, axis=-1, keepdims=True)
            raised = jnp.exp(scores - top)
            total = jnp.sum(raised, axis=-1, keepdims=True)
            lse_out[head, at] = top + jnp.log(total)
            probs = (raised * (1.0 / total)).astype(BF16)
            part = nn(probs, v).astype(BF16)
            for i in range(rows // block):
                made[start // block + i, :, head * HEAD_DIM : (head + 1) * HEAD_DIM] = part[
                    i * block : (i + 1) * block
                ]
        for i in range(rows // block):
            index = start // block + i
            pl.when(member != index % plan.quad)(lambda index=index: mixed_copy(index).start())

            @pl.when(member == index % plan.quad)
            def _(index=index):
                turn = lax.rem(half + index // plan.quad, 2)
                mixed[pl.ds(member, 1), pl.ds(turn, 1)] = made[index][None, None]

        if number == len(spans) // 2:
            for i in range(2 * third, plan.group - 1):
                columns_on(i)
            gather.level(2)
    gather.level(3)
    for index in range(plan.ctx):
        pl.when(member != index % plan.quad)(lambda index=index: mixed_copy(index).wait_send())
    for source in range(plan.quad):

        @pl.when(member != source)
        def _(source=source):
            for turn in range(2):
                remote(
                    made.at[0], mixed.at[source, turn], m_send.at[0], m_recv.at[source, turn], here
                ).wait_recv()

    gather.finish()
    own.wait()
    if owned:
        load = pltpu.make_async_copy(gyall.at[:, :, plan.block :], w_tail, tail_sem)
        load.start()
        load.wait()
        owner_forward(plan, ctx, far, half, xs, w_seq, mixed, gysrc, w_tail, *owned)
    for copy in pending:
        copy.wait_send()
    for i in range(plan.group):
        remote(win.at[0], win_all.at[0], z_send.at[0], z_recv.at[i], here).wait_recv()
    pad, hidden = plan.pad_rows, plan.hidden_pad
    if plan.tiled:
        count = plan.quad * plan.rows

        @pl.loop(0, plan.devices // plan.quad)
        def _(i):
            at = pl.ds(pl.multiple_of(i * count, 16), count)
            value = win_all[pl.ds(i * plan.quad, plan.quad)].astype(F32)
            for gate in range(2):
                part = value[:, gate * pad : (gate + 1) * pad].reshape(count, hidden)
                w_in[at, gate * hidden : (gate + 1) * hidden] = part.astype(BF16)

    else:
        w_in[:, :hidden] = natural_rows(plan, win_all[:, :pad])
        w_in[:, hidden:] = natural_rows(plan, win_all[:, pad:])


def front(plan, length, tok, wq, win, gyw, cosine, sine, collective_id):
    slots, heads, block, width = plan.slots, plan.heads, plan.block, plan.width
    highs, ys = plan.quad // 2, plan.dp // 2
    owned = (
        jax.ShapeDtypeStruct((plan.local + MIX_ROWS, width), BF16),
        jax.ShapeDtypeStruct((plan.local, width), F32),
        jax.ShapeDtypeStruct((8, plan.local), F32),
        jax.ShapeDtypeStruct((width, width), BF16),
    )
    on = max(2 * plan.quad * max(ys - 1, 1), 2 * plan.quad + (ys - 1) * plan.ctx, plan.quad)
    return pl.pallas_call(
        functools.partial(front_kernel, plan),
        out_shape=(
            jax.ShapeDtypeStruct((plan.ctx, block, width), BF16),
            jax.ShapeDtypeStruct((width, plan.wide), BF16),
            jax.ShapeDtypeStruct((slots, width), BF16),
            jax.ShapeDtypeStruct((slots, 2 * plan.head_cols), BF16),
            jax.ShapeDtypeStruct((slots, plan.head_cols), BF16),
            jax.ShapeDtypeStruct((heads, slots, 1), F32),
            jax.ShapeDtypeStruct((plan.quad, 2, block, plan.head_cols), BF16),
            jax.ShapeDtypeStruct((plan.group, 2) + gyw.shape[1:], BF16),
            jax.ShapeDtypeStruct((width, 2 * plan.hidden_pad), BF16),
            jax.ShapeDtypeStruct(gyw.shape, BF16),
        )
        + (owned if plan.tiled else ()),
        in_specs=[pl.BlockSpec(memory_space=pltpu.SMEM)] + [VMEM] * 6,
        out_specs=(VMEM,) * 7 + (HBM,) + (VMEM,) * (6 if plan.tiled else 2),
        scratch_shapes=[
            pltpu.VMEM((plan.devices,) + wq.shape[1:], BF16),
            pltpu.VMEM(wq.shape, BF16),
            pltpu.VMEM((plan.devices,) + win.shape[1:], BF16),
            pltpu.VMEM((slots, plan.wide), F32),
            pltpu.VMEM((plan.ctx, block, plan.head_cols), BF16),
            pltpu.VMEM((plan.group, 2, gyw.shape[1] - block, width), BF16),
            DMA((2, 2 * highs)),
            DMA((2, 2, highs)),
            DMA((3,)),
            DMA((3,)),
            DMA((2, 2, on)),
            DMA((plan.devices,)),
            DMA((plan.group - 1,)),
            DMA((plan.group - 1,)),
            DMA((plan.group,)),
            DMA((plan.group,)),
            DMA,
            DMA,
            DMA((plan.ctx,)),
            DMA((plan.quad, 2)),
        ]
        + gather_sems(plan),
        compiler_params=params(collective_id),
        cost_estimate=busy(90),
        name="front",
    )(length, tok, wq, win, gyw, cosine, sine)


OUT_ORDERS = (("low", "y", "high"), ("y", "low", "high"))


class OutSum:
    def __init__(self, grid, at, src, work, core_buf, bufs, load_sem, core_send, core_recv, send, recv):
        self.grid, self.at, self.src = grid, at, src
        self.work, self.core_buf, self.bufs = work, core_buf, bufs
        self.load_sem, self.core_send, self.core_recv = load_sem, core_send, core_recv
        self.send, self.recv = send, recv
        self.loaded = set()
        rows = work.shape[1] // 2
        self.rows = [slice(0, rows), slice(rows, 2 * rows)]
        self.index = [
            {o: i for i, o in enumerate(o for o in STEP_ORDER if any(o))} for _ in OUT_ORDERS
        ]

    def pair(self, offset):
        where = dict(self.at)
        for axis, step in named(offset).items():
            if step:
                where = self.grid.moved(where, axis, step)
        slot = self.grid.slot(named(offset))
        partner = self.grid.device(self.grid.moved(self.at, "core", 1))
        away = remote(
            self.src.at[self.grid.block(self.grid.moved(where, "core", 1))],
            self.core_buf.at[slot],
            self.core_send.at[slot],
            self.core_recv.at[slot],
            partner,
        )
        load = pltpu.make_async_copy(
            self.src.at[self.grid.block(where)], self.work.at[slot], self.load_sem.at[slot]
        )
        return away, load

    def start(self):
        for offset in STEP_ORDER[::-1]:
            for copy in self.pair(offset):
                copy.start()

    def onward(self, part, offset, axis):
        index, rows = self.index[part][offset], self.rows[part]
        return remote(
            self.work.at[self.grid.slot(named(offset)), rows],
            self.bufs.at[index, rows],
            self.send.at[part, index],
            self.recv.at[part, index],
            self.grid.device(self.grid.moved(self.at, axis, 1)),
        )

    def phase(self, number):
        for offset in STEP_ORDER:
            for part, order in enumerate(OUT_ORDERS):
                phase, feeds = feeds_of(order, offset)
                if phase != number:
                    continue
                if offset not in self.loaded:
                    self.loaded.add(offset)
                    for copy in self.pair(offset):
                        copy.wait()
                for feed, axis in zip(feeds, order):
                    self.onward(part, feed, axis).wait_recv()
                slot, rows = self.grid.slot(named(offset)), self.rows[part]

                @pl.loop(0, (rows.stop - rows.start) // 16)
                def _(i, slot=slot, part=part, feeds=feeds, start=rows.start):
                    span = pl.ds(pl.multiple_of(start + i * 16, 16), 16)
                    value = self.work[slot, span].astype(F32)
                    value = value + self.core_buf[slot, span].astype(F32)
                    for feed in feeds:
                        value = value + self.bufs[self.index[part][feed], span].astype(F32)
                    self.work[slot, span] = value.astype(BF16)

                if number < 3:
                    self.onward(part, offset, order[number]).start()

    def finish(self):
        for offset in STEP_ORDER:
            for part, order in enumerate(OUT_ORDERS):
                phase, _ = feeds_of(order, offset)
                if phase < 3:
                    self.onward(part, offset, order[phase]).wait_send()


class Fold:
    def __init__(self, plan, src, dst, core_buf, y_buf, added, sems):
        self.plan, self.src, self.dst = plan, src, dst
        self.core_buf, self.y_buf, self.added = core_buf, y_buf, added
        self.core_send, self.core_recv, self.y_send, self.y_recv, self.send, self.recv = sems
        self.dp, self.ctx = place()
        self.core, self.y = lax.rem(self.dp, 2), lax.div(self.dp, 2)
        self.ys = plan.dp // 2

    def core_copies(self):
        partner = (self.dp + 1 - 2 * self.core, self.ctx)
        return [
            remote(
                self.src.at[y * 2 + 1 - self.core],
                self.core_buf.at[y],
                self.core_send.at[y],
                self.core_recv.at[y],
                partner,
            )
            for y in range(self.ys)
        ]

    def y_copies(self):
        copies = []
        for step in range(1, self.ys):
            to = lax.rem(self.y + step, self.ys)
            copies.append(
                remote(
                    self.core_buf.at[to],
                    self.y_buf.at[step - 1],
                    self.y_send.at[step - 1],
                    self.y_recv.at[step - 1],
                    (to * 2 + self.core, self.ctx),
                )
            )
        return copies

    def owner_copies(self):
        copies = []
        for step in range(1, self.plan.ctx):
            to = lax.rem(self.ctx + step, self.plan.ctx)
            copies.append(
                remote(
                    self.added.at[to],
                    self.dst.at[self.ctx],
                    self.send.at[step - 1],
                    self.recv.at[step - 1],
                    (self.dp, to),
                )
            )
        return copies

    def start(self):
        for copy in self.core_copies():
            copy.start()

    def along_y(self):
        for copy in self.core_copies():
            copy.wait()

        @pl.loop(0, self.plan.ctx)
        def _(i):
            for y in range(self.ys):
                mine = self.src[y * 2 + self.core, i].astype(F32)
                self.core_buf[y, i] = (mine + self.core_buf[y, i].astype(F32)).astype(BF16)

        for copy in self.y_copies():
            copy.start()

    def to_owners(self):
        for copy in self.y_copies():
            copy.wait()

        @pl.loop(0, self.plan.ctx)
        def _(i):
            total = self.core_buf[self.y, i].astype(F32)
            for step in range(1, self.ys):
                total = total + self.y_buf[step - 1, i].astype(F32)
            self.added[i] = total.astype(BF16)

        for copy in self.owner_copies():
            copy.start()
        self.dst[pl.ds(self.ctx, 1)] = self.added[pl.ds(self.ctx, 1)]

    def finish(self):
        for copy in self.owner_copies():
            copy.wait()


def padded_rows(plan, value, count):
    if plan.pad_rows != plan.rows:
        row = lax.broadcasted_iota(jnp.int32, (count * plan.pad_rows, count * plan.rows), 0)
        col = lax.broadcasted_iota(jnp.int32, (count * plan.pad_rows, count * plan.rows), 1)
        inside = lax.rem(row, plan.pad_rows)
        wanted = lax.div(row, plan.pad_rows) * plan.rows + inside
        hit = (col == wanted) & (inside < plan.rows)
        value = nn(hit.astype(BF16), value.astype(BF16))
    return value.reshape(count, plan.pad_rows, value.shape[-1])


def fold_scratch(plan, rows, width):
    shape = (plan.ctx, rows, width)
    ys = plan.dp // 2
    return [
        pltpu.VMEM((ys,) + shape, BF16),
        pltpu.VMEM((max(ys - 1, 1),) + shape, BF16),
        pltpu.VMEM(shape, BF16),
        DMA((ys,)),
        DMA((ys,)),
        DMA((max(ys - 1, 1),)),
        DMA((max(ys - 1, 1),)),
        DMA((plan.ctx - 1,)),
        DMA((plan.ctx - 1,)),
    ]


def back_kernel(plan, summed, length_ref, x, w, cosine, sine, normed, qk_in, v_in, lse, dw_in, dw_out, out_part, middle, *rest):
    given = 6 if plan.tiled else 4
    back_body(plan, summed, length_ref, x, w, cosine, sine, normed, qk_in, v_in, lse, dw_in, dw_out, out_part, middle, rest[:given], *rest[given:])


def back_body(plan, summed, length_ref, x, w, cosine, sine, normed, qk_in, v_in, lse, dw_in, dw_out, out_part, middle, given, rwq, rwo, rwin, far_out, act_out, grad_out, dqkv, dk_acc, dv_acc, upstream_all, dnp, rdn, dwq, far_in, dealt, out_away, grad_away, act_away, d_send, d_recv, n_send, n_recv, w_send, w_recv, e_send, e_recv, s_send, s_recv, *refs):
    dp, ctx = place()
    core, y = lax.rem(dp, 2), lax.div(dp, 2)
    half, member = lax.div(ctx, plan.quad), lax.rem(ctx, plan.quad)
    far = (1 - half) * plan.quad + member
    mine = dp * plan.quad + member
    across = (dp, far)
    members = quad_members(plan, half, member)
    targets = half_members(plan, mine)
    devices = [
        (lax.div(target, plan.quad), half * plan.quad + lax.rem(target, plan.quad))
        for target in targets
    ]
    meet(
        devices
        + [across]
        + [
            (dp, (1 - half) * plan.quad + lax.rem(member + step, plan.quad))
            for step in range(1, plan.quad)
        ]
    )
    fold_refs, out_refs = refs[:18], refs[18:]
    out_sum = None
    if not summed:
        grid = Grid(plan)
        out_sum = OutSum(grid, grid.here(), out_part, *out_refs[:8])
        out_sum.start()
    if plan.tiled:
        n2g_sum, gates, n2x, gysrc, w_mix, mixed = given
        dmixed, dwo, rows8, middle_grad = out_refs[8:]
        attn_grad = owner_back(plan, n2g_sum, gates, n2x, gysrc, w_mix, mixed, middle, w, *out_refs[8:])
    else:
        dmixed, dwo, small, middle_grad = given
    arriving = []
    for i, (peer, to) in enumerate(members):
        for j, at in enumerate((ctx, far)):
            copy = remote(
                dmixed.at[to, j],
                upstream_all.at[at],
                d_send.at[2 * i + j],
                d_recv.at[2 * i + j],
                (dp, peer),
            )
            copy.start()
            arriving.append(copy)
    count = len(fold_refs) // 2
    mix_fold = Fold(plan, dwo, rwo, *fold_refs[:3], fold_refs[3:count])
    qkv_fold = Fold(plan, dwq, rwq, *fold_refs[count : count + 3], fold_refs[count + 3 :])
    if plan.tiled:
        for i in range(plan.quad):
            part = tn(mixed[i].reshape(plan.local, plan.head_cols), attn_grad)
            dwo[i] = padded_rows(plan, part, plan.ctx).astype(BF16)
    mix_fold.start()
    swaps = [
        remote(dw_in.at[2 * i + 1 - half], far_in.at[i], w_send.at[i], w_recv.at[i], across)
        for i in range(plan.dp)
    ]
    hidden, pad = plan.hidden_pad, plan.pad_rows

    def deal_copy(target):
        tdp, tmember = divmod(target, plan.quad)
        return remote(
            dealt.at[target],
            rwin.at[mine],
            e_send.at[target],
            e_recv.at[mine],
            (tdp, half * plan.quad + tmember),
        )

    def deal(i):
        swaps[i].wait()
        value = dw_in[pl.ds(2 * i + half, 1)][0].astype(F32) + far_in[i].astype(F32)
        value = padded_rows(plan, value, plan.quad)
        value = jnp.concatenate([value[:, :, :hidden], value[:, :, hidden:]], axis=1)
        dealt[i * plan.quad : (i + 1) * plan.quad] = value.astype(BF16)
        for target in range(i * plan.quad, (i + 1) * plan.quad):
            pl.when(mine != target)(lambda target=target: deal_copy(target).start())

            @pl.when(mine == target)
            def _(target=target):
                rwin[target] = dealt[target]

    for copy in swaps:
        copy.start()
    out_away[...] = dw_out[:, pl.ds(1 - half, 1)][:, 0].astype(BF16)
    swap_out = remote(out_away, far_out, s_send.at[2], s_recv.at[2], across)
    upstream_all[pl.ds(ctx, 1)] = dmixed[pl.ds(member, 1), 0]
    upstream_all[pl.ds(far, 1)] = dmixed[pl.ds(member, 1), 1]
    length = length_ref[0]
    rows, slots, heads, block = QUERY_ROWS, plan.slots, plan.heads, plan.block
    qk_width = 2 * HEAD_DIM
    dqkv[...] = jnp.zeros_like(dqkv)
    for copy in arriving:
        copy.wait()

    def token_copy(index):
        side, to = divmod(index, plan.quad)
        turn = lax.rem(half + side, 2)
        return remote(
            dnp.at[index],
            rdn.at[member, turn],
            n_send.at[index],
            n_recv.at[member, turn],
            (dp, half * plan.quad + to),
        )

    gains = jnp.zeros((1, plan.width), F32)
    spans = list(range(slots - rows, -1, -rows))
    for number, start in enumerate(spans):
        at = slice(start, start + rows)
        end = start + rows
        for head in range(heads):
            base = head * qk_width
            v_cols = slice(head * HEAD_DIM, (head + 1) * HEAD_DIM)
            q = qk_in[at, base : base + HEAD_DIM] * BF16(0.125)
            k = qk_in[:end, base + HEAD_DIM : base + qk_width]
            v = v_in[:end, v_cols]
            upstream = jnp.concatenate(
                [upstream_all[start // block + i, :, v_cols] for i in range(rows // block)], axis=0
            )
            probs = jnp.exp(masked_scores(q, k, start, length) - lse[head, at])
            dv = tn(probs.astype(BF16), upstream)
            prob_grad = nt(upstream, v)
            inner = jnp.sum(probs * prob_grad, axis=-1, keepdims=True)
            score_grad = (probs * (prob_grad - inner)).astype(BF16)
            dq = nn(score_grad, k) * 0.125
            dk = tn(score_grad, q)
            if end == slots:
                dk_acc[head] = dk
                dv_acc[head] = dv
            else:
                dk_acc[head, :end] += dk
                dv_acc[head, :end] += dv
            dqk = jnp.concatenate([dq, dk_acc[head, at]], axis=-1)
            dqkv[at, base : base + qk_width] = (
                dqk * cosine[at] - swapped_halves(dqk) * sine[at]
            ).astype(BF16)
            v_base = heads * qk_width + head * HEAD_DIM
            dqkv[at, v_base : v_base + HEAD_DIM] = dv_acc[head, at].astype(BF16)
        part = nt(dqkv[at], w[...])
        for i in range(rows // block):
            index = start // block + i
            dnp[index] = part[i * block : (i + 1) * block].astype(BF16)
            pl.when(member != index % plan.quad)(lambda index=index: token_copy(index).start())

            @pl.when(member == index % plan.quad)
            def _(index=index):
                turn = lax.rem(half + index // plan.quad, 2)
                rdn[pl.ds(member, 1), pl.ds(turn, 1)] = dnp[index][None, None]

        values = x[at].astype(F32)
        inverse = lax.rsqrt(jnp.mean(values * values, axis=-1, keepdims=True) + EPSILON)
        gains = gains + jnp.sum(part * values * inverse, axis=0, keepdims=True)
        if number == 0:
            mix_fold.along_y()
            if out_sum:
                out_sum.phase(0)
        if number == len(spans) - 2:
            mix_fold.to_owners()
            if out_sum:
                out_sum.phase(1)
    swap_out.start()
    deal(0)
    first = plan.qkv_cols - (plan.wide - 128)
    if plan.tiled:
        row = lax.broadcasted_iota(jnp.int32, (8, plan.width), 0)
        ends = [jnp.zeros((n, plan.width), F32) for n in (first, 120 - first)]
        extra = jnp.concatenate([ends[0], jnp.where(row == 0, gains, rows8[...]), ends[1]], axis=0)
        extra = jnp.transpose(extra, (1, 0))
    else:
        column = jnp.transpose(jnp.broadcast_to(gains, (128, plan.width)), (1, 0))
        lane = lax.broadcasted_iota(jnp.int32, column.shape, 1)
        extra = jnp.where(lane == first, column, small[...])
    last = plan.wide // 128 - 1

    @pl.loop(0, last + 1)
    def _(i):
        cols = pl.ds(pl.multiple_of(i * 128, 128), 128)
        value = tn(normed[...], dqkv[:, cols])
        value = jnp.where(i == last, value + extra, value)
        value = padded_rows(plan, value, plan.devices).astype(BF16)
        dwq[:, :, :, cols] = value.reshape(plan.dp, plan.ctx, plan.pad_rows, 128)

    qkv_fold.start()
    local, width = plan.local, plan.width
    if out_sum:
        out_sum.phase(2)
    for source in range(plan.quad):

        @pl.when(member != source)
        def _(source=source):
            for turn in range(2):
                remote(
                    dnp.at[0], rdn.at[source, turn], n_send.at[0], n_recv.at[source, turn], (dp, ctx)
                ).wait_recv()

    gain_row = around_gains(plan, w)[:1]
    piece = 32

    for j, own in enumerate((ctx, far)):

        @pl.loop(0, block // piece)
        def _(i, j=j, own=own):
            rows_in = pl.ds(pl.multiple_of(i * piece, piece), piece)
            total = rdn[0, j, rows_in].astype(F32)
            for source in range(1, plan.quad):
                total = total + rdn[source, j, rows_in].astype(F32)
            values = x[pl.ds(pl.multiple_of(own * block + i * piece, piece), piece)].astype(F32)
            inverse = lax.rsqrt(jnp.mean(values * values, axis=-1, keepdims=True) + EPSILON)
            scaled = total * gain_row
            result = (
                middle_grad[pl.ds(pl.multiple_of(j * block + i * piece, piece), piece)]
                + inverse * scaled
                - values
                * inverse
                * inverse
                * inverse
                * jnp.mean(scaled * values, axis=-1, keepdims=True)
            )
            if j == 0:
                grad_out[pl.ds(half, 1), rows_in] = result.astype(BF16)[None]
            else:
                grad_away[rows_in] = result.astype(BF16)

    swap_grad = remote(grad_away, grad_out.at[half], s_send.at[1], s_recv.at[1], across)
    swap_grad.start()
    qkv_fold.along_y()
    if out_sum:
        out_sum.phase(3)
    branches = out_sum.work.at[0] if out_sum else out_part

    for j in range(2):

        @pl.loop(0, block // piece)
        def _(i, j=j):
            rows_in = pl.ds(pl.multiple_of(i * piece, piece), piece)
            rows_all = pl.ds(pl.multiple_of(j * block + i * piece, piece), piece)
            value = (middle[rows_all] + branches[rows_all].astype(F32)).astype(BF16)
            if j == 0:
                act_out[pl.ds(half, 1), rows_in] = value[None]
            else:
                act_away[rows_in] = value

    swap_act = remote(act_away, act_out.at[half], s_send.at[0], s_recv.at[0], across)
    swap_act.start()
    for i in range(1, plan.dp):
        deal(i)
        if i == 1:
            qkv_fold.to_owners()
    mix_fold.finish()
    qkv_fold.finish()
    swap_act.wait()
    swap_grad.wait()
    swap_out.wait()
    for target in range(plan.group):

        @pl.when(mine != target)
        def _(target=target):
            deal_copy(target).wait_send()
            remote(
                dealt.at[0], rwin.at[target], e_send.at[0], e_recv.at[target], (dp, ctx)
            ).wait_recv()

    for index in range(plan.ctx):
        pl.when(member != index % plan.quad)(lambda index=index: token_copy(index).wait_send())
    if out_sum:
        out_sum.finish()


def back(plan, length, x, w, cosine, sine, normed, qk, v, lse, dw_in, dw_out, out_part, middle, given, collective_id):
    slots, block, width = plan.slots, plan.block, plan.width
    count = 2 * (plan.quad - 1)
    dealt = (plan.group, 2 * plan.pad_rows, plan.hidden_pad)
    summed = out_part.ndim == 2
    rows = (plan.local, width)
    out_scratch = [
        pltpu.VMEM((8,) + rows, BF16),
        pltpu.VMEM((8,) + rows, BF16),
        pltpu.VMEM((7,) + rows, BF16),
        DMA((8,)),
        DMA((8,)),
        DMA((8,)),
        DMA((2, 7)),
        DMA((2, 7)),
        pltpu.VMEM((plan.quad, 2, block, plan.head_cols), BF16),
        pltpu.VMEM((plan.dp, plan.ctx, plan.rows, width), BF16),
        pltpu.VMEM((8, width), F32),
        pltpu.VMEM((plan.local, width), F32),
    ]
    return pl.pallas_call(
        functools.partial(back_kernel, plan, summed),
        out_shape=(
            jax.ShapeDtypeStruct((plan.ctx, plan.pad_rows, plan.wide), BF16),
            jax.ShapeDtypeStruct((plan.ctx, plan.rows, width), BF16),
            jax.ShapeDtypeStruct(dealt, BF16),
            jax.ShapeDtypeStruct((plan.branches, plan.own_hidden, width), BF16),
            jax.ShapeDtypeStruct((2, block, width), BF16),
            jax.ShapeDtypeStruct((2, block, width), BF16),
        ),
        in_specs=[pl.BlockSpec(memory_space=pltpu.SMEM)]
        + [VMEM] * 10
        + [VMEM if summed else HBM]
        + [VMEM] * (1 + len(given)),
        out_specs=(VMEM,) * 6,
        scratch_shapes=[
            pltpu.VMEM((slots, plan.wide), BF16),
            pltpu.VMEM((plan.heads, slots, HEAD_DIM), F32),
            pltpu.VMEM((plan.heads, slots, HEAD_DIM), F32),
            pltpu.VMEM((plan.ctx, block, plan.head_cols), BF16),
            pltpu.VMEM((plan.ctx, block, width), BF16),
            pltpu.VMEM((plan.quad, 2, block, width), BF16),
            pltpu.VMEM((plan.dp, plan.ctx, plan.pad_rows, plan.wide), BF16),
            pltpu.VMEM((plan.dp,) + dw_in.shape[1:], BF16),
            pltpu.VMEM(dealt, BF16),
            pltpu.VMEM((plan.branches, plan.own_hidden, width), BF16),
            pltpu.VMEM((block, width), BF16),
            pltpu.VMEM((block, width), BF16),
            DMA((count,)),
            DMA((count,)),
            DMA((plan.ctx,)),
            DMA((plan.quad, 2)),
            DMA((plan.dp,)),
            DMA((plan.dp,)),
            DMA((plan.group,)),
            DMA((plan.group,)),
            DMA((3,)),
            DMA((3,)),
        ]
        + fold_scratch(plan, plan.rows, width)
        + fold_scratch(plan, plan.pad_rows, plan.wide)
        + ([] if summed else out_scratch),
        compiler_params=params(collective_id),
        cost_estimate=busy(90),
        name="back",
    )(length, x, w, cosine, sine, normed, qk, v, lse, dw_in, dw_out, out_part, middle, *given)


def ffn_kernel(plan, members, n2x, gy, w_in, w_out, pick, out, n2g, dw_in, dw_out):
    hidden, local = plan.hidden_pad, plan.local

    @pl.when(pl.program_id(0) == 0)
    def start():
        dw_in[...] = jnp.zeros_like(dw_in)
        dw_out[...] = jnp.zeros_like(dw_out)

    tokens = members * local
    width = plan.width
    normed = n2x[:, :local].reshape(tokens, width)
    upstream = gy[:, :, : plan.block].reshape(tokens, width)
    mixing = jnp.concatenate(
        [tn(n2x[i, local:, :local], pick[...]) for i in range(members)], axis=0
    )
    pre = nn(normed, w_in[...])
    gate, up = pre[:, :hidden], pre[:, hidden:]
    sigmoid = jax.nn.sigmoid(gate)
    silu = gate * sigmoid
    act = (silu * up).astype(BF16).astype(F32)
    act_mixed = (act * mixing).astype(BF16)
    out[...] = nn(act_mixed, w_out[...]).astype(BF16).reshape(members, local, width)
    act_grad = nt(upstream, w_out[...])
    choice = nt(pick[...], (act * act_grad).astype(BF16)).astype(BF16)
    act_grad = act_grad * mixing
    gate_grad = act_grad * up * sigmoid * (1.0 + gate * (1.0 - sigmoid))
    pre_grad = jnp.concatenate([gate_grad, act_grad * silu], axis=-1).astype(BF16)
    n2g[:, :local] = nt(pre_grad, w_in[...]).astype(BF16).reshape(members, local, width)
    pad = jnp.zeros((MIX_ROWS, width - local), BF16)
    for i in range(members):
        n2g[i, local:] = jnp.concatenate(
            [choice[:, i * local : (i + 1) * local], pad], axis=-1
        )
    dw_in[...] += tn(normed, pre_grad)
    dw_out[...] += tn(act_mixed, upstream)


def ffn(plan, n2x, gy, w_in, w_out, pick):
    members = 2
    local, width, hidden = plan.local, plan.width, plan.hidden_pad
    whole = lambda i: (0, 0)
    part = lambda i: (i, 0, 0)
    return pl.pallas_call(
        functools.partial(ffn_kernel, plan, members),
        grid=(plan.group // members,),
        out_shape=(
            jax.ShapeDtypeStruct((plan.group, local, width), BF16),
            jax.ShapeDtypeStruct((plan.group, local + MIX_ROWS, width), BF16),
            jax.ShapeDtypeStruct((width, 2 * hidden), F32),
            jax.ShapeDtypeStruct((hidden, width), F32),
        ),
        in_specs=[
            pl.BlockSpec((members, local + MIX_ROWS, width), part),
            pl.BlockSpec((members,) + gy.shape[1:], lambda i: (i, 0, 0, 0)),
            pl.BlockSpec((width, 2 * hidden), whole),
            pl.BlockSpec((hidden, width), whole),
            pl.BlockSpec((MIX_ROWS, hidden), whole),
        ],
        out_specs=(
            pl.BlockSpec((members, local, width), part),
            pl.BlockSpec((members, local + MIX_ROWS, width), part),
            pl.BlockSpec((width, 2 * hidden), whole),
            pl.BlockSpec((hidden, width), whole),
        ),
        compiler_params=params(),
        name="ffn",
    )(n2x, gy, w_in, w_out, pick)


STEP_ORDER = ((0, 0, 0), (0, 0, 1), (0, 1, 0), (1, 0, 1), (1, 1, 0), (1, 1, 1), (0, 1, 1), (1, 0, 0))
PART_ORDERS = (("high", "low", "y"), ("low", "y", "high"), ("y", "high", "low"))
PAUSES = {
    3: (('g0', 7), ('g0', 2), ('g0', 1), ('g1', 1), ('g2', 1)),
    4: (('g1', 2), ('g2', 7), ('g2', 2), ('g1', 7)),
    5: (('g0', 4), ('g0', 3), ('g1', 3)),
    7: (('g2', 3), ('g0', 6), ('g2', 6), ('s2', 1)),
    8: (('g1', 4), ('g2', 4)),
    9: (('g1', 6),),
    10: (('s1', 2),),
    11: (('g0', 5), ('g2', 5)),
    13: (('g1', 5), ('s0', 3), ('s2', 3)),
    16: (('s0', 4), ('s1', 4)),
    19: (('s0', 5), ('s1', 5), ('s2', 5)),
    20: (('s0', 2),),
    22: (('s1', 6), ('s2', 6)),
    23: (('s1', 3), ('s2', 4), ('s0', 6)),
    24: (('s0', 7), ('s2', 7), ('s1', 1), ('s2', 2), ('s1', 7), ('s0', 1), ('s2', 0), ('s0', 0), ('s1', 0)),
}


def part_rows(rows):
    cuts = [round_up(rows * i // 3, 16) for i in range(3)] + [rows]
    return [slice(a, b) for a, b in zip(cuts, cuts[1:])]


def named(offset):
    return dict(zip(("high", "low", "y"), offset))


def feeds_of(order, offset):
    at = named(offset)
    phase = min([i for i, axis in enumerate(order) if at[axis]], default=3)
    names = ("high", "low", "y")
    return phase, [tuple(1 if n == axis else at[n] for n in names) for axis in order[:phase]]


def fused_kernel(plan, n2x, gy, w_in, w_out, pick, total, dw_in, dw_out, out_all, n2all, gybuf, acc, away, work, core_buf, bufs, outbuf, gy_sem, out_sem, g_send, g_recv, gc_send, gc_recv, c_send, c_recv, r_send, r_recv):
    grid = Grid(plan)
    at = grid.here()
    local, width, hidden = plan.local, plan.width, plan.hidden_pad
    steps = len(STEP_ORDER)
    partner = grid.device(grid.moved(at, "core", 1))
    here = grid.device(at)
    parts = range(len(PART_ORDERS))
    in_rows, sum_rows = part_rows(local + MIX_ROWS), part_rows(local + MIX_ROWS)

    def absolute(offset):
        where = dict(at)
        for axis, step in named(offset).items():
            if step:
                where = grid.moved(where, axis, step)
        return where

    def slot_of(offset):
        return grid.slot(named(offset))

    def level_of(part, offset):
        reached = named(offset)
        return max([i + 1 for i, axis in enumerate(PART_ORDERS[part]) if reached[axis]], default=0)

    send_index = {}
    for part in parts:
        count = 0
        for offset in STEP_ORDER:
            for axis in PART_ORDERS[part][level_of(part, offset) :]:
                send_index[part, offset, axis] = count
                count += 1

    def pass_on(part, offset):
        level = level_of(part, offset)
        block = grid.block(absolute(offset))
        slot = slot_of(offset)
        span = in_rows[part]
        landing = n2all.at[block, span]
        if level:
            remote(landing, landing, g_send.at[part, 0], g_recv.at[part, slot], here).wait_recv()
        source = landing if level else n2x.at[span]
        for axis in PART_ORDERS[part][level:]:
            seen = grid.slot({**named(offset), axis: 1})
            remote(
                source,
                landing,
                g_send.at[part, send_index[part, offset, axis]],
                g_recv.at[part, seen],
                grid.device(grid.moved(at, axis, 1)),
            ).start()
        remote(source, landing, gc_send.at[part, slot], gc_recv.at[part, slot], partner).start()

    listed = [(kind[0], int(kind[1]), STEP_ORDER[place]) for row in PAUSES.values() for kind, place in row]
    buf_index, seen_slots, first_sums = {}, set(), set()
    for kind, part, offset in listed:
        if kind == "s":
            if offset not in seen_slots:
                seen_slots.add(offset)
                first_sums.add((part, offset))
            if any(offset):
                buf_index[part, offset] = sum(1 for other, _ in buf_index if other == part)

    def add_up(part, offset):
        phase, feeds = feeds_of(PART_ORDERS[part], offset)
        axis = PART_ORDERS[part][phase] if phase < 3 else None
        slot = slot_of(offset)
        span = sum_rows[part]
        if (part, offset) in first_sums:
            remote(away.at[0], core_buf.at[slot], c_send.at[0], c_recv.at[slot], here).wait_recv()
        for feed in feeds:
            index = buf_index[part, feed]
            ref = bufs.at[index, span]
            remote(ref, ref, r_send.at[part, 0], r_recv.at[part, index], here).wait_recv()

        @pl.loop(0, (span.stop - span.start) // 16)
        def _(i):
            rows = pl.ds(pl.multiple_of(span.start + i * 16, 16), 16)
            value = work[slot, rows].astype(F32) + core_buf[slot, rows].astype(F32)
            for feed in feeds:
                value = value + bufs[buf_index[part, feed], rows].astype(F32)
            if axis is None:
                total[rows] = value
            else:
                work[slot, rows] = value.astype(BF16)

        if axis is not None:
            index = buf_index[part, offset]
            remote(
                work.at[slot, span],
                bufs.at[index, span],
                r_send.at[part, index],
                r_recv.at[part, index],
                grid.device(grid.moved(at, axis, 1)),
            ).start()

    def pause(number):
        for kind, place in PAUSES.get(number, ()):
            act = pass_on if kind[0] == "g" else add_up
            act(int(kind[1]), STEP_ORDER[place])

    def pauses(step, turn):
        for i in range(steps):
            if 3 * i + turn in PAUSES:
                pl.when(step == i)(functools.partial(pause, 3 * i + turn))

    def bit(step, index):
        value = 0
        for i, offset in enumerate(STEP_ORDER):
            if offset[index]:
                value = value + jnp.where(step == i, 1, 0)
        return value

    def blocks_of(step):
        where = dict(at)
        offsets = {}
        for index, axis in enumerate(("high", "low", "y")):
            offsets[axis] = bit(step, index)
            where[axis] = lax.rem(at[axis] + offsets[axis], 2)
        mine = grid.block(where)
        other = grid.block(grid.moved(where, "core", 1))
        return mine, other, grid.slot(offsets)

    def gy_loads(step, turn):
        mine, other, _ = blocks_of(step)
        return [
            pltpu.make_async_copy(gy.at[mine, :, : plan.block], gybuf.at[turn, 0], gy_sem.at[turn, 0]),
            pltpu.make_async_copy(gy.at[other, :, : plan.block], gybuf.at[turn, 1], gy_sem.at[turn, 1]),
        ]

    def out_copy(turn, i, block):
        return pltpu.make_async_copy(outbuf.at[turn, i], out_all.at[block], out_sem.at[turn, i])

    for load in gy_loads(0, 0):
        load.start()
    meet(grid.peers(at))
    for part in parts:
        pass_on(part, STEP_ORDER[0])
    n2all[pl.ds(grid.block(at), 1)] = n2x[...][None]

    @pl.loop(0, width // 64)
    def _(i):
        acc[pl.ds(pl.multiple_of(i * 64, 64), 64)] = jnp.zeros((64, 2 * hidden), F32)

    @pl.loop(0, hidden // 64)
    def _(i):
        dw_out[pl.ds(pl.multiple_of(i * 64, 64), 64)] = jnp.zeros((64, width), F32)

    @pl.loop(0, steps)
    def _(step):
        pauses(step, 0)
        mine, other, slot = blocks_of(step)
        turn = lax.rem(step, 2)

        @pl.when(step + 1 < steps)
        def _():
            for load in gy_loads(step + 1, 1 - turn):
                load.start()

        for part in parts:
            ref = n2all.at[other, in_rows[part]]
            remote(ref, ref, gc_send.at[part, 0], gc_recv.at[part, slot], here).wait_recv()
        for load in gy_loads(step, turn):
            load.wait()
        pair = (mine, other)
        normed = jnp.concatenate([n2all[b, :local] for b in pair], axis=0)
        upstream = gybuf[turn].reshape(2 * local, width)
        mixing = jnp.concatenate([tn(n2all[b, local:, :local], pick[...]) for b in pair], axis=0)
        pre = nn(normed, w_in[...])
        gate, up = pre[:, :hidden], pre[:, hidden:]
        sigmoid = jax.nn.sigmoid(gate)
        silu = gate * sigmoid
        act = (silu * up).astype(BF16).astype(F32)
        act_mixed = (act * mixing).astype(BF16)
        pauses(step, 1)

        @pl.when(step >= 2)
        def _():
            for i, block in enumerate(pair):
                out_copy(turn, i, block).wait()

        out = nn(act_mixed, w_out[...]).astype(BF16)
        for i, block in enumerate(pair):
            outbuf[turn, i] = out[i * local : (i + 1) * local]
            out_copy(turn, i, block).start()
        act_grad = nt(upstream, w_out[...])
        choice = nt(pick[...], (act * act_grad).astype(BF16)).astype(BF16)
        act_grad = act_grad * mixing
        gate_grad = act_grad * up * sigmoid * (1.0 + gate * (1.0 - sigmoid))
        pre_grad = jnp.concatenate([gate_grad, act_grad * silu], axis=-1).astype(BF16)
        n2g = nt(pre_grad, w_in[...]).astype(BF16)

        @pl.when(step >= 2)
        def _():
            remote(away.at[turn], core_buf.at[0], c_send.at[turn], c_recv.at[0], partner).wait_send()

        pad = jnp.zeros((MIX_ROWS, width - local), BF16)
        for i, (ref, index) in enumerate(((work, slot), (away, turn))):
            span = slice(i * local, (i + 1) * local)
            ref[index, :local] = n2g[span]
            ref[index, local:] = jnp.concatenate([choice[:, span], pad], axis=-1)
        remote(away.at[turn], core_buf.at[slot], c_send.at[turn], c_recv.at[slot], partner).start()
        pauses(step, 2)
        acc[...] += tn(normed, pre_grad)
        dw_out[...] += tn(act_mixed, upstream)

    pause(3 * steps)
    for turn in range(2):
        for i in range(2):
            out_copy(turn, i, 0).wait()

    @pl.loop(0, width // 64)
    def _(i):
        rows = pl.ds(pl.multiple_of(i * 64, 64), 64)
        dw_in[rows] = acc[rows].astype(BF16)

    for turn in range(2):
        remote(away.at[turn], core_buf.at[0], c_send.at[turn], c_recv.at[0], partner).wait_send()
    for part in parts:
        ref, block = n2all.at[0, in_rows[part]], bufs.at[0, sum_rows[part]]
        for slot in range(steps):
            remote(ref, ref, gc_send.at[part, slot], g_recv.at[part, 0], partner).wait_send()
        for index in range(steps - 1):
            remote(ref, ref, g_send.at[part, index], g_recv.at[part, 0], partner).wait_send()
            remote(block, block, r_send.at[part, index], r_recv.at[part, 0], partner).wait_send()


def fused(plan, n2x, gy, w_in, w_out, pick, collective_id):
    local, width, hidden = plan.local, plan.width, plan.hidden_pad
    steps = len(STEP_ORDER)
    rows = local + MIX_ROWS
    return pl.pallas_call(
        functools.partial(fused_kernel, plan),
        out_shape=(
            jax.ShapeDtypeStruct((rows, width), F32),
            jax.ShapeDtypeStruct((width, 2 * hidden), BF16),
            jax.ShapeDtypeStruct((hidden, width), F32),
            jax.ShapeDtypeStruct((plan.group, local, width), BF16),
        ),
        in_specs=[VMEM, HBM, VMEM, VMEM, VMEM],
        out_specs=(VMEM,) * 3 + (HBM,),
        scratch_shapes=[
            pltpu.VMEM((plan.group, local + MIX_ROWS, width), BF16),
            pltpu.VMEM((2, 2, 2, plan.block, width), BF16),
            pltpu.VMEM((width, 2 * hidden), F32),
            pltpu.VMEM((2, rows, width), BF16),
            pltpu.VMEM((steps, rows, width), BF16),
            pltpu.VMEM((steps, rows, width), BF16),
            pltpu.VMEM((steps - 1, rows, width), BF16),
            pltpu.VMEM((2, 2, local, width), BF16),
            DMA((2, 2)),
            DMA((2, 2)),
            DMA((3, steps - 1)),
            DMA((3, steps)),
            DMA((3, steps)),
            DMA((3, steps)),
            DMA((2,)),
            DMA((steps,)),
            DMA((3, steps - 1)),
            DMA((3, steps - 1)),
        ],
        compiler_params=params(collective_id),
        cost_estimate=busy(100),
        name="fused",
    )(n2x, gy, w_in, w_out, pick)


def turned(value):
    return pltpu.roll(value, 64, 1)


def half_tiles(plan):
    return lax.broadcasted_iota(jnp.int32, (plan.rows, 128), 1) < 64


def column_tiles(plan, pair, gate):
    per = plan.quad // 2
    start = gate * FF + lax.div(pair, per) * (plan.ctx * 64) + lax.rem(pair, per) * 128
    first = lax.div(pair, per) * plan.quad + lax.rem(pair, per) * 2
    return [pl.ds(pl.multiple_of(start + half * plan.quad * 64, 128), 128) for half in range(2)], first


def pack_kernel(plan, both, attn, extra, wq, win):
    low = half_tiles(plan)

    @pl.loop(0, plan.group // 2)
    def _(pair):
        for branch in range(plan.branches):
            made = [[], []]
            for gate in range(2):
                cols, first = column_tiles(plan, pair, gate)
                mine, far = (both[branch, :, col].astype(F32) for col in cols)
                made[0].append(jnp.where(low, mine, turned(far)))
                made[1].append(jnp.where(low, turned(mine), far))
            for i in range(2):
                value = jnp.concatenate(made[i], axis=0).astype(BF16)
                win[pl.ds(first + i, 1), :, branch * 128 : (branch + 1) * 128] = value[None]

    def tile(part, head):
        start = part * HEADS * HEAD_DIM + head // 2 * 128
        return attn[:, start : start + 128].astype(F32)

    def placed(part, head, side):
        value = tile(part, head)
        return value if head % 2 == side else turned(value)

    for member in range(plan.quad):
        heads = [member * 3 + i for i in range(3)]
        for i, head in enumerate(heads):
            value = jnp.where(low, placed(0, head, 0), placed(1, head, 1))
            wq[member, :, i * 128 : (i + 1) * 128] = value.astype(BF16)
        value = jnp.where(low, placed(2, heads[0], 0), placed(2, heads[1], 1))
        wq[member, :, 384:512] = value.astype(BF16)
        value = jnp.where(low, placed(2, heads[2], 0), extra[...].astype(F32))
        wq[member, :, 512:640] = value.astype(BF16)


def pack(plan, both, attn, extra):
    return pl.pallas_call(
        functools.partial(pack_kernel, plan),
        out_shape=(
            jax.ShapeDtypeStruct((plan.quad, plan.rows, plan.wide), BF16),
            jax.ShapeDtypeStruct((plan.group, 2 * plan.rows, plan.hidden_pad), BF16),
        ),
        in_specs=[VMEM] * 3,
        out_specs=(VMEM,) * 2,
        compiler_params=params(),
        cost_estimate=busy(3),
        name="pack",
    )(both, attn, extra)


def unpack_kernel(plan, r_in, r_qkv, r_mix, dw_out, far_out, dense_in, expert_in, attn_in, attn_out, small, dense_out, expert_out):
    low = half_tiles(plan)
    rows = plan.rows

    @pl.loop(0, plan.group // 2)
    def _(pair):
        first = column_tiles(plan, pair, 0)[1]
        for branch in range(plan.branches):
            cols = slice(branch * 128, (branch + 1) * 128)
            sources = [r_in[first + i, :, cols].astype(F32) for i in range(2)]
            for gate in range(2):
                one, two = (value[gate * rows : (gate + 1) * rows] for value in sources)
                places = column_tiles(plan, pair, gate)[0]
                values = jnp.where(low, one, turned(two)), jnp.where(low, turned(one), two)
                for place_at, value in zip(places, values):
                    if branch == 0:
                        dense_in[:, place_at] = value
                    else:
                        expert_in[:, branch - 1, place_at] = value

    def tile(member, number):
        cols = slice(number * 128, (number + 1) * 128)
        return r_qkv[member, :, cols].astype(F32) + r_qkv[plan.quad + member, :, cols].astype(F32)

    def put(part, head, value):
        start = part * HEADS * HEAD_DIM + head // 2 * 128
        attn_in[:, start : start + 128] = value

    for head in range(0, HEADS, 2):
        one, two = (tile((head + i) // 3, (head + i) % 3) for i in range(2))
        put(0, head, jnp.where(low, one, turned(two)))
        put(1, head, jnp.where(low, turned(one), two))
        halves = []
        for i in range(2):
            member, at = divmod(head + i, 3)
            value = tile(member, 3 + at // 2)
            halves.append(value if at % 2 == i else turned(value))
        put(2, head, jnp.where(low, halves[0], halves[1]))
    total = tile(0, 4)
    for member in range(1, plan.quad):
        total = total + tile(member, 4)
    small[...] = total
    mixed = r_mix[0].astype(F32)
    for i in range(1, plan.ctx):
        mixed = mixed + r_mix[i].astype(F32)
    attn_out[...] = mixed
    half = lax.div(lax.axis_index("ctx"), plan.quad)
    for branch in range(plan.branches):
        value = dw_out[branch, pl.ds(half, 1)][0] + far_out[branch].astype(F32)
        if branch == 0:
            dense_out[...] = value
        else:
            expert_out[:, branch - 1, :] = value


def unpack(plan, r_in, r_qkv, r_mix, dw_out, far_out):
    rows, width, own = plan.rows, plan.width, plan.own_hidden
    return pl.pallas_call(
        functools.partial(unpack_kernel, plan),
        out_shape=(
            jax.ShapeDtypeStruct((rows, 2 * FF), F32),
            jax.ShapeDtypeStruct((rows, plan.experts, 2 * FF), F32),
            jax.ShapeDtypeStruct((rows, 3 * HEADS * HEAD_DIM), F32),
            jax.ShapeDtypeStruct((rows, width), F32),
            jax.ShapeDtypeStruct((rows, 128), F32),
            jax.ShapeDtypeStruct((own, width), F32),
            jax.ShapeDtypeStruct((own, plan.experts, width), F32),
        ),
        in_specs=[VMEM] * 5,
        out_specs=(VMEM,) * 7,
        compiler_params=params(),
        cost_estimate=busy(5),
        name="unpack",
    )(r_in, r_qkv, r_mix, dw_out, far_out)


def grid_block(plan, dp, ctx):
    return dp * plan.quad + lax.rem(ctx, plan.quad)


def by_half(half, mine, far, axis):
    return jnp.where(
        half == 0, jnp.stack([mine, far], axis), jnp.stack([far, mine], axis)
    )


def rope_tables(plan):
    half, step = HEAD_DIM // 2, 64
    frequency = np.float32(10000.0) ** (-np.arange(half, dtype=np.float32) / np.float32(half))
    frequency = np.tile(frequency.astype(np.float64), 4)[None]
    coarse = np.arange(0, plan.slots, step)[:, None] * frequency
    fine = np.arange(step)[:, None] * frequency
    sign = np.tile(np.repeat([-1.0, 1.0], half), 2)[None]
    (ca, sa), (cb, sb) = (
        (jnp.asarray(np.cos(a), F32), jnp.asarray(np.sin(a), F32)) for a in (coarse, fine)
    )
    ca, sa, cb, sb = ca[:, None], sa[:, None], cb[None], sb[None]
    cosine = (ca * cb - sa * sb).reshape(plan.slots, 128)
    sine = ((sa * cb + ca * sb) * jnp.asarray(sign, F32)).reshape(plan.slots, 128)
    return cosine, sine


def pick_table(plan):
    table = np.zeros((MIX_ROWS, plan.hidden_pad), np.float32)
    span = HALVES * plan.own_hidden
    for expert in range(plan.experts):
        cols = slice((1 + expert) * span, (2 + expert) * span)
        table[2 + expert, cols] = 1.0
        table[10 + expert, cols] = 1.0
    table[0, :span] = 1.0
    return jnp.asarray(table, BF16)


def pack_qkv(plan, attn_in, attn_gain, ffn_gain, router):
    rows, quad, heads = plan.rows, plan.quad, plan.heads
    qkv = attn_in.reshape(rows, 3, HEADS, HEAD_DIM)
    qkv = jnp.pad(qkv, ((0, 0), (0, 0), (0, quad * heads - HEADS), (0, 0)))
    qkv = qkv.reshape(rows, 3, quad, heads, HEAD_DIM)
    qk = jnp.transpose(qkv[:, :2], (2, 0, 3, 1, 4)).reshape(quad, rows, 2 * plan.head_cols)
    v = jnp.transpose(qkv[:, 2], (1, 0, 2, 3)).reshape(quad, rows, plan.head_cols)
    extra = jnp.concatenate([attn_gain[:, None], ffn_gain[:, None], router], axis=1)
    extra = jnp.pad(extra, ((0, 0), (0, plan.wide - plan.qkv_cols - extra.shape[1])))
    extra = jnp.broadcast_to(extra[None], (quad,) + extra.shape)
    packed = jnp.concatenate([qk, v, extra], axis=-1)
    return jnp.pad(packed, ((0, 0), (0, plan.pad_rows - rows), (0, 0)))


def unpack_qkv(plan, packed):
    rows, quad, heads = plan.rows, plan.quad, plan.heads
    qk = packed[..., : 2 * plan.head_cols].reshape(quad, rows, heads, 2, HEAD_DIM)
    v = packed[..., 2 * plan.head_cols : plan.qkv_cols].reshape(quad, rows, heads, 1, HEAD_DIM)
    qkv = jnp.transpose(jnp.concatenate([qk, v], axis=3), (1, 3, 0, 2, 4))
    qkv = qkv.reshape(rows, 3, quad * heads, HEAD_DIM)[:, :, :HEADS]
    return qkv.reshape(rows, 3 * HEADS * HEAD_DIM)


def pack_in(plan, dense_in, expert_in):
    rows, own = plan.rows, plan.own_hidden
    both = jnp.concatenate([dense_in[:, None], expert_in], axis=1)
    both = both.reshape(rows, plan.branches, 2, plan.dp, HALVES, plan.quad, own)
    both = jnp.transpose(both, (3, 5, 2, 0, 1, 4, 6))
    both = both.reshape(plan.group, 2, rows, plan.hidden)
    pads = ((0, 0), (0, 0), (0, plan.pad_rows - rows), (0, plan.hidden_pad - plan.hidden))
    return jnp.pad(both, pads).reshape(plan.group, 2 * plan.pad_rows, plan.hidden_pad)


def unpack_in(plan, packed):
    rows, own = plan.rows, plan.own_hidden
    both = packed.reshape(plan.group, 2, plan.pad_rows, plan.hidden_pad)
    both = both[:, :, :rows, : plan.hidden]
    both = both.reshape(plan.dp, plan.quad, 2, rows, plan.branches, HALVES, own)
    both = jnp.transpose(both, (3, 4, 2, 0, 5, 1, 6))
    both = both.reshape(rows, plan.branches, 2 * FF).astype(F32)
    return both[:, 0], both[:, 1:]


def shards(
    tokens,
    lengths,
    routes,
    cotangent,
    attn_gain,
    attn_in,
    attn_out,
    ffn_gain,
    router,
    dense_in,
    dense_out,
    expert_in,
    expert_out,
):
    micro, seqs, block, width = tokens.shape
    experts = expert_in.shape[1]
    plan = Plan(lax.axis_size("dp"), lax.axis_size("ctx"), block, width, experts)
    assert micro == HALVES and seqs == 1 and plan.ctx % 4 == 0 and plan.dp % 2 == 0
    quad, local = plan.quad, plan.local
    dp, ctx = place()
    half, member = lax.div(ctx, quad), lax.rem(ctx, quad)
    across = [(i, (i + quad) % plan.ctx) for i in range(plan.ctx)]

    def swap(value):
        return lax.ppermute(value, "ctx", across)

    def pick_mine(value):
        return lax.dynamic_index_in_dim(value, half, 0, keepdims=False)

    def pick_far(value):
        return lax.dynamic_index_in_dim(value, 1 - half, 0, keepdims=False)

    slot = ctx * block + jnp.arange(block, dtype=jnp.int32)
    valid = (slot[None] < lengths).astype(BF16)
    grad_all = cotangent[:, 0] * valid[..., None]
    tail = round_up(plan.rows + 2, 16)
    route_rows = jnp.transpose(routes[:, 0], (0, 2, 1)).astype(BF16)
    route_rows = jnp.pad(route_rows, ((0, 0), (0, tail - plan.rows - 2), (0, width - block)))
    length = pick_mine(lengths)
    out_own = jnp.concatenate([dense_out[:, None], expert_out], axis=1)
    out_own = jnp.transpose(out_own, (1, 0, 2))
    out_far = swap(out_own)
    gyw = jnp.concatenate(
        [grad_all, jnp.broadcast_to(attn_out, (2,) + attn_out.shape), route_rows], axis=1
    )

    if plan.tiled:
        both = jnp.concatenate([dense_in[None], jnp.transpose(expert_in, (1, 0, 2))])
        extra = jnp.concatenate([attn_gain[:, None], ffn_gain[:, None], router], axis=1)
        extra = jnp.pad(extra, ((0, 0), (64, 64 - extra.shape[1])))
        wq, win = pack(plan, both, attn_in, extra)
    else:
        wq = pack_qkv(plan, attn_in, attn_gain, ffn_gain, router)
        win = pack_in(plan, dense_in, expert_in)

    cosine, sine = rope_tables(plan)
    xs, w_seq, normed_seq, qk, v, lse, mixed, gy, w_in, gysrc, *owned = front(
        plan,
        length,
        tokens[:, 0],
        wq,
        win,
        gyw,
        cosine,
        sine,
        1,
    )
    x_seq = xs.reshape(plan.slots, width)
    if plan.tiled:
        n2x, middle, gates, w_mix = owned
    else:
        extra = w_seq[:, plan.qkv_cols :]
        gain_one = extra[:, 0].astype(F32)[None]
        gain_two = extra[:, 1].astype(F32)[None]
        w_route = extra[:, 2 : 2 + experts]
        mixed = jnp.transpose(mixed, (1, 2, 0, 3)).reshape(local, quad * plan.head_cols)[:, :width]
        w_mix = gy[:, :, block : block + plan.rows].reshape(plan.dp, quad, 2, plan.rows, width)
        w_mix = by_half(half, w_mix[:, :, 0], w_mix[:, :, 1], 1).reshape(width, width)

        x = jnp.stack(
            [
                lax.dynamic_index_in_dim(xs, ctx, 0, keepdims=False),
                lax.dynamic_index_in_dim(xs, (1 - half) * quad + member, 0, keepdims=False),
            ]
        )
        x = x.reshape(local, width).astype(F32)
        middle = x + nn(mixed, w_mix)
        inverse_two = lax.rsqrt(jnp.mean(middle * middle, axis=-1, keepdims=True) + EPSILON)
        normed_two = (middle * inverse_two * gain_two).astype(BF16)
        own = lax.dynamic_index_in_dim(gy, grid_block(plan, dp, ctx), 0, keepdims=False)
        grad_y = own[:, :block].reshape(local, width)
        route_local = own[:, block + plan.rows : block + plan.rows + 2, :block]
        route_local = jnp.transpose(route_local, (0, 2, 1)).reshape(local, 2)
        logits = nn(normed_two, w_route)
        choose = (route_local[..., None] == jnp.arange(experts, dtype=BF16)).astype(F32)
        picked = jnp.sum(choose * logits[:, None, :], axis=-1)
        gates = jax.nn.softmax(picked, axis=-1)
        mixing = jnp.sum(gates[..., None] * choose, axis=1)
        mixing_t = mixing.T
        mixing_high = mixing_t.astype(BF16)
        mixing_low = (mixing_t - mixing_high.astype(F32)).astype(BF16)
        pads = ((2, 6 - experts), (0, 0))
        mix_rows = jnp.concatenate([jnp.pad(mixing_high, pads), jnp.pad(mixing_low, pads)])
        mix_rows = mix_rows.at[0].set(1.0)
        mix_rows = jnp.pad(mix_rows, ((0, 0), (0, width - local)))
        n2x = jnp.concatenate([normed_two, mix_rows])

    w_out = by_half(half, out_own, out_far, 1).reshape(plan.hidden, width)
    w_out = jnp.pad(w_out, ((0, plan.hidden_pad - plan.hidden), (0, 0)))
    if plan.dp == 4 and quad == 4:
        n2g_sum, dw_in, dw_out, out_part = fused(plan, n2x, gy, w_in, w_out, pick_table(plan), 3)
    else:
        n2x = gather(plan, n2x, 3)
        out_part, n2g_part, dw_in, dw_out = ffn(plan, n2x, gy, w_in, w_out, pick_table(plan))
        n2g_sum = reduce(plan, n2g_part, 5)
        out_part = reduce(plan, out_part, 7)

    if plan.tiled:
        given = (n2g_sum, gates, n2x, gysrc, w_mix, mixed)
    else:
        normed_two_grad = n2g_sum[:local]
        mixing_grad = n2g_sum[local + 2 : local + 2 + experts, :local].T
        choice_grad = jnp.sum(choose * mixing_grad[:, None, :], axis=-1)
        pick_grad = gates * (choice_grad - jnp.sum(gates * choice_grad, axis=-1, keepdims=True))
        logit_grad = jnp.sum(pick_grad[..., None] * choose, axis=1).astype(BF16)
        router_grad = tn(normed_two, logit_grad)
        normed_two_grad = normed_two_grad + nt(logit_grad, w_route)
        gain_two_grad = jnp.sum(normed_two_grad * middle * inverse_two, axis=0)
        scaled = normed_two_grad * gain_two
        middle_grad = (
            grad_y.astype(F32)
            + inverse_two * scaled
            - middle * inverse_two**3 * jnp.mean(scaled * middle, axis=-1, keepdims=True)
        )
        attn_grad = middle_grad.astype(BF16)
        dw_mix = tn(mixed, attn_grad).astype(BF16).reshape(plan.dp, plan.ctx, plan.rows, width)
        mixed_grad = nt(attn_grad, w_mix).astype(BF16)
        mixed_grad = jnp.pad(mixed_grad, ((0, 0), (0, quad * plan.head_cols - width)))
        mixed_grad = mixed_grad.reshape(2, block, quad, plan.head_cols)
        first = plan.qkv_cols - (plan.wide - 128)
        small = jnp.concatenate([gain_two_grad[:, None], router_grad], axis=1)
        small = jnp.pad(small, ((0, 0), (first + 1, 127 - first - small.shape[1])))
        given = (jnp.transpose(mixed_grad, (2, 0, 1, 3)), dw_mix, small, middle_grad)
    dw_out = dw_out[: plan.hidden].reshape(plan.branches, HALVES, plan.own_hidden, width)
    r_qkv, r_mix, r_in, far_out, activations, input_grad = back(
        plan,
        length,
        x_seq,
        w_seq,
        cosine,
        sine,
        normed_seq,
        qk,
        v,
        lse,
        dw_in.astype(BF16).reshape(plan.dp * HALVES, quad * plan.rows, 2 * plan.hidden_pad),
        dw_out,
        out_part,
        middle,
        given,
        4,
    )

    if plan.tiled:
        dense_in_grad, expert_in_grad, attn_in_grad, attn_out_grad, small, dense_out_grad, expert_out_grad = unpack(
            plan, r_in, r_qkv, r_mix, dw_out, far_out
        )
        small = small[:, 64 : 66 + experts]
    else:
        r_qkv = r_qkv[:, : plan.rows].astype(F32).reshape(HALVES, quad, plan.rows, plan.wide)
        r_qkv = jnp.sum(r_qkv, axis=0)
        attn_in_grad = unpack_qkv(plan, r_qkv)
        small = jnp.sum(r_qkv[:, :, plan.qkv_cols :], axis=0)
        attn_out_grad = jnp.sum(r_mix.astype(F32), axis=0)
        dense_in_grad, expert_in_grad = unpack_in(plan, r_in)
        dw_out = pick_mine(jnp.moveaxis(dw_out, 1, 0)) + far_out.astype(F32)
        dense_out_grad, expert_out_grad = dw_out[0], jnp.transpose(dw_out[1:], (1, 0, 2))
    return (
        activations[:, None],
        input_grad[:, None],
        small[:, 0],
        attn_in_grad,
        attn_out_grad,
        small[:, 1],
        small[:, 2 : 2 + experts],
        dense_in_grad,
        dense_out_grad,
        expert_in_grad,
        expert_out_grad,
    )


def solution(mesh):
    rows = P(("dp", "ctx"))
    matrix = P(("dp", "ctx"), None)
    cube = P(("dp", "ctx"), None, None)
    slots = P(None, "dp", "ctx", None)
    in_specs = (
        slots,
        P(None, "dp"),
        slots,
        slots,
        rows,
        matrix,
        matrix,
        rows,
        matrix,
        matrix,
        matrix,
        cube,
        cube,
    )
    out_specs = (
        slots,
        slots,
        rows,
        matrix,
        matrix,
        rows,
        matrix,
        matrix,
        matrix,
        cube,
        cube,
    )
    return jax.shard_map(shards, mesh=mesh, in_specs=in_specs, out_specs=out_specs, check_vma=False)
```

```python
import functools

import jax
import jax.numpy as jnp
import numpy as np
from jax import lax
from jax.experimental import pallas as pl
from jax.experimental.pallas import tpu as pltpu
from jax.sharding import PartitionSpec as P

HEADS = 12
HEAD_DIM = 64
FF = 2048
EPSILON = 1e-05
HALVES = 2
QUERY_ROWS = 256
MIX_ROWS = 16
MESH = pl.DeviceIdType.MESH
BF16 = jnp.bfloat16
F32 = jnp.float32


def round_up(value, step):
    return -(-value // step) * step


class Plan:
    def __init__(self, dp, ctx, block, width, experts):
        self.dp, self.ctx, self.block, self.width, self.experts = dp, ctx, block, width, experts
        self.quad = ctx // HALVES
        self.devices = dp * ctx
        self.group = dp * self.quad
        self.slots = ctx * block
        self.rows = width // self.devices
        self.pad_rows = round_up(self.rows, 8)
        self.heads = -(-HEADS // self.quad)
        self.head_cols = self.heads * HEAD_DIM
        self.qkv_cols = 3 * self.head_cols
        self.wide = round_up(self.qkv_cols + 2 + experts, 128)
        self.own_hidden = FF // self.devices
        self.branches = 1 + experts
        self.hidden = self.branches * HALVES * self.own_hidden
        self.hidden_pad = round_up(self.hidden, 128)
        self.local = HALVES * block
        self.tiled = (
            self.own_hidden == 64
            and self.rows % 8 == 0
            and self.quad == 4
            and self.heads == 3
            and self.wide == self.qkv_cols + 64
        )


def place():
    return lax.axis_index("dp"), lax.axis_index("ctx")


def params(collective_id=None, limit=60 * 1024 * 1024):
    if collective_id is None:
        return pltpu.CompilerParams(vmem_limit_bytes=limit)
    return pltpu.CompilerParams(
        vmem_limit_bytes=limit, collective_id=collective_id, has_side_effects=True
    )


def remote(src, dst, send_sem, recv_sem, device):
    return pltpu.make_async_remote_copy(
        src_ref=src,
        dst_ref=dst,
        send_sem=send_sem,
        recv_sem=recv_sem,
        device_id=device,
        device_id_type=MESH,
    )


def busy(microseconds):
    return pl.CostEstimate(
        flops=0, bytes_accessed=int(microseconds * 3.4e6), transcendentals=0
    )


def meet(devices):
    barrier = pltpu.get_barrier_semaphore()
    for device in devices:
        pl.semaphore_signal(barrier, inc=1, device_id=device, device_id_type=MESH)
    pl.semaphore_wait(barrier, len(devices))


def other_devices(plan, dp, ctx):
    flat = dp * plan.ctx + ctx
    result = []
    for step in range(1, plan.devices):
        target = lax.rem(flat + step, plan.devices)
        result.append((lax.div(target, plan.ctx), lax.rem(target, plan.ctx)))
    return result


def quad_members(plan, half, member):
    return [
        (half * plan.quad + lax.rem(member + step, plan.quad), lax.rem(member + step, plan.quad))
        for step in range(1, plan.quad)
    ]


VMEM = pl.BlockSpec(memory_space=pltpu.VMEM)
HBM = pl.BlockSpec(memory_space=pl.ANY)
DMA = pltpu.SemaphoreType.DMA


def half_members(plan, mine):
    return [lax.rem(mine + step, plan.group) for step in range(1, plan.group)]


class Grid:
    def __init__(self, plan):
        self.plan = plan
        self.sizes = {"y": plan.dp // 2, "high": plan.quad // 2, "low": 2}

    def here(self):
        dp, ctx = place()
        member = lax.rem(ctx, self.plan.quad)
        return {
            "core": lax.rem(dp, 2),
            "y": lax.div(dp, 2),
            "high": lax.div(member, 2),
            "low": lax.rem(member, 2),
            "half": lax.div(ctx, self.plan.quad),
        }

    def device(self, at):
        return (
            at["y"] * 2 + at["core"],
            at["half"] * self.plan.quad + at["high"] * 2 + at["low"],
        )

    def block(self, at):
        return (at["y"] * 2 + at["core"]) * self.plan.quad + at["high"] * 2 + at["low"]

    def moved(self, at, axis, step):
        result = dict(at)
        if axis == "core":
            result["core"] = 1 - at["core"]
        else:
            result[axis] = lax.rem(at[axis] + step, self.sizes[axis])
        return result

    def peers(self, at):
        result = [self.moved(at, "core", 1)]
        for axis, size in self.sizes.items():
            result += [self.moved(at, axis, step) for step in range(1, size)]
        return [self.device(peer) for peer in result]

    def slot(self, offsets):
        return (offsets["y"] * self.sizes["high"] + offsets["high"]) * 2 + offsets["low"]


GATHER_ORDERS = (("high", "low", "y"), ("high", "y", "low"))


class Gather:
    def __init__(self, grid, at, src, dst, send, recv, core_send, core_recv):
        self.grid, self.at, self.src, self.dst = grid, at, src, dst
        self.send, self.recv, self.core_send, self.core_recv = send, recv, core_send, core_recv

    def groups(self, order):
        sizes = self.grid.sizes
        levels = [[{"y": 0, "high": 0, "low": 0}], [], [], []]
        for level, axis in enumerate(order):
            base = [o for group in levels[: level + 1] for o in group]
            levels[level + 1] = [
                {**offsets, axis: step} for offsets in base for step in range(1, sizes[axis])
            ]
        return levels

    def absolute(self, offsets):
        where = dict(self.at)
        for axis, step in offsets.items():
            if step:
                where = self.grid.moved(where, axis, step)
        return where

    def run_level(self, order, level):
        grid, at = self.grid, self.at
        index = 0
        for current, group in enumerate(self.groups(order)):
            for offsets in group:
                if current == level:
                    block = grid.block(self.absolute(offsets))
                    if level:
                        remote(
                            self.src,
                            self.dst.at[block],
                            self.send.at[0],
                            self.recv.at[grid.slot(offsets)],
                            grid.device(at),
                        ).wait_recv()
                    source = self.dst.at[block] if level else self.src
                    remote(
                        source,
                        self.dst.at[block],
                        self.core_send.at[grid.slot(offsets)],
                        self.core_recv.at[grid.slot(offsets)],
                        grid.device(grid.moved(at, "core", 1)),
                    ).start()
                for axis in order[current:]:
                    for step in range(1, grid.sizes[axis]):
                        if current == level:
                            seen = {**offsets, axis: grid.sizes[axis] - step}
                            remote(
                                source,
                                self.dst.at[block],
                                self.send.at[index],
                                self.recv.at[grid.slot(seen)],
                                grid.device(grid.moved(at, axis, step)),
                            ).start()
                        index += 1

    def level(self, level):
        for color, order in enumerate(GATHER_ORDERS):
            pl.when(self.at["core"] == color)(functools.partial(self.run_level, order, level))

    def finish(self):
        plan, here = self.grid.plan, self.grid.device(self.at)

        def sent(order):
            for index in range(gather_sends(plan, order)):
                remote(self.src, self.dst.at[0], self.send.at[index], self.recv.at[0], here).wait_send()

        for color, order in enumerate(GATHER_ORDERS):
            pl.when(self.at["core"] == color)(functools.partial(sent, order))
        for slot in range(plan.group // 2):
            remote(
                self.src, self.dst.at[0], self.core_send.at[slot], self.core_recv.at[slot], here
            ).wait()


def gather_kernel(plan, src, dst, send, recv, core_send, core_recv):
    grid = Grid(plan)
    at = grid.here()
    meet(grid.peers(at))
    dst[pl.ds(grid.block(at), 1)] = src[...][None]
    blocks = Gather(grid, at, src, dst, send, recv, core_send, core_recv)
    for level in range(4):
        blocks.level(level)
    blocks.finish()


def gather_sems(plan):
    half = plan.group // 2
    count = max(gather_sends(plan, order) for order in GATHER_ORDERS)
    return [DMA((count,)), DMA((half,)), DMA((half,)), DMA((half,))]


def gather_sends(plan, order):
    sizes = Grid(plan).sizes
    held, total = 1, 0
    for axis in order:
        total += held * (sizes[axis] - 1)
        held *= sizes[axis]
    return total


def gather(plan, block, collective_id):
    return pl.pallas_call(
        functools.partial(gather_kernel, plan),
        out_shape=jax.ShapeDtypeStruct((plan.group,) + block.shape, block.dtype),
        in_specs=[VMEM],
        out_specs=VMEM,
        scratch_shapes=gather_sems(plan),
        compiler_params=params(collective_id),
        cost_estimate=busy(35),
        name="gather",
    )(block)


def reduce_kernel(plan, src, out, work, core_buf, bufs, load_sem, core_send, core_recv, send, recv):
    grid = Grid(plan)
    at = grid.here()
    zero = {"y": 0, "high": 0, "low": 0}
    meet(grid.peers(at))

    def run(order):
        levels = [[], [], [], []]
        held = [dict(zero)]
        levels[3] = [dict(zero)]
        for level in (2, 1, 0):
            axis = order[level]
            base = [o for later in levels[level + 1 :] for o in later]
            levels[level] = [
                {**offsets, axis: step} for offsets in base for step in range(1, grid.sizes[axis])
            ]
        del held

        def absolute(offsets):
            where = dict(at)
            for axis, step in offsets.items():
                if step:
                    where = grid.moved(where, axis, step)
            return where

        sequence = [o for group in levels for o in group]
        partner = grid.device(grid.moved(at, "core", 1))
        core_copies = []
        loads = []
        for offsets in sequence:
            where = absolute(offsets)
            slot = grid.slot(offsets)
            copy = remote(
                src.at[grid.block(grid.moved(where, "core", 1))],
                core_buf.at[slot],
                core_send.at[slot],
                core_recv.at[slot],
                partner,
            )
            copy.start()
            core_copies.append(copy)
            load = pltpu.make_async_copy(
                src.at[grid.block(where)], work.at[slot], load_sem.at[slot]
            )
            load.start()
            loads.append(load)
        arrived = {}
        sends = []
        index = 0
        position = 0
        for level in range(4):
            for offsets in levels[level]:
                slot = grid.slot(offsets)
                core_copies[position].wait_recv()
                loads[position].wait()
                position += 1
                total = work[slot].astype(F32) + core_buf[slot].astype(F32)
                for buffer in arrived.get(slot, ()):
                    remote(work.at[slot], bufs.at[buffer], send.at[0], recv.at[buffer], partner).wait_recv()
                    total = total + bufs[buffer].astype(F32)
                if level == 3:
                    out[...] = total.astype(out.dtype)
                    continue
                work[slot] = total.astype(BF16)
                axis = order[level]
                step = offsets[axis]
                copy = remote(
                    work.at[slot],
                    bufs.at[index],
                    send.at[index],
                    recv.at[index],
                    grid.device(grid.moved(at, axis, step)),
                )
                copy.start()
                sends.append(copy)
                landing = grid.slot({**offsets, axis: 0})
                arrived.setdefault(landing, []).append(index)
                index += 1
        for copy in sends:
            copy.wait_send()
        for copy in core_copies:
            copy.wait_send()

    for color, order in enumerate(GATHER_ORDERS):
        pl.when(at["core"] == color)(functools.partial(run, order[::-1]))


def reduce(plan, blocks, collective_id):
    half = plan.group // 2
    shape = blocks.shape[1:]
    count = max(gather_sends(plan, order) for order in GATHER_ORDERS)
    return pl.pallas_call(
        functools.partial(reduce_kernel, plan),
        out_shape=jax.ShapeDtypeStruct(shape, F32),
        in_specs=[HBM],
        out_specs=VMEM,
        scratch_shapes=[
            pltpu.VMEM((half,) + shape, BF16),
            pltpu.VMEM((half,) + shape, BF16),
            pltpu.VMEM((count,) + shape, BF16),
            DMA((half,)),
            DMA((half,)),
            DMA((half,)),
            DMA((count,)),
            DMA((count,)),
        ],
        compiler_params=params(collective_id),
        name="reduce",
    )(blocks)


def nt(left, right):
    return lax.dot_general(left, right, (((1,), (1,)), ((), ())), preferred_element_type=F32)


def nn(left, right):
    return lax.dot_general(left, right, (((1,), (0,)), ((), ())), preferred_element_type=F32)


def tn(left, right):
    return lax.dot_general(left, right, (((0,), (0,)), ((), ())), preferred_element_type=F32)


def swapped_halves(value):
    lane = lax.broadcasted_iota(jnp.int32, value.shape, 1)
    first = lax.rem(lane, HEAD_DIM) < HEAD_DIM // 2
    half = HEAD_DIM // 2
    return jnp.where(
        first, pltpu.roll(value, 2 * HEAD_DIM - half, 1), pltpu.roll(value, half, 1)
    )


def masked_scores(q, k, first_row, length):
    scores = nt(q, k)
    row = lax.broadcasted_iota(jnp.int32, scores.shape, 0) + first_row
    col = lax.broadcasted_iota(jnp.int32, scores.shape, 1)
    return jnp.where((col <= row) & (col < length), scores, -1000000000.0)


def natural_rows(plan, blocks):
    flat = blocks.astype(F32).reshape(plan.devices * plan.pad_rows, blocks.shape[-1])
    if plan.pad_rows == plan.rows:
        return flat.astype(BF16)
    row = lax.broadcasted_iota(jnp.int32, (plan.width, flat.shape[0]), 0)
    col = lax.broadcasted_iota(jnp.int32, (plan.width, flat.shape[0]), 1)
    source = lax.div(row, plan.rows) * plan.pad_rows + lax.rem(row, plan.rows)
    return nn((col == source).astype(BF16), flat.astype(BF16)).astype(BF16)


def around_gains(plan, w_seq):
    first = plan.qkv_cols - (plan.wide - 128)
    return jnp.transpose(w_seq[:, plan.wide - 128 :].astype(F32), (1, 0))[first : first + 8]


def chosen(local, routes):
    row = lax.broadcasted_iota(jnp.int32, (8, local), 0).astype(F32)
    return row - 2.0 == routes


def owner_forward(plan, ctx, far, half, xs, w_seq, mixed, gysrc, w_tail, n2x, middle, gates, w_mix):
    block, local, width, cols = plan.block, plan.local, plan.width, plan.head_cols
    rows = plan.quad * plan.rows

    @pl.loop(0, HALVES * plan.dp)
    def _(i):
        turn = lax.rem(lax.rem(i, HALVES) + half, 2)
        value = w_tail[pl.ds(lax.div(i, HALVES) * plan.quad, plan.quad), pl.ds(turn, 1)]
        value = value[:, 0].astype(F32)[:, : plan.rows].reshape(rows, width)
        w_mix[pl.ds(pl.multiple_of(i * rows, 16), rows)] = value.astype(BF16)

    total = jnp.concatenate([xs[pl.ds(ctx, 1)][0], xs[pl.ds(far, 1)][0]], axis=0).astype(F32)
    for member in range(plan.quad):
        total = total + nn(
            mixed[member].reshape(local, cols), w_mix[member * cols : (member + 1) * cols]
        )
    middle[...] = total
    inverse = lax.rsqrt(jnp.mean(total * total, axis=-1, keepdims=True) + EPSILON)
    normed = (total * inverse * around_gains(plan, w_seq)[1:2]).astype(BF16)
    n2x[:local] = normed
    first = plan.qkv_cols - (plan.wide - 128)
    logits = jnp.transpose(nn(normed, w_seq[:, plan.wide - 128 :]), (1, 0))[first : first + 8]
    tail = gysrc[:, block + 16 :, :block].astype(F32)
    routes = [
        jnp.concatenate([tail[i, plan.rows - 16 + k : plan.rows - 15 + k] for i in range(2)], axis=1)
        for k in range(2)
    ]
    picks = [chosen(local, route) for route in routes]
    scores = [jnp.sum(jnp.where(pick, logits, 0.0), axis=0, keepdims=True) for pick in picks]
    top = jnp.maximum(scores[0], scores[1])
    raised = [jnp.exp(score - top) for score in scores]
    gate = [value / (raised[0] + raised[1]) for value in raised]
    mixing = jnp.where(picks[0], gate[0], 0.0) + jnp.where(picks[1], gate[1], 0.0)
    high = mixing.astype(BF16).astype(F32)
    row = lax.broadcasted_iota(jnp.int32, (8, local), 0)
    mix_rows = jnp.concatenate([jnp.where(row == 0, 1.0, high), mixing - high], axis=0)
    n2x[local:] = jnp.concatenate(
        [mix_rows.astype(BF16), jnp.zeros((MIX_ROWS, width - local), BF16)], axis=1
    )
    gates[...] = jnp.concatenate(gate + routes + [jnp.zeros((4, local), F32)], axis=0)


def owner_back(plan, n2g_sum, gates, n2x, gysrc, w_mix, mixed, middle, w_seq, dmixed, dwo, rows8, middle_grad):
    block, local, width, cols = plan.block, plan.local, plan.width, plan.head_cols
    around = around_gains(plan, w_seq)
    choice = n2g_sum[local : local + 8, :local]
    picks = [chosen(local, gates[2 + k : 3 + k]) for k in range(2)]
    gate = [gates[k : k + 1] for k in range(2)]
    taken = [jnp.sum(jnp.where(pick, choice, 0.0), axis=0, keepdims=True) for pick in picks]
    inner = gate[0] * taken[0] + gate[1] * taken[1]
    logit_grad = sum(
        jnp.where(picks[k], gate[k] * (taken[k] - inner), 0.0) for k in range(2)
    ).astype(BF16)
    router_grad = nn(logit_grad, n2x[:local])
    grad = n2g_sum[:local] + tn(logit_grad, around.astype(BF16))
    values = middle[...]
    inverse = lax.rsqrt(jnp.mean(values * values, axis=-1, keepdims=True) + EPSILON)
    gain_grad = jnp.sum(grad * values * inverse, axis=0, keepdims=True)
    row = lax.broadcasted_iota(jnp.int32, (8, width), 0)
    rows8[...] = jnp.where(row == 1, gain_grad, router_grad)
    scaled = grad * around[1:2]
    result = (
        gysrc[:, :block].reshape(local, width).astype(F32)
        + inverse * scaled
        - values * inverse * inverse * inverse * jnp.mean(scaled * values, axis=-1, keepdims=True)
    )
    middle_grad[...] = result
    upstream = result.astype(BF16)
    for member in range(plan.quad):
        part = nt(upstream, w_mix[member * cols : (member + 1) * cols])
        dmixed[member] = part.astype(BF16).reshape(2, block, cols)
    return upstream


def front_kernel(plan, length_ref, tok, wq, win, gyw, cosine, sine, xs, w_seq, normed, qk_out, v_out, lse_out, mixed, gyall, w_in, gysrc, *rest):
    owned, rest = (rest[:4], rest[4:]) if plan.tiled else ((), rest)
    front_body(plan, length_ref, tok, wq, win, gyw, cosine, sine, xs, w_seq, normed, qk_out, v_out, lse_out, mixed, gyall, w_in, gysrc, owned, *rest)


def front_body(plan, length_ref, tok, wq, win, gyw, cosine, sine, xs, w_seq, normed, qk_out, v_out, lse_out, mixed, gyall, w_in, gysrc, owned, wall, wqx, win_all, qkv, made, w_tail, x_send, x_recv, s_send, s_recv, q_send, q_recv, f_send, f_recv, z_send, z_recv, own_sem, tail_sem, m_send, m_recv, *gather_sem):
    dp, ctx = place()
    half, member = lax.div(ctx, plan.quad), lax.rem(ctx, plan.quad)
    far = (1 - half) * plan.quad + member
    flat, flat_far = dp * plan.ctx + ctx, dp * plan.ctx + far
    mine = dp * plan.quad + member
    grid = Grid(plan)
    spot = grid.here()
    here = (dp, ctx)
    across = (dp, far)
    targets = half_members(plan, mine)
    devices = [
        (lax.div(target, plan.quad), half * plan.quad + lax.rem(target, plan.quad))
        for target in targets
    ]
    members = quad_members(plan, half, member)
    highs, ys = grid.sizes["high"], grid.sizes["y"]
    meet(devices + [across])
    pending = []

    def send(*args):
        copy = remote(*args)
        copy.start()
        pending.append(copy)

    swap_x = remote(tok.at[1 - half], xs.at[ctx], s_send.at[0], s_recv.at[0], across)
    swap_w = remote(wq, wqx, s_send.at[1], s_recv.at[1], across)
    swap_gy = remote(gyw.at[1 - half], gysrc.at[1], s_send.at[2], s_recv.at[2], across)
    swap_x.start()
    swap_w.start()

    def member_of(high, low):
        return half * plan.quad + lax.rem(spot["high"] + high, highs) * 2 + lax.rem(spot["low"] + low, 2)

    def token_block(side, high):
        at = half if side == 0 else 1 - half
        return at * plan.quad + lax.rem(spot["high"] + high, highs) * 2 + spot["low"]

    def token_sends(side, source):
        block = token_block(side, 0)
        for step in range(1, highs):
            index = side * (highs - 1) + step - 1
            send(source, xs.at[block], x_send.at[0, index], x_recv.at[0, side, highs - step - 1], (dp, member_of(step, 0)))
        send(source, xs.at[block], x_send.at[1, side * highs], x_recv.at[1, side, 0], (dp, member_of(0, 1)))

    def token_forward(side):
        for high in range(1, highs):
            block = token_block(side, high)
            remote(xs.at[block], xs.at[block], x_send.at[0, 0], x_recv.at[0, side, high - 1], here).wait_recv()
            send(xs.at[block], xs.at[block], x_send.at[1, side * highs + high], x_recv.at[1, side, high], (dp, member_of(0, 1)))

    def slice_sends(side, source, block):
        for i, (peer, to) in enumerate(members):
            send(source.at[to], wall.at[block], q_send.at[0, side, i], q_recv.at[block], (dp, peer))

    core_device = grid.device(grid.moved(spot, "core", 1))
    counter = [0, 0]

    def slice_on(block, source, along_y):
        if along_y:
            for step in range(1, ys):
                send(source, wall.at[block], q_send.at[1, 0, counter[0]], q_recv.at[block], grid.device(grid.moved(spot, "y", step)))
                counter[0] += 1
        send(source, wall.at[block], q_send.at[1, 1, counter[1]], q_recv.at[block], core_device)
        counter[1] += 1

    def slice_wait(block):
        remote(wq.at[0], wall.at[block], q_send.at[0, 0, 0], q_recv.at[block], here).wait_recv()

    token_sends(0, tok.at[half])
    slice_sends(0, wq, flat)
    slice_on(flat, wq.at[member], True)
    gysrc[0] = gyw[pl.ds(half, 1)][0]
    xs[pl.ds(ctx, 1)] = tok[pl.ds(half, 1)]
    wall[pl.ds(flat, 1)] = wq[pl.ds(member, 1)]
    swap_x.wait()
    token_sends(1, xs.at[far])
    swap_w.wait()
    slice_sends(1, wqx, flat_far)
    slice_on(flat_far, wqx.at[member], True)
    swap_gy.start()
    token_forward(0)
    for i, (peer, _) in enumerate(members):
        block = dp * plan.ctx + peer
        slice_wait(block)
        slice_on(block, wall.at[block], True)
    token_forward(1)
    for _, to in members:
        block = dp * plan.ctx + (1 - half) * plan.quad + to
        slice_wait(block)
        slice_on(block, wall.at[block], True)
    wall[pl.ds(flat_far, 1)] = wqx[pl.ds(member, 1)]

    for i, (target, device) in enumerate(zip(targets, devices)):
        send(win.at[target], win_all.at[flat], f_send.at[i], f_recv.at[i], device)
    send(win.at[mine], win_all.at[flat], z_send.at[0], z_recv.at[0], across)
    win_all[pl.ds(flat, 1)] = win[pl.ds(mine, 1)]

    def columns_on(i):
        source = lax.rem(mine + plan.group - 1 - i, plan.group)
        block = lax.div(source, plan.quad) * plan.ctx + half * plan.quad + lax.rem(source, plan.quad)
        remote(win.at[0], win_all.at[block], f_send.at[0], f_recv.at[i], here).wait_recv()
        send(win_all.at[block], win_all.at[block], z_send.at[1 + i], z_recv.at[1 + i], across)

    for step in range(1, ys):
        other = lax.rem(spot["y"] + step, ys) * 2 + spot["core"]
        for place_ctx in range(plan.ctx):
            block = other * plan.ctx + place_ctx
            slice_wait(block)
            slice_on(block, wall.at[block], False)
    swap_gy.wait()
    gather = Gather(grid, spot, gysrc, gyall, *gather_sem)
    own = pltpu.make_async_copy(gysrc, gyall.at[grid.block(spot)], own_sem)
    own.start()
    gather.level(0)
    for y in range(ys):
        for place_ctx in range(plan.ctx):
            slice_wait((y * 2 + 1 - spot["core"]) * plan.ctx + place_ctx)
    for side in range(2):
        for high in range(highs):
            block = half if side == 0 else 1 - half
            block = block * plan.quad + lax.rem(spot["high"] + high, highs) * 2 + 1 - spot["low"]
            remote(xs.at[block], xs.at[block], x_send.at[0, 0], x_recv.at[1, side, high], here).wait_recv()

    length = length_ref[0]
    rows, block = QUERY_ROWS, plan.block
    slots = plan.slots
    w_seq[...] = natural_rows(plan, wall[...])
    tail = w_seq[:, plan.wide - 128 :].astype(F32)
    gain = jnp.transpose(tail, (1, 0))[plan.qkv_cols - plan.wide + 128 :][:1]

    @pl.loop(0, slots // rows)
    def _(i):
        at = pl.ds(pl.multiple_of(i * rows, rows), rows)
        values = xs[pl.ds(i * (rows // block), rows // block)].reshape(rows, plan.width)
        values = values.astype(F32)
        inverse = lax.rsqrt(jnp.mean(values * values, axis=-1, keepdims=True) + EPSILON)
        normed[at] = (values * inverse * gain).astype(BF16)
        qkv[at] = nn(normed[at], w_seq[...])
    heads = plan.heads
    qk_width = 2 * HEAD_DIM
    third = (plan.group - 1) // 3
    for i in range(third):
        columns_on(i)
    for head in range(heads):
        cols = slice(head * qk_width, (head + 1) * qk_width)
        qk = qkv[:, cols]
        qk_out[:, cols] = (qk * cosine[...] + swapped_halves(qk) * sine[...]).astype(BF16)
    v_cols = slice(heads * qk_width, heads * 3 * HEAD_DIM)
    v_out[...] = qkv[:, v_cols].astype(BF16)
    gather.level(1)
    for i in range(third, 2 * third):
        columns_on(i)

    def mixed_copy(index):
        side, to = divmod(index, plan.quad)
        turn = lax.rem(half + side, 2)
        return remote(
            made.at[index],
            mixed.at[member, turn],
            m_send.at[index],
            m_recv.at[member, turn],
            (dp, half * plan.quad + to),
        )

    spans = list(range(0, slots, rows))
    for number, start in enumerate(spans):
        at = slice(start, start + rows)
        end = start + rows
        for head in range(heads):
            base = head * qk_width
            q = qk_out[at, base : base + HEAD_DIM] * BF16(0.125)
            k = qk_out[:end, base + HEAD_DIM : base + qk_width]
            v = v_out[:end, head * HEAD_DIM : (head + 1) * HEAD_DIM]
            scores = masked_scores(q, k, start, length)
            top = jnp.max(scores, axis=-1, keepdims=True)
            raised = jnp.exp(scores - top)
            total = jnp.sum(raised, axis=-1, keepdims=True)
            lse_out[head, at] = top + jnp.log(total)
            probs = (raised * (1.0 / total)).astype(BF16)
            part = nn(probs, v).astype(BF16)
            for i in range(rows // block):
                made[start // block + i, :, head * HEAD_DIM : (head + 1) * HEAD_DIM] = part[
                    i * block : (i + 1) * block
                ]
        for i in range(rows // block):
            index = start // block + i
            pl.when(member != index % plan.quad)(lambda index=index: mixed_copy(index).start())

            @pl.when(member == index % plan.quad)
            def _(index=index):
                turn = lax.rem(half + index // plan.quad, 2)
                mixed[pl.ds(member, 1), pl.ds(turn, 1)] = made[index][None, None]

        if number == len(spans) // 2:
            for i in range(2 * third, plan.group - 1):
                columns_on(i)
            gather.level(2)
    gather.level(3)
    for index in range(plan.ctx):
        pl.when(member != index % plan.quad)(lambda index=index: mixed_copy(index).wait_send())
    for source in range(plan.quad):

        @pl.when(member != source)
        def _(source=source):
            for turn in range(2):
                remote(
                    made.at[0], mixed.at[source, turn], m_send.at[0], m_recv.at[source, turn], here
                ).wait_recv()

    gather.finish()
    own.wait()
    if owned:
        load = pltpu.make_async_copy(gyall.at[:, :, plan.block :], w_tail, tail_sem)
        load.start()
        load.wait()
        owner_forward(plan, ctx, far, half, xs, w_seq, mixed, gysrc, w_tail, *owned)
    for copy in pending:
        copy.wait_send()
    for i in range(plan.group):
        remote(win.at[0], win_all.at[0], z_send.at[0], z_recv.at[i], here).wait_recv()
    pad, hidden = plan.pad_rows, plan.hidden_pad
    if plan.tiled:
        count = plan.quad * plan.rows

        @pl.loop(0, plan.devices // plan.quad)
        def _(i):
            at = pl.ds(pl.multiple_of(i * count, 16), count)
            value = win_all[pl.ds(i * plan.quad, plan.quad)].astype(F32)
            for gate in range(2):
                part = value[:, gate * pad : (gate + 1) * pad].reshape(count, hidden)
                w_in[at, gate * hidden : (gate + 1) * hidden] = part.astype(BF16)

    else:
        w_in[:, :hidden] = natural_rows(plan, win_all[:, :pad])
        w_in[:, hidden:] = natural_rows(plan, win_all[:, pad:])


def front(plan, length, tok, wq, win, gyw, cosine, sine, collective_id):
    slots, heads, block, width = plan.slots, plan.heads, plan.block, plan.width
    highs, ys = plan.quad // 2, plan.dp // 2
    owned = (
        jax.ShapeDtypeStruct((plan.local + MIX_ROWS, width), BF16),
        jax.ShapeDtypeStruct((plan.local, width), F32),
        jax.ShapeDtypeStruct((8, plan.local), F32),
        jax.ShapeDtypeStruct((width, width), BF16),
    )
    on = max(2 * plan.quad * max(ys - 1, 1), 2 * plan.quad + (ys - 1) * plan.ctx, plan.quad)
    return pl.pallas_call(
        functools.partial(front_kernel, plan),
        out_shape=(
            jax.ShapeDtypeStruct((plan.ctx, block, width), BF16),
            jax.ShapeDtypeStruct((width, plan.wide), BF16),
            jax.ShapeDtypeStruct((slots, width), BF16),
            jax.ShapeDtypeStruct((slots, 2 * plan.head_cols), BF16),
            jax.ShapeDtypeStruct((slots, plan.head_cols), BF16),
            jax.ShapeDtypeStruct((heads, slots, 1), F32),
            jax.ShapeDtypeStruct((plan.quad, 2, block, plan.head_cols), BF16),
            jax.ShapeDtypeStruct((plan.group, 2) + gyw.shape[1:], BF16),
            jax.ShapeDtypeStruct((width, 2 * plan.hidden_pad), BF16),
            jax.ShapeDtypeStruct(gyw.shape, BF16),
        )
        + (owned if plan.tiled else ()),
        in_specs=[pl.BlockSpec(memory_space=pltpu.SMEM)] + [VMEM] * 6,
        out_specs=(VMEM,) * 7 + (HBM,) + (VMEM,) * (6 if plan.tiled else 2),
        scratch_shapes=[
            pltpu.VMEM((plan.devices,) + wq.shape[1:], BF16),
            pltpu.VMEM(wq.shape, BF16),
            pltpu.VMEM((plan.devices,) + win.shape[1:], BF16),
            pltpu.VMEM((slots, plan.wide), F32),
            pltpu.VMEM((plan.ctx, block, plan.head_cols), BF16),
            pltpu.VMEM((plan.group, 2, gyw.shape[1] - block, width), BF16),
            DMA((2, 2 * highs)),
            DMA((2, 2, highs)),
            DMA((3,)),
            DMA((3,)),
            DMA((2, 2, on)),
            DMA((plan.devices,)),
            DMA((plan.group - 1,)),
            DMA((plan.group - 1,)),
            DMA((plan.group,)),
            DMA((plan.group,)),
            DMA,
            DMA,
            DMA((plan.ctx,)),
            DMA((plan.quad, 2)),
        ]
        + gather_sems(plan),
        compiler_params=params(collective_id),
        cost_estimate=busy(90),
        name="front",
    )(length, tok, wq, win, gyw, cosine, sine)


OUT_ORDERS = (("low", "y", "high"), ("y", "low", "high"))


class OutSum:
    def __init__(self, grid, at, src, work, core_buf, bufs, load_sem, core_send, core_recv, send, recv):
        self.grid, self.at, self.src = grid, at, src
        self.work, self.core_buf, self.bufs = work, core_buf, bufs
        self.load_sem, self.core_send, self.core_recv = load_sem, core_send, core_recv
        self.send, self.recv = send, recv
        self.loaded = set()
        rows = work.shape[1] // 2
        self.rows = [slice(0, rows), slice(rows, 2 * rows)]
        self.index = [
            {o: i for i, o in enumerate(o for o in STEP_ORDER if any(o))} for _ in OUT_ORDERS
        ]

    def pair(self, offset):
        where = dict(self.at)
        for axis, step in named(offset).items():
            if step:
                where = self.grid.moved(where, axis, step)
        slot = self.grid.slot(named(offset))
        partner = self.grid.device(self.grid.moved(self.at, "core", 1))
        away = remote(
            self.src.at[self.grid.block(self.grid.moved(where, "core", 1))],
            self.core_buf.at[slot],
            self.core_send.at[slot],
            self.core_recv.at[slot],
            partner,
        )
        load = pltpu.make_async_copy(
            self.src.at[self.grid.block(where)], self.work.at[slot], self.load_sem.at[slot]
        )
        return away, load

    def start(self):
        for offset in STEP_ORDER[::-1]:
            for copy in self.pair(offset):
                copy.start()

    def onward(self, part, offset, axis):
        index, rows = self.index[part][offset], self.rows[part]
        return remote(
            self.work.at[self.grid.slot(named(offset)), rows],
            self.bufs.at[index, rows],
            self.send.at[part, index],
            self.recv.at[part, index],
            self.grid.device(self.grid.moved(self.at, axis, 1)),
        )

    def phase(self, number):
        for offset in STEP_ORDER:
            for part, order in enumerate(OUT_ORDERS):
                phase, feeds = feeds_of(order, offset)
                if phase != number:
                    continue
                if offset not in self.loaded:
                    self.loaded.add(offset)
                    for copy in self.pair(offset):
                        copy.wait()
                for feed, axis in zip(feeds, order):
                    self.onward(part, feed, axis).wait_recv()
                slot, rows = self.grid.slot(named(offset)), self.rows[part]

                @pl.loop(0, (rows.stop - rows.start) // 16)
                def _(i, slot=slot, part=part, feeds=feeds, start=rows.start):
                    span = pl.ds(pl.multiple_of(start + i * 16, 16), 16)
                    value = self.work[slot, span].astype(F32)
                    value = value + self.core_buf[slot, span].astype(F32)
                    for feed in feeds:
                        value = value + self.bufs[self.index[part][feed], span].astype(F32)
                    self.work[slot, span] = value.astype(BF16)

                if number < 3:
                    self.onward(part, offset, order[number]).start()

    def finish(self):
        for offset in STEP_ORDER:
            for part, order in enumerate(OUT_ORDERS):
                phase, _ = feeds_of(order, offset)
                if phase < 3:
                    self.onward(part, offset, order[phase]).wait_send()


class Fold:
    def __init__(self, plan, src, dst, core_buf, y_buf, added, sems):
        self.plan, self.src, self.dst = plan, src, dst
        self.core_buf, self.y_buf, self.added = core_buf, y_buf, added
        self.core_send, self.core_recv, self.y_send, self.y_recv, self.send, self.recv = sems
        self.dp, self.ctx = place()
        self.core, self.y = lax.rem(self.dp, 2), lax.div(self.dp, 2)
        self.ys = plan.dp // 2

    def core_copies(self):
        partner = (self.dp + 1 - 2 * self.core, self.ctx)
        return [
            remote(
                self.src.at[y * 2 + 1 - self.core],
                self.core_buf.at[y],
                self.core_send.at[y],
                self.core_recv.at[y],
                partner,
            )
            for y in range(self.ys)
        ]

    def y_copies(self):
        copies = []
        for step in range(1, self.ys):
            to = lax.rem(self.y + step, self.ys)
            copies.append(
                remote(
                    self.core_buf.at[to],
                    self.y_buf.at[step - 1],
                    self.y_send.at[step - 1],
                    self.y_recv.at[step - 1],
                    (to * 2 + self.core, self.ctx),
                )
            )
        return copies

    def owner_copies(self):
        copies = []
        for step in range(1, self.plan.ctx):
            to = lax.rem(self.ctx + step, self.plan.ctx)
            copies.append(
                remote(
                    self.added.at[to],
                    self.dst.at[self.ctx],
                    self.send.at[step - 1],
                    self.recv.at[step - 1],
                    (self.dp, to),
                )
            )
        return copies

    def start(self):
        for copy in self.core_copies():
            copy.start()

    def along_y(self):
        for copy in self.core_copies():
            copy.wait()

        @pl.loop(0, self.plan.ctx)
        def _(i):
            for y in range(self.ys):
                mine = self.src[y * 2 + self.core, i].astype(F32)
                self.core_buf[y, i] = (mine + self.core_buf[y, i].astype(F32)).astype(BF16)

        for copy in self.y_copies():
            copy.start()

    def to_owners(self):
        for copy in self.y_copies():
            copy.wait()

        @pl.loop(0, self.plan.ctx)
        def _(i):
            total = self.core_buf[self.y, i].astype(F32)
            for step in range(1, self.ys):
                total = total + self.y_buf[step - 1, i].astype(F32)
            self.added[i] = total.astype(BF16)

        for copy in self.owner_copies():
            copy.start()
        self.dst[pl.ds(self.ctx, 1)] = self.added[pl.ds(self.ctx, 1)]

    def finish(self):
        for copy in self.owner_copies():
            copy.wait()


def padded_rows(plan, value, count):
    if plan.pad_rows != plan.rows:
        row = lax.broadcasted_iota(jnp.int32, (count * plan.pad_rows, count * plan.rows), 0)
        col = lax.broadcasted_iota(jnp.int32, (count * plan.pad_rows, count * plan.rows), 1)
        inside = lax.rem(row, plan.pad_rows)
        wanted = lax.div(row, plan.pad_rows) * plan.rows + inside
        hit = (col == wanted) & (inside < plan.rows)
        value = nn(hit.astype(BF16), value.astype(BF16))
    return value.reshape(count, plan.pad_rows, value.shape[-1])


def fold_scratch(plan, rows, width):
    shape = (plan.ctx, rows, width)
    ys = plan.dp // 2
    return [
        pltpu.VMEM((ys,) + shape, BF16),
        pltpu.VMEM((max(ys - 1, 1),) + shape, BF16),
        pltpu.VMEM(shape, BF16),
        DMA((ys,)),
        DMA((ys,)),
        DMA((max(ys - 1, 1),)),
        DMA((max(ys - 1, 1),)),
        DMA((plan.ctx - 1,)),
        DMA((plan.ctx - 1,)),
    ]


def back_kernel(plan, summed, length_ref, x, w, cosine, sine, normed, qk_in, v_in, lse, dw_in, dw_out, out_part, middle, *rest):
    given = 6 if plan.tiled else 4
    back_body(plan, summed, length_ref, x, w, cosine, sine, normed, qk_in, v_in, lse, dw_in, dw_out, out_part, middle, rest[:given], *rest[given:])


def back_body(plan, summed, length_ref, x, w, cosine, sine, normed, qk_in, v_in, lse, dw_in, dw_out, out_part, middle, given, rwq, rwo, rwin, far_out, act_out, grad_out, dqkv, dk_acc, dv_acc, upstream_all, dnp, rdn, dwq, far_in, dealt, out_away, grad_away, act_away, d_send, d_recv, n_send, n_recv, w_send, w_recv, e_send, e_recv, s_send, s_recv, *refs):
    dp, ctx = place()
    core, y = lax.rem(dp, 2), lax.div(dp, 2)
    half, member = lax.div(ctx, plan.quad), lax.rem(ctx, plan.quad)
    far = (1 - half) * plan.quad + member
    mine = dp * plan.quad + member
    across = (dp, far)
    members = quad_members(plan, half, member)
    targets = half_members(plan, mine)
    devices = [
        (lax.div(target, plan.quad), half * plan.quad + lax.rem(target, plan.quad))
        for target in targets
    ]
    meet(
        devices
        + [across]
        + [
            (dp, (1 - half) * plan.quad + lax.rem(member + step, plan.quad))
            for step in range(1, plan.quad)
        ]
    )
    fold_refs, out_refs = refs[:18], refs[18:]
    out_sum = None
    if not summed:
        grid = Grid(plan)
        out_sum = OutSum(grid, grid.here(), out_part, *out_refs[:8])
        out_sum.start()
    if plan.tiled:
        n2g_sum, gates, n2x, gysrc, w_mix, mixed = given
        dmixed, dwo, rows8, middle_grad = out_refs[8:]
        attn_grad = owner_back(plan, n2g_sum, gates, n2x, gysrc, w_mix, mixed, middle, w, *out_refs[8:])
    else:
        dmixed, dwo, small, middle_grad = given
    arriving = []
    for i, (peer, to) in enumerate(members):
        for j, at in enumerate((ctx, far)):
            copy = remote(
                dmixed.at[to, j],
                upstream_all.at[at],
                d_send.at[2 * i + j],
                d_recv.at[2 * i + j],
                (dp, peer),
            )
            copy.start()
            arriving.append(copy)
    count = len(fold_refs) // 2
    mix_fold = Fold(plan, dwo, rwo, *fold_refs[:3], fold_refs[3:count])
    qkv_fold = Fold(plan, dwq, rwq, *fold_refs[count : count + 3], fold_refs[count + 3 :])
    if plan.tiled:
        for i in range(plan.quad):
            part = tn(mixed[i].reshape(plan.local, plan.head_cols), attn_grad)
            dwo[i] = padded_rows(plan, part, plan.ctx).astype(BF16)
    mix_fold.start()
    swaps = [
        remote(dw_in.at[2 * i + 1 - half], far_in.at[i], w_send.at[i], w_recv.at[i], across)
        for i in range(plan.dp)
    ]
    hidden, pad = plan.hidden_pad, plan.pad_rows

    def deal_copy(target):
        tdp, tmember = divmod(target, plan.quad)
        return remote(
            dealt.at[target],
            rwin.at[mine],
            e_send.at[target],
            e_recv.at[mine],
            (tdp, half * plan.quad + tmember),
        )

    def deal(i):
        swaps[i].wait()
        value = dw_in[pl.ds(2 * i + half, 1)][0].astype(F32) + far_in[i].astype(F32)
        value = padded_rows(plan, value, plan.quad)
        value = jnp.concatenate([value[:, :, :hidden], value[:, :, hidden:]], axis=1)
        dealt[i * plan.quad : (i + 1) * plan.quad] = value.astype(BF16)
        for target in range(i * plan.quad, (i + 1) * plan.quad):
            pl.when(mine != target)(lambda target=target: deal_copy(target).start())

            @pl.when(mine == target)
            def _(target=target):
                rwin[target] = dealt[target]

    for copy in swaps:
        copy.start()
    out_away[...] = dw_out[:, pl.ds(1 - half, 1)][:, 0].astype(BF16)
    swap_out = remote(out_away, far_out, s_send.at[2], s_recv.at[2], across)
    upstream_all[pl.ds(ctx, 1)] = dmixed[pl.ds(member, 1), 0]
    upstream_all[pl.ds(far, 1)] = dmixed[pl.ds(member, 1), 1]
    length = length_ref[0]
    rows, slots, heads, block = QUERY_ROWS, plan.slots, plan.heads, plan.block
    qk_width = 2 * HEAD_DIM
    dqkv[...] = jnp.zeros_like(dqkv)
    for copy in arriving:
        copy.wait()

    def token_copy(index):
        side, to = divmod(index, plan.quad)
        turn = lax.rem(half + side, 2)
        return remote(
            dnp.at[index],
            rdn.at[member, turn],
            n_send.at[index],
            n_recv.at[member, turn],
            (dp, half * plan.quad + to),
        )

    gains = jnp.zeros((1, plan.width), F32)
    spans = list(range(slots - rows, -1, -rows))
    for number, start in enumerate(spans):
        at = slice(start, start + rows)
        end = start + rows
        for head in range(heads):
            base = head * qk_width
            v_cols = slice(head * HEAD_DIM, (head + 1) * HEAD_DIM)
            q = qk_in[at, base : base + HEAD_DIM] * BF16(0.125)
            k = qk_in[:end, base + HEAD_DIM : base + qk_width]
            v = v_in[:end, v_cols]
            upstream = jnp.concatenate(
                [upstream_all[start // block + i, :, v_cols] for i in range(rows // block)], axis=0
            )
            probs = jnp.exp(masked_scores(q, k, start, length) - lse[head, at])
            dv = tn(probs.astype(BF16), upstream)
            prob_grad = nt(upstream, v)
            inner = jnp.sum(probs * prob_grad, axis=-1, keepdims=True)
            score_grad = (probs * (prob_grad - inner)).astype(BF16)
            dq = nn(score_grad, k) * 0.125
            dk = tn(score_grad, q)
            if end == slots:
                dk_acc[head] = dk
                dv_acc[head] = dv
            else:
                dk_acc[head, :end] += dk
                dv_acc[head, :end] += dv
            dqk = jnp.concatenate([dq, dk_acc[head, at]], axis=-1)
            dqkv[at, base : base + qk_width] = (
                dqk * cosine[at] - swapped_halves(dqk) * sine[at]
            ).astype(BF16)
            v_base = heads * qk_width + head * HEAD_DIM
            dqkv[at, v_base : v_base + HEAD_DIM] = dv_acc[head, at].astype(BF16)
        part = nt(dqkv[at], w[...])
        for i in range(rows // block):
            index = start // block + i
            dnp[index] = part[i * block : (i + 1) * block].astype(BF16)
            pl.when(member != index % plan.quad)(lambda index=index: token_copy(index).start())

            @pl.when(member == index % plan.quad)
            def _(index=index):
                turn = lax.rem(half + index // plan.quad, 2)
                rdn[pl.ds(member, 1), pl.ds(turn, 1)] = dnp[index][None, None]

        values = x[at].astype(F32)
        inverse = lax.rsqrt(jnp.mean(values * values, axis=-1, keepdims=True) + EPSILON)
        gains = gains + jnp.sum(part * values * inverse, axis=0, keepdims=True)
        if number == 0:
            mix_fold.along_y()
            if out_sum:
                out_sum.phase(0)
        if number == len(spans) - 2:
            mix_fold.to_owners()
            if out_sum:
                out_sum.phase(1)
    swap_out.start()
    deal(0)
    first = plan.qkv_cols - (plan.wide - 128)
    if plan.tiled:
        row = lax.broadcasted_iota(jnp.int32, (8, plan.width), 0)
        ends = [jnp.zeros((n, plan.width), F32) for n in (first, 120 - first)]
        extra = jnp.concatenate([ends[0], jnp.where(row == 0, gains, rows8[...]), ends[1]], axis=0)
        extra = jnp.transpose(extra, (1, 0))
    else:
        column = jnp.transpose(jnp.broadcast_to(gains, (128, plan.width)), (1, 0))
        lane = lax.broadcasted_iota(jnp.int32, column.shape, 1)
        extra = jnp.where(lane == first, column, small[...])
    last = plan.wide // 128 - 1

    @pl.loop(0, last + 1)
    def _(i):
        cols = pl.ds(pl.multiple_of(i * 128, 128), 128)
        value = tn(normed[...], dqkv[:, cols])
        value = jnp.where(i == last, value + extra, value)
        value = padded_rows(plan, value, plan.devices).astype(BF16)
        dwq[:, :, :, cols] = value.reshape(plan.dp, plan.ctx, plan.pad_rows, 128)

    qkv_fold.start()
    local, width = plan.local, plan.width
    if out_sum:
        out_sum.phase(2)
    for source in range(plan.quad):

        @pl.when(member != source)
        def _(source=source):
            for turn in range(2):
                remote(
                    dnp.at[0], rdn.at[source, turn], n_send.at[0], n_recv.at[source, turn], (dp, ctx)
                ).wait_recv()

    gain_row = around_gains(plan, w)[:1]
    piece = 32

    for j, own in enumerate((ctx, far)):

        @pl.loop(0, block // piece)
        def _(i, j=j, own=own):
            rows_in = pl.ds(pl.multiple_of(i * piece, piece), piece)
            total = rdn[0, j, rows_in].astype(F32)
            for source in range(1, plan.quad):
                total = total + rdn[source, j, rows_in].astype(F32)
            values = x[pl.ds(pl.multiple_of(own * block + i * piece, piece), piece)].astype(F32)
            inverse = lax.rsqrt(jnp.mean(values * values, axis=-1, keepdims=True) + EPSILON)
            scaled = total * gain_row
            result = (
                middle_grad[pl.ds(pl.multiple_of(j * block + i * piece, piece), piece)]
                + inverse * scaled
                - values
                * inverse
                * inverse
                * inverse
                * jnp.mean(scaled * values, axis=-1, keepdims=True)
            )
            if j == 0:
                grad_out[pl.ds(half, 1), rows_in] = result.astype(BF16)[None]
            else:
                grad_away[rows_in] = result.astype(BF16)

    swap_grad = remote(grad_away, grad_out.at[half], s_send.at[1], s_recv.at[1], across)
    swap_grad.start()
    qkv_fold.along_y()
    if out_sum:
        out_sum.phase(3)
    branches = out_sum.work.at[0] if out_sum else out_part

    for j in range(2):

        @pl.loop(0, block // piece)
        def _(i, j=j):
            rows_in = pl.ds(pl.multiple_of(i * piece, piece), piece)
            rows_all = pl.ds(pl.multiple_of(j * block + i * piece, piece), piece)
            value = (middle[rows_all] + branches[rows_all].astype(F32)).astype(BF16)
            if j == 0:
                act_out[pl.ds(half, 1), rows_in] = value[None]
            else:
                act_away[rows_in] = value

    swap_act = remote(act_away, act_out.at[half], s_send.at[0], s_recv.at[0], across)
    swap_act.start()
    for i in range(1, plan.dp):
        deal(i)
        if i == 1:
            qkv_fold.to_owners()
    mix_fold.finish()
    qkv_fold.finish()
    swap_act.wait()
    swap_grad.wait()
    swap_out.wait()
    for target in range(plan.group):

        @pl.when(mine != target)
        def _(target=target):
            deal_copy(target).wait_send()
            remote(
                dealt.at[0], rwin.at[target], e_send.at[0], e_recv.at[target], (dp, ctx)
            ).wait_recv()

    for index in range(plan.ctx):
        pl.when(member != index % plan.quad)(lambda index=index: token_copy(index).wait_send())
    if out_sum:
        out_sum.finish()


def back(plan, length, x, w, cosine, sine, normed, qk, v, lse, dw_in, dw_out, out_part, middle, given, collective_id):
    slots, block, width = plan.slots, plan.block, plan.width
    count = 2 * (plan.quad - 1)
    dealt = (plan.group, 2 * plan.pad_rows, plan.hidden_pad)
    summed = out_part.ndim == 2
    rows = (plan.local, width)
    out_scratch = [
        pltpu.VMEM((8,) + rows, BF16),
        pltpu.VMEM((8,) + rows, BF16),
        pltpu.VMEM((7,) + rows, BF16),
        DMA((8,)),
        DMA((8,)),
        DMA((8,)),
        DMA((2, 7)),
        DMA((2, 7)),
        pltpu.VMEM((plan.quad, 2, block, plan.head_cols), BF16),
        pltpu.VMEM((plan.dp, plan.ctx, plan.rows, width), BF16),
        pltpu.VMEM((8, width), F32),
        pltpu.VMEM((plan.local, width), F32),
    ]
    return pl.pallas_call(
        functools.partial(back_kernel, plan, summed),
        out_shape=(
            jax.ShapeDtypeStruct((plan.ctx, plan.pad_rows, plan.wide), BF16),
            jax.ShapeDtypeStruct((plan.ctx, plan.rows, width), BF16),
            jax.ShapeDtypeStruct(dealt, BF16),
            jax.ShapeDtypeStruct((plan.branches, plan.own_hidden, width), BF16),
            jax.ShapeDtypeStruct((2, block, width), BF16),
            jax.ShapeDtypeStruct((2, block, width), BF16),
        ),
        in_specs=[pl.BlockSpec(memory_space=pltpu.SMEM)]
        + [VMEM] * 10
        + [VMEM if summed else HBM]
        + [VMEM] * (1 + len(given)),
        out_specs=(VMEM,) * 6,
        scratch_shapes=[
            pltpu.VMEM((slots, plan.wide), BF16),
            pltpu.VMEM((plan.heads, slots, HEAD_DIM), F32),
            pltpu.VMEM((plan.heads, slots, HEAD_DIM), F32),
            pltpu.VMEM((plan.ctx, block, plan.head_cols), BF16),
            pltpu.VMEM((plan.ctx, block, width), BF16),
            pltpu.VMEM((plan.quad, 2, block, width), BF16),
            pltpu.VMEM((plan.dp, plan.ctx, plan.pad_rows, plan.wide), BF16),
            pltpu.VMEM((plan.dp,) + dw_in.shape[1:], BF16),
            pltpu.VMEM(dealt, BF16),
            pltpu.VMEM((plan.branches, plan.own_hidden, width), BF16),
            pltpu.VMEM((block, width), BF16),
            pltpu.VMEM((block, width), BF16),
            DMA((count,)),
            DMA((count,)),
            DMA((plan.ctx,)),
            DMA((plan.quad, 2)),
            DMA((plan.dp,)),
            DMA((plan.dp,)),
            DMA((plan.group,)),
            DMA((plan.group,)),
            DMA((3,)),
            DMA((3,)),
        ]
        + fold_scratch(plan, plan.rows, width)
        + fold_scratch(plan, plan.pad_rows, plan.wide)
        + ([] if summed else out_scratch),
        compiler_params=params(collective_id),
        cost_estimate=busy(90),
        name="back",
    )(length, x, w, cosine, sine, normed, qk, v, lse, dw_in, dw_out, out_part, middle, *given)


def ffn_kernel(plan, members, n2x, gy, w_in, w_out, pick, out, n2g, dw_in, dw_out):
    hidden, local = plan.hidden_pad, plan.local

    @pl.when(pl.program_id(0) == 0)
    def start():
        dw_in[...] = jnp.zeros_like(dw_in)
        dw_out[...] = jnp.zeros_like(dw_out)

    tokens = members * local
    width = plan.width
    normed = n2x[:, :local].reshape(tokens, width)
    upstream = gy[:, :, : plan.block].reshape(tokens, width)
    mixing = jnp.concatenate(
        [tn(n2x[i, local:, :local], pick[...]) for i in range(members)], axis=0
    )
    pre = nn(normed, w_in[...])
    gate, up = pre[:, :hidden], pre[:, hidden:]
    sigmoid = jax.nn.sigmoid(gate)
    silu = gate * sigmoid
    act = (silu * up).astype(BF16).astype(F32)
    act_mixed = (act * mixing).astype(BF16)
    out[...] = nn(act_mixed, w_out[...]).astype(BF16).reshape(members, local, width)
    act_grad = nt(upstream, w_out[...])
    choice = nt(pick[...], (act * act_grad).astype(BF16)).astype(BF16)
    act_grad = act_grad * mixing
    gate_grad = act_grad * up * sigmoid * (1.0 + gate * (1.0 - sigmoid))
    pre_grad = jnp.concatenate([gate_grad, act_grad * silu], axis=-1).astype(BF16)
    n2g[:, :local] = nt(pre_grad, w_in[...]).astype(BF16).reshape(members, local, width)
    pad = jnp.zeros((MIX_ROWS, width - local), BF16)
    for i in range(members):
        n2g[i, local:] = jnp.concatenate(
            [choice[:, i * local : (i + 1) * local], pad], axis=-1
        )
    dw_in[...] += tn(normed, pre_grad)
    dw_out[...] += tn(act_mixed, upstream)


def ffn(plan, n2x, gy, w_in, w_out, pick):
    members = 2
    local, width, hidden = plan.local, plan.width, plan.hidden_pad
    whole = lambda i: (0, 0)
    part = lambda i: (i, 0, 0)
    return pl.pallas_call(
        functools.partial(ffn_kernel, plan, members),
        grid=(plan.group // members,),
        out_shape=(
            jax.ShapeDtypeStruct((plan.group, local, width), BF16),
            jax.ShapeDtypeStruct((plan.group, local + MIX_ROWS, width), BF16),
            jax.ShapeDtypeStruct((width, 2 * hidden), F32),
            jax.ShapeDtypeStruct((hidden, width), F32),
        ),
        in_specs=[
            pl.BlockSpec((members, local + MIX_ROWS, width), part),
            pl.BlockSpec((members,) + gy.shape[1:], lambda i: (i, 0, 0, 0)),
            pl.BlockSpec((width, 2 * hidden), whole),
            pl.BlockSpec((hidden, width), whole),
            pl.BlockSpec((MIX_ROWS, hidden), whole),
        ],
        out_specs=(
            pl.BlockSpec((members, local, width), part),
            pl.BlockSpec((members, local + MIX_ROWS, width), part),
            pl.BlockSpec((width, 2 * hidden), whole),
            pl.BlockSpec((hidden, width), whole),
        ),
        compiler_params=params(),
        name="ffn",
    )(n2x, gy, w_in, w_out, pick)


STEP_ORDER = ((0, 0, 0), (0, 0, 1), (0, 1, 0), (1, 0, 1), (1, 1, 0), (1, 1, 1), (0, 1, 1), (1, 0, 0))
PART_ORDERS = (("high", "low", "y"), ("low", "y", "high"), ("y", "high", "low"))
PAUSES = {
    3: (('g0', 7), ('g0', 2), ('g0', 1), ('g1', 1), ('g2', 1)),
    4: (('g1', 2), ('g2', 7), ('g2', 2), ('g1', 7)),
    5: (('g0', 4), ('g0', 3), ('g1', 3)),
    7: (('g2', 3), ('g0', 6), ('g2', 6), ('s2', 1)),
    8: (('g1', 4), ('g2', 4)),
    9: (('g1', 6),),
    10: (('s1', 2),),
    11: (('g0', 5), ('g2', 5)),
    13: (('g1', 5), ('s0', 3), ('s2', 3)),
    16: (('s0', 4), ('s1', 4)),
    19: (('s0', 5), ('s1', 5), ('s2', 5)),
    20: (('s0', 2),),
    22: (('s1', 6), ('s2', 6)),
    23: (('s1', 3), ('s2', 4), ('s0', 6)),
    24: (('s0', 7), ('s2', 7), ('s1', 1), ('s2', 2), ('s1', 7), ('s0', 1), ('s2', 0), ('s0', 0), ('s1', 0)),
}


def part_rows(rows):
    cuts = [round_up(rows * i // 3, 16) for i in range(3)] + [rows]
    return [slice(a, b) for a, b in zip(cuts, cuts[1:])]


def named(offset):
    return dict(zip(("high", "low", "y"), offset))


def feeds_of(order, offset):
    at = named(offset)
    phase = min([i for i, axis in enumerate(order) if at[axis]], default=3)
    names = ("high", "low", "y")
    return phase, [tuple(1 if n == axis else at[n] for n in names) for axis in order[:phase]]


def fused_kernel(plan, n2x, gy, w_in, w_out, pick, total, dw_in, dw_out, out_all, n2all, gybuf, acc, away, work, core_buf, bufs, outbuf, gy_sem, out_sem, g_send, g_recv, gc_send, gc_recv, c_send, c_recv, r_send, r_recv):
    grid = Grid(plan)
    at = grid.here()
    local, width, hidden = plan.local, plan.width, plan.hidden_pad
    steps = len(STEP_ORDER)
    partner = grid.device(grid.moved(at, "core", 1))
    here = grid.device(at)
    parts = range(len(PART_ORDERS))
    in_rows, sum_rows = part_rows(local + MIX_ROWS), part_rows(local + MIX_ROWS)

    def absolute(offset):
        where = dict(at)
        for axis, step in named(offset).items():
            if step:
                where = grid.moved(where, axis, step)
        return where

    def slot_of(offset):
        return grid.slot(named(offset))

    def level_of(part, offset):
        reached = named(offset)
        return max([i + 1 for i, axis in enumerate(PART_ORDERS[part]) if reached[axis]], default=0)

    send_index = {}
    for part in parts:
        count = 0
        for offset in STEP_ORDER:
            for axis in PART_ORDERS[part][level_of(part, offset) :]:
                send_index[part, offset, axis] = count
                count += 1

    def pass_on(part, offset):
        level = level_of(part, offset)
        block = grid.block(absolute(offset))
        slot = slot_of(offset)
        span = in_rows[part]
        landing = n2all.at[block, span]
        if level:
            remote(landing, landing, g_send.at[part, 0], g_recv.at[part, slot], here).wait_recv()
        source = landing if level else n2x.at[span]
        for axis in PART_ORDERS[part][level:]:
            seen = grid.slot({**named(offset), axis: 1})
            remote(
                source,
                landing,
                g_send.at[part, send_index[part, offset, axis]],
                g_recv.at[part, seen],
                grid.device(grid.moved(at, axis, 1)),
            ).start()
        remote(source, landing, gc_send.at[part, slot], gc_recv.at[part, slot], partner).start()

    listed = [(kind[0], int(kind[1]), STEP_ORDER[place]) for row in PAUSES.values() for kind, place in row]
    buf_index, seen_slots, first_sums = {}, set(), set()
    for kind, part, offset in listed:
        if kind == "s":
            if offset not in seen_slots:
                seen_slots.add(offset)
                first_sums.add((part, offset))
            if any(offset):
                buf_index[part, offset] = sum(1 for other, _ in buf_index if other == part)

    def add_up(part, offset):
        phase, feeds = feeds_of(PART_ORDERS[part], offset)
        axis = PART_ORDERS[part][phase] if phase < 3 else None
        slot = slot_of(offset)
        span = sum_rows[part]
        if (part, offset) in first_sums:
            remote(away.at[0], core_buf.at[slot], c_send.at[0], c_recv.at[slot], here).wait_recv()
        for feed in feeds:
            index = buf_index[part, feed]
            ref = bufs.at[index, span]
            remote(ref, ref, r_send.at[part, 0], r_recv.at[part, index], here).wait_recv()

        @pl.loop(0, (span.stop - span.start) // 16)
        def _(i):
            rows = pl.ds(pl.multiple_of(span.start + i * 16, 16), 16)
            value = work[slot, rows].astype(F32) + core_buf[slot, rows].astype(F32)
            for feed in feeds:
                value = value + bufs[buf_index[part, feed], rows].astype(F32)
            if axis is None:
                total[rows] = value
            else:
                work[slot, rows] = value.astype(BF16)

        if axis is not None:
            index = buf_index[part, offset]
            remote(
                work.at[slot, span],
                bufs.at[index, span],
                r_send.at[part, index],
                r_recv.at[part, index],
                grid.device(grid.moved(at, axis, 1)),
            ).start()

    def pause(number):
        for kind, place in PAUSES.get(number, ()):
            act = pass_on if kind[0] == "g" else add_up
            act(int(kind[1]), STEP_ORDER[place])

    def pauses(step, turn):
        for i in range(steps):
            if 3 * i + turn in PAUSES:
                pl.when(step == i)(functools.partial(pause, 3 * i + turn))

    def bit(step, index):
        value = 0
        for i, offset in enumerate(STEP_ORDER):
            if offset[index]:
                value = value + jnp.where(step == i, 1, 0)
        return value

    def blocks_of(step):
        where = dict(at)
        offsets = {}
        for index, axis in enumerate(("high", "low", "y")):
            offsets[axis] = bit(step, index)
            where[axis] = lax.rem(at[axis] + offsets[axis], 2)
        mine = grid.block(where)
        other = grid.block(grid.moved(where, "core", 1))
        return mine, other, grid.slot(offsets)

    def gy_loads(step, turn):
        mine, other, _ = blocks_of(step)
        return [
            pltpu.make_async_copy(gy.at[mine, :, : plan.block], gybuf.at[turn, 0], gy_sem.at[turn, 0]),
            pltpu.make_async_copy(gy.at[other, :, : plan.block], gybuf.at[turn, 1], gy_sem.at[turn, 1]),
        ]

    def out_copy(turn, i, block):
        return pltpu.make_async_copy(outbuf.at[turn, i], out_all.at[block], out_sem.at[turn, i])

    for load in gy_loads(0, 0):
        load.start()
    meet(grid.peers(at))
    for part in parts:
        pass_on(part, STEP_ORDER[0])
    n2all[pl.ds(grid.block(at), 1)] = n2x[...][None]

    @pl.loop(0, width // 64)
    def _(i):
        acc[pl.ds(pl.multiple_of(i * 64, 64), 64)] = jnp.zeros((64, 2 * hidden), F32)

    @pl.loop(0, hidden // 64)
    def _(i):
        dw_out[pl.ds(pl.multiple_of(i * 64, 64), 64)] = jnp.zeros((64, width), F32)

    @pl.loop(0, steps)
    def _(step):
        pauses(step, 0)
        mine, other, slot = blocks_of(step)
        turn = lax.rem(step, 2)

        @pl.when(step + 1 < steps)
        def _():
            for load in gy_loads(step + 1, 1 - turn):
                load.start()

        for part in parts:
            ref = n2all.at[other, in_rows[part]]
            remote(ref, ref, gc_send.at[part, 0], gc_recv.at[part, slot], here).wait_recv()
        for load in gy_loads(step, turn):
            load.wait()
        pair = (mine, other)
        normed = jnp.concatenate([n2all[b, :local] for b in pair], axis=0)
        upstream = gybuf[turn].reshape(2 * local, width)
        mixing = jnp.concatenate([tn(n2all[b, local:, :local], pick[...]) for b in pair], axis=0)
        pre = nn(normed, w_in[...])
        gate, up = pre[:, :hidden], pre[:, hidden:]
        sigmoid = jax.nn.sigmoid(gate)
        silu = gate * sigmoid
        act = (silu * up).astype(BF16).astype(F32)
        act_mixed = (act * mixing).astype(BF16)
        pauses(step, 1)

        @pl.when(step >= 2)
        def _():
            for i, block in enumerate(pair):
                out_copy(turn, i, block).wait()

        out = nn(act_mixed, w_out[...]).astype(BF16)
        for i, block in enumerate(pair):
            outbuf[turn, i] = out[i * local : (i + 1) * local]
            out_copy(turn, i, block).start()
        act_grad = nt(upstream, w_out[...])
        choice = nt(pick[...], (act * act_grad).astype(BF16)).astype(BF16)
        act_grad = act_grad * mixing
        gate_grad = act_grad * up * sigmoid * (1.0 + gate * (1.0 - sigmoid))
        pre_grad = jnp.concatenate([gate_grad, act_grad * silu], axis=-1).astype(BF16)
        n2g = nt(pre_grad, w_in[...]).astype(BF16)

        @pl.when(step >= 2)
        def _():
            remote(away.at[turn], core_buf.at[0], c_send.at[turn], c_recv.at[0], partner).wait_send()

        pad = jnp.zeros((MIX_ROWS, width - local), BF16)
        for i, (ref, index) in enumerate(((work, slot), (away, turn))):
            span = slice(i * local, (i + 1) * local)
            ref[index, :local] = n2g[span]
            ref[index, local:] = jnp.concatenate([choice[:, span], pad], axis=-1)
        remote(away.at[turn], core_buf.at[slot], c_send.at[turn], c_recv.at[slot], partner).start()
        pauses(step, 2)
        acc[...] += tn(normed, pre_grad)
        dw_out[...] += tn(act_mixed, upstream)

    pause(3 * steps)
    for turn in range(2):
        for i in range(2):
            out_copy(turn, i, 0).wait()

    @pl.loop(0, width // 64)
    def _(i):
        rows = pl.ds(pl.multiple_of(i * 64, 64), 64)
        dw_in[rows] = acc[rows].astype(BF16)

    for turn in range(2):
        remote(away.at[turn], core_buf.at[0], c_send.at[turn], c_recv.at[0], partner).wait_send()
    for part in parts:
        ref, block = n2all.at[0, in_rows[part]], bufs.at[0, sum_rows[part]]
        for slot in range(steps):
            remote(ref, ref, gc_send.at[part, slot], g_recv.at[part, 0], partner).wait_send()
        for index in range(steps - 1):
            remote(ref, ref, g_send.at[part, index], g_recv.at[part, 0], partner).wait_send()
            remote(block, block, r_send.at[part, index], r_recv.at[part, 0], partner).wait_send()


def fused(plan, n2x, gy, w_in, w_out, pick, collective_id):
    local, width, hidden = plan.local, plan.width, plan.hidden_pad
    steps = len(STEP_ORDER)
    rows = local + MIX_ROWS
    return pl.pallas_call(
        functools.partial(fused_kernel, plan),
        out_shape=(
            jax.ShapeDtypeStruct((rows, width), F32),
            jax.ShapeDtypeStruct((width, 2 * hidden), BF16),
            jax.ShapeDtypeStruct((hidden, width), F32),
            jax.ShapeDtypeStruct((plan.group, local, width), BF16),
        ),
        in_specs=[VMEM, HBM, VMEM, VMEM, VMEM],
        out_specs=(VMEM,) * 3 + (HBM,),
        scratch_shapes=[
            pltpu.VMEM((plan.group, local + MIX_ROWS, width), BF16),
            pltpu.VMEM((2, 2, 2, plan.block, width), BF16),
            pltpu.VMEM((width, 2 * hidden), F32),
            pltpu.VMEM((2, rows, width), BF16),
            pltpu.VMEM((steps, rows, width), BF16),
            pltpu.VMEM((steps, rows, width), BF16),
            pltpu.VMEM((steps - 1, rows, width), BF16),
            pltpu.VMEM((2, 2, local, width), BF16),
            DMA((2, 2)),
            DMA((2, 2)),
            DMA((3, steps - 1)),
            DMA((3, steps)),
            DMA((3, steps)),
            DMA((3, steps)),
            DMA((2,)),
            DMA((steps,)),
            DMA((3, steps - 1)),
            DMA((3, steps - 1)),
        ],
        compiler_params=params(collective_id),
        cost_estimate=busy(100),
        name="fused",
    )(n2x, gy, w_in, w_out, pick)


def turned(value):
    return pltpu.roll(value, 64, 1)


def half_tiles(plan):
    return lax.broadcasted_iota(jnp.int32, (plan.rows, 128), 1) < 64


def column_tiles(plan, pair, gate):
    per = plan.quad // 2
    start = gate * FF + lax.div(pair, per) * (plan.ctx * 64) + lax.rem(pair, per) * 128
    first = lax.div(pair, per) * plan.quad + lax.rem(pair, per) * 2
    return [pl.ds(pl.multiple_of(start + half * plan.quad * 64, 128), 128) for half in range(2)], first


def pack_kernel(plan, both, attn, extra, wq, win):
    low = half_tiles(plan)

    @pl.loop(0, plan.group // 2)
    def _(pair):
        for branch in range(plan.branches):
            made = [[], []]
            for gate in range(2):
                cols, first = column_tiles(plan, pair, gate)
                mine, far = (both[branch, :, col].astype(F32) for col in cols)
                made[0].append(jnp.where(low, mine, turned(far)))
                made[1].append(jnp.where(low, turned(mine), far))
            for i in range(2):
                value = jnp.concatenate(made[i], axis=0).astype(BF16)
                win[pl.ds(first + i, 1), :, branch * 128 : (branch + 1) * 128] = value[None]

    def tile(part, head):
        start = part * HEADS * HEAD_DIM + head // 2 * 128
        return attn[:, start : start + 128].astype(F32)

    def placed(part, head, side):
        value = tile(part, head)
        return value if head % 2 == side else turned(value)

    for member in range(plan.quad):
        heads = [member * 3 + i for i in range(3)]
        for i, head in enumerate(heads):
            value = jnp.where(low, placed(0, head, 0), placed(1, head, 1))
            wq[member, :, i * 128 : (i + 1) * 128] = value.astype(BF16)
        value = jnp.where(low, placed(2, heads[0], 0), placed(2, heads[1], 1))
        wq[member, :, 384:512] = value.astype(BF16)
        value = jnp.where(low, placed(2, heads[2], 0), extra[...].astype(F32))
        wq[member, :, 512:640] = value.astype(BF16)


def pack(plan, both, attn, extra):
    return pl.pallas_call(
        functools.partial(pack_kernel, plan),
        out_shape=(
            jax.ShapeDtypeStruct((plan.quad, plan.rows, plan.wide), BF16),
            jax.ShapeDtypeStruct((plan.group, 2 * plan.rows, plan.hidden_pad), BF16),
        ),
        in_specs=[VMEM] * 3,
        out_specs=(VMEM,) * 2,
        compiler_params=params(),
        cost_estimate=busy(3),
        name="pack",
    )(both, attn, extra)


def unpack_kernel(plan, r_in, r_qkv, r_mix, dw_out, far_out, act, grad, dense_in, expert_in, attn_in, attn_out, gain_one, gain_two, router, dense_out, expert_out, act_out, grad_out):
    act_out[...] = act[...]
    grad_out[...] = grad[...]
    low = half_tiles(plan)
    rows = plan.rows

    @pl.loop(0, plan.group // 2)
    def _(pair):
        first = column_tiles(plan, pair, 0)[1]
        for branch in range(plan.branches):
            cols = slice(branch * 128, (branch + 1) * 128)
            sources = [r_in[first + i, :, cols].astype(F32) for i in range(2)]
            for gate in range(2):
                one, two = (value[gate * rows : (gate + 1) * rows] for value in sources)
                places = column_tiles(plan, pair, gate)[0]
                values = jnp.where(low, one, turned(two)), jnp.where(low, turned(one), two)
                for place_at, value in zip(places, values):
                    if branch == 0:
                        dense_in[:, place_at] = value
                    else:
                        expert_in[:, branch - 1, place_at] = value

    def tile(member, number):
        cols = slice(number * 128, (number + 1) * 128)
        return r_qkv[member, :, cols].astype(F32) + r_qkv[plan.quad + member, :, cols].astype(F32)

    def put(part, head, value):
        start = part * HEADS * HEAD_DIM + head // 2 * 128
        attn_in[:, start : start + 128] = value

    for head in range(0, HEADS, 2):
        one, two = (tile((head + i) // 3, (head + i) % 3) for i in range(2))
        put(0, head, jnp.where(low, one, turned(two)))
        put(1, head, jnp.where(low, turned(one), two))
        halves = []
        for i in range(2):
            member, at = divmod(head + i, 3)
            value = tile(member, 3 + at // 2)
            halves.append(value if at % 2 == i else turned(value))
        put(2, head, jnp.where(low, halves[0], halves[1]))
    total = tile(0, 4)
    for member in range(1, plan.quad):
        total = total + tile(member, 4)
    columns = jnp.transpose(jnp.concatenate([total] * 2, axis=0)[:32], (1, 0))
    gain_one[...] = columns[64:72, :rows][:1]
    gain_two[...] = columns[64:72, :rows][1:2]
    router[...] = total[:, 66 : 66 + plan.experts]
    mixed = r_mix[0].astype(F32)
    for i in range(1, plan.ctx):
        mixed = mixed + r_mix[i].astype(F32)
    attn_out[...] = mixed
    half = lax.div(lax.axis_index("ctx"), plan.quad)
    for branch in range(plan.branches):
        value = dw_out[branch, pl.ds(half, 1)][0] + far_out[branch].astype(F32)
        if branch == 0:
            dense_out[...] = value
        else:
            expert_out[:, branch - 1, :] = value


def unpack(plan, r_in, r_qkv, r_mix, dw_out, far_out, act, grad):
    rows, width, own = plan.rows, plan.width, plan.own_hidden
    return pl.pallas_call(
        functools.partial(unpack_kernel, plan),
        out_shape=(
            jax.ShapeDtypeStruct((rows, 2 * FF), F32),
            jax.ShapeDtypeStruct((rows, plan.experts, 2 * FF), F32),
            jax.ShapeDtypeStruct((rows, 3 * HEADS * HEAD_DIM), F32),
            jax.ShapeDtypeStruct((rows, width), F32),
            jax.ShapeDtypeStruct((1, rows), F32),
            jax.ShapeDtypeStruct((1, rows), F32),
            jax.ShapeDtypeStruct((rows, plan.experts), F32),
            jax.ShapeDtypeStruct((own, width), F32),
            jax.ShapeDtypeStruct((own, plan.experts, width), F32),
            jax.ShapeDtypeStruct(act.shape, BF16),
            jax.ShapeDtypeStruct(grad.shape, BF16),
        ),
        in_specs=[VMEM] * 7,
        out_specs=(VMEM,) * 11,
        compiler_params=params(),
        cost_estimate=busy(5),
        name="unpack",
    )(r_in, r_qkv, r_mix, dw_out, far_out, act, grad)


def grid_block(plan, dp, ctx):
    return dp * plan.quad + lax.rem(ctx, plan.quad)


def by_half(half, mine, far, axis):
    return jnp.where(
        half == 0, jnp.stack([mine, far], axis), jnp.stack([far, mine], axis)
    )


def rope_tables(plan):
    half, step = HEAD_DIM // 2, 64
    frequency = np.float32(10000.0) ** (-np.arange(half, dtype=np.float32) / np.float32(half))
    frequency = np.tile(frequency.astype(np.float64), 4)[None]
    coarse = np.arange(0, plan.slots, step)[:, None] * frequency
    fine = np.arange(step)[:, None] * frequency
    sign = np.tile(np.repeat([-1.0, 1.0], half), 2)[None]
    (ca, sa), (cb, sb) = (
        (jnp.asarray(np.cos(a), F32), jnp.asarray(np.sin(a), F32)) for a in (coarse, fine)
    )
    ca, sa, cb, sb = ca[:, None], sa[:, None], cb[None], sb[None]
    cosine = (ca * cb - sa * sb).reshape(plan.slots, 128)
    sine = ((sa * cb + ca * sb) * jnp.asarray(sign, F32)).reshape(plan.slots, 128)
    return cosine, sine


def pick_table(plan):
    table = np.zeros((MIX_ROWS, plan.hidden_pad), np.float32)
    span = HALVES * plan.own_hidden
    for expert in range(plan.experts):
        cols = slice((1 + expert) * span, (2 + expert) * span)
        table[2 + expert, cols] = 1.0
        table[10 + expert, cols] = 1.0
    table[0, :span] = 1.0
    return jnp.asarray(table, BF16)


def pack_qkv(plan, attn_in, attn_gain, ffn_gain, router):
    rows, quad, heads = plan.rows, plan.quad, plan.heads
    qkv = attn_in.reshape(rows, 3, HEADS, HEAD_DIM)
    qkv = jnp.pad(qkv, ((0, 0), (0, 0), (0, quad * heads - HEADS), (0, 0)))
    qkv = qkv.reshape(rows, 3, quad, heads, HEAD_DIM)
    qk = jnp.transpose(qkv[:, :2], (2, 0, 3, 1, 4)).reshape(quad, rows, 2 * plan.head_cols)
    v = jnp.transpose(qkv[:, 2], (1, 0, 2, 3)).reshape(quad, rows, plan.head_cols)
    extra = jnp.concatenate([attn_gain[:, None], ffn_gain[:, None], router], axis=1)
    extra = jnp.pad(extra, ((0, 0), (0, plan.wide - plan.qkv_cols - extra.shape[1])))
    extra = jnp.broadcast_to(extra[None], (quad,) + extra.shape)
    packed = jnp.concatenate([qk, v, extra], axis=-1)
    return jnp.pad(packed, ((0, 0), (0, plan.pad_rows - rows), (0, 0)))


def unpack_qkv(plan, packed):
    rows, quad, heads = plan.rows, plan.quad, plan.heads
    qk = packed[..., : 2 * plan.head_cols].reshape(quad, rows, heads, 2, HEAD_DIM)
    v = packed[..., 2 * plan.head_cols : plan.qkv_cols].reshape(quad, rows, heads, 1, HEAD_DIM)
    qkv = jnp.transpose(jnp.concatenate([qk, v], axis=3), (1, 3, 0, 2, 4))
    qkv = qkv.reshape(rows, 3, quad * heads, HEAD_DIM)[:, :, :HEADS]
    return qkv.reshape(rows, 3 * HEADS * HEAD_DIM)


def pack_in(plan, dense_in, expert_in):
    rows, own = plan.rows, plan.own_hidden
    both = jnp.concatenate([dense_in[:, None], expert_in], axis=1)
    both = both.reshape(rows, plan.branches, 2, plan.dp, HALVES, plan.quad, own)
    both = jnp.transpose(both, (3, 5, 2, 0, 1, 4, 6))
    both = both.reshape(plan.group, 2, rows, plan.hidden)
    pads = ((0, 0), (0, 0), (0, plan.pad_rows - rows), (0, plan.hidden_pad - plan.hidden))
    return jnp.pad(both, pads).reshape(plan.group, 2 * plan.pad_rows, plan.hidden_pad)


def unpack_in(plan, packed):
    rows, own = plan.rows, plan.own_hidden
    both = packed.reshape(plan.group, 2, plan.pad_rows, plan.hidden_pad)
    both = both[:, :, :rows, : plan.hidden]
    both = both.reshape(plan.dp, plan.quad, 2, rows, plan.branches, HALVES, own)
    both = jnp.transpose(both, (3, 4, 2, 0, 5, 1, 6))
    both = both.reshape(rows, plan.branches, 2 * FF).astype(F32)
    return both[:, 0], both[:, 1:]


def shards(
    tokens,
    lengths,
    routes,
    cotangent,
    attn_gain,
    attn_in,
    attn_out,
    ffn_gain,
    router,
    dense_in,
    dense_out,
    expert_in,
    expert_out,
):
    micro, seqs, block, width = tokens.shape
    experts = expert_in.shape[1]
    plan = Plan(lax.axis_size("dp"), lax.axis_size("ctx"), block, width, experts)
    assert micro == HALVES and seqs == 1 and plan.ctx % 4 == 0 and plan.dp % 2 == 0
    quad, local = plan.quad, plan.local
    dp, ctx = place()
    half, member = lax.div(ctx, quad), lax.rem(ctx, quad)
    across = [(i, (i + quad) % plan.ctx) for i in range(plan.ctx)]

    def swap(value):
        return lax.ppermute(value, "ctx", across)

    def pick_mine(value):
        return lax.dynamic_index_in_dim(value, half, 0, keepdims=False)

    def pick_far(value):
        return lax.dynamic_index_in_dim(value, 1 - half, 0, keepdims=False)

    slot = ctx * block + jnp.arange(block, dtype=jnp.int32)
    valid = (slot[None] < lengths).astype(BF16)
    grad_all = cotangent[:, 0] * valid[..., None]
    tail = round_up(plan.rows + 2, 16)
    route_rows = jnp.transpose(routes[:, 0], (0, 2, 1)).astype(BF16)
    route_rows = jnp.pad(route_rows, ((0, 0), (0, tail - plan.rows - 2), (0, width - block)))
    length = pick_mine(lengths)
    out_own = jnp.concatenate([dense_out[:, None], expert_out], axis=1)
    out_own = jnp.transpose(out_own, (1, 0, 2))
    out_far = swap(out_own)
    gyw = jnp.concatenate(
        [grad_all, jnp.broadcast_to(attn_out, (2,) + attn_out.shape), route_rows], axis=1
    )

    if plan.tiled:
        both = jnp.concatenate([dense_in[None], jnp.transpose(expert_in, (1, 0, 2))])
        extra = jnp.concatenate([attn_gain[:, None], ffn_gain[:, None], router], axis=1)
        extra = jnp.pad(extra, ((0, 0), (64, 64 - extra.shape[1])))
        wq, win = pack(plan, both, attn_in, extra)
    else:
        wq = pack_qkv(plan, attn_in, attn_gain, ffn_gain, router)
        win = pack_in(plan, dense_in, expert_in)

    cosine, sine = rope_tables(plan)
    xs, w_seq, normed_seq, qk, v, lse, mixed, gy, w_in, gysrc, *owned = front(
        plan,
        length,
        tokens[:, 0],
        wq,
        win,
        gyw,
        cosine,
        sine,
        1,
    )
    x_seq = xs.reshape(plan.slots, width)
    if plan.tiled:
        n2x, middle, gates, w_mix = owned
    else:
        extra = w_seq[:, plan.qkv_cols :]
        gain_one = extra[:, 0].astype(F32)[None]
        gain_two = extra[:, 1].astype(F32)[None]
        w_route = extra[:, 2 : 2 + experts]
        mixed = jnp.transpose(mixed, (1, 2, 0, 3)).reshape(local, quad * plan.head_cols)[:, :width]
        w_mix = gy[:, :, block : block + plan.rows].reshape(plan.dp, quad, 2, plan.rows, width)
        w_mix = by_half(half, w_mix[:, :, 0], w_mix[:, :, 1], 1).reshape(width, width)

        x = jnp.stack(
            [
                lax.dynamic_index_in_dim(xs, ctx, 0, keepdims=False),
                lax.dynamic_index_in_dim(xs, (1 - half) * quad + member, 0, keepdims=False),
            ]
        )
        x = x.reshape(local, width).astype(F32)
        middle = x + nn(mixed, w_mix)
        inverse_two = lax.rsqrt(jnp.mean(middle * middle, axis=-1, keepdims=True) + EPSILON)
        normed_two = (middle * inverse_two * gain_two).astype(BF16)
        own = lax.dynamic_index_in_dim(gy, grid_block(plan, dp, ctx), 0, keepdims=False)
        grad_y = own[:, :block].reshape(local, width)
        route_local = own[:, block + plan.rows : block + plan.rows + 2, :block]
        route_local = jnp.transpose(route_local, (0, 2, 1)).reshape(local, 2)
        logits = nn(normed_two, w_route)
        choose = (route_local[..., None] == jnp.arange(experts, dtype=BF16)).astype(F32)
        picked = jnp.sum(choose * logits[:, None, :], axis=-1)
        gates = jax.nn.softmax(picked, axis=-1)
        mixing = jnp.sum(gates[..., None] * choose, axis=1)
        mixing_t = mixing.T
        mixing_high = mixing_t.astype(BF16)
        mixing_low = (mixing_t - mixing_high.astype(F32)).astype(BF16)
        pads = ((2, 6 - experts), (0, 0))
        mix_rows = jnp.concatenate([jnp.pad(mixing_high, pads), jnp.pad(mixing_low, pads)])
        mix_rows = mix_rows.at[0].set(1.0)
        mix_rows = jnp.pad(mix_rows, ((0, 0), (0, width - local)))
        n2x = jnp.concatenate([normed_two, mix_rows])

    w_out = by_half(half, out_own, out_far, 1).reshape(plan.hidden, width)
    w_out = jnp.pad(w_out, ((0, plan.hidden_pad - plan.hidden), (0, 0)))
    if plan.dp == 4 and quad == 4:
        n2g_sum, dw_in, dw_out, out_part = fused(plan, n2x, gy, w_in, w_out, pick_table(plan), 3)
    else:
        n2x = gather(plan, n2x, 3)
        out_part, n2g_part, dw_in, dw_out = ffn(plan, n2x, gy, w_in, w_out, pick_table(plan))
        n2g_sum = reduce(plan, n2g_part, 5)
        out_part = reduce(plan, out_part, 7)

    if plan.tiled:
        given = (n2g_sum, gates, n2x, gysrc, w_mix, mixed)
    else:
        normed_two_grad = n2g_sum[:local]
        mixing_grad = n2g_sum[local + 2 : local + 2 + experts, :local].T
        choice_grad = jnp.sum(choose * mixing_grad[:, None, :], axis=-1)
        pick_grad = gates * (choice_grad - jnp.sum(gates * choice_grad, axis=-1, keepdims=True))
        logit_grad = jnp.sum(pick_grad[..., None] * choose, axis=1).astype(BF16)
        router_grad = tn(normed_two, logit_grad)
        normed_two_grad = normed_two_grad + nt(logit_grad, w_route)
        gain_two_grad = jnp.sum(normed_two_grad * middle * inverse_two, axis=0)
        scaled = normed_two_grad * gain_two
        middle_grad = (
            grad_y.astype(F32)
            + inverse_two * scaled
            - middle * inverse_two**3 * jnp.mean(scaled * middle, axis=-1, keepdims=True)
        )
        attn_grad = middle_grad.astype(BF16)
        dw_mix = tn(mixed, attn_grad).astype(BF16).reshape(plan.dp, plan.ctx, plan.rows, width)
        mixed_grad = nt(attn_grad, w_mix).astype(BF16)
        mixed_grad = jnp.pad(mixed_grad, ((0, 0), (0, quad * plan.head_cols - width)))
        mixed_grad = mixed_grad.reshape(2, block, quad, plan.head_cols)
        first = plan.qkv_cols - (plan.wide - 128)
        small = jnp.concatenate([gain_two_grad[:, None], router_grad], axis=1)
        small = jnp.pad(small, ((0, 0), (first + 1, 127 - first - small.shape[1])))
        given = (jnp.transpose(mixed_grad, (2, 0, 1, 3)), dw_mix, small, middle_grad)
    dw_out = dw_out[: plan.hidden].reshape(plan.branches, HALVES, plan.own_hidden, width)
    r_qkv, r_mix, r_in, far_out, activations, input_grad = back(
        plan,
        length,
        x_seq,
        w_seq,
        cosine,
        sine,
        normed_seq,
        qk,
        v,
        lse,
        dw_in.astype(BF16).reshape(plan.dp * HALVES, quad * plan.rows, 2 * plan.hidden_pad),
        dw_out,
        out_part,
        middle,
        given,
        4,
    )

    if plan.tiled:
        results = unpack(plan, r_in, r_qkv, r_mix, dw_out, far_out, activations, input_grad)
        dense_in_grad, expert_in_grad, attn_in_grad, attn_out_grad = results[:4]
        gain_one_grad, gain_two_grad, router_grad = results[4].reshape(-1), results[5].reshape(-1), results[6]
        dense_out_grad, expert_out_grad, activations, input_grad = results[7:]
    else:
        r_qkv = r_qkv[:, : plan.rows].astype(F32).reshape(HALVES, quad, plan.rows, plan.wide)
        r_qkv = jnp.sum(r_qkv, axis=0)
        attn_in_grad = unpack_qkv(plan, r_qkv)
        small = jnp.sum(r_qkv[:, :, plan.qkv_cols :], axis=0)
        attn_out_grad = jnp.sum(r_mix.astype(F32), axis=0)
        gain_one_grad, gain_two_grad, router_grad = small[:, 0], small[:, 1], small[:, 2 : 2 + experts]
        dense_in_grad, expert_in_grad = unpack_in(plan, r_in)
        dw_out = pick_mine(jnp.moveaxis(dw_out, 1, 0)) + far_out.astype(F32)
        dense_out_grad, expert_out_grad = dw_out[0], jnp.transpose(dw_out[1:], (1, 0, 2))
    return (
        activations[:, None],
        input_grad[:, None],
        gain_one_grad,
        attn_in_grad,
        attn_out_grad,
        gain_two_grad,
        router_grad,
        dense_in_grad,
        dense_out_grad,
        expert_in_grad,
        expert_out_grad,
    )


def solution(mesh):
    rows = P(("dp", "ctx"))
    matrix = P(("dp", "ctx"), None)
    cube = P(("dp", "ctx"), None, None)
    slots = P(None, "dp", "ctx", None)
    in_specs = (
        slots,
        P(None, "dp"),
        slots,
        slots,
        rows,
        matrix,
        matrix,
        rows,
        matrix,
        matrix,
        matrix,
        cube,
        cube,
    )
    out_specs = (
        slots,
        slots,
        rows,
        matrix,
        matrix,
        rows,
        matrix,
        matrix,
        matrix,
        cube,
        cube,
    )
    return jax.shard_map(shards, mesh=mesh, in_specs=in_specs, out_specs=out_specs, check_vma=False)
```

```python
import functools

import jax
import jax.numpy as jnp
import numpy as np
from jax import lax
from jax.experimental import pallas as pl
from jax.experimental.pallas import tpu as pltpu
from jax.sharding import PartitionSpec as P

HEADS = 12
HEAD_DIM = 64
FF = 2048
EPSILON = 1e-05
HALVES = 2
QUERY_ROWS = 256
MIX_ROWS = 16
MESH = pl.DeviceIdType.MESH
BF16 = jnp.bfloat16
F32 = jnp.float32


def round_up(value, step):
    return -(-value // step) * step


class Plan:
    def __init__(self, dp, ctx, block, width, experts):
        self.dp, self.ctx, self.block, self.width, self.experts = dp, ctx, block, width, experts
        self.quad = ctx // HALVES
        self.devices = dp * ctx
        self.group = dp * self.quad
        self.slots = ctx * block
        self.rows = width // self.devices
        self.pad_rows = round_up(self.rows, 8)
        self.heads = -(-HEADS // self.quad)
        self.head_cols = self.heads * HEAD_DIM
        self.qkv_cols = 3 * self.head_cols
        self.wide = round_up(self.qkv_cols + 2 + experts, 128)
        self.own_hidden = FF // self.devices
        self.branches = 1 + experts
        self.hidden = self.branches * HALVES * self.own_hidden
        self.hidden_pad = round_up(self.hidden, 128)
        self.local = HALVES * block
        self.tiled = (
            self.own_hidden == 64
            and self.rows % 8 == 0
            and self.quad == 4
            and self.heads == 3
            and self.wide == self.qkv_cols + 64
        )


def place():
    return lax.axis_index("dp"), lax.axis_index("ctx")


def params(collective_id=None, limit=60 * 1024 * 1024):
    if collective_id is None:
        return pltpu.CompilerParams(vmem_limit_bytes=limit)
    return pltpu.CompilerParams(
        vmem_limit_bytes=limit, collective_id=collective_id, has_side_effects=True
    )


def remote(src, dst, send_sem, recv_sem, device):
    return pltpu.make_async_remote_copy(
        src_ref=src,
        dst_ref=dst,
        send_sem=send_sem,
        recv_sem=recv_sem,
        device_id=device,
        device_id_type=MESH,
    )


def busy(microseconds):
    return pl.CostEstimate(
        flops=0, bytes_accessed=int(microseconds * 3.4e6), transcendentals=0
    )


def meet(devices):
    barrier = pltpu.get_barrier_semaphore()
    for device in devices:
        pl.semaphore_signal(barrier, inc=1, device_id=device, device_id_type=MESH)
    pl.semaphore_wait(barrier, len(devices))


def other_devices(plan, dp, ctx):
    flat = dp * plan.ctx + ctx
    result = []
    for step in range(1, plan.devices):
        target = lax.rem(flat + step, plan.devices)
        result.append((lax.div(target, plan.ctx), lax.rem(target, plan.ctx)))
    return result


def quad_members(plan, half, member):
    return [
        (half * plan.quad + lax.rem(member + step, plan.quad), lax.rem(member + step, plan.quad))
        for step in range(1, plan.quad)
    ]


VMEM = pl.BlockSpec(memory_space=pltpu.VMEM)
HBM = pl.BlockSpec(memory_space=pl.ANY)
DMA = pltpu.SemaphoreType.DMA


def half_members(plan, mine):
    return [lax.rem(mine + step, plan.group) for step in range(1, plan.group)]


class Grid:
    def __init__(self, plan):
        self.plan = plan
        self.sizes = {"y": plan.dp // 2, "high": plan.quad // 2, "low": 2}

    def here(self):
        dp, ctx = place()
        member = lax.rem(ctx, self.plan.quad)
        return {
            "core": lax.rem(dp, 2),
            "y": lax.div(dp, 2),
            "high": lax.div(member, 2),
            "low": lax.rem(member, 2),
            "half": lax.div(ctx, self.plan.quad),
        }

    def device(self, at):
        return (
            at["y"] * 2 + at["core"],
            at["half"] * self.plan.quad + at["high"] * 2 + at["low"],
        )

    def block(self, at):
        return (at["y"] * 2 + at["core"]) * self.plan.quad + at["high"] * 2 + at["low"]

    def moved(self, at, axis, step):
        result = dict(at)
        if axis == "core":
            result["core"] = 1 - at["core"]
        else:
            result[axis] = lax.rem(at[axis] + step, self.sizes[axis])
        return result

    def peers(self, at):
        result = [self.moved(at, "core", 1)]
        for axis, size in self.sizes.items():
            result += [self.moved(at, axis, step) for step in range(1, size)]
        return [self.device(peer) for peer in result]

    def slot(self, offsets):
        return (offsets["y"] * self.sizes["high"] + offsets["high"]) * 2 + offsets["low"]


GATHER_ORDERS = (("high", "low", "y"), ("high", "y", "low"))


class Gather:
    def __init__(self, grid, at, src, dst, send, recv, core_send, core_recv):
        self.grid, self.at, self.src, self.dst = grid, at, src, dst
        self.send, self.recv, self.core_send, self.core_recv = send, recv, core_send, core_recv

    def groups(self, order):
        sizes = self.grid.sizes
        levels = [[{"y": 0, "high": 0, "low": 0}], [], [], []]
        for level, axis in enumerate(order):
            base = [o for group in levels[: level + 1] for o in group]
            levels[level + 1] = [
                {**offsets, axis: step} for offsets in base for step in range(1, sizes[axis])
            ]
        return levels

    def absolute(self, offsets):
        where = dict(self.at)
        for axis, step in offsets.items():
            if step:
                where = self.grid.moved(where, axis, step)
        return where

    def run_level(self, order, level):
        grid, at = self.grid, self.at
        index = 0
        for current, group in enumerate(self.groups(order)):
            for offsets in group:
                if current == level:
                    block = grid.block(self.absolute(offsets))
                    if level:
                        remote(
                            self.src,
                            self.dst.at[block],
                            self.send.at[0],
                            self.recv.at[grid.slot(offsets)],
                            grid.device(at),
                        ).wait_recv()
                    source = self.dst.at[block] if level else self.src
                    remote(
                        source,
                        self.dst.at[block],
                        self.core_send.at[grid.slot(offsets)],
                        self.core_recv.at[grid.slot(offsets)],
                        grid.device(grid.moved(at, "core", 1)),
                    ).start()
                for axis in order[current:]:
                    for step in range(1, grid.sizes[axis]):
                        if current == level:
                            seen = {**offsets, axis: grid.sizes[axis] - step}
                            remote(
                                source,
                                self.dst.at[block],
                                self.send.at[index],
                                self.recv.at[grid.slot(seen)],
                                grid.device(grid.moved(at, axis, step)),
                            ).start()
                        index += 1

    def level(self, level):
        for color, order in enumerate(GATHER_ORDERS):
            pl.when(self.at["core"] == color)(functools.partial(self.run_level, order, level))

    def finish(self):
        plan, here = self.grid.plan, self.grid.device(self.at)

        def sent(order):
            for index in range(gather_sends(plan, order)):
                remote(self.src, self.dst.at[0], self.send.at[index], self.recv.at[0], here).wait_send()

        for color, order in enumerate(GATHER_ORDERS):
            pl.when(self.at["core"] == color)(functools.partial(sent, order))
        for slot in range(plan.group // 2):
            remote(
                self.src, self.dst.at[0], self.core_send.at[slot], self.core_recv.at[slot], here
            ).wait()


def gather_kernel(plan, src, dst, send, recv, core_send, core_recv):
    grid = Grid(plan)
    at = grid.here()
    meet(grid.peers(at))
    dst[pl.ds(grid.block(at), 1)] = src[...][None]
    blocks = Gather(grid, at, src, dst, send, recv, core_send, core_recv)
    for level in range(4):
        blocks.level(level)
    blocks.finish()


def gather_sems(plan):
    half = plan.group // 2
    count = max(gather_sends(plan, order) for order in GATHER_ORDERS)
    return [DMA((count,)), DMA((half,)), DMA((half,)), DMA((half,))]


def gather_sends(plan, order):
    sizes = Grid(plan).sizes
    held, total = 1, 0
    for axis in order:
        total += held * (sizes[axis] - 1)
        held *= sizes[axis]
    return total


def gather(plan, block, collective_id):
    return pl.pallas_call(
        functools.partial(gather_kernel, plan),
        out_shape=jax.ShapeDtypeStruct((plan.group,) + block.shape, block.dtype),
        in_specs=[VMEM],
        out_specs=VMEM,
        scratch_shapes=gather_sems(plan),
        compiler_params=params(collective_id),
        cost_estimate=busy(35),
        name="gather",
    )(block)


def reduce_kernel(plan, src, out, work, core_buf, bufs, load_sem, core_send, core_recv, send, recv):
    grid = Grid(plan)
    at = grid.here()
    zero = {"y": 0, "high": 0, "low": 0}
    meet(grid.peers(at))

    def run(order):
        levels = [[], [], [], []]
        held = [dict(zero)]
        levels[3] = [dict(zero)]
        for level in (2, 1, 0):
            axis = order[level]
            base = [o for later in levels[level + 1 :] for o in later]
            levels[level] = [
                {**offsets, axis: step} for offsets in base for step in range(1, grid.sizes[axis])
            ]
        del held

        def absolute(offsets):
            where = dict(at)
            for axis, step in offsets.items():
                if step:
                    where = grid.moved(where, axis, step)
            return where

        sequence = [o for group in levels for o in group]
        partner = grid.device(grid.moved(at, "core", 1))
        core_copies = []
        loads = []
        for offsets in sequence:
            where = absolute(offsets)
            slot = grid.slot(offsets)
            copy = remote(
                src.at[grid.block(grid.moved(where, "core", 1))],
                core_buf.at[slot],
                core_send.at[slot],
                core_recv.at[slot],
                partner,
            )
            copy.start()
            core_copies.append(copy)
            load = pltpu.make_async_copy(
                src.at[grid.block(where)], work.at[slot], load_sem.at[slot]
            )
            load.start()
            loads.append(load)
        arrived = {}
        sends = []
        index = 0
        position = 0
        for level in range(4):
            for offsets in levels[level]:
                slot = grid.slot(offsets)
                core_copies[position].wait_recv()
                loads[position].wait()
                position += 1
                total = work[slot].astype(F32) + core_buf[slot].astype(F32)
                for buffer in arrived.get(slot, ()):
                    remote(work.at[slot], bufs.at[buffer], send.at[0], recv.at[buffer], partner).wait_recv()
                    total = total + bufs[buffer].astype(F32)
                if level == 3:
                    out[...] = total.astype(out.dtype)
                    continue
                work[slot] = total.astype(BF16)
                axis = order[level]
                step = offsets[axis]
                copy = remote(
                    work.at[slot],
                    bufs.at[index],
                    send.at[index],
                    recv.at[index],
                    grid.device(grid.moved(at, axis, step)),
                )
                copy.start()
                sends.append(copy)
                landing = grid.slot({**offsets, axis: 0})
                arrived.setdefault(landing, []).append(index)
                index += 1
        for copy in sends:
            copy.wait_send()
        for copy in core_copies:
            copy.wait_send()

    for color, order in enumerate(GATHER_ORDERS):
        pl.when(at["core"] == color)(functools.partial(run, order[::-1]))


def reduce(plan, blocks, collective_id):
    half = plan.group // 2
    shape = blocks.shape[1:]
    count = max(gather_sends(plan, order) for order in GATHER_ORDERS)
    return pl.pallas_call(
        functools.partial(reduce_kernel, plan),
        out_shape=jax.ShapeDtypeStruct(shape, F32),
        in_specs=[HBM],
        out_specs=VMEM,
        scratch_shapes=[
            pltpu.VMEM((half,) + shape, BF16),
            pltpu.VMEM((half,) + shape, BF16),
            pltpu.VMEM((count,) + shape, BF16),
            DMA((half,)),
            DMA((half,)),
            DMA((half,)),
            DMA((count,)),
            DMA((count,)),
        ],
        compiler_params=params(collective_id),
        name="reduce",
    )(blocks)


def nt(left, right):
    return lax.dot_general(left, right, (((1,), (1,)), ((), ())), preferred_element_type=F32)


def nn(left, right):
    return lax.dot_general(left, right, (((1,), (0,)), ((), ())), preferred_element_type=F32)


def tn(left, right):
    return lax.dot_general(left, right, (((0,), (0,)), ((), ())), preferred_element_type=F32)


def swapped_halves(value):
    lane = lax.broadcasted_iota(jnp.int32, value.shape, 1)
    first = lax.rem(lane, HEAD_DIM) < HEAD_DIM // 2
    half = HEAD_DIM // 2
    return jnp.where(
        first, pltpu.roll(value, 2 * HEAD_DIM - half, 1), pltpu.roll(value, half, 1)
    )


def masked_scores(q, k, first_row, length):
    scores = nt(q, k)
    row = lax.broadcasted_iota(jnp.int32, scores.shape, 0) + first_row
    col = lax.broadcasted_iota(jnp.int32, scores.shape, 1)
    return jnp.where((col <= row) & (col < length), scores, -1000000000.0)


def natural_rows(plan, blocks):
    flat = blocks.astype(F32).reshape(plan.devices * plan.pad_rows, blocks.shape[-1])
    if plan.pad_rows == plan.rows:
        return flat.astype(BF16)
    row = lax.broadcasted_iota(jnp.int32, (plan.width, flat.shape[0]), 0)
    col = lax.broadcasted_iota(jnp.int32, (plan.width, flat.shape[0]), 1)
    source = lax.div(row, plan.rows) * plan.pad_rows + lax.rem(row, plan.rows)
    return nn((col == source).astype(BF16), flat.astype(BF16)).astype(BF16)


def around_gains(plan, w_seq):
    first = plan.qkv_cols - (plan.wide - 128)
    return jnp.transpose(w_seq[:, plan.wide - 128 :].astype(F32), (1, 0))[first : first + 8]


def chosen(local, routes):
    row = lax.broadcasted_iota(jnp.int32, (8, local), 0).astype(F32)
    return row - 2.0 == routes


def owner_forward(plan, ctx, far, half, xs, w_seq, mixed, gysrc, w_tail, n2x, middle, gates, w_mix):
    block, local, width, cols = plan.block, plan.local, plan.width, plan.head_cols
    rows = plan.quad * plan.rows

    @pl.loop(0, HALVES * plan.dp)
    def _(i):
        turn = lax.rem(lax.rem(i, HALVES) + half, 2)
        value = w_tail[pl.ds(lax.div(i, HALVES) * plan.quad, plan.quad), pl.ds(turn, 1)]
        value = value[:, 0].astype(F32)[:, : plan.rows].reshape(rows, width)
        w_mix[pl.ds(pl.multiple_of(i * rows, 16), rows)] = value.astype(BF16)

    total = jnp.concatenate([xs[pl.ds(ctx, 1)][0], xs[pl.ds(far, 1)][0]], axis=0).astype(F32)
    for member in range(plan.quad):
        total = total + nn(
            mixed[member].reshape(local, cols), w_mix[member * cols : (member + 1) * cols]
        )
    middle[...] = total
    inverse = lax.rsqrt(jnp.mean(total * total, axis=-1, keepdims=True) + EPSILON)
    normed = (total * inverse * around_gains(plan, w_seq)[1:2]).astype(BF16)
    n2x[:local] = normed
    first = plan.qkv_cols - (plan.wide - 128)
    logits = jnp.transpose(nn(normed, w_seq[:, plan.wide - 128 :]), (1, 0))[first : first + 8]
    tail = gysrc[:, block + 16 :, :block].astype(F32)
    routes = [
        jnp.concatenate([tail[i, plan.rows - 16 + k : plan.rows - 15 + k] for i in range(2)], axis=1)
        for k in range(2)
    ]
    picks = [chosen(local, route) for route in routes]
    scores = [jnp.sum(jnp.where(pick, logits, 0.0), axis=0, keepdims=True) for pick in picks]
    top = jnp.maximum(scores[0], scores[1])
    raised = [jnp.exp(score - top) for score in scores]
    gate = [value / (raised[0] + raised[1]) for value in raised]
    mixing = jnp.where(picks[0], gate[0], 0.0) + jnp.where(picks[1], gate[1], 0.0)
    high = mixing.astype(BF16).astype(F32)
    row = lax.broadcasted_iota(jnp.int32, (8, local), 0)
    mix_rows = jnp.concatenate([jnp.where(row == 0, 1.0, high), mixing - high], axis=0)
    n2x[local:] = jnp.concatenate(
        [mix_rows.astype(BF16), jnp.zeros((MIX_ROWS, width - local), BF16)], axis=1
    )
    gates[...] = jnp.concatenate(gate + routes + [jnp.zeros((4, local), F32)], axis=0)


def owner_back(plan, n2g_sum, gates, n2x, gysrc, w_mix, mixed, middle, w_seq, dmixed, dwo, rows8, middle_grad):
    block, local, width, cols = plan.block, plan.local, plan.width, plan.head_cols
    around = around_gains(plan, w_seq)
    choice = n2g_sum[local : local + 8, :local]
    picks = [chosen(local, gates[2 + k : 3 + k]) for k in range(2)]
    gate = [gates[k : k + 1] for k in range(2)]
    taken = [jnp.sum(jnp.where(pick, choice, 0.0), axis=0, keepdims=True) for pick in picks]
    inner = gate[0] * taken[0] + gate[1] * taken[1]
    logit_grad = sum(
        jnp.where(picks[k], gate[k] * (taken[k] - inner), 0.0) for k in range(2)
    ).astype(BF16)
    router_grad = nn(logit_grad, n2x[:local])
    grad = n2g_sum[:local] + tn(logit_grad, around.astype(BF16))
    values = middle[...]
    inverse = lax.rsqrt(jnp.mean(values * values, axis=-1, keepdims=True) + EPSILON)
    gain_grad = jnp.sum(grad * values * inverse, axis=0, keepdims=True)
    row = lax.broadcasted_iota(jnp.int32, (8, width), 0)
    rows8[...] = jnp.where(row == 1, gain_grad, router_grad)
    scaled = grad * around[1:2]
    result = (
        gysrc[:, :block].reshape(local, width).astype(F32)
        + inverse * scaled
        - values * inverse * inverse * inverse * jnp.mean(scaled * values, axis=-1, keepdims=True)
    )
    middle_grad[...] = result
    upstream = result.astype(BF16)
    for member in range(plan.quad):
        part = nt(upstream, w_mix[member * cols : (member + 1) * cols])
        dmixed[member] = part.astype(BF16).reshape(2, block, cols)
    return upstream


def front_kernel(plan, length_ref, tok, wq, win, gyw, cosine, sine, xs, w_seq, normed, qk_out, v_out, lse_out, mixed, gyall, w_in, gysrc, *rest):
    owned, rest = (rest[:4], rest[4:]) if plan.tiled else ((), rest)
    front_body(plan, length_ref, tok, wq, win, gyw, cosine, sine, xs, w_seq, normed, qk_out, v_out, lse_out, mixed, gyall, w_in, gysrc, owned, *rest)


def front_body(plan, length_ref, tok, wq, win, gyw, cosine, sine, xs, w_seq, normed, qk_out, v_out, lse_out, mixed, gyall, w_in, gysrc, owned, wall, wqx, win_all, qkv, made, w_tail, x_send, x_recv, s_send, s_recv, q_send, q_recv, f_send, f_recv, z_send, z_recv, own_sem, tail_sem, m_send, m_recv, *gather_sem):
    dp, ctx = place()
    half, member = lax.div(ctx, plan.quad), lax.rem(ctx, plan.quad)
    far = (1 - half) * plan.quad + member
    flat, flat_far = dp * plan.ctx + ctx, dp * plan.ctx + far
    mine = dp * plan.quad + member
    grid = Grid(plan)
    spot = grid.here()
    here = (dp, ctx)
    across = (dp, far)
    targets = half_members(plan, mine)
    devices = [
        (lax.div(target, plan.quad), half * plan.quad + lax.rem(target, plan.quad))
        for target in targets
    ]
    members = quad_members(plan, half, member)
    highs, ys = grid.sizes["high"], grid.sizes["y"]
    meet(devices + [across])
    pending = []

    def send(*args):
        copy = remote(*args)
        copy.start()
        pending.append(copy)

    swap_x = remote(tok.at[1 - half], xs.at[ctx], s_send.at[0], s_recv.at[0], across)
    swap_w = remote(wq, wqx, s_send.at[1], s_recv.at[1], across)
    swap_gy = remote(gyw.at[1 - half], gysrc.at[1], s_send.at[2], s_recv.at[2], across)
    swap_x.start()
    swap_w.start()

    def member_of(high, low):
        return half * plan.quad + lax.rem(spot["high"] + high, highs) * 2 + lax.rem(spot["low"] + low, 2)

    def token_block(side, high):
        at = half if side == 0 else 1 - half
        return at * plan.quad + lax.rem(spot["high"] + high, highs) * 2 + spot["low"]

    def token_sends(side, source):
        block = token_block(side, 0)
        for step in range(1, highs):
            index = side * (highs - 1) + step - 1
            send(source, xs.at[block], x_send.at[0, index], x_recv.at[0, side, highs - step - 1], (dp, member_of(step, 0)))
        send(source, xs.at[block], x_send.at[1, side * highs], x_recv.at[1, side, 0], (dp, member_of(0, 1)))

    def token_forward(side):
        for high in range(1, highs):
            block = token_block(side, high)
            remote(xs.at[block], xs.at[block], x_send.at[0, 0], x_recv.at[0, side, high - 1], here).wait_recv()
            send(xs.at[block], xs.at[block], x_send.at[1, side * highs + high], x_recv.at[1, side, high], (dp, member_of(0, 1)))

    def slice_sends(side, source, block):
        for i, (peer, to) in enumerate(members):
            send(source.at[to], wall.at[block], q_send.at[0, side, i], q_recv.at[block], (dp, peer))

    core_device = grid.device(grid.moved(spot, "core", 1))
    counter = [0, 0]

    def slice_on(block, source, along_y):
        if along_y:
            for step in range(1, ys):
                send(source, wall.at[block], q_send.at[1, 0, counter[0]], q_recv.at[block], grid.device(grid.moved(spot, "y", step)))
                counter[0] += 1
        send(source, wall.at[block], q_send.at[1, 1, counter[1]], q_recv.at[block], core_device)
        counter[1] += 1

    def slice_wait(block):
        remote(wq.at[0], wall.at[block], q_send.at[0, 0, 0], q_recv.at[block], here).wait_recv()

    token_sends(0, tok.at[half])
    slice_sends(0, wq, flat)
    slice_on(flat, wq.at[member], True)
    gysrc[0] = gyw[pl.ds(half, 1)][0]
    xs[pl.ds(ctx, 1)] = tok[pl.ds(half, 1)]
    wall[pl.ds(flat, 1)] = wq[pl.ds(member, 1)]
    swap_x.wait()
    token_sends(1, xs.at[far])
    swap_w.wait()
    slice_sends(1, wqx, flat_far)
    slice_on(flat_far, wqx.at[member], True)
    swap_gy.start()
    token_forward(0)
    for i, (peer, _) in enumerate(members):
        block = dp * plan.ctx + peer
        slice_wait(block)
        slice_on(block, wall.at[block], True)
    token_forward(1)
    for _, to in members:
        block = dp * plan.ctx + (1 - half) * plan.quad + to
        slice_wait(block)
        slice_on(block, wall.at[block], True)
    wall[pl.ds(flat_far, 1)] = wqx[pl.ds(member, 1)]

    for i, (target, device) in enumerate(zip(targets, devices)):
        send(win.at[target], win_all.at[flat], f_send.at[i], f_recv.at[i], device)
    send(win.at[mine], win_all.at[flat], z_send.at[0], z_recv.at[0], across)
    win_all[pl.ds(flat, 1)] = win[pl.ds(mine, 1)]

    def columns_on(i):
        source = lax.rem(mine + plan.group - 1 - i, plan.group)
        block = lax.div(source, plan.quad) * plan.ctx + half * plan.quad + lax.rem(source, plan.quad)
        remote(win.at[0], win_all.at[block], f_send.at[0], f_recv.at[i], here).wait_recv()
        send(win_all.at[block], win_all.at[block], z_send.at[1 + i], z_recv.at[1 + i], across)

    for step in range(1, ys):
        other = lax.rem(spot["y"] + step, ys) * 2 + spot["core"]
        for place_ctx in range(plan.ctx):
            block = other * plan.ctx + place_ctx
            slice_wait(block)
            slice_on(block, wall.at[block], False)
    swap_gy.wait()
    gather = Gather(grid, spot, gysrc, gyall, *gather_sem)
    own = pltpu.make_async_copy(gysrc, gyall.at[grid.block(spot)], own_sem)
    own.start()
    gather.level(0)
    for y in range(ys):
        for place_ctx in range(plan.ctx):
            slice_wait((y * 2 + 1 - spot["core"]) * plan.ctx + place_ctx)
    for side in range(2):
        for high in range(highs):
            block = half if side == 0 else 1 - half
            block = block * plan.quad + lax.rem(spot["high"] + high, highs) * 2 + 1 - spot["low"]
            remote(xs.at[block], xs.at[block], x_send.at[0, 0], x_recv.at[1, side, high], here).wait_recv()

    length = length_ref[0]
    rows, block = QUERY_ROWS, plan.block
    slots = plan.slots
    w_seq[...] = natural_rows(plan, wall[...])
    tail = w_seq[:, plan.wide - 128 :].astype(F32)
    gain = jnp.transpose(tail, (1, 0))[plan.qkv_cols - plan.wide + 128 :][:1]

    @pl.loop(0, slots // rows)
    def _(i):
        at = pl.ds(pl.multiple_of(i * rows, rows), rows)
        values = xs[pl.ds(i * (rows // block), rows // block)].reshape(rows, plan.width)
        values = values.astype(F32)
        inverse = lax.rsqrt(jnp.mean(values * values, axis=-1, keepdims=True) + EPSILON)
        normed[at] = (values * inverse * gain).astype(BF16)
        qkv[at] = nn(normed[at], w_seq[...])
    heads = plan.heads
    qk_width = 2 * HEAD_DIM
    third = (plan.group - 1) // 3
    for i in range(third):
        columns_on(i)
    for head in range(heads):
        cols = slice(head * qk_width, (head + 1) * qk_width)
        qk = qkv[:, cols]
        qk_out[:, cols] = (qk * cosine[...] + swapped_halves(qk) * sine[...]).astype(BF16)
    v_cols = slice(heads * qk_width, heads * 3 * HEAD_DIM)
    v_out[...] = qkv[:, v_cols].astype(BF16)
    gather.level(1)
    for i in range(third, 2 * third):
        columns_on(i)

    def mixed_copy(index):
        side, to = divmod(index, plan.quad)
        turn = lax.rem(half + side, 2)
        return remote(
            made.at[index],
            mixed.at[member, turn],
            m_send.at[index],
            m_recv.at[member, turn],
            (dp, half * plan.quad + to),
        )

    spans = list(range(0, slots, rows))
    for number, start in enumerate(spans):
        at = slice(start, start + rows)
        end = start + rows
        for head in range(heads):
            base = head * qk_width
            q = qk_out[at, base : base + HEAD_DIM] * BF16(0.125)
            k = qk_out[:end, base + HEAD_DIM : base + qk_width]
            v = v_out[:end, head * HEAD_DIM : (head + 1) * HEAD_DIM]
            scores = masked_scores(q, k, start, length)
            top = jnp.max(scores, axis=-1, keepdims=True)
            raised = jnp.exp(scores - top)
            total = jnp.sum(raised, axis=-1, keepdims=True)
            lse_out[head, at] = top + jnp.log(total)
            probs = (raised * (1.0 / total)).astype(BF16)
            part = nn(probs, v).astype(BF16)
            for i in range(rows // block):
                made[start // block + i, :, head * HEAD_DIM : (head + 1) * HEAD_DIM] = part[
                    i * block : (i + 1) * block
                ]
        for i in range(rows // block):
            index = start // block + i
            pl.when(member != index % plan.quad)(lambda index=index: mixed_copy(index).start())

            @pl.when(member == index % plan.quad)
            def _(index=index):
                turn = lax.rem(half + index // plan.quad, 2)
                mixed[pl.ds(member, 1), pl.ds(turn, 1)] = made[index][None, None]

        if number == len(spans) // 2:
            for i in range(2 * third, plan.group - 1):
                columns_on(i)
            gather.level(2)
    gather.level(3)
    for index in range(plan.ctx):
        pl.when(member != index % plan.quad)(lambda index=index: mixed_copy(index).wait_send())
    for source in range(plan.quad):

        @pl.when(member != source)
        def _(source=source):
            for turn in range(2):
                remote(
                    made.at[0], mixed.at[source, turn], m_send.at[0], m_recv.at[source, turn], here
                ).wait_recv()

    gather.finish()
    own.wait()
    if owned:
        load = pltpu.make_async_copy(gyall.at[:, :, plan.block :], w_tail, tail_sem)
        load.start()
        load.wait()
        owner_forward(plan, ctx, far, half, xs, w_seq, mixed, gysrc, w_tail, *owned)
    for copy in pending:
        copy.wait_send()
    for i in range(plan.group):
        remote(win.at[0], win_all.at[0], z_send.at[0], z_recv.at[i], here).wait_recv()
    pad, hidden = plan.pad_rows, plan.hidden_pad
    if plan.tiled:
        count = plan.quad * plan.rows

        @pl.loop(0, plan.devices // plan.quad)
        def _(i):
            at = pl.ds(pl.multiple_of(i * count, 16), count)
            value = win_all[pl.ds(i * plan.quad, plan.quad)].astype(F32)
            for gate in range(2):
                part = value[:, gate * pad : (gate + 1) * pad].reshape(count, hidden)
                w_in[at, gate * hidden : (gate + 1) * hidden] = part.astype(BF16)

    else:
        w_in[:, :hidden] = natural_rows(plan, win_all[:, :pad])
        w_in[:, hidden:] = natural_rows(plan, win_all[:, pad:])


def front(plan, length, tok, wq, win, gyw, cosine, sine, collective_id):
    slots, heads, block, width = plan.slots, plan.heads, plan.block, plan.width
    highs, ys = plan.quad // 2, plan.dp // 2
    owned = (
        jax.ShapeDtypeStruct((plan.local + MIX_ROWS, width), BF16),
        jax.ShapeDtypeStruct((plan.local, width), F32),
        jax.ShapeDtypeStruct((8, plan.local), F32),
        jax.ShapeDtypeStruct((width, width), BF16),
    )
    on = max(2 * plan.quad * max(ys - 1, 1), 2 * plan.quad + (ys - 1) * plan.ctx, plan.quad)
    return pl.pallas_call(
        functools.partial(front_kernel, plan),
        out_shape=(
            jax.ShapeDtypeStruct((plan.ctx, block, width), BF16),
            jax.ShapeDtypeStruct((width, plan.wide), BF16),
            jax.ShapeDtypeStruct((slots, width), BF16),
            jax.ShapeDtypeStruct((slots, 2 * plan.head_cols), BF16),
            jax.ShapeDtypeStruct((slots, plan.head_cols), BF16),
            jax.ShapeDtypeStruct((heads, slots, 1), F32),
            jax.ShapeDtypeStruct((plan.quad, 2, block, plan.head_cols), BF16),
            jax.ShapeDtypeStruct((plan.group, 2) + gyw.shape[1:], BF16),
            jax.ShapeDtypeStruct((width, 2 * plan.hidden_pad), BF16),
            jax.ShapeDtypeStruct(gyw.shape, BF16),
        )
        + (owned if plan.tiled else ()),
        in_specs=[pl.BlockSpec(memory_space=pltpu.SMEM)] + [VMEM] * 6,
        out_specs=(VMEM,) * 7 + (HBM,) + (VMEM,) * (6 if plan.tiled else 2),
        scratch_shapes=[
            pltpu.VMEM((plan.devices,) + wq.shape[1:], BF16),
            pltpu.VMEM(wq.shape, BF16),
            pltpu.VMEM((plan.devices,) + win.shape[1:], BF16),
            pltpu.VMEM((slots, plan.wide), F32),
            pltpu.VMEM((plan.ctx, block, plan.head_cols), BF16),
            pltpu.VMEM((plan.group, 2, gyw.shape[1] - block, width), BF16),
            DMA((2, 2 * highs)),
            DMA((2, 2, highs)),
            DMA((3,)),
            DMA((3,)),
            DMA((2, 2, on)),
            DMA((plan.devices,)),
            DMA((plan.group - 1,)),
            DMA((plan.group - 1,)),
            DMA((plan.group,)),
            DMA((plan.group,)),
            DMA,
            DMA,
            DMA((plan.ctx,)),
            DMA((plan.quad, 2)),
        ]
        + gather_sems(plan),
        compiler_params=params(collective_id),
        cost_estimate=busy(90),
        name="front",
    )(length, tok, wq, win, gyw, cosine, sine)


OUT_ORDERS = (("low", "y", "high"), ("y", "low", "high"))


class OutSum:
    def __init__(self, grid, at, src, work, core_buf, bufs, load_sem, core_send, core_recv, send, recv):
        self.grid, self.at, self.src = grid, at, src
        self.work, self.core_buf, self.bufs = work, core_buf, bufs
        self.load_sem, self.core_send, self.core_recv = load_sem, core_send, core_recv
        self.send, self.recv = send, recv
        self.loaded = set()
        rows = work.shape[1] // 2
        self.rows = [slice(0, rows), slice(rows, 2 * rows)]
        self.index = [
            {o: i for i, o in enumerate(o for o in STEP_ORDER if any(o))} for _ in OUT_ORDERS
        ]

    def pair(self, offset):
        where = dict(self.at)
        for axis, step in named(offset).items():
            if step:
                where = self.grid.moved(where, axis, step)
        slot = self.grid.slot(named(offset))
        partner = self.grid.device(self.grid.moved(self.at, "core", 1))
        away = remote(
            self.src.at[self.grid.block(self.grid.moved(where, "core", 1))],
            self.core_buf.at[slot],
            self.core_send.at[slot],
            self.core_recv.at[slot],
            partner,
        )
        load = pltpu.make_async_copy(
            self.src.at[self.grid.block(where)], self.work.at[slot], self.load_sem.at[slot]
        )
        return away, load

    def start(self):
        for offset in STEP_ORDER[::-1]:
            for copy in self.pair(offset):
                copy.start()

    def onward(self, part, offset, axis):
        index, rows = self.index[part][offset], self.rows[part]
        return remote(
            self.work.at[self.grid.slot(named(offset)), rows],
            self.bufs.at[index, rows],
            self.send.at[part, index],
            self.recv.at[part, index],
            self.grid.device(self.grid.moved(self.at, axis, 1)),
        )

    def phase(self, number):
        for offset in STEP_ORDER:
            for part, order in enumerate(OUT_ORDERS):
                phase, feeds = feeds_of(order, offset)
                if phase != number:
                    continue
                if offset not in self.loaded:
                    self.loaded.add(offset)
                    for copy in self.pair(offset):
                        copy.wait()
                for feed, axis in zip(feeds, order):
                    self.onward(part, feed, axis).wait_recv()
                slot, rows = self.grid.slot(named(offset)), self.rows[part]

                @pl.loop(0, (rows.stop - rows.start) // 16)
                def _(i, slot=slot, part=part, feeds=feeds, start=rows.start):
                    span = pl.ds(pl.multiple_of(start + i * 16, 16), 16)
                    value = self.work[slot, span].astype(F32)
                    value = value + self.core_buf[slot, span].astype(F32)
                    for feed in feeds:
                        value = value + self.bufs[self.index[part][feed], span].astype(F32)
                    self.work[slot, span] = value.astype(BF16)

                if number < 3:
                    self.onward(part, offset, order[number]).start()

    def finish(self):
        for offset in STEP_ORDER:
            for part, order in enumerate(OUT_ORDERS):
                phase, _ = feeds_of(order, offset)
                if phase < 3:
                    self.onward(part, offset, order[phase]).wait_send()


class Fold:
    def __init__(self, plan, src, dst, core_buf, y_buf, added, sems, quad_refs=()):
        self.quad_refs = quad_refs
        self.plan, self.src, self.dst = plan, src, dst
        self.core_buf, self.y_buf, self.added = core_buf, y_buf, added
        self.core_send, self.core_recv, self.y_send, self.y_recv, self.send, self.recv = sems
        self.dp, self.ctx = place()
        self.core, self.y = lax.rem(self.dp, 2), lax.div(self.dp, 2)
        self.ys = plan.dp // 2

    def core_copies(self):
        partner = (self.dp + 1 - 2 * self.core, self.ctx)
        return [
            remote(
                self.src.at[y * 2 + 1 - self.core],
                self.core_buf.at[y],
                self.core_send.at[y],
                self.core_recv.at[y],
                partner,
            )
            for y in range(self.ys)
        ]

    def y_copies(self):
        copies = []
        for step in range(1, self.ys):
            to = lax.rem(self.y + step, self.ys)
            copies.append(
                remote(
                    self.core_buf.at[to],
                    self.y_buf.at[step - 1],
                    self.y_send.at[step - 1],
                    self.y_recv.at[step - 1],
                    (to * 2 + self.core, self.ctx),
                )
            )
        return copies

    def owner_copies(self):
        copies = []
        for step in range(1, self.plan.ctx):
            to = lax.rem(self.ctx + step, self.plan.ctx)
            copies.append(
                remote(
                    self.added.at[to],
                    self.dst.at[self.ctx],
                    self.send.at[step - 1],
                    self.recv.at[step - 1],
                    (self.dp, to),
                )
            )
        return copies

    def start(self):
        for copy in self.core_copies():
            copy.start()

    def along_y(self):
        for copy in self.core_copies():
            copy.wait()

        @pl.loop(0, self.plan.ctx)
        def _(i):
            for y in range(self.ys):
                mine = self.src[y * 2 + self.core, i].astype(F32)
                self.core_buf[y, i] = (mine + self.core_buf[y, i].astype(F32)).astype(BF16)

        for copy in self.y_copies():
            copy.start()

    def to_owners(self):
        for copy in self.y_copies():
            copy.wait()

        @pl.loop(0, self.plan.ctx)
        def _(i):
            total = self.core_buf[self.y, i].astype(F32)
            for step in range(1, self.ys):
                total = total + self.y_buf[step - 1, i].astype(F32)
            self.added[i] = total.astype(BF16)

        if self.quad_refs:
            quad_buf, _ = self.quad_refs
            half, member = lax.div(self.ctx, self.plan.quad), lax.rem(self.ctx, self.plan.quad)
            for copy in self.quad_copies():
                copy.start()
            for j, side in enumerate((half, 1 - half)):
                quad_buf[pl.ds(member, 1), j] = self.added[pl.ds(side * self.plan.quad + member, 1)]
            return
        for copy in self.owner_copies():
            copy.start()
        self.dst[pl.ds(self.ctx, 1)] = self.added[pl.ds(self.ctx, 1)]

    def quad_copies(self):
        quad_buf, _ = self.quad_refs
        half, member = lax.div(self.ctx, self.plan.quad), lax.rem(self.ctx, self.plan.quad)
        copies = []
        for i, (peer, to) in enumerate(quad_members(self.plan, half, member)):
            for j, side in enumerate((half, 1 - half)):
                copies.append(
                    remote(
                        self.added.at[side * self.plan.quad + to],
                        quad_buf.at[member, j],
                        self.send.at[2 * i + j],
                        self.recv.at[2 * i + j],
                        (self.dp, peer),
                    )
                )
        return copies

    def far_copy(self):
        last = 2 * (self.plan.quad - 1)
        far = lax.rem(self.ctx + self.plan.quad, self.plan.ctx)
        away = self.quad_refs[1]
        return remote(away, self.dst.at[1], self.send.at[last], self.recv.at[last], (self.dp, far))

    def across(self):
        quad_buf, away = self.quad_refs
        for copy in self.quad_copies():
            copy.wait()
        for j in range(2):
            total = quad_buf[0, j].astype(F32)
            for i in range(1, self.plan.quad):
                total = total + quad_buf[i, j].astype(F32)
            if j == 0:
                self.dst[0] = total.astype(BF16)
            else:
                away[...] = total.astype(BF16)
        self.far_copy().start()

    def finish(self):
        if self.quad_refs:
            self.far_copy().wait()
            return
        for copy in self.owner_copies():
            copy.wait()


def padded_rows(plan, value, count):
    if plan.pad_rows != plan.rows:
        row = lax.broadcasted_iota(jnp.int32, (count * plan.pad_rows, count * plan.rows), 0)
        col = lax.broadcasted_iota(jnp.int32, (count * plan.pad_rows, count * plan.rows), 1)
        inside = lax.rem(row, plan.pad_rows)
        wanted = lax.div(row, plan.pad_rows) * plan.rows + inside
        hit = (col == wanted) & (inside < plan.rows)
        value = nn(hit.astype(BF16), value.astype(BF16))
    return value.reshape(count, plan.pad_rows, value.shape[-1])


def fold_scratch(plan, rows, width):
    shape = (plan.ctx, rows, width)
    ys = plan.dp // 2
    return [
        pltpu.VMEM((ys,) + shape, BF16),
        pltpu.VMEM((max(ys - 1, 1),) + shape, BF16),
        pltpu.VMEM(shape, BF16),
        DMA((ys,)),
        DMA((ys,)),
        DMA((max(ys - 1, 1),)),
        DMA((max(ys - 1, 1),)),
        DMA((plan.ctx - 1,)),
        DMA((plan.ctx - 1,)),
    ]


def back_kernel(plan, summed, length_ref, x, w, cosine, sine, normed, qk_in, v_in, lse, dw_in, dw_out, out_part, middle, *rest):
    given = 6 if plan.tiled else 4
    back_body(plan, summed, length_ref, x, w, cosine, sine, normed, qk_in, v_in, lse, dw_in, dw_out, out_part, middle, rest[:given], *rest[given:])


def back_body(plan, summed, length_ref, x, w, cosine, sine, normed, qk_in, v_in, lse, dw_in, dw_out, out_part, middle, given, rwq, rwo, rwin, far_out, act_out, grad_out, dqkv, dk_acc, dv_acc, upstream_all, dnp, rdn, dwq, far_in, dealt, out_away, grad_away, act_away, d_send, d_recv, n_send, n_recv, w_send, w_recv, e_send, e_recv, s_send, s_recv, *refs):
    dp, ctx = place()
    core, y = lax.rem(dp, 2), lax.div(dp, 2)
    half, member = lax.div(ctx, plan.quad), lax.rem(ctx, plan.quad)
    far = (1 - half) * plan.quad + member
    mine = dp * plan.quad + member
    across = (dp, far)
    members = quad_members(plan, half, member)
    targets = half_members(plan, mine)
    devices = [
        (lax.div(target, plan.quad), half * plan.quad + lax.rem(target, plan.quad))
        for target in targets
    ]
    meet(
        devices
        + [across]
        + [
            (dp, (1 - half) * plan.quad + lax.rem(member + step, plan.quad))
            for step in range(1, plan.quad)
        ]
    )
    fold_refs, out_refs = refs[:20], refs[20:]
    out_sum = None
    if not summed:
        grid = Grid(plan)
        out_sum = OutSum(grid, grid.here(), out_part, *out_refs[:8])
        out_sum.start()
    if plan.tiled:
        n2g_sum, gates, n2x, gysrc, w_mix, mixed = given
        dmixed, dwo, rows8, middle_grad = out_refs[8:]
        attn_grad = owner_back(plan, n2g_sum, gates, n2x, gysrc, w_mix, mixed, middle, w, *out_refs[8:])
    else:
        dmixed, dwo, small, middle_grad = given
    arriving = []
    for i, (peer, to) in enumerate(members):
        for j, at in enumerate((ctx, far)):
            copy = remote(
                dmixed.at[to, j],
                upstream_all.at[at],
                d_send.at[2 * i + j],
                d_recv.at[2 * i + j],
                (dp, peer),
            )
            copy.start()
            arriving.append(copy)
    mix_fold = Fold(plan, dwo, rwo, *fold_refs[:3], fold_refs[3:9], fold_refs[9:11])
    qkv_fold = Fold(plan, dwq, rwq, *fold_refs[11:14], fold_refs[14:20])
    if plan.tiled:
        for i in range(plan.quad):
            part = tn(mixed[i].reshape(plan.local, plan.head_cols), attn_grad)
            dwo[i] = padded_rows(plan, part, plan.ctx).astype(BF16)
    mix_fold.start()
    swaps = [
        remote(dw_in.at[2 * i + 1 - half], far_in.at[i], w_send.at[i], w_recv.at[i], across)
        for i in range(plan.dp)
    ]
    hidden, pad = plan.hidden_pad, plan.pad_rows

    def deal_copy(target):
        tdp, tmember = divmod(target, plan.quad)
        return remote(
            dealt.at[target],
            rwin.at[mine],
            e_send.at[target],
            e_recv.at[mine],
            (tdp, half * plan.quad + tmember),
        )

    def deal(i):
        swaps[i].wait()
        value = dw_in[pl.ds(2 * i + half, 1)][0].astype(F32) + far_in[i].astype(F32)
        value = padded_rows(plan, value, plan.quad)
        value = jnp.concatenate([value[:, :, :hidden], value[:, :, hidden:]], axis=1)
        dealt[i * plan.quad : (i + 1) * plan.quad] = value.astype(BF16)
        for target in range(i * plan.quad, (i + 1) * plan.quad):
            pl.when(mine != target)(lambda target=target: deal_copy(target).start())

            @pl.when(mine == target)
            def _(target=target):
                rwin[target] = dealt[target]

    for copy in swaps:
        copy.start()
    out_away[...] = dw_out[:, pl.ds(1 - half, 1)][:, 0].astype(BF16)
    swap_out = remote(out_away, far_out, s_send.at[2], s_recv.at[2], across)
    upstream_all[pl.ds(ctx, 1)] = dmixed[pl.ds(member, 1), 0]
    upstream_all[pl.ds(far, 1)] = dmixed[pl.ds(member, 1), 1]
    length = length_ref[0]
    rows, slots, heads, block = QUERY_ROWS, plan.slots, plan.heads, plan.block
    qk_width = 2 * HEAD_DIM
    dqkv[...] = jnp.zeros_like(dqkv)
    for copy in arriving:
        copy.wait()

    def token_copy(index):
        side, to = divmod(index, plan.quad)
        turn = lax.rem(half + side, 2)
        return remote(
            dnp.at[index],
            rdn.at[member, turn],
            n_send.at[index],
            n_recv.at[member, turn],
            (dp, half * plan.quad + to),
        )

    gains = jnp.zeros((1, plan.width), F32)
    spans = list(range(slots - rows, -1, -rows))
    for number, start in enumerate(spans):
        at = slice(start, start + rows)
        end = start + rows
        for head in range(heads):
            base = head * qk_width
            v_cols = slice(head * HEAD_DIM, (head + 1) * HEAD_DIM)
            q = qk_in[at, base : base + HEAD_DIM] * BF16(0.125)
            k = qk_in[:end, base + HEAD_DIM : base + qk_width]
            v = v_in[:end, v_cols]
            upstream = jnp.concatenate(
                [upstream_all[start // block + i, :, v_cols] for i in range(rows // block)], axis=0
            )
            probs = jnp.exp(masked_scores(q, k, start, length) - lse[head, at])
            dv = tn(probs.astype(BF16), upstream)
            prob_grad = nt(upstream, v)
            inner = jnp.sum(probs * prob_grad, axis=-1, keepdims=True)
            score_grad = (probs * (prob_grad - inner)).astype(BF16)
            dq = nn(score_grad, k) * 0.125
            dk = tn(score_grad, q)
            if end == slots:
                dk_acc[head] = dk
                dv_acc[head] = dv
            else:
                dk_acc[head, :end] += dk
                dv_acc[head, :end] += dv
            dqk = jnp.concatenate([dq, dk_acc[head, at]], axis=-1)
            dqkv[at, base : base + qk_width] = (
                dqk * cosine[at] - swapped_halves(dqk) * sine[at]
            ).astype(BF16)
            v_base = heads * qk_width + head * HEAD_DIM
            dqkv[at, v_base : v_base + HEAD_DIM] = dv_acc[head, at].astype(BF16)
        part = nt(dqkv[at], w[...])
        for i in range(rows // block):
            index = start // block + i
            dnp[index] = part[i * block : (i + 1) * block].astype(BF16)
            pl.when(member != index % plan.quad)(lambda index=index: token_copy(index).start())

            @pl.when(member == index % plan.quad)
            def _(index=index):
                turn = lax.rem(half + index // plan.quad, 2)
                rdn[pl.ds(member, 1), pl.ds(turn, 1)] = dnp[index][None, None]

        values = x[at].astype(F32)
        inverse = lax.rsqrt(jnp.mean(values * values, axis=-1, keepdims=True) + EPSILON)
        gains = gains + jnp.sum(part * values * inverse, axis=0, keepdims=True)
        if number == 0:
            mix_fold.along_y()
            if out_sum:
                out_sum.phase(0)
        if number == len(spans) - 2:
            mix_fold.to_owners()
            if out_sum:
                out_sum.phase(1)
    swap_out.start()
    deal(0)
    first = plan.qkv_cols - (plan.wide - 128)
    if plan.tiled:
        row = lax.broadcasted_iota(jnp.int32, (8, plan.width), 0)
        ends = [jnp.zeros((n, plan.width), F32) for n in (first, 120 - first)]
        extra = jnp.concatenate([ends[0], jnp.where(row == 0, gains, rows8[...]), ends[1]], axis=0)
        extra = jnp.transpose(extra, (1, 0))
    else:
        column = jnp.transpose(jnp.broadcast_to(gains, (128, plan.width)), (1, 0))
        lane = lax.broadcasted_iota(jnp.int32, column.shape, 1)
        extra = jnp.where(lane == first, column, small[...])
    last = plan.wide // 128 - 1

    @pl.loop(0, last + 1)
    def _(i):
        cols = pl.ds(pl.multiple_of(i * 128, 128), 128)
        value = tn(normed[...], dqkv[:, cols])
        value = jnp.where(i == last, value + extra, value)
        value = padded_rows(plan, value, plan.devices).astype(BF16)
        dwq[:, :, :, cols] = value.reshape(plan.dp, plan.ctx, plan.pad_rows, 128)

    mix_fold.across()
    qkv_fold.start()
    qkv_fold.along_y()
    local, width = plan.local, plan.width
    if out_sum:
        out_sum.phase(2)
    for source in range(plan.quad):

        @pl.when(member != source)
        def _(source=source):
            for turn in range(2):
                remote(
                    dnp.at[0], rdn.at[source, turn], n_send.at[0], n_recv.at[source, turn], (dp, ctx)
                ).wait_recv()

    gain_row = around_gains(plan, w)[:1]
    piece = 32

    for j, own in enumerate((ctx, far)):

        @pl.loop(0, block // piece)
        def _(i, j=j, own=own):
            rows_in = pl.ds(pl.multiple_of(i * piece, piece), piece)
            total = rdn[0, j, rows_in].astype(F32)
            for source in range(1, plan.quad):
                total = total + rdn[source, j, rows_in].astype(F32)
            values = x[pl.ds(pl.multiple_of(own * block + i * piece, piece), piece)].astype(F32)
            inverse = lax.rsqrt(jnp.mean(values * values, axis=-1, keepdims=True) + EPSILON)
            scaled = total * gain_row
            result = (
                middle_grad[pl.ds(pl.multiple_of(j * block + i * piece, piece), piece)]
                + inverse * scaled
                - values
                * inverse
                * inverse
                * inverse
                * jnp.mean(scaled * values, axis=-1, keepdims=True)
            )
            if j == 0:
                grad_out[pl.ds(half, 1), rows_in] = result.astype(BF16)[None]
            else:
                grad_away[rows_in] = result.astype(BF16)

    swap_grad = remote(grad_away, grad_out.at[half], s_send.at[1], s_recv.at[1], across)
    swap_grad.start()
    if out_sum:
        out_sum.phase(3)
    branches = out_sum.work.at[0] if out_sum else out_part

    for j in range(2):

        @pl.loop(0, block // piece)
        def _(i, j=j):
            rows_in = pl.ds(pl.multiple_of(i * piece, piece), piece)
            rows_all = pl.ds(pl.multiple_of(j * block + i * piece, piece), piece)
            value = (middle[rows_all] + branches[rows_all].astype(F32)).astype(BF16)
            if j == 0:
                act_out[pl.ds(half, 1), rows_in] = value[None]
            else:
                act_away[rows_in] = value

    swap_act = remote(act_away, act_out.at[half], s_send.at[0], s_recv.at[0], across)
    swap_act.start()
    for i in range(1, plan.dp):
        deal(i)
        if i == 1:
            qkv_fold.to_owners()
    mix_fold.finish()
    qkv_fold.finish()
    swap_act.wait()
    swap_grad.wait()
    swap_out.wait()
    for target in range(plan.group):

        @pl.when(mine != target)
        def _(target=target):
            deal_copy(target).wait_send()
            remote(
                dealt.at[0], rwin.at[target], e_send.at[0], e_recv.at[target], (dp, ctx)
            ).wait_recv()

    for index in range(plan.ctx):
        pl.when(member != index % plan.quad)(lambda index=index: token_copy(index).wait_send())
    if out_sum:
        out_sum.finish()


def back(plan, length, x, w, cosine, sine, normed, qk, v, lse, dw_in, dw_out, out_part, middle, given, collective_id):
    slots, block, width = plan.slots, plan.block, plan.width
    count = 2 * (plan.quad - 1)
    dealt = (plan.group, 2 * plan.pad_rows, plan.hidden_pad)
    summed = out_part.ndim == 2
    rows = (plan.local, width)
    out_scratch = [
        pltpu.VMEM((8,) + rows, BF16),
        pltpu.VMEM((8,) + rows, BF16),
        pltpu.VMEM((7,) + rows, BF16),
        DMA((8,)),
        DMA((8,)),
        DMA((8,)),
        DMA((2, 7)),
        DMA((2, 7)),
        pltpu.VMEM((plan.quad, 2, block, plan.head_cols), BF16),
        pltpu.VMEM((plan.dp, plan.ctx, plan.rows, width), BF16),
        pltpu.VMEM((8, width), F32),
        pltpu.VMEM((plan.local, width), F32),
    ]
    return pl.pallas_call(
        functools.partial(back_kernel, plan, summed),
        out_shape=(
            jax.ShapeDtypeStruct((plan.ctx, plan.pad_rows, plan.wide), BF16),
            jax.ShapeDtypeStruct((2, plan.rows, width), BF16),
            jax.ShapeDtypeStruct(dealt, BF16),
            jax.ShapeDtypeStruct((plan.branches, plan.own_hidden, width), BF16),
            jax.ShapeDtypeStruct((2, block, width), BF16),
            jax.ShapeDtypeStruct((2, block, width), BF16),
        ),
        in_specs=[pl.BlockSpec(memory_space=pltpu.SMEM)]
        + [VMEM] * 10
        + [VMEM if summed else HBM]
        + [VMEM] * (1 + len(given)),
        out_specs=(VMEM,) * 6,
        scratch_shapes=[
            pltpu.VMEM((slots, plan.wide), BF16),
            pltpu.VMEM((plan.heads, slots, HEAD_DIM), F32),
            pltpu.VMEM((plan.heads, slots, HEAD_DIM), F32),
            pltpu.VMEM((plan.ctx, block, plan.head_cols), BF16),
            pltpu.VMEM((plan.ctx, block, width), BF16),
            pltpu.VMEM((plan.quad, 2, block, width), BF16),
            pltpu.VMEM((plan.dp, plan.ctx, plan.pad_rows, plan.wide), BF16),
            pltpu.VMEM((plan.dp,) + dw_in.shape[1:], BF16),
            pltpu.VMEM(dealt, BF16),
            pltpu.VMEM((plan.branches, plan.own_hidden, width), BF16),
            pltpu.VMEM((block, width), BF16),
            pltpu.VMEM((block, width), BF16),
            DMA((count,)),
            DMA((count,)),
            DMA((plan.ctx,)),
            DMA((plan.quad, 2)),
            DMA((plan.dp,)),
            DMA((plan.dp,)),
            DMA((plan.group,)),
            DMA((plan.group,)),
            DMA((3,)),
            DMA((3,)),
        ]
        + fold_scratch(plan, plan.rows, width)
        + [
            pltpu.VMEM((plan.quad, 2, plan.rows, width), BF16),
            pltpu.VMEM((plan.rows, width), BF16),
        ]
        + fold_scratch(plan, plan.pad_rows, plan.wide)
        + ([] if summed else out_scratch),
        compiler_params=params(collective_id),
        cost_estimate=busy(90),
        name="back",
    )(length, x, w, cosine, sine, normed, qk, v, lse, dw_in, dw_out, out_part, middle, *given)


def ffn_kernel(plan, members, n2x, gy, w_in, w_out, pick, out, n2g, dw_in, dw_out):
    hidden, local = plan.hidden_pad, plan.local

    @pl.when(pl.program_id(0) == 0)
    def start():
        dw_in[...] = jnp.zeros_like(dw_in)
        dw_out[...] = jnp.zeros_like(dw_out)

    tokens = members * local
    width = plan.width
    normed = n2x[:, :local].reshape(tokens, width)
    upstream = gy[:, :, : plan.block].reshape(tokens, width)
    mixing = jnp.concatenate(
        [tn(n2x[i, local:, :local], pick[...]) for i in range(members)], axis=0
    )
    pre = nn(normed, w_in[...])
    gate, up = pre[:, :hidden], pre[:, hidden:]
    sigmoid = jax.nn.sigmoid(gate)
    silu = gate * sigmoid
    act = (silu * up).astype(BF16).astype(F32)
    act_mixed = (act * mixing).astype(BF16)
    out[...] = nn(act_mixed, w_out[...]).astype(BF16).reshape(members, local, width)
    act_grad = nt(upstream, w_out[...])
    choice = nt(pick[...], (act * act_grad).astype(BF16)).astype(BF16)
    act_grad = act_grad * mixing
    gate_grad = act_grad * up * sigmoid * (1.0 + gate * (1.0 - sigmoid))
    pre_grad = jnp.concatenate([gate_grad, act_grad * silu], axis=-1).astype(BF16)
    n2g[:, :local] = nt(pre_grad, w_in[...]).astype(BF16).reshape(members, local, width)
    pad = jnp.zeros((MIX_ROWS, width - local), BF16)
    for i in range(members):
        n2g[i, local:] = jnp.concatenate(
            [choice[:, i * local : (i + 1) * local], pad], axis=-1
        )
    dw_in[...] += tn(normed, pre_grad)
    dw_out[...] += tn(act_mixed, upstream)


def ffn(plan, n2x, gy, w_in, w_out, pick):
    members = 2
    local, width, hidden = plan.local, plan.width, plan.hidden_pad
    whole = lambda i: (0, 0)
    part = lambda i: (i, 0, 0)
    return pl.pallas_call(
        functools.partial(ffn_kernel, plan, members),
        grid=(plan.group // members,),
        out_shape=(
            jax.ShapeDtypeStruct((plan.group, local, width), BF16),
            jax.ShapeDtypeStruct((plan.group, local + MIX_ROWS, width), BF16),
            jax.ShapeDtypeStruct((width, 2 * hidden), F32),
            jax.ShapeDtypeStruct((hidden, width), F32),
        ),
        in_specs=[
            pl.BlockSpec((members, local + MIX_ROWS, width), part),
            pl.BlockSpec((members,) + gy.shape[1:], lambda i: (i, 0, 0, 0)),
            pl.BlockSpec((width, 2 * hidden), whole),
            pl.BlockSpec((hidden, width), whole),
            pl.BlockSpec((MIX_ROWS, hidden), whole),
        ],
        out_specs=(
            pl.BlockSpec((members, local, width), part),
            pl.BlockSpec((members, local + MIX_ROWS, width), part),
            pl.BlockSpec((width, 2 * hidden), whole),
            pl.BlockSpec((hidden, width), whole),
        ),
        compiler_params=params(),
        name="ffn",
    )(n2x, gy, w_in, w_out, pick)


STEP_ORDER = ((0, 0, 0), (0, 0, 1), (0, 1, 0), (1, 0, 1), (1, 1, 0), (1, 1, 1), (0, 1, 1), (1, 0, 0))
PART_ORDERS = (("high", "low", "y"), ("low", "y", "high"), ("y", "high", "low"))
PAUSES = {
    3: (('g0', 7), ('g0', 2), ('g0', 1), ('g1', 1), ('g2', 1)),
    4: (('g1', 2), ('g2', 7), ('g2', 2), ('g1', 7)),
    5: (('g0', 4), ('g0', 3), ('g1', 3)),
    7: (('g2', 3), ('g0', 6), ('g2', 6), ('s2', 1)),
    8: (('g1', 4), ('g2', 4)),
    9: (('g1', 6),),
    10: (('s1', 2),),
    11: (('g0', 5), ('g2', 5)),
    13: (('g1', 5), ('s0', 3), ('s2', 3)),
    16: (('s0', 4), ('s1', 4)),
    19: (('s0', 5), ('s1', 5), ('s2', 5)),
    20: (('s0', 2),),
    22: (('s1', 6), ('s2', 6)),
    23: (('s1', 3), ('s2', 4), ('s0', 6)),
    24: (('s0', 7), ('s2', 7), ('s1', 1), ('s2', 2), ('s1', 7), ('s0', 1), ('s2', 0), ('s0', 0), ('s1', 0)),
}


def part_rows(rows):
    cuts = [round_up(rows * i // 3, 16) for i in range(3)] + [rows]
    return [slice(a, b) for a, b in zip(cuts, cuts[1:])]


def named(offset):
    return dict(zip(("high", "low", "y"), offset))


def feeds_of(order, offset):
    at = named(offset)
    phase = min([i for i, axis in enumerate(order) if at[axis]], default=3)
    names = ("high", "low", "y")
    return phase, [tuple(1 if n == axis else at[n] for n in names) for axis in order[:phase]]


def fused_kernel(plan, n2x, gy, w_in, w_out, pick, total, dw_in, dw_out, out_all, n2all, gybuf, acc, away, work, core_buf, bufs, outbuf, gy_sem, out_sem, g_send, g_recv, gc_send, gc_recv, c_send, c_recv, r_send, r_recv):
    grid = Grid(plan)
    at = grid.here()
    local, width, hidden = plan.local, plan.width, plan.hidden_pad
    steps = len(STEP_ORDER)
    partner = grid.device(grid.moved(at, "core", 1))
    here = grid.device(at)
    parts = range(len(PART_ORDERS))
    in_rows, sum_rows = part_rows(local + MIX_ROWS), part_rows(local + MIX_ROWS)

    def absolute(offset):
        where = dict(at)
        for axis, step in named(offset).items():
            if step:
                where = grid.moved(where, axis, step)
        return where

    def slot_of(offset):
        return grid.slot(named(offset))

    def level_of(part, offset):
        reached = named(offset)
        return max([i + 1 for i, axis in enumerate(PART_ORDERS[part]) if reached[axis]], default=0)

    send_index = {}
    for part in parts:
        count = 0
        for offset in STEP_ORDER:
            for axis in PART_ORDERS[part][level_of(part, offset) :]:
                send_index[part, offset, axis] = count
                count += 1

    def pass_on(part, offset):
        level = level_of(part, offset)
        block = grid.block(absolute(offset))
        slot = slot_of(offset)
        span = in_rows[part]
        landing = n2all.at[block, span]
        if level:
            remote(landing, landing, g_send.at[part, 0], g_recv.at[part, slot], here).wait_recv()
        source = landing if level else n2x.at[span]
        for axis in PART_ORDERS[part][level:]:
            seen = grid.slot({**named(offset), axis: 1})
            remote(
                source,
                landing,
                g_send.at[part, send_index[part, offset, axis]],
                g_recv.at[part, seen],
                grid.device(grid.moved(at, axis, 1)),
            ).start()
        remote(source, landing, gc_send.at[part, slot], gc_recv.at[part, slot], partner).start()

    listed = [(kind[0], int(kind[1]), STEP_ORDER[place]) for row in PAUSES.values() for kind, place in row]
    buf_index, seen_slots, first_sums = {}, set(), set()
    for kind, part, offset in listed:
        if kind == "s":
            if offset not in seen_slots:
                seen_slots.add(offset)
                first_sums.add((part, offset))
            if any(offset):
                buf_index[part, offset] = sum(1 for other, _ in buf_index if other == part)

    def add_up(part, offset):
        phase, feeds = feeds_of(PART_ORDERS[part], offset)
        axis = PART_ORDERS[part][phase] if phase < 3 else None
        slot = slot_of(offset)
        span = sum_rows[part]
        if (part, offset) in first_sums:
            remote(away.at[0], core_buf.at[slot], c_send.at[0], c_recv.at[slot], here).wait_recv()
        for feed in feeds:
            index = buf_index[part, feed]
            ref = bufs.at[index, span]
            remote(ref, ref, r_send.at[part, 0], r_recv.at[part, index], here).wait_recv()

        @pl.loop(0, (span.stop - span.start) // 16)
        def _(i):
            rows = pl.ds(pl.multiple_of(span.start + i * 16, 16), 16)
            value = work[slot, rows].astype(F32) + core_buf[slot, rows].astype(F32)
            for feed in feeds:
                value = value + bufs[buf_index[part, feed], rows].astype(F32)
            if axis is None:
                total[rows] = value
            else:
                work[slot, rows] = value.astype(BF16)

        if axis is not None:
            index = buf_index[part, offset]
            remote(
                work.at[slot, span],
                bufs.at[index, span],
                r_send.at[part, index],
                r_recv.at[part, index],
                grid.device(grid.moved(at, axis, 1)),
            ).start()

    def pause(number):
        for kind, place in PAUSES.get(number, ()):
            act = pass_on if kind[0] == "g" else add_up
            act(int(kind[1]), STEP_ORDER[place])

    def pauses(step, turn):
        for i in range(steps):
            if 3 * i + turn in PAUSES:
                pl.when(step == i)(functools.partial(pause, 3 * i + turn))

    def bit(step, index):
        value = 0
        for i, offset in enumerate(STEP_ORDER):
            if offset[index]:
                value = value + jnp.where(step == i, 1, 0)
        return value

    def blocks_of(step):
        where = dict(at)
        offsets = {}
        for index, axis in enumerate(("high", "low", "y")):
            offsets[axis] = bit(step, index)
            where[axis] = lax.rem(at[axis] + offsets[axis], 2)
        mine = grid.block(where)
        other = grid.block(grid.moved(where, "core", 1))
        return mine, other, grid.slot(offsets)

    def gy_loads(step, turn):
        mine, other, _ = blocks_of(step)
        return [
            pltpu.make_async_copy(gy.at[mine, :, : plan.block], gybuf.at[turn, 0], gy_sem.at[turn, 0]),
            pltpu.make_async_copy(gy.at[other, :, : plan.block], gybuf.at[turn, 1], gy_sem.at[turn, 1]),
        ]

    def out_copy(turn, i, block):
        return pltpu.make_async_copy(outbuf.at[turn, i], out_all.at[block], out_sem.at[turn, i])

    for load in gy_loads(0, 0):
        load.start()
    meet(grid.peers(at))
    for part in parts:
        pass_on(part, STEP_ORDER[0])
    n2all[pl.ds(grid.block(at), 1)] = n2x[...][None]

    @pl.loop(0, width // 64)
    def _(i):
        acc[pl.ds(pl.multiple_of(i * 64, 64), 64)] = jnp.zeros((64, 2 * hidden), F32)

    @pl.loop(0, hidden // 64)
    def _(i):
        dw_out[pl.ds(pl.multiple_of(i * 64, 64), 64)] = jnp.zeros((64, width), F32)

    @pl.loop(0, steps)
    def _(step):
        pauses(step, 0)
        mine, other, slot = blocks_of(step)
        turn = lax.rem(step, 2)

        @pl.when(step + 1 < steps)
        def _():
            for load in gy_loads(step + 1, 1 - turn):
                load.start()

        for part in parts:
            ref = n2all.at[other, in_rows[part]]
            remote(ref, ref, gc_send.at[part, 0], gc_recv.at[part, slot], here).wait_recv()
        for load in gy_loads(step, turn):
            load.wait()
        pair = (mine, other)
        normed = jnp.concatenate([n2all[b, :local] for b in pair], axis=0)
        upstream = gybuf[turn].reshape(2 * local, width)
        mixing = jnp.concatenate([tn(n2all[b, local:, :local], pick[...]) for b in pair], axis=0)
        pre = nn(normed, w_in[...])
        gate, up = pre[:, :hidden], pre[:, hidden:]
        sigmoid = jax.nn.sigmoid(gate)
        silu = gate * sigmoid
        act = (silu * up).astype(BF16).astype(F32)
        act_mixed = (act * mixing).astype(BF16)
        pauses(step, 1)

        @pl.when(step >= 2)
        def _():
            for i, block in enumerate(pair):
                out_copy(turn, i, block).wait()

        out = nn(act_mixed, w_out[...]).astype(BF16)
        for i, block in enumerate(pair):
            outbuf[turn, i] = out[i * local : (i + 1) * local]
            out_copy(turn, i, block).start()
        act_grad = nt(upstream, w_out[...])
        choice = nt(pick[...], (act * act_grad).astype(BF16)).astype(BF16)
        act_grad = act_grad * mixing
        gate_grad = act_grad * up * sigmoid * (1.0 + gate * (1.0 - sigmoid))
        pre_grad = jnp.concatenate([gate_grad, act_grad * silu], axis=-1).astype(BF16)
        n2g = nt(pre_grad, w_in[...]).astype(BF16)

        @pl.when(step >= 2)
        def _():
            remote(away.at[turn], core_buf.at[0], c_send.at[turn], c_recv.at[0], partner).wait_send()

        pad = jnp.zeros((MIX_ROWS, width - local), BF16)
        for i, (ref, index) in enumerate(((work, slot), (away, turn))):
            span = slice(i * local, (i + 1) * local)
            ref[index, :local] = n2g[span]
            ref[index, local:] = jnp.concatenate([choice[:, span], pad], axis=-1)
        remote(away.at[turn], core_buf.at[slot], c_send.at[turn], c_recv.at[slot], partner).start()
        pauses(step, 2)
        acc[...] += tn(normed, pre_grad)
        dw_out[...] += tn(act_mixed, upstream)

    pause(3 * steps)
    for turn in range(2):
        for i in range(2):
            out_copy(turn, i, 0).wait()

    @pl.loop(0, width // 64)
    def _(i):
        rows = pl.ds(pl.multiple_of(i * 64, 64), 64)
        dw_in[rows] = acc[rows].astype(BF16)

    for turn in range(2):
        remote(away.at[turn], core_buf.at[0], c_send.at[turn], c_recv.at[0], partner).wait_send()
    for part in parts:
        ref, block = n2all.at[0, in_rows[part]], bufs.at[0, sum_rows[part]]
        for slot in range(steps):
            remote(ref, ref, gc_send.at[part, slot], g_recv.at[part, 0], partner).wait_send()
        for index in range(steps - 1):
            remote(ref, ref, g_send.at[part, index], g_recv.at[part, 0], partner).wait_send()
            remote(block, block, r_send.at[part, index], r_recv.at[part, 0], partner).wait_send()


def fused(plan, n2x, gy, w_in, w_out, pick, collective_id):
    local, width, hidden = plan.local, plan.width, plan.hidden_pad
    steps = len(STEP_ORDER)
    rows = local + MIX_ROWS
    return pl.pallas_call(
        functools.partial(fused_kernel, plan),
        out_shape=(
            jax.ShapeDtypeStruct((rows, width), F32),
            jax.ShapeDtypeStruct((width, 2 * hidden), BF16),
            jax.ShapeDtypeStruct((hidden, width), F32),
            jax.ShapeDtypeStruct((plan.group, local, width), BF16),
        ),
        in_specs=[VMEM, HBM, VMEM, VMEM, VMEM],
        out_specs=(VMEM,) * 3 + (HBM,),
        scratch_shapes=[
            pltpu.VMEM((plan.group, local + MIX_ROWS, width), BF16),
            pltpu.VMEM((2, 2, 2, plan.block, width), BF16),
            pltpu.VMEM((width, 2 * hidden), F32),
            pltpu.VMEM((2, rows, width), BF16),
            pltpu.VMEM((steps, rows, width), BF16),
            pltpu.VMEM((steps, rows, width), BF16),
            pltpu.VMEM((steps - 1, rows, width), BF16),
            pltpu.VMEM((2, 2, local, width), BF16),
            DMA((2, 2)),
            DMA((2, 2)),
            DMA((3, steps - 1)),
            DMA((3, steps)),
            DMA((3, steps)),
            DMA((3, steps)),
            DMA((2,)),
            DMA((steps,)),
            DMA((3, steps - 1)),
            DMA((3, steps - 1)),
        ],
        compiler_params=params(collective_id),
        cost_estimate=busy(100),
        name="fused",
    )(n2x, gy, w_in, w_out, pick)


def turned(value):
    return pltpu.roll(value, 64, 1)


def half_tiles(plan):
    return lax.broadcasted_iota(jnp.int32, (plan.rows, 128), 1) < 64


def column_tiles(plan, pair, gate):
    per = plan.quad // 2
    start = gate * FF + lax.div(pair, per) * (plan.ctx * 64) + lax.rem(pair, per) * 128
    first = lax.div(pair, per) * plan.quad + lax.rem(pair, per) * 2
    return [pl.ds(pl.multiple_of(start + half * plan.quad * 64, 128), 128) for half in range(2)], first


def pack_kernel(plan, both, attn, extra, wq, win):
    low = half_tiles(plan)

    @pl.loop(0, plan.group // 2)
    def _(pair):
        for branch in range(plan.branches):
            made = [[], []]
            for gate in range(2):
                cols, first = column_tiles(plan, pair, gate)
                mine, far = (both[branch, :, col].astype(F32) for col in cols)
                made[0].append(jnp.where(low, mine, turned(far)))
                made[1].append(jnp.where(low, turned(mine), far))
            for i in range(2):
                value = jnp.concatenate(made[i], axis=0).astype(BF16)
                win[pl.ds(first + i, 1), :, branch * 128 : (branch + 1) * 128] = value[None]

    def tile(part, head):
        start = part * HEADS * HEAD_DIM + head // 2 * 128
        return attn[:, start : start + 128].astype(F32)

    def placed(part, head, side):
        value = tile(part, head)
        return value if head % 2 == side else turned(value)

    for member in range(plan.quad):
        heads = [member * 3 + i for i in range(3)]
        for i, head in enumerate(heads):
            value = jnp.where(low, placed(0, head, 0), placed(1, head, 1))
            wq[member, :, i * 128 : (i + 1) * 128] = value.astype(BF16)
        value = jnp.where(low, placed(2, heads[0], 0), placed(2, heads[1], 1))
        wq[member, :, 384:512] = value.astype(BF16)
        value = jnp.where(low, placed(2, heads[2], 0), extra[...].astype(F32))
        wq[member, :, 512:640] = value.astype(BF16)


def pack(plan, both, attn, extra):
    return pl.pallas_call(
        functools.partial(pack_kernel, plan),
        out_shape=(
            jax.ShapeDtypeStruct((plan.quad, plan.rows, plan.wide), BF16),
            jax.ShapeDtypeStruct((plan.group, 2 * plan.rows, plan.hidden_pad), BF16),
        ),
        in_specs=[VMEM] * 3,
        out_specs=(VMEM,) * 2,
        compiler_params=params(),
        cost_estimate=busy(3),
        name="pack",
    )(both, attn, extra)


def unpack_kernel(plan, r_in, r_qkv, r_mix, dw_out, far_out, act, grad, dense_in, expert_in, attn_in, attn_out, gain_one, gain_two, router, dense_out, expert_out, act_out, grad_out):
    act_out[...] = act[...]
    grad_out[...] = grad[...]
    low = half_tiles(plan)
    rows = plan.rows

    @pl.loop(0, plan.group // 2)
    def _(pair):
        first = column_tiles(plan, pair, 0)[1]
        for branch in range(plan.branches):
            cols = slice(branch * 128, (branch + 1) * 128)
            sources = [r_in[first + i, :, cols].astype(F32) for i in range(2)]
            for gate in range(2):
                one, two = (value[gate * rows : (gate + 1) * rows] for value in sources)
                places = column_tiles(plan, pair, gate)[0]
                values = jnp.where(low, one, turned(two)), jnp.where(low, turned(one), two)
                for place_at, value in zip(places, values):
                    if branch == 0:
                        dense_in[:, place_at] = value
                    else:
                        expert_in[:, branch - 1, place_at] = value

    def tile(member, number):
        cols = slice(number * 128, (number + 1) * 128)
        return r_qkv[member, :, cols].astype(F32) + r_qkv[plan.quad + member, :, cols].astype(F32)

    def put(part, head, value):
        start = part * HEADS * HEAD_DIM + head // 2 * 128
        attn_in[:, start : start + 128] = value

    for head in range(0, HEADS, 2):
        one, two = (tile((head + i) // 3, (head + i) % 3) for i in range(2))
        put(0, head, jnp.where(low, one, turned(two)))
        put(1, head, jnp.where(low, turned(one), two))
        halves = []
        for i in range(2):
            member, at = divmod(head + i, 3)
            value = tile(member, 3 + at // 2)
            halves.append(value if at % 2 == i else turned(value))
        put(2, head, jnp.where(low, halves[0], halves[1]))
    total = tile(0, 4)
    for member in range(1, plan.quad):
        total = total + tile(member, 4)
    columns = jnp.transpose(jnp.concatenate([total] * 2, axis=0)[:32], (1, 0))
    gain_one[...] = columns[64:72, :rows][:1]
    gain_two[...] = columns[64:72, :rows][1:2]
    router[...] = total[:, 66 : 66 + plan.experts]
    attn_out[...] = r_mix[0].astype(F32) + r_mix[1].astype(F32)
    half = lax.div(lax.axis_index("ctx"), plan.quad)
    for branch in range(plan.branches):
        value = dw_out[branch, pl.ds(half, 1)][0] + far_out[branch].astype(F32)
        if branch == 0:
            dense_out[...] = value
        else:
            expert_out[:, branch - 1, :] = value


def unpack(plan, r_in, r_qkv, r_mix, dw_out, far_out, act, grad):
    rows, width, own = plan.rows, plan.width, plan.own_hidden
    return pl.pallas_call(
        functools.partial(unpack_kernel, plan),
        out_shape=(
            jax.ShapeDtypeStruct((rows, 2 * FF), F32),
            jax.ShapeDtypeStruct((rows, plan.experts, 2 * FF), F32),
            jax.ShapeDtypeStruct((rows, 3 * HEADS * HEAD_DIM), F32),
            jax.ShapeDtypeStruct((rows, width), F32),
            jax.ShapeDtypeStruct((1, rows), F32),
            jax.ShapeDtypeStruct((1, rows), F32),
            jax.ShapeDtypeStruct((rows, plan.experts), F32),
            jax.ShapeDtypeStruct((own, width), F32),
            jax.ShapeDtypeStruct((own, plan.experts, width), F32),
            jax.ShapeDtypeStruct(act.shape, BF16),
            jax.ShapeDtypeStruct(grad.shape, BF16),
        ),
        in_specs=[VMEM] * 7,
        out_specs=(VMEM,) * 11,
        compiler_params=params(),
        cost_estimate=busy(5),
        name="unpack",
    )(r_in, r_qkv, r_mix, dw_out, far_out, act, grad)


def grid_block(plan, dp, ctx):
    return dp * plan.quad + lax.rem(ctx, plan.quad)


def by_half(half, mine, far, axis):
    return jnp.where(
        half == 0, jnp.stack([mine, far], axis), jnp.stack([far, mine], axis)
    )


def rope_tables(plan):
    half, step = HEAD_DIM // 2, 64
    frequency = np.float32(10000.0) ** (-np.arange(half, dtype=np.float32) / np.float32(half))
    frequency = np.tile(frequency.astype(np.float64), 4)[None]
    coarse = np.arange(0, plan.slots, step)[:, None] * frequency
    fine = np.arange(step)[:, None] * frequency
    sign = np.tile(np.repeat([-1.0, 1.0], half), 2)[None]
    (ca, sa), (cb, sb) = (
        (jnp.asarray(np.cos(a), F32), jnp.asarray(np.sin(a), F32)) for a in (coarse, fine)
    )
    ca, sa, cb, sb = ca[:, None], sa[:, None], cb[None], sb[None]
    cosine = (ca * cb - sa * sb).reshape(plan.slots, 128)
    sine = ((sa * cb + ca * sb) * jnp.asarray(sign, F32)).reshape(plan.slots, 128)
    return cosine, sine


def pick_table(plan):
    table = np.zeros((MIX_ROWS, plan.hidden_pad), np.float32)
    span = HALVES * plan.own_hidden
    for expert in range(plan.experts):
        cols = slice((1 + expert) * span, (2 + expert) * span)
        table[2 + expert, cols] = 1.0
        table[10 + expert, cols] = 1.0
    table[0, :span] = 1.0
    return jnp.asarray(table, BF16)


def pack_qkv(plan, attn_in, attn_gain, ffn_gain, router):
    rows, quad, heads = plan.rows, plan.quad, plan.heads
    qkv = attn_in.reshape(rows, 3, HEADS, HEAD_DIM)
    qkv = jnp.pad(qkv, ((0, 0), (0, 0), (0, quad * heads - HEADS), (0, 0)))
    qkv = qkv.reshape(rows, 3, quad, heads, HEAD_DIM)
    qk = jnp.transpose(qkv[:, :2], (2, 0, 3, 1, 4)).reshape(quad, rows, 2 * plan.head_cols)
    v = jnp.transpose(qkv[:, 2], (1, 0, 2, 3)).reshape(quad, rows, plan.head_cols)
    extra = jnp.concatenate([attn_gain[:, None], ffn_gain[:, None], router], axis=1)
    extra = jnp.pad(extra, ((0, 0), (0, plan.wide - plan.qkv_cols - extra.shape[1])))
    extra = jnp.broadcast_to(extra[None], (quad,) + extra.shape)
    packed = jnp.concatenate([qk, v, extra], axis=-1)
    return jnp.pad(packed, ((0, 0), (0, plan.pad_rows - rows), (0, 0)))


def unpack_qkv(plan, packed):
    rows, quad, heads = plan.rows, plan.quad, plan.heads
    qk = packed[..., : 2 * plan.head_cols].reshape(quad, rows, heads, 2, HEAD_DIM)
    v = packed[..., 2 * plan.head_cols : plan.qkv_cols].reshape(quad, rows, heads, 1, HEAD_DIM)
    qkv = jnp.transpose(jnp.concatenate([qk, v], axis=3), (1, 3, 0, 2, 4))
    qkv = qkv.reshape(rows, 3, quad * heads, HEAD_DIM)[:, :, :HEADS]
    return qkv.reshape(rows, 3 * HEADS * HEAD_DIM)


def pack_in(plan, dense_in, expert_in):
    rows, own = plan.rows, plan.own_hidden
    both = jnp.concatenate([dense_in[:, None], expert_in], axis=1)
    both = both.reshape(rows, plan.branches, 2, plan.dp, HALVES, plan.quad, own)
    both = jnp.transpose(both, (3, 5, 2, 0, 1, 4, 6))
    both = both.reshape(plan.group, 2, rows, plan.hidden)
    pads = ((0, 0), (0, 0), (0, plan.pad_rows - rows), (0, plan.hidden_pad - plan.hidden))
    return jnp.pad(both, pads).reshape(plan.group, 2 * plan.pad_rows, plan.hidden_pad)


def unpack_in(plan, packed):
    rows, own = plan.rows, plan.own_hidden
    both = packed.reshape(plan.group, 2, plan.pad_rows, plan.hidden_pad)
    both = both[:, :, :rows, : plan.hidden]
    both = both.reshape(plan.dp, plan.quad, 2, rows, plan.branches, HALVES, own)
    both = jnp.transpose(both, (3, 4, 2, 0, 5, 1, 6))
    both = both.reshape(rows, plan.branches, 2 * FF).astype(F32)
    return both[:, 0], both[:, 1:]


def shards(
    tokens,
    lengths,
    routes,
    cotangent,
    attn_gain,
    attn_in,
    attn_out,
    ffn_gain,
    router,
    dense_in,
    dense_out,
    expert_in,
    expert_out,
):
    micro, seqs, block, width = tokens.shape
    experts = expert_in.shape[1]
    plan = Plan(lax.axis_size("dp"), lax.axis_size("ctx"), block, width, experts)
    assert micro == HALVES and seqs == 1 and plan.ctx % 4 == 0 and plan.dp % 2 == 0
    quad, local = plan.quad, plan.local
    dp, ctx = place()
    half, member = lax.div(ctx, quad), lax.rem(ctx, quad)
    across = [(i, (i + quad) % plan.ctx) for i in range(plan.ctx)]

    def swap(value):
        return lax.ppermute(value, "ctx", across)

    def pick_mine(value):
        return lax.dynamic_index_in_dim(value, half, 0, keepdims=False)

    def pick_far(value):
        return lax.dynamic_index_in_dim(value, 1 - half, 0, keepdims=False)

    slot = ctx * block + jnp.arange(block, dtype=jnp.int32)
    valid = (slot[None] < lengths).astype(BF16)
    grad_all = cotangent[:, 0] * valid[..., None]
    tail = round_up(plan.rows + 2, 16)
    route_rows = jnp.transpose(routes[:, 0], (0, 2, 1)).astype(BF16)
    route_rows = jnp.pad(route_rows, ((0, 0), (0, tail - plan.rows - 2), (0, width - block)))
    length = pick_mine(lengths)
    out_own = jnp.concatenate([dense_out[:, None], expert_out], axis=1)
    out_own = jnp.transpose(out_own, (1, 0, 2))
    out_far = swap(out_own)
    gyw = jnp.concatenate(
        [grad_all, jnp.broadcast_to(attn_out, (2,) + attn_out.shape), route_rows], axis=1
    )

    if plan.tiled:
        both = jnp.concatenate([dense_in[None], jnp.transpose(expert_in, (1, 0, 2))])
        extra = jnp.concatenate([attn_gain[:, None], ffn_gain[:, None], router], axis=1)
        extra = jnp.pad(extra, ((0, 0), (64, 64 - extra.shape[1])))
        wq, win = pack(plan, both, attn_in, extra)
    else:
        wq = pack_qkv(plan, attn_in, attn_gain, ffn_gain, router)
        win = pack_in(plan, dense_in, expert_in)

    cosine, sine = rope_tables(plan)
    xs, w_seq, normed_seq, qk, v, lse, mixed, gy, w_in, gysrc, *owned = front(
        plan,
        length,
        tokens[:, 0],
        wq,
        win,
        gyw,
        cosine,
        sine,
        1,
    )
    x_seq = xs.reshape(plan.slots, width)
    if plan.tiled:
        n2x, middle, gates, w_mix = owned
    else:
        extra = w_seq[:, plan.qkv_cols :]
        gain_one = extra[:, 0].astype(F32)[None]
        gain_two = extra[:, 1].astype(F32)[None]
        w_route = extra[:, 2 : 2 + experts]
        mixed = jnp.transpose(mixed, (1, 2, 0, 3)).reshape(local, quad * plan.head_cols)[:, :width]
        w_mix = gy[:, :, block : block + plan.rows].reshape(plan.dp, quad, 2, plan.rows, width)
        w_mix = by_half(half, w_mix[:, :, 0], w_mix[:, :, 1], 1).reshape(width, width)

        x = jnp.stack(
            [
                lax.dynamic_index_in_dim(xs, ctx, 0, keepdims=False),
                lax.dynamic_index_in_dim(xs, (1 - half) * quad + member, 0, keepdims=False),
            ]
        )
        x = x.reshape(local, width).astype(F32)
        middle = x + nn(mixed, w_mix)
        inverse_two = lax.rsqrt(jnp.mean(middle * middle, axis=-1, keepdims=True) + EPSILON)
        normed_two = (middle * inverse_two * gain_two).astype(BF16)
        own = lax.dynamic_index_in_dim(gy, grid_block(plan, dp, ctx), 0, keepdims=False)
        grad_y = own[:, :block].reshape(local, width)
        route_local = own[:, block + plan.rows : block + plan.rows + 2, :block]
        route_local = jnp.transpose(route_local, (0, 2, 1)).reshape(local, 2)
        logits = nn(normed_two, w_route)
        choose = (route_local[..., None] == jnp.arange(experts, dtype=BF16)).astype(F32)
        picked = jnp.sum(choose * logits[:, None, :], axis=-1)
        gates = jax.nn.softmax(picked, axis=-1)
        mixing = jnp.sum(gates[..., None] * choose, axis=1)
        mixing_t = mixing.T
        mixing_high = mixing_t.astype(BF16)
        mixing_low = (mixing_t - mixing_high.astype(F32)).astype(BF16)
        pads = ((2, 6 - experts), (0, 0))
        mix_rows = jnp.concatenate([jnp.pad(mixing_high, pads), jnp.pad(mixing_low, pads)])
        mix_rows = mix_rows.at[0].set(1.0)
        mix_rows = jnp.pad(mix_rows, ((0, 0), (0, width - local)))
        n2x = jnp.concatenate([normed_two, mix_rows])

    w_out = by_half(half, out_own, out_far, 1).reshape(plan.hidden, width)
    w_out = jnp.pad(w_out, ((0, plan.hidden_pad - plan.hidden), (0, 0)))
    if plan.dp == 4 and quad == 4:
        n2g_sum, dw_in, dw_out, out_part = fused(plan, n2x, gy, w_in, w_out, pick_table(plan), 3)
    else:
        n2x = gather(plan, n2x, 3)
        out_part, n2g_part, dw_in, dw_out = ffn(plan, n2x, gy, w_in, w_out, pick_table(plan))
        n2g_sum = reduce(plan, n2g_part, 5)
        out_part = reduce(plan, out_part, 7)

    if plan.tiled:
        given = (n2g_sum, gates, n2x, gysrc, w_mix, mixed)
    else:
        normed_two_grad = n2g_sum[:local]
        mixing_grad = n2g_sum[local + 2 : local + 2 + experts, :local].T
        choice_grad = jnp.sum(choose * mixing_grad[:, None, :], axis=-1)
        pick_grad = gates * (choice_grad - jnp.sum(gates * choice_grad, axis=-1, keepdims=True))
        logit_grad = jnp.sum(pick_grad[..., None] * choose, axis=1).astype(BF16)
        router_grad = tn(normed_two, logit_grad)
        normed_two_grad = normed_two_grad + nt(logit_grad, w_route)
        gain_two_grad = jnp.sum(normed_two_grad * middle * inverse_two, axis=0)
        scaled = normed_two_grad * gain_two
        middle_grad = (
            grad_y.astype(F32)
            + inverse_two * scaled
            - middle * inverse_two**3 * jnp.mean(scaled * middle, axis=-1, keepdims=True)
        )
        attn_grad = middle_grad.astype(BF16)
        dw_mix = tn(mixed, attn_grad).astype(BF16).reshape(plan.dp, plan.ctx, plan.rows, width)
        mixed_grad = nt(attn_grad, w_mix).astype(BF16)
        mixed_grad = jnp.pad(mixed_grad, ((0, 0), (0, quad * plan.head_cols - width)))
        mixed_grad = mixed_grad.reshape(2, block, quad, plan.head_cols)
        first = plan.qkv_cols - (plan.wide - 128)
        small = jnp.concatenate([gain_two_grad[:, None], router_grad], axis=1)
        small = jnp.pad(small, ((0, 0), (first + 1, 127 - first - small.shape[1])))
        given = (jnp.transpose(mixed_grad, (2, 0, 1, 3)), dw_mix, small, middle_grad)
    dw_out = dw_out[: plan.hidden].reshape(plan.branches, HALVES, plan.own_hidden, width)
    r_qkv, r_mix, r_in, far_out, activations, input_grad = back(
        plan,
        length,
        x_seq,
        w_seq,
        cosine,
        sine,
        normed_seq,
        qk,
        v,
        lse,
        dw_in.astype(BF16).reshape(plan.dp * HALVES, quad * plan.rows, 2 * plan.hidden_pad),
        dw_out,
        out_part,
        middle,
        given,
        4,
    )

    if plan.tiled:
        results = unpack(plan, r_in, r_qkv, r_mix, dw_out, far_out, activations, input_grad)
        dense_in_grad, expert_in_grad, attn_in_grad, attn_out_grad = results[:4]
        gain_one_grad, gain_two_grad, router_grad = results[4].reshape(-1), results[5].reshape(-1), results[6]
        dense_out_grad, expert_out_grad, activations, input_grad = results[7:]
    else:
        r_qkv = r_qkv[:, : plan.rows].astype(F32).reshape(HALVES, quad, plan.rows, plan.wide)
        r_qkv = jnp.sum(r_qkv, axis=0)
        attn_in_grad = unpack_qkv(plan, r_qkv)
        small = jnp.sum(r_qkv[:, :, plan.qkv_cols :], axis=0)
        attn_out_grad = jnp.sum(r_mix.astype(F32), axis=0)
        gain_one_grad, gain_two_grad, router_grad = small[:, 0], small[:, 1], small[:, 2 : 2 + experts]
        dense_in_grad, expert_in_grad = unpack_in(plan, r_in)
        dw_out = pick_mine(jnp.moveaxis(dw_out, 1, 0)) + far_out.astype(F32)
        dense_out_grad, expert_out_grad = dw_out[0], jnp.transpose(dw_out[1:], (1, 0, 2))
    return (
        activations[:, None],
        input_grad[:, None],
        gain_one_grad,
        attn_in_grad,
        attn_out_grad,
        gain_two_grad,
        router_grad,
        dense_in_grad,
        dense_out_grad,
        expert_in_grad,
        expert_out_grad,
    )


def solution(mesh):
    rows = P(("dp", "ctx"))
    matrix = P(("dp", "ctx"), None)
    cube = P(("dp", "ctx"), None, None)
    slots = P(None, "dp", "ctx", None)
    in_specs = (
        slots,
        P(None, "dp"),
        slots,
        slots,
        rows,
        matrix,
        matrix,
        rows,
        matrix,
        matrix,
        matrix,
        cube,
        cube,
    )
    out_specs = (
        slots,
        slots,
        rows,
        matrix,
        matrix,
        rows,
        matrix,
        matrix,
        matrix,
        cube,
        cube,
    )
    return jax.shard_map(shards, mesh=mesh, in_specs=in_specs, out_specs=out_specs, check_vma=False)
```
